32 devices in a mesh: batch: 2 (over y), seq: 16 (over z, x, core).
Axes of the slice: x: 2, y: 2, z: 4, core: 2. Of those that a mesh axis runs over, the one named last changes fastest.
Arguments:
- tokens: bfloat16 [32, 64, 32, 768], P('batch', None, 'seq'), may hold values from -6 to 6
- lengths: int32 [32], P('batch'), may hold values from 256 to 2048
- labels: int32 [32, 64, 32], P('batch', None, 'seq'), may hold values from 0 to 767
- picked: int32 [32, 64, 32], P('batch', None, 'seq'), may hold values 0 or 1
- cotangent: bfloat16 [32, 64, 32, 768], P('batch', None, 'seq'), may hold values from -6 to 6
- w_in: bfloat16 [1, 768, 3072], P(None, None, ('batch', 'seq')), may hold values from -0.21875 to 0.21875
- b_in: bfloat16 [1, 3072], P(None, ('batch', 'seq')), may hold values from -1.796875 to 1.796875
- w_out: bfloat16 [1, 3072, 768], P(None, ('batch', 'seq')), may hold values from -0.109375 to 0.109375
- shifts: bfloat16 [1, 3, 768], P(None, None, ('batch', 'seq')), may hold values from -1.796875 to 1.796875
- norm_gains: bfloat16 [1, 2, 768], P(None, None, ('batch', 'seq')), may hold values from 0.25 to 1.75
Outputs:
- mixed: bfloat16 [32, 64, 32, 768], P('batch', None, 'seq')
- input_grad: bfloat16 [32, 64, 32, 768], P('batch', None, 'seq')
- grad_w_in: float32 [1, 768, 3072], P(None, None, ('batch', 'seq'))
- grad_b_in: float32 [1, 3072], P(None, ('batch', 'seq'))
- grad_w_out: float32 [1, 3072, 768], P(None, ('batch', 'seq'))
- grad_shifts: float32 [1, 3, 768], P(None, None, ('batch', 'seq'))
- grad_gains: float32 [1, 2, 768], P(None, None, ('batch', 'seq'))
- match_rate: float32 [], replicated
The draws below stay inside these ranges and needn't reach their ends.
All inputs are finite; a program needn't handle non-finite values. No bound on the sum of `picked` on one device may be relied on, other than what follows from the above.
Results may differ from the reference program's by a relative error of at most 0.0095.
Values may be sent and summed in bfloat16 or wider, within the bound.
No kernel may reach another device: no remote copies, remote signals or barrier semaphores. Data moves between devices by JAX's collectives and lax.ppermute only.
A program may use at most 192 MiB of HBM per device.

```python
import math
import jax
import jax.numpy as jnp
from jax import lax

D = 768
FF = 3072
L1 = 64
L2 = 32
LAYERS = 1
L = 2048
SEQS_ALL = 32


def place_ends(entries, rng, smallest, high):
    longest = entries.shape.index(max(entries.shape))
    spots = []
    for shift in (0, 1):
        where = [jax.random.randint(jax.random.fold_in(rng, axis), (), 0, length) for axis, length in enumerate(entries.shape)]
        where[longest] = (where[longest] + shift) % entries.shape[longest]
        spots.append(tuple(where))
    return entries.at[spots[0]].set(smallest).at[spots[1]].set(high)


def block_scale(stream_key, shape, cuts, smallest, high):
    factor_of = 1.0
    for axis_at, parts in cuts:
        draws = jax.random.uniform(jax.random.fold_in(jax.random.fold_in(stream_key, 6), axis_at), (parts,), jnp.float32, smallest / len(cuts), high / len(cuts))
        factor_of = factor_of * jnp.repeat(jnp.exp(draws), shape[axis_at] // parts).reshape((-1,) + (1,) * (len(shape) - 1 - axis_at))
    return factor_of


def normal_values(rng, shape, scale, bound, pieces=(), kind=jnp.bfloat16):
    loudness = block_scale(rng, shape, pieces, -0.22, 0.18) if pieces else 1.0
    drawn = jax.random.normal(rng, shape, jnp.float32) * scale * loudness
    return jnp.minimum(jnp.maximum(drawn, -bound), bound).astype(kind)


def setup_inputs(seed: int = 0) -> dict:
    seeds = jax.random.split(jax.random.key(seed), 11)
    return {
        "tokens": normal_values(seeds[0], (SEQS_ALL, L1, L2, D), 1.0, 6.0, ((0, 2), (2, 16))),
        "lengths": place_ends(jax.random.randint(seeds[1], (SEQS_ALL,), L // 8, L + 1), jax.random.fold_in(seeds[1], 1), L // 8, L).astype(jnp.int32),
        "labels": place_ends(jax.random.randint(seeds[2], (SEQS_ALL, L1, L2), 0, D), jax.random.fold_in(seeds[2], 1), 0, D - 1).astype(jnp.int32),
        "picked": place_ends((jax.random.randint(seeds[3], (SEQS_ALL, L1, L2), 0, 20) < 3).astype(jnp.int32), jax.random.fold_in(seeds[3], 1), 0, 1),
        "cotangent": normal_values(seeds[4], (SEQS_ALL, L1, L2, D), 1.0, 6.0, ((0, 2), (2, 16))),
        "w_in": normal_values(seeds[5], (LAYERS, D, FF), D ** -0.5, 0.21875, ((2, 32),)),
        "b_in": normal_values(seeds[6], (LAYERS, FF), 0.3, 1.796875, ((1, 32),)),
        "w_out": normal_values(seeds[7], (LAYERS, FF, D), FF ** -0.5, 0.109375, ((1, 32),)),
        "shifts": normal_values(seeds[8], (LAYERS, 3, D), 0.3, 1.796875, ((2, 32),)),
        "norm_gains": jnp.clip(1.0 + 0.15 * jax.random.normal(seeds[9], (LAYERS, 2, D), jnp.float32), 0.25, 1.75).astype(jnp.bfloat16),
    }


EPSILON = 1e-12
ROOT_TWO_PI = 0.7978845608028654
HIGHEST = lax.Precision.HIGHEST

@jax.custom_vjp
def low(v):
    return lax.optimization_barrier(v.astype(jnp.bfloat16)).astype(jnp.float32)

@jax.custom_vjp
def low_back(v):
    return v

def low_keep(v):
    return (low(v), None)

def low_pass(kept, grad):
    return (grad,)

def back_keep(v):
    return (v, None)

def back_low(kept, grad):
    return (low(grad),)
low.defvjp(low_keep, low_pass)
low_back.defvjp(back_keep, back_low)

def tables(points):
    numbers = jnp.arange(points, dtype=jnp.int32)
    product_mod = numbers[:, None] * numbers[None, :] % points
    angles = product_mod.astype(jnp.float32) * (2.0 * math.pi / points)
    factor = 1.0 / math.sqrt(points)
    return (low(jnp.cos(angles) * factor), low(jnp.sin(angles) * factor))

def twiddles():
    row_index = jnp.arange(L1, dtype=jnp.int32)[:, None]
    col_index = jnp.arange(L2, dtype=jnp.int32)[None, :]
    angles = (row_index * col_index % L).astype(jnp.float32) * (2.0 * math.pi / L)
    return (jnp.cos(angles)[None, :, :, None], jnp.sin(angles)[None, :, :, None])

def layer_norm(values, gain_rows, shift_rows):
    center = values - lax.optimization_barrier(jnp.mean(values, axis=-1, keepdims=True))
    spread = lax.optimization_barrier(jnp.mean(center * center, axis=-1, keepdims=True))
    return center * lax.rsqrt(spread + EPSILON) * gain_rows + shift_rows

def gelu(values):
    return 0.5 * values * (1.0 + jnp.tanh(ROOT_TWO_PI * (values + 0.044715 * values * values * values)))

def fourier(x_layer, constants):
    short_cos, short_sin, long_cos, long_sin, wide_cos, wide_sin, twiddle_cos, twiddle_sin = constants
    first_cos = low_back(jnp.einsum('kn,gnmd->gkmd', short_cos, x_layer, precision=HIGHEST))
    first_sin = low_back(jnp.einsum('kn,gnmd->gkmd', short_sin, x_layer, precision=HIGHEST))
    turned_cos = low_back(low(first_cos * twiddle_cos - first_sin * twiddle_sin))
    turned_sin = low_back(low(first_cos * twiddle_sin + first_sin * twiddle_cos))
    spectrum_cos = jnp.einsum('kn,gjnd->gkjd', long_cos, turned_cos, precision=HIGHEST) - jnp.einsum('kn,gjnd->gkjd', long_sin, turned_sin, precision=HIGHEST)
    spectrum_sin = jnp.einsum('kn,gjnd->gkjd', long_sin, turned_cos, precision=HIGHEST) + jnp.einsum('kn,gjnd->gkjd', long_cos, turned_sin, precision=HIGHEST)
    spectrum_cos = low(low_back(spectrum_cos))
    spectrum_sin = low(low_back(spectrum_sin))
    mixed = jnp.einsum('gkjd,de->gkje', spectrum_cos, wide_cos, precision=HIGHEST) - jnp.einsum('gkjd,de->gkje', spectrum_sin, wide_sin, precision=HIGHEST)
    return low_back(mixed).reshape(x_layer.shape[0], L, D)

def layer(x_layer, w_first, b_first, w_second, shift_rows, gain_rows, constants):
    group_size = x_layer.shape[0]
    mixed = fourier(x_layer, constants)
    residual = low_back(x_layer).reshape(group_size, L, D) + mixed
    normed = layer_norm(residual, gain_rows[0], shift_rows[1])
    pre_act = low_back(jnp.einsum('gtd,df->gtf', low(normed), w_first, precision=HIGHEST)) + b_first
    summed = normed + low_back(jnp.einsum('gtf,fd->gtd', low(gelu(pre_act)), w_second, precision=HIGHEST)) + shift_rows[0]
    return layer_norm(summed, gain_rows[1], shift_rows[2])

def network(tokens, w_in, b_in, w_out, shifts, norm_gains, valid_mask, constants):

    def one_step(inputs):
        sequence_block, valid_block = inputs
        x_layer = sequence_block * valid_block[..., None]
        result = None
        for number in range(LAYERS):
            result = layer(x_layer, w_in[number], b_in[number], w_out[number], shifts[number], norm_gains[number], constants)
            if number + 1 < LAYERS:
                x_layer = low(low_back(result)).reshape(sequence_block.shape)
        return result
    per_step = min(2, SEQS_ALL)
    blocks = tokens.reshape(SEQS_ALL // per_step, per_step, L1, L2, D)
    valid_blocks = valid_mask.reshape(SEQS_ALL // per_step, per_step, L1, L2)
    return lax.map(jax.checkpoint(one_step), (blocks, valid_blocks))

def reference(tokens, lengths, labels, picked, cotangent, w_in, b_in, w_out, shifts, norm_gains):
    positions = L2 * jnp.arange(L1, dtype=jnp.int32)[:, None] + jnp.arange(L2, dtype=jnp.int32)[None, :]
    valid_mask = (positions[None] < lengths[:, None, None]).astype(jnp.float32)
    constants = tables(L1) + tables(L2) + tables(D) + twiddles()

    def forward(tokens32, w_first, b_first, w_second, shift_all, gain_all):
        return network(tokens32, w_first, b_first, w_second, shift_all, gain_all, valid_mask, constants)
    result, pullback = jax.vjp(forward, tokens.astype(jnp.float32), w_in.astype(jnp.float32), b_in.astype(jnp.float32), w_out.astype(jnp.float32), shifts.astype(jnp.float32), norm_gains.astype(jnp.float32))
    seed_grad = cotangent.astype(jnp.float32).reshape(result.shape)
    grad_tokens, grad_w_in, grad_b_in, grad_w_out, grad_shifts, grad_gains = pullback(seed_grad)
    mixed = result.reshape(SEQS_ALL, L1, L2, D).astype(jnp.bfloat16)
    input_grad = grad_tokens.astype(jnp.bfloat16)
    logits = mixed.astype(jnp.float32)
    highest = lax.optimization_barrier(jnp.max(logits, axis=-1))
    denominator = lax.optimization_barrier(jnp.sum(jnp.exp(logits - highest[..., None]), axis=-1))
    at_label = jnp.take_along_axis(logits, labels[..., None], axis=-1)[..., 0]
    chance = jnp.exp(at_label - highest) / denominator
    weight = picked.astype(jnp.float32) * valid_mask
    match_rate = D * jnp.sum(weight * chance) / jnp.maximum(jnp.sum(weight), 1.0)
    return (mixed, input_grad, grad_w_in, grad_b_in, grad_w_out, grad_shifts, grad_gains, match_rate)
```

```python
import math

import jax
import jax.numpy as jnp
from jax import lax
from jax.sharding import PartitionSpec as P

D = 768
L1 = 64
L2 = 32
L = 2048

EPSILON = 1e-12
ROOT_TWO_PI = 0.7978845608028654
F32 = jnp.float32
BF16 = jnp.bfloat16


def layer_norm(values, gain_rows, shift_rows):
    center = values - jnp.mean(values, axis=-1, keepdims=True)
    spread = jnp.mean(center * center, axis=-1, keepdims=True)
    return center * lax.rsqrt(spread + EPSILON) * gain_rows + shift_rows


def gelu(values):
    return (
        0.5
        * values
        * (1.0 + jnp.tanh(ROOT_TWO_PI * (values + 0.044715 * values * values * values)))
    )


def table_pair(points):
    numbers = jnp.arange(points, dtype=jnp.int32)
    product_mod = numbers[:, None] * numbers[None, :] % points
    angles = product_mod.astype(F32) * (2.0 * math.pi / points)
    factor = 1.0 / math.sqrt(points)
    return (
        (jnp.cos(angles) * factor).astype(BF16),
        (jnp.sin(angles) * factor).astype(BF16),
    )


def twiddles():
    row_index = jnp.arange(L1, dtype=jnp.int32)[None, :]
    col_index = jnp.arange(L2, dtype=jnp.int32)[:, None]
    angles = (row_index * col_index % L).astype(F32) * (2.0 * math.pi / L)
    return jnp.cos(angles)[:, :, None], jnp.sin(angles)[:, :, None]


def swap(values, step):
    axis, mask = step
    size = lax.axis_size(axis)
    return lax.ppermute(values, axis, [(i, i ^ mask) for i in range(size)])


def bits(size):
    masks = []
    mask = size // 2
    while mask >= 1:
        masks.append(mask)
        mask //= 2
    return masks


def xor_gather(block, steps):
    held = block[None]
    for step in steps:
        held = jnp.concatenate([held, swap(held, step)], axis=0)
    return held


def xor_scatter(held, steps):
    for step in reversed(steps):
        half = held.shape[0] // 2
        arrived = swap(held[half:].astype(BF16), step)
        held = held[:half].astype(F32) + arrived.astype(F32)
    return held[0]


def body(tokens, lengths, labels, picked, cotangent, w_in, b_in, w_out, shifts, norm_gains):
    groups = lax.axis_size("seq")
    me = lax.axis_index("seq")
    columns = tokens.shape[2]
    share = w_in.shape[2]

    steps = (
        [("seq", mask) for mask in bits(groups)[:-1]]
        + [("batch", mask) for mask in bits(lax.axis_size("batch"))]
        + [("seq", 1)]
    )
    early = len(bits(groups)) - 1

    own = jnp.stack([w_in[0].T, w_out[0]])
    held = own[None]
    for step in steps[: early - 1]:
        held = jnp.concatenate([held, swap(held, step)], axis=0)
    tokens_late, held = lax.optimization_barrier((tokens, held))
    for step in steps[early - 1 :]:
        held = jnp.concatenate([held, swap(held, step)], axis=0)
    hidden_units = held.shape[0] * share
    w_first = held[:, 0].reshape(hidden_units, D)
    w_second = held[:, 1].reshape(hidden_units, D)
    packed = jnp.concatenate([shifts[0].reshape(-1), norm_gains[0].reshape(-1)])
    packed = lax.all_gather(packed, ("batch", "seq"), axis=0)
    rows = packed.reshape(packed.shape[0], 5, -1).transpose(1, 0, 2).reshape(5, D)
    shifts_f = rows[:3].astype(F32)
    gains_f = rows[3:].astype(F32)
    b_first = xor_gather(b_in[0].astype(F32), steps).reshape(hidden_units)

    short_cos, short_sin = table_pair(L1)
    long_cos, long_sin = table_pair(L2)
    wide_cos, wide_sin = table_pair(D)
    short_table = jnp.concatenate([short_cos, short_sin], axis=0)
    long_table = jnp.stack([jnp.stack([long_cos, -long_sin]), jnp.stack([long_sin, long_cos])])
    both = jnp.eye(2, dtype=BF16)
    pair_table = jnp.einsum("qukm,bc->qkbcum", long_table, both).reshape(4 * L2, 4 * L2)
    wide = jnp.stack([wide_cos, -wide_sin])
    twiddle_cos, twiddle_sin = twiddles()

    x_all = lax.all_to_all(tokens_late, "seq", split_axis=0, concat_axis=0, tiled=True)
    x_all, late_cotangent = lax.optimization_barrier((x_all, cotangent))
    g_all = lax.all_to_all(late_cotangent, "seq", split_axis=0, concat_axis=0, tiled=True)

    length = lengths[me]
    spots = (
        L2 * jnp.arange(L1, dtype=jnp.int32)[None, :] + jnp.arange(L2, dtype=jnp.int32)[:, None]
    )
    x_rows = x_all.transpose(0, 2, 1, 3).reshape(L2, L1, D)
    x_rows = jnp.where((spots < length)[:, :, None], x_rows, jnp.zeros_like(x_rows))

    first = jnp.einsum("kn,mnd->mkd", short_table, x_rows, preferred_element_type=F32)
    first_cos, first_sin = first[:, :L1], first[:, L1:]
    turned_cos = (first_cos * twiddle_cos - first_sin * twiddle_sin).astype(BF16)
    turned_sin = (first_cos * twiddle_sin + first_sin * twiddle_cos).astype(BF16)
    turned = jnp.stack([turned_cos, turned_sin]).reshape(2, L2, 2, L2, D)
    turned = turned.transpose(3, 2, 0, 1, 4).reshape(L2, 4 * L2, D)
    spectrum = jnp.einsum("rk,lkd->lrd", pair_table, turned, preferred_element_type=F32)
    spectrum = spectrum.astype(BF16).reshape(L2, 2, L1, D)
    mixed = jnp.einsum("lund,ude->lne", spectrum, wide, preferred_element_type=F32)
    residual = (x_rows.astype(F32) + mixed).reshape(L, D)

    normed = layer_norm(residual, gains_f[0], shifts_f[1])
    normed_low = normed.astype(BF16)
    pre_act = (
        jnp.einsum("td,fd->tf", normed_low, w_first, preferred_element_type=F32) + b_first
    )
    act_low = gelu(pre_act).astype(BF16)
    summed = normed + jnp.dot(act_low, w_second, preferred_element_type=F32) + shifts_f[0]
    layer_out = layer_norm(summed, gains_f[1], shifts_f[2]).astype(BF16)
    out_rows = layer_out.reshape(groups, columns, L1, D)
    out_rows = lax.all_to_all(out_rows, "seq", split_axis=0, concat_axis=0, tiled=True)
    current = out_rows.transpose(0, 2, 1, 3)

    grad_out = g_all.transpose(0, 2, 1, 3).reshape(L, D).astype(F32)
    unused, pull_second = jax.vjp(layer_norm, summed, gains_f[1], shifts_f[2])
    grad_summed, grad_gain_two, grad_shift_two = pull_second(grad_out)
    grad_bias_two = jnp.sum(grad_summed, axis=0)
    summed_low = grad_summed.astype(BF16)
    grad_w_second = jnp.einsum("tf,td->fd", act_low, summed_low, preferred_element_type=F32)
    grad_act = jnp.einsum("td,fd->tf", summed_low, w_second, preferred_element_type=F32)
    unused_act, pull_gelu = jax.vjp(gelu, pre_act)
    grad_pre = pull_gelu(grad_act)[0]
    grad_b_first = jnp.sum(grad_pre, axis=0)
    pre_low = grad_pre.astype(BF16)
    grad_w_first = jnp.einsum("tf,td->fd", pre_low, normed_low, preferred_element_type=F32)
    grad_normed = grad_summed + jnp.dot(pre_low, w_first, preferred_element_type=F32)
    normed_again, pull_first = jax.vjp(layer_norm, residual, gains_f[0], shifts_f[1])
    grad_residual, grad_gain_one, grad_shift_one = pull_first(grad_normed)
    residual_low = grad_residual.astype(BF16).reshape(L2, L1, D)
    grad_spectrum = jnp.einsum("lne,ude->lund", residual_low, wide, preferred_element_type=F32)
    grad_spectrum = grad_spectrum.astype(BF16).reshape(L2, 4 * L2, D)
    grad_turned = jnp.einsum("rk,lrd->lkd", pair_table, grad_spectrum, preferred_element_type=F32)
    grad_turned = grad_turned.astype(BF16).reshape(L2, 2, 2, L2, D).transpose(2, 3, 1, 0, 4)
    grad_turned = grad_turned.reshape(2, L2, L1, D)
    grad_cos, grad_sin = grad_turned[0], grad_turned[1]
    back_cos = grad_cos * twiddle_cos + grad_sin * twiddle_sin
    back_sin = grad_sin * twiddle_cos - grad_cos * twiddle_sin
    stacked = jnp.concatenate([back_cos, back_sin], axis=1).astype(BF16)
    grad_x = residual_low.astype(F32) + jnp.einsum(
        "kn,mkd->mnd", short_table, stacked, preferred_element_type=F32
    )
    grad_x = jnp.where((spots < length)[:, :, None], grad_x, 0.0).astype(BF16)
    grad_x = grad_x.reshape(groups, columns, L1, D)
    grad_x = lax.all_to_all(grad_x, "seq", split_axis=0, concat_axis=0, tiled=True)
    input_grad = grad_x.transpose(0, 2, 1, 3)

    grad_first = xor_scatter(grad_w_first.reshape(-1, share, D), steps)
    grad_second = xor_scatter(grad_w_second.reshape(-1, share, D), steps)

    hidden_total = hidden_units
    here = lax.axis_index("batch") * groups + me
    blocks = grad_b_first.reshape(-1, share)
    block_of = []
    for number in range(blocks.shape[0]):
        code_seq, code_batch = 0, 0
        for place, (axis, mask) in enumerate(steps):
            if number >> place & 1:
                if axis == "seq":
                    code_seq ^= mask
                else:
                    code_batch ^= mask
        block_of.append(code_batch * groups + code_seq)
    owner = jnp.array(block_of, dtype=jnp.int32) ^ here
    one_hot = (owner[None, :] == jnp.arange(blocks.shape[0], dtype=jnp.int32)[:, None]).astype(F32)
    ordered = jnp.sum(one_hot[:, :, None] * blocks[None], axis=1).reshape(hidden_total // D, D)

    shift_of = jnp.arange(columns, dtype=jnp.int32) + me * columns
    place_of = L2 * jnp.arange(L1, dtype=jnp.int32)[:, None] + shift_of[None, :]
    valid_mask = place_of[None] < lengths[:, None, None]
    logits = out_rows.astype(F32)
    label_rows = labels.transpose(0, 2, 1)
    highest = jnp.max(logits, axis=-1)
    powers = jnp.exp(logits - highest[..., None])
    denominator = jnp.sum(powers, axis=-1)
    features = jnp.arange(D, dtype=jnp.int32)
    top = jnp.sum(jnp.where(features == label_rows[..., None], powers, 0.0), axis=-1)
    chance = top / denominator
    weight = (picked.astype(F32) * valid_mask.astype(F32)).transpose(0, 2, 1)
    sums = jnp.stack([jnp.sum(weight * chance), jnp.sum(weight)])
    sums = jnp.pad(sums, (0, D - 2))[None]
    rest = jnp.concatenate(
        [
            jnp.stack(
                [grad_bias_two, grad_shift_one, grad_shift_two, grad_gain_one, grad_gain_two]
            ),
            ordered,
            sums,
        ]
    )
    rest = lax.psum(rest, ("batch", "seq"))
    slice_of = D // (lax.axis_size("batch") * groups)
    norms = lax.dynamic_slice_in_dim(rest[:5], here * slice_of, slice_of, axis=1)
    grad_b_in = lax.dynamic_slice_in_dim(rest[5:-1].reshape(-1), here * share, share, axis=0)
    match_rate = D * rest[-1, 0] / jnp.maximum(rest[-1, 1], 1.0)
    return (
        current,
        input_grad,
        grad_first.T[None],
        grad_b_in[None],
        grad_second[None],
        norms[:3][None],
        norms[3:][None],
        match_rate,
    )


def solution(mesh):
    in_specs = (
        P("batch", None, "seq", None),
        P("batch"),
        P("batch", None, "seq"),
        P("batch", None, "seq"),
        P("batch", None, "seq", None),
        P(None, None, ("batch", "seq")),
        P(None, ("batch", "seq")),
        P(None, ("batch", "seq"), None),
        P(None, None, ("batch", "seq")),
        P(None, None, ("batch", "seq")),
    )
    out_specs = (
        P("batch", None, "seq", None),
        P("batch", None, "seq", None),
        P(None, None, ("batch", "seq")),
        P(None, ("batch", "seq")),
        P(None, ("batch", "seq"), None),
        P(None, None, ("batch", "seq")),
        P(None, None, ("batch", "seq")),
        P(),
    )
    return jax.shard_map(body, mesh=mesh, in_specs=in_specs, out_specs=out_specs, check_vma=False)
```

```python
import math

import jax
import jax.numpy as jnp
from jax import lax
from jax.sharding import PartitionSpec as P

D = 768
L1 = 64
L2 = 32
L = 2048

EPSILON = 1e-12
ROOT_TWO_PI = 0.7978845608028654
F32 = jnp.float32
BF16 = jnp.bfloat16


def layer_norm(values, gain_rows, shift_rows):
    center = values - jnp.mean(values, axis=-1, keepdims=True)
    spread = jnp.mean(center * center, axis=-1, keepdims=True)
    return center * lax.rsqrt(spread + EPSILON) * gain_rows + shift_rows


def gelu(values):
    return (
        0.5
        * values
        * (1.0 + jnp.tanh(ROOT_TWO_PI * (values + 0.044715 * values * values * values)))
    )


def table_pair(points):
    numbers = jnp.arange(points, dtype=jnp.int32)
    product_mod = numbers[:, None] * numbers[None, :] % points
    angles = product_mod.astype(F32) * (2.0 * math.pi / points)
    factor = 1.0 / math.sqrt(points)
    return (
        (jnp.cos(angles) * factor).astype(BF16),
        (jnp.sin(angles) * factor).astype(BF16),
    )


def twiddles():
    row_index = jnp.arange(L1, dtype=jnp.int32)[None, :]
    col_index = jnp.arange(L2, dtype=jnp.int32)[:, None]
    angles = (row_index * col_index % L).astype(F32) * (2.0 * math.pi / L)
    return jnp.cos(angles)[:, :, None], jnp.sin(angles)[:, :, None]


def swap(values, step):
    axis, mask = step
    size = lax.axis_size(axis)
    return lax.ppermute(values, axis, [(i, i ^ mask) for i in range(size)])


def bits(size):
    masks = []
    mask = size // 2
    while mask >= 1:
        masks.append(mask)
        mask //= 2
    return masks


def widen(held, step):
    return jnp.concatenate([held, swap(held, step)], axis=0)


def xor_sum(values, steps):
    for step in steps:
        values = values + swap(values, step)
    return values


def xor_scatter(held, steps, kind):
    for step in reversed(steps):
        half = held.shape[0] // 2
        arrived = swap(held[half:].astype(kind), step)
        held = held[:half].astype(F32) + arrived.astype(F32)
    return held[0]


def block_codes(steps, groups):
    codes = [0]
    for axis, mask in steps:
        code = mask if axis == "seq" else mask * groups
        codes = codes + [held ^ code for held in codes]
    return jnp.array(codes, dtype=jnp.int32)


def body(tokens, lengths, labels, picked, cotangent, w_in, b_in, w_out, shifts, norm_gains):
    groups = lax.axis_size("seq")
    me = lax.axis_index("seq")
    here = lax.axis_index("batch") * groups + me
    columns = tokens.shape[2]
    share = w_in.shape[2]
    part = shifts.shape[2]
    blocks = groups * lax.axis_size("batch")

    steps = (
        [("seq", mask) for mask in bits(groups)[:-1]]
        + [("batch", mask) for mask in bits(lax.axis_size("batch"))]
        + [("seq", 1)]
    )
    early = len(bits(groups)) - 2
    codes = block_codes(steps, groups)
    owner = codes ^ here
    one_hot = (owner[:, None] == jnp.arange(blocks, dtype=jnp.int32)[None, :]).astype(F32)

    first_held = w_in[0].T[None]
    second_held = w_out[0][None]
    for step in steps[:early]:
        first_held = widen(first_held, step)
        second_held = widen(second_held, step)
    small = jnp.concatenate([b_in[0], shifts[0].reshape(-1), norm_gains[0].reshape(-1)])
    small = small.astype(F32)[None]
    small, first_held, second_held = lax.optimization_barrier((small, first_held, second_held))
    late_small = swap(small, steps[-1])
    first_x = swap(first_held, steps[early])
    second_x = swap(second_held, steps[early])
    tokens_late, small, late_small = lax.optimization_barrier((tokens, small, late_small))
    first_held = jnp.concatenate([first_held, first_x], axis=0)
    second_held = jnp.concatenate([second_held, second_x], axis=0)
    for step in steps[early + 1 :]:
        first_held = widen(first_held, step)
        second_held = widen(second_held, step)
    w_first = first_held.reshape(blocks * share, D)
    w_second = second_held.reshape(blocks * share, D)
    for step in steps[:-1]:
        small = widen(small, step)
    small = widen(small, steps[-1])
    b_first = small[:, :share].reshape(blocks * share)
    rows = jnp.sum(one_hot[:, :, None] * small[:, None, share:], axis=0)
    rows = rows.reshape(blocks, 5, part).transpose(1, 0, 2).reshape(5, D)
    shifts_f = rows[:3]
    gains_f = rows[3:]

    short_cos, short_sin = table_pair(L1)
    long_cos, long_sin = table_pair(L2)
    wide_cos, wide_sin = table_pair(D)
    short_table = jnp.concatenate([short_cos, short_sin], axis=0)
    long_table = jnp.stack([jnp.stack([long_cos, -long_sin]), jnp.stack([long_sin, long_cos])])
    both = jnp.eye(2, dtype=BF16)
    pair_table = jnp.einsum("qukm,bc->qkbcum", long_table, both).reshape(4 * L2, 4 * L2)
    wide = jnp.stack([wide_cos, -wide_sin])
    twiddle_cos, twiddle_sin = twiddles()

    marks = jnp.where(picked > 0, labels, -1).transpose(0, 2, 1).reshape(groups, columns * L1)
    marks = lax.all_to_all(marks, "seq", split_axis=0, concat_axis=0, tiled=True)
    x_all = lax.all_to_all(tokens_late, "seq", split_axis=0, concat_axis=0, tiled=True)
    x_all, late_cotangent = lax.optimization_barrier((x_all, cotangent))
    g_all = lax.all_to_all(late_cotangent, "seq", split_axis=0, concat_axis=0, tiled=True)

    length = lengths[me]
    spots = (
        L2 * jnp.arange(L1, dtype=jnp.int32)[None, :] + jnp.arange(L2, dtype=jnp.int32)[:, None]
    )
    valid = spots < length
    x_rows = x_all.transpose(0, 2, 1, 3).reshape(L2, L1, D)
    x_rows = jnp.where(valid[:, :, None], x_rows, jnp.zeros_like(x_rows))

    first = jnp.einsum("kn,mnd->mkd", short_table, x_rows, preferred_element_type=F32)
    first_cos, first_sin = first[:, :L1], first[:, L1:]
    turned_cos = (first_cos * twiddle_cos - first_sin * twiddle_sin).astype(BF16)
    turned_sin = (first_cos * twiddle_sin + first_sin * twiddle_cos).astype(BF16)
    turned = jnp.stack([turned_cos, turned_sin]).reshape(2, L2, 2, L2, D)
    turned = turned.transpose(3, 2, 0, 1, 4).reshape(L2, 4 * L2, D)
    spectrum = jnp.einsum("rk,lkd->lrd", pair_table, turned, preferred_element_type=F32)
    spectrum = spectrum.astype(BF16).reshape(L2, 2, L1, D)
    mixed = jnp.einsum("lund,ude->lne", spectrum, wide, preferred_element_type=F32)
    residual = (x_rows.astype(F32) + mixed).reshape(L, D)

    normed = layer_norm(residual, gains_f[0], shifts_f[1])
    normed_low = normed.astype(BF16)
    pre_act = (
        jnp.einsum("td,fd->tf", normed_low, w_first, preferred_element_type=F32) + b_first
    )
    act_low = gelu(pre_act).astype(BF16)
    summed = normed + jnp.dot(act_low, w_second, preferred_element_type=F32) + shifts_f[0]
    layer_out = layer_norm(summed, gains_f[1], shifts_f[2]).astype(BF16)
    out_rows = layer_out.reshape(groups, columns, L1, D)
    out_rows = lax.all_to_all(out_rows, "seq", split_axis=0, concat_axis=0, tiled=True)
    current = out_rows.transpose(0, 2, 1, 3)

    logits = layer_out.astype(F32)
    label_rows = marks.reshape(L)
    highest = jnp.max(logits, axis=-1, keepdims=True)
    powers = jnp.exp(logits - highest)
    denominator = jnp.sum(powers, axis=-1)
    features = jnp.arange(D, dtype=jnp.int32)
    top = jnp.sum(jnp.where(features == label_rows[:, None], powers, 0.0), axis=-1)
    weight = jnp.where(valid.reshape(L) & (label_rows >= 0), 1.0, 0.0)
    sums = jnp.stack([jnp.sum(weight * (top / denominator)), jnp.sum(weight)])
    sums = xor_sum(sums, steps)
    match_rate = D * sums[0] / jnp.maximum(sums[1], 1.0)

    grad_out = g_all.transpose(0, 2, 1, 3).reshape(L, D).astype(F32)
    unused, pull_second = jax.vjp(layer_norm, summed, gains_f[1], shifts_f[2])
    grad_summed, grad_gain_two, grad_shift_two = pull_second(grad_out)
    grad_bias_two = jnp.sum(grad_summed, axis=0)
    summed_low = grad_summed.astype(BF16)
    grad_w_second = jnp.einsum("tf,td->fd", act_low, summed_low, preferred_element_type=F32)
    grad_act = jnp.einsum("td,fd->tf", summed_low, w_second, preferred_element_type=F32)
    unused_act, pull_gelu = jax.vjp(gelu, pre_act)
    grad_pre = pull_gelu(grad_act)[0]
    grad_b_first = jnp.sum(grad_pre, axis=0)
    pre_low = grad_pre.astype(BF16)
    grad_w_first = jnp.einsum("tf,td->fd", pre_low, normed_low, preferred_element_type=F32)
    grad_normed = grad_summed + jnp.dot(pre_low, w_first, preferred_element_type=F32)
    normed_again, pull_first = jax.vjp(layer_norm, residual, gains_f[0], shifts_f[1])
    grad_residual, grad_gain_one, grad_shift_one = pull_first(grad_normed)
    residual_low = grad_residual.astype(BF16).reshape(L2, L1, D)
    grad_spectrum = jnp.einsum("lne,ude->lund", residual_low, wide, preferred_element_type=F32)
    grad_spectrum = grad_spectrum.astype(BF16).reshape(L2, 4 * L2, D)
    grad_turned = jnp.einsum("rk,lrd->lkd", pair_table, grad_spectrum, preferred_element_type=F32)
    grad_turned = grad_turned.astype(BF16).reshape(L2, 2, 2, L2, D).transpose(2, 3, 1, 0, 4)
    grad_turned = grad_turned.reshape(2, L2, L1, D)
    grad_cos, grad_sin = grad_turned[0], grad_turned[1]
    back_cos = grad_cos * twiddle_cos + grad_sin * twiddle_sin
    back_sin = grad_sin * twiddle_cos - grad_cos * twiddle_sin
    stacked = jnp.concatenate([back_cos, back_sin], axis=1).astype(BF16)
    grad_x = residual_low.astype(F32) + jnp.einsum(
        "kn,mkd->mnd", short_table, stacked, preferred_element_type=F32
    )
    grad_x = jnp.where(valid[:, :, None], grad_x, 0.0).astype(BF16)
    grad_x = grad_x.reshape(groups, columns, L1, D)
    grad_x = lax.all_to_all(grad_x, "seq", split_axis=0, concat_axis=0, tiled=True)
    input_grad = grad_x.transpose(0, 2, 1, 3)

    grad_first = xor_scatter(grad_w_first.reshape(blocks, share, D), steps, BF16)
    grad_second = xor_scatter(grad_w_second.reshape(blocks, share, D), steps, BF16)
    norms = jnp.stack(
        [grad_bias_two, grad_shift_one, grad_shift_two, grad_gain_one, grad_gain_two]
    )
    norms = norms.reshape(5, blocks, part).transpose(1, 0, 2).reshape(blocks, 5 * part)
    norms = jnp.sum(one_hot[:, :, None] * norms[None], axis=1)
    small_grads = jnp.concatenate([grad_b_first.reshape(blocks, share), norms], axis=1)
    small_grads = xor_scatter(small_grads, steps, F32)
    norms = small_grads[share:].reshape(5, part)
    return (
        current,
        input_grad,
        grad_first.T[None],
        small_grads[:share][None],
        grad_second[None],
        norms[:3][None],
        norms[3:][None],
        match_rate,
    )


def solution(mesh):
    in_specs = (
        P("batch", None, "seq", None),
        P("batch"),
        P("batch", None, "seq"),
        P("batch", None, "seq"),
        P("batch", None, "seq", None),
        P(None, None, ("batch", "seq")),
        P(None, ("batch", "seq")),
        P(None, ("batch", "seq"), None),
        P(None, None, ("batch", "seq")),
        P(None, None, ("batch", "seq")),
    )
    out_specs = (
        P("batch", None, "seq", None),
        P("batch", None, "seq", None),
        P(None, None, ("batch", "seq")),
        P(None, ("batch", "seq")),
        P(None, ("batch", "seq"), None),
        P(None, None, ("batch", "seq")),
        P(None, None, ("batch", "seq")),
        P(),
    )
    return jax.shard_map(body, mesh=mesh, in_specs=in_specs, out_specs=out_specs, check_vma=False)
```

```python
import functools
import math

import jax
import jax.numpy as jnp
from jax import lax
from jax.experimental import pallas as pl
from jax.experimental.pallas import tpu as pltpu
from jax.sharding import PartitionSpec as P

D = 768
L1 = 64
L2 = 32
L = 2048

EPSILON = 1e-12
ROOT_TWO_PI = 0.7978845608028654
CUBIC = ROOT_TWO_PI * 0.044715
F32 = jnp.float32
BF16 = jnp.bfloat16
VMEM_BYTES = 60 << 20


def layer_norm(values, gain_rows, shift_rows):
    center = values - jnp.mean(values, axis=-1, keepdims=True)
    spread = jnp.mean(center * center, axis=-1, keepdims=True)
    return center * lax.rsqrt(spread + EPSILON) * gain_rows + shift_rows


def product(left, right):
    return lax.dot_general(left, right, (((1,), (0,)), ((), ())), preferred_element_type=F32)


def product_over_rows(left, right):
    return lax.dot_general(left, right, (((0,), (0,)), ((), ())), preferred_element_type=F32)


def forward_kernel(u_ref, base_ref, w1_ref, b_ref, w2_ref, act_ref, slope_ref, y_ref, turn_ref, *, tile):
    @pl.when(pl.program_id(0) == 0)
    def _():
        y_ref[...] = base_ref[...]

    turn_ref[...] = w1_ref[...].T

    def step(i, carry):
        rows = pl.ds(pl.multiple_of(i * tile, tile), tile)
        z = product(u_ref[rows, :], turn_ref[...]) + b_ref[...]
        square = z * z
        t = jnp.tanh(z * (ROOT_TWO_PI + CUBIC * square))
        half = 0.5 + 0.5 * t
        a = z * half
        low = a.astype(BF16)
        act_ref[rows, :] = low
        slope = half + (a - a * t) * (ROOT_TWO_PI + (3.0 * CUBIC) * square)
        slope_ref[rows, :] = slope.astype(BF16)
        y_ref[rows, :] += product(low, w2_ref[...])
        return carry

    lax.fori_loop(0, u_ref.shape[0] // tile, step, 0)


def feed_forward(u, base, w1, b, w2, chunk=768, tile=1024):
    tokens, width = u.shape
    units = w1.shape[0]
    whole = lambda: pl.BlockSpec((tokens, width), lambda c: (0, 0), pipeline_mode=pl.Buffered(1))
    weight = lambda: pl.BlockSpec((chunk, width), lambda c: (c, 0))
    acts = lambda: pl.BlockSpec((tokens, chunk), lambda c: (0, c))
    return pl.pallas_call(
        functools.partial(forward_kernel, tile=tile),
        grid=(units // chunk,),
        in_specs=[whole(), whole(), weight(), pl.BlockSpec((1, chunk), lambda c: (0, c)), weight()],
        out_specs=[acts(), acts(), pl.BlockSpec((tokens, width), lambda c: (0, 0))],
        out_shape=[
            jax.ShapeDtypeStruct((tokens, units), BF16),
            jax.ShapeDtypeStruct((tokens, units), BF16),
            jax.ShapeDtypeStruct((tokens, width), F32),
        ],
        scratch_shapes=[pltpu.VMEM((width, chunk), BF16)],
        compiler_params=pltpu.CompilerParams(vmem_limit_bytes=VMEM_BYTES),
        cost_estimate=pl.CostEstimate(
            flops=4 * tokens * units * width, transcendentals=tokens * units, bytes_accessed=60 << 20
        ),
        name="feed_forward",
    )(u, base, w1, b, w2)


def backward_kernel(
    e_ref, u_ref, base_ref, act_ref, slope_ref, w1_ref, w2_ref, dw1_ref, dw2_ref, db_ref, du_ref, f_ref, turn_ref, *, tile
):
    @pl.when(pl.program_id(0) == 0)
    def _():
        du_ref[...] = base_ref[...]

    turn_ref[...] = w2_ref[...].T

    def step(i, db):
        rows = pl.ds(pl.multiple_of(i * tile, tile), tile)
        dz = product(e_ref[rows, :], turn_ref[...]) * slope_ref[rows, :].astype(F32)
        low = dz.astype(BF16)
        f_ref[rows, :] = low
        du_ref[rows, :] += product(low, w1_ref[...])
        return db + jnp.sum(dz.reshape(tile // 8, 8, -1), axis=0)

    chunk = w1_ref.shape[0]
    db = lax.fori_loop(0, e_ref.shape[0] // tile, step, jnp.zeros((8, chunk), F32))
    db_ref[...] = jnp.sum(db, axis=0, keepdims=True)
    dw2_ref[...] = product_over_rows(act_ref[...], e_ref[...]).astype(BF16)
    dw1_ref[...] = product_over_rows(f_ref[...], u_ref[...]).astype(BF16)


def feed_backward(e, u, base, act, slope, w1, w2, start, units, chunk=512, tile=1024):
    tokens, width = u.shape
    first = start // chunk
    whole = lambda: pl.BlockSpec((tokens, width), lambda c: (0, 0), pipeline_mode=pl.Buffered(1))
    weight = lambda: pl.BlockSpec((chunk, width), lambda c: (c + first, 0))
    acts = lambda: pl.BlockSpec((tokens, chunk), lambda c: (0, c + first))
    grads = lambda: pl.BlockSpec((chunk, width), lambda c: (c, 0))
    return pl.pallas_call(
        functools.partial(backward_kernel, tile=tile),
        grid=(units // chunk,),
        in_specs=[whole(), whole(), whole(), acts(), acts(), weight(), weight()],
        out_specs=[
            grads(),
            grads(),
            pl.BlockSpec((1, chunk), lambda c: (0, c)),
            pl.BlockSpec((tokens, width), lambda c: (0, 0)),
        ],
        out_shape=[
            jax.ShapeDtypeStruct((units, width), BF16),
            jax.ShapeDtypeStruct((units, width), BF16),
            jax.ShapeDtypeStruct((1, units), F32),
            jax.ShapeDtypeStruct((tokens, width), F32),
        ],
        scratch_shapes=[pltpu.VMEM((tokens, chunk), BF16), pltpu.VMEM((width, chunk), BF16)],
        compiler_params=pltpu.CompilerParams(vmem_limit_bytes=VMEM_BYTES),
        cost_estimate=pl.CostEstimate(
            flops=8 * tokens * units * width, transcendentals=0, bytes_accessed=40 << 20
        ),
        name="feed_backward",
    )(e, u, base, act, slope, w1, w2)


def table_pair(points, scale=None):
    numbers = jnp.arange(points, dtype=jnp.int32)
    coarse = 32 * jnp.arange(points // 32, dtype=jnp.int32)
    fine = jnp.arange(32, dtype=jnp.int32)

    def waves(rows):
        angles = (rows[:, None] * numbers[None, :] % points).astype(F32) * (2.0 * math.pi / points)
        return jnp.cos(angles), jnp.sin(angles)

    factor = 1.0 / math.sqrt(points)
    if points <= 64:
        cosine, sine = waves(numbers)
    else:
        coarse_cos, coarse_sin = waves(coarse)
        fine_cos, fine_sin = waves(fine)
        coarse_cos, coarse_sin, fine_cos, fine_sin = lax.optimization_barrier(
            (coarse_cos, coarse_sin, fine_cos, fine_sin)
        )
        coarse_cos, coarse_sin = coarse_cos[:, None], coarse_sin[:, None]
        fine_cos, fine_sin = fine_cos[None], fine_sin[None]
        cosine = (coarse_cos * fine_cos - coarse_sin * fine_sin).reshape(points, points)
        sine = (coarse_sin * fine_cos + coarse_cos * fine_sin).reshape(points, points)
    return (cosine * factor).astype(BF16), (sine * factor).astype(BF16)


def twiddles():
    row_index = jnp.arange(L1, dtype=jnp.int32)[None, :]
    col_index = jnp.arange(L2, dtype=jnp.int32)[:, None]
    angles = (row_index * col_index % L).astype(F32) * (2.0 * math.pi / L)
    return jnp.cos(angles)[:, :, None], jnp.sin(angles)[:, :, None]


def swap(values, step):
    axis, mask = step
    size = lax.axis_size(axis)
    return lax.ppermute(values, axis, [(i, i ^ mask) for i in range(size)])


def bits(size):
    masks = []
    mask = size // 2
    while mask >= 1:
        masks.append(mask)
        mask //= 2
    return masks


def widen(held, step):
    return jnp.concatenate([held, swap(held, step)], axis=0)


def xor_sum(values, steps):
    for step in steps:
        values = values + swap(values, step)
    return values


def widen_codes(codes, steps, groups):
    for axis, mask in steps:
        code = mask if axis == "seq" else mask * groups
        codes = codes + [held ^ code for held in codes]
    return codes


def spread(plane, steps_batch, step_core):
    pieces = [plane]
    for step in steps_batch:
        pieces = pieces + [swap(piece, step) for piece in pieces]
    whole = []
    for piece in pieces:
        whole += [piece, swap(piece, step_core)]
    return jnp.concatenate(whole, axis=0)


def fold(held, arrived):
    return held.astype(F32) + arrived.astype(F32)


def fold_core(blocks, pieces, step_core, kind):
    share = blocks.reshape((pieces, 2, -1) + blocks.shape[1:])
    return [fold(share[i, 0], swap(share[i, 1].astype(kind), step_core)) for i in range(pieces)]


def fold_planes(pieces, steps_batch, kind):
    for step in reversed(steps_batch):
        half = len(pieces) // 2
        pieces = [
            fold(pieces[i], swap(pieces[i + half].astype(kind), step)) for i in range(half)
        ]
    return pieces[0]


def fold_rest(held, steps_plane, kind):
    for step in reversed(steps_plane):
        half = held.shape[0] // 2
        held = fold(held[:half], swap(held[half:].astype(kind), step))
    return held[0]


def body(tokens, lengths, labels, picked, cotangent, w_in, b_in, w_out, shifts, norm_gains):
    groups = lax.axis_size("seq")
    me = lax.axis_index("seq")
    here = lax.axis_index("batch") * groups + me
    columns = tokens.shape[2]
    share = w_in.shape[2]
    part = shifts.shape[2]
    blocks = groups * lax.axis_size("batch")

    steps_plane = [("seq", mask) for mask in bits(groups)[:-1]]
    steps_batch = [("batch", mask) for mask in bits(lax.axis_size("batch"))]
    step_core = ("seq", 1)
    steps = [step_core] + steps_plane + steps_batch
    numbers = jnp.arange(blocks, dtype=jnp.int32)

    codes = []
    for code in widen_codes([0], steps_batch, groups):
        codes += widen_codes(widen_codes([code], steps_plane, groups), [step_core], groups)
    owner = jnp.array(codes, dtype=jnp.int32) ^ here
    one_hot = (owner[:, None] == numbers[None, :]).astype(F32)
    small_owner = jnp.array(widen_codes([0], steps, groups), dtype=jnp.int32) ^ here
    small_hot = (small_owner[:, None] == numbers[None, :]).astype(F32)

    first_held = w_in[0].T[None]
    second_held = w_out[0][None]
    bias_held = b_in
    for step in steps_plane[:-1]:
        first_held = widen(first_held, step)
        second_held = widen(second_held, step)
    small = jnp.concatenate([shifts[0].reshape(-1), norm_gains[0].reshape(-1)])
    small = small.astype(F32)[None]
    small, first_held, second_held = lax.optimization_barrier((small, first_held, second_held))
    small = widen(small, step_core)
    first_x = swap(first_held, steps_plane[-1])
    second_x = swap(second_held, steps_plane[-1])
    marks = jnp.where(picked > 0, labels, -1).transpose(0, 2, 1).reshape(groups, columns * L1)
    marks = lax.all_to_all(marks, "seq", split_axis=0, concat_axis=0, tiled=True)
    tokens_late, small, marks = lax.optimization_barrier((tokens, small, marks))
    first_held = jnp.concatenate([first_held, first_x], axis=0)
    second_held = jnp.concatenate([second_held, second_x], axis=0)

    wide_cos, wide_sin = table_pair(D)
    wide = jnp.stack([wide_cos, -wide_sin])
    twiddle_cos, twiddle_sin = twiddles()
    first_held, second_held, wide, twiddle_cos, twiddle_sin = lax.optimization_barrier(
        (first_held, second_held, wide, twiddle_cos, twiddle_sin)
    )
    w_first = spread(first_held, steps_batch, step_core).reshape(blocks * share, D)
    w_second = spread(second_held, steps_batch, step_core).reshape(blocks * share, D)
    for step in steps_plane:
        bias_held = widen(bias_held, step)
    b_first = spread(bias_held, steps_batch, step_core).reshape(1, blocks * share).astype(F32)
    for step in steps[1:]:
        small = widen(small, step)
    rows = jnp.sum(small_hot[:, :, None] * small[:, None], axis=0)
    rows = rows.reshape(blocks, 5, part).transpose(1, 0, 2).reshape(5, D)
    shifts_f = rows[:3]
    gains_f = rows[3:]

    short_cos, short_sin = table_pair(L1)
    long_cos, long_sin = table_pair(L2)
    short_table = jnp.concatenate([short_cos, short_sin], axis=0)
    long_table = jnp.stack([jnp.stack([long_cos, -long_sin]), jnp.stack([long_sin, long_cos])])
    both = jnp.eye(2, dtype=BF16)
    pair_table = jnp.einsum("qukm,bc->qkbcum", long_table, both).reshape(4 * L2, 4 * L2)

    x_all = lax.all_to_all(tokens_late, "seq", split_axis=0, concat_axis=0, tiled=True)
    x_all, late_cotangent = lax.optimization_barrier((x_all, cotangent))
    g_all = lax.all_to_all(late_cotangent, "seq", split_axis=0, concat_axis=0, tiled=True)

    length = lengths[me]
    spots = (
        L2 * jnp.arange(L1, dtype=jnp.int32)[None, :] + jnp.arange(L2, dtype=jnp.int32)[:, None]
    )
    valid = spots < length
    x_rows = x_all.transpose(0, 2, 1, 3).reshape(L2, L1, D)
    x_rows = jnp.where(valid[:, :, None], x_rows, jnp.zeros_like(x_rows))

    first = jnp.einsum("kn,mnd->mkd", short_table, x_rows, preferred_element_type=F32)
    first_cos, first_sin = first[:, :L1], first[:, L1:]
    turned_cos = (first_cos * twiddle_cos - first_sin * twiddle_sin).astype(BF16)
    turned_sin = (first_cos * twiddle_sin + first_sin * twiddle_cos).astype(BF16)
    turned = jnp.stack([turned_cos, turned_sin]).reshape(2, L2, 2, L2, D)
    turned = turned.transpose(3, 2, 0, 1, 4).reshape(L2, 4 * L2, D)
    spectrum = jnp.einsum("rk,lkd->lrd", pair_table, turned, preferred_element_type=F32)
    spectrum = spectrum.astype(BF16).reshape(L2, 2, L1, D)
    mixed = jnp.einsum("lund,ude->lne", spectrum, wide, preferred_element_type=F32)
    residual = (x_rows.astype(F32) + mixed).reshape(L, D)

    normed = layer_norm(residual, gains_f[0], shifts_f[1])
    normed_low = normed.astype(BF16)
    act_low, slope, summed = feed_forward(
        normed_low, normed + shifts_f[0], w_first, b_first, w_second
    )
    layer_out = layer_norm(summed, gains_f[1], shifts_f[2]).astype(BF16)
    out_rows = layer_out.reshape(groups, columns, L1, D)
    out_rows = lax.all_to_all(out_rows, "seq", split_axis=0, concat_axis=0, tiled=True)
    current = out_rows.transpose(0, 2, 1, 3)

    logits = layer_out.astype(F32)
    label_rows = marks.reshape(L)
    highest = jnp.max(logits, axis=-1, keepdims=True)
    powers = jnp.exp(logits - highest)
    denominator = jnp.sum(powers, axis=-1)
    features = jnp.arange(D, dtype=jnp.int32)
    top = jnp.sum(jnp.where(features == label_rows[:, None], powers, 0.0), axis=-1)
    weight = jnp.where(valid.reshape(L) & (label_rows >= 0), 1.0, 0.0)
    sums = jnp.stack([jnp.sum(weight * (top / denominator)), jnp.sum(weight)])
    sums = xor_sum(sums, steps)
    match_rate = D * sums[0] / jnp.maximum(sums[1], 1.0)

    grad_out = g_all.transpose(0, 2, 1, 3).reshape(L, D).astype(F32)
    unused, pull_second = jax.vjp(layer_norm, summed, gains_f[1], shifts_f[2])
    grad_summed, grad_gain_two, grad_shift_two = pull_second(grad_out)
    grad_bias_two = jnp.sum(grad_summed, axis=0)
    summed_low = grad_summed.astype(BF16)
    units = blocks * share
    planes = lax.axis_size("batch")
    upper = feed_backward(
        summed_low, normed_low, grad_summed, act_low, slope, w_first, w_second, units // 2, units // 2
    )
    lower = feed_backward(
        summed_low, normed_low, upper[3], act_low, slope, w_first, w_second, 0, units // 2
    )
    grad_normed = lower[3]
    folded = []
    for number in range(2):
        halves = [
            fold_core(side[number].reshape(blocks // 2, share, D), planes // 2, step_core, BF16)
            for side in (lower, upper)
        ]
        folded.append(fold_planes(halves[0] + halves[1], steps_batch, BF16))
    grad_b_first = jnp.concatenate([lower[2], upper[2]], axis=1)
    normed_again, pull_first = jax.vjp(layer_norm, residual, gains_f[0], shifts_f[1])
    grad_residual, grad_gain_one, grad_shift_one = pull_first(grad_normed)
    residual_low = grad_residual.astype(BF16).reshape(L2, L1, D)
    grad_spectrum = jnp.einsum("lne,ude->lund", residual_low, wide, preferred_element_type=F32)
    grad_spectrum = grad_spectrum.astype(BF16).reshape(L2, 4 * L2, D)
    grad_turned = jnp.einsum("rk,lrd->lkd", pair_table, grad_spectrum, preferred_element_type=F32)
    grad_turned = grad_turned.astype(BF16).reshape(L2, 2, 2, L2, D).transpose(2, 3, 1, 0, 4)
    grad_turned = grad_turned.reshape(2, L2, L1, D)
    grad_cos, grad_sin = grad_turned[0], grad_turned[1]
    back_cos = grad_cos * twiddle_cos + grad_sin * twiddle_sin
    back_sin = grad_sin * twiddle_cos - grad_cos * twiddle_sin
    stacked = jnp.concatenate([back_cos, back_sin], axis=1).astype(BF16)
    grad_x = residual_low.astype(F32) + jnp.einsum(
        "kn,mkd->mnd", short_table, stacked, preferred_element_type=F32
    )
    grad_x = jnp.where(valid[:, :, None], grad_x, 0.0).astype(BF16)
    grad_x = grad_x.reshape(groups, columns, L1, D)
    grad_x, folded = lax.optimization_barrier((grad_x, folded))
    grad_first, grad_second = [fold_rest(held, steps_plane, BF16) for held in folded]
    grad_x = lax.all_to_all(grad_x, "seq", split_axis=0, concat_axis=0, tiled=True)
    input_grad = grad_x.transpose(0, 2, 1, 3)

    norms = jnp.stack(
        [grad_bias_two, grad_shift_one, grad_shift_two, grad_gain_one, grad_gain_two]
    )
    norms = norms.reshape(5, blocks, part).transpose(1, 0, 2).reshape(blocks, 5 * part)
    norms = jnp.sum(one_hot[:, :, None] * norms[None], axis=1)
    small_grads = jnp.concatenate([grad_b_first.reshape(blocks, share), norms], axis=1)
    small_grads = fold_core(small_grads, planes, step_core, F32)
    small_grads = fold_rest(fold_planes(small_grads, steps_batch, F32), steps_plane, F32)
    norms = small_grads[share:].reshape(5, part)
    return (
        current,
        input_grad,
        grad_first.T[None],
        small_grads[:share][None],
        grad_second[None],
        norms[:3][None],
        norms[3:][None],
        match_rate,
    )


def solution(mesh):
    in_specs = (
        P("batch", None, "seq", None),
        P("batch"),
        P("batch", None, "seq"),
        P("batch", None, "seq"),
        P("batch", None, "seq", None),
        P(None, None, ("batch", "seq")),
        P(None, ("batch", "seq")),
        P(None, ("batch", "seq"), None),
        P(None, None, ("batch", "seq")),
        P(None, None, ("batch", "seq")),
    )
    out_specs = (
        P("batch", None, "seq", None),
        P("batch", None, "seq", None),
        P(None, None, ("batch", "seq")),
        P(None, ("batch", "seq")),
        P(None, ("batch", "seq"), None),
        P(None, None, ("batch", "seq")),
        P(None, None, ("batch", "seq")),
        P(),
    )
    return jax.shard_map(body, mesh=mesh, in_specs=in_specs, out_specs=out_specs, check_vma=False)
```

```python
import functools
import math

import jax
import jax.numpy as jnp
from jax import lax
from jax.experimental import pallas as pl
from jax.experimental.layout import Layout, with_layout_constraint
from jax.experimental.pallas import tpu as pltpu
from jax.sharding import PartitionSpec as P

D = 768
L1 = 64
L2 = 32
L = 2048

EPSILON = 1e-12
ROOT_TWO_PI = 0.7978845608028654
CUBIC = ROOT_TWO_PI * 0.044715
F32 = jnp.float32
BF16 = jnp.bfloat16
VMEM_BYTES = 60 << 20


def layer_norm(values, gain_rows, shift_rows):
    center = values - jnp.mean(values, axis=-1, keepdims=True)
    spread = jnp.mean(center * center, axis=-1, keepdims=True)
    return center * lax.rsqrt(spread + EPSILON) * gain_rows + shift_rows


def product(left, right):
    return lax.dot_general(left, right, (((1,), (0,)), ((), ())), preferred_element_type=F32)


def product_over_rows(left, right):
    return lax.dot_general(left, right, (((0,), (0,)), ((), ())), preferred_element_type=F32)


def fetch_weights(pieces, holder, sems, chunk):
    rows = pieces[0].shape[0]
    step = pl.program_id(0)
    copies = [
        pltpu.make_async_copy(piece, holder.at[pl.ds(i * rows, rows), :], sems.at[i])
        for i, piece in enumerate(pieces)
    ]

    @pl.when(step == 0)
    def _():
        for copy in copies:
            copy.start()

    for number in range(rows * len(pieces) // chunk):
        needed = [copy for i, copy in enumerate(copies) if i * rows // chunk == number]
        if needed:

            @pl.when(step == number)
            def _():
                for copy in needed:
                    copy.wait()


def forward_kernel(*refs, tile, count, chunk):
    u_ref, base_ref, b_ref = refs[:3]
    firsts, seconds = refs[3 : 3 + count], refs[3 + count : 3 + 2 * count]
    act_ref, slope_ref, y_ref, w1_ref, w2_ref, turn_ref, sem1, sem2, sem3 = refs[3 + 2 * count :]
    start = pltpu.make_async_copy(base_ref, y_ref, sem3.at[0])

    @pl.when(pl.program_id(0) == 0)
    def _():
        start.start()

    fetch_weights(firsts, w1_ref, sem1, chunk)
    fetch_weights(seconds, w2_ref, sem2, chunk)
    here = pl.ds(pl.multiple_of(pl.program_id(0) * chunk, chunk), chunk)

    @pl.when(pl.program_id(0) == 0)
    def _():
        start.wait()

    turn_ref[...] = w1_ref[here, :].T

    def step(i, carry):
        rows = pl.ds(pl.multiple_of(i * tile, tile), tile)
        z = product(u_ref[rows, :], turn_ref[...]) + b_ref[...]
        square = z * z
        t = jnp.tanh(z * (ROOT_TWO_PI + CUBIC * square))
        half = 0.5 + 0.5 * t
        a = z * half
        low = a.astype(BF16)
        act_ref[rows, :] = low
        slope = half + (a - a * t) * (ROOT_TWO_PI + (3.0 * CUBIC) * square)
        slope_ref[rows, :] = slope.astype(BF16)
        y_ref[rows, :] += product(low, w2_ref[here, :])
        return carry

    lax.fori_loop(0, u_ref.shape[0] // tile, step, 0)


def whole_block(shape, buffers=1):
    return pl.BlockSpec(shape, lambda c: (0, 0), pipeline_mode=pl.Buffered(buffers))


def feed_forward(u, base, firsts, b, seconds, chunk=768, tile=1024):
    tokens, width = u.shape
    count = len(firsts)
    units = count * firsts[0].shape[0]
    acts = lambda: pl.BlockSpec((tokens, chunk), lambda c: (0, c))
    far = [pl.BlockSpec(memory_space=pl.ANY)] * (2 * count)
    return pl.pallas_call(
        functools.partial(forward_kernel, tile=tile, count=count, chunk=chunk),
        grid=(units // chunk,),
        in_specs=[
            whole_block((tokens, width)),
            pl.BlockSpec(memory_space=pl.ANY),
            pl.BlockSpec((1, chunk), lambda c: (0, c)),
        ]
        + far,
        out_specs=[acts(), acts(), pl.BlockSpec((tokens, width), lambda c: (0, 0))],
        out_shape=[
            jax.ShapeDtypeStruct((tokens, units), BF16),
            jax.ShapeDtypeStruct((tokens, units), BF16),
            jax.ShapeDtypeStruct((tokens, width), F32),
        ],
        scratch_shapes=[
            pltpu.VMEM((units, width), BF16),
            pltpu.VMEM((units, width), BF16),
            pltpu.VMEM((width, chunk), BF16),
            pltpu.SemaphoreType.DMA((count,)),
            pltpu.SemaphoreType.DMA((count,)),
            pltpu.SemaphoreType.DMA((1,)),
        ],
        compiler_params=pltpu.CompilerParams(vmem_limit_bytes=VMEM_BYTES),
        cost_estimate=pl.CostEstimate(
            flops=4 * tokens * units * width, transcendentals=tokens * units, bytes_accessed=60 << 20
        ),
        name="feed_forward",
    )(u, base, b, *firsts, *seconds)


def backward_kernel(*refs, tile, count, chunk):
    e_ref, u_ref, base_ref, act_ref, slope_ref = refs[:5]
    firsts, seconds = refs[5 : 5 + count], refs[5 + count : 5 + 2 * count]
    dw1_ref, dw2_ref, db_ref, du_ref, w1_ref, w2_ref, f_ref, turn_ref, sem1, sem2, sem3 = (
        refs[5 + 2 * count :]
    )
    start = pltpu.make_async_copy(base_ref, du_ref, sem3.at[0])

    @pl.when(pl.program_id(0) == 0)
    def _():
        start.start()

    fetch_weights(firsts, w1_ref, sem1, chunk)
    fetch_weights(seconds, w2_ref, sem2, chunk)
    here = pl.ds(pl.multiple_of(pl.program_id(0) * chunk, chunk), chunk)

    @pl.when(pl.program_id(0) == 0)
    def _():
        start.wait()

    turn_ref[...] = w2_ref[here, :].T

    def step(i, db):
        rows = pl.ds(pl.multiple_of(i * tile, tile), tile)
        dz = product(e_ref[rows, :], turn_ref[...]) * slope_ref[rows, :].astype(F32)
        low = dz.astype(BF16)
        f_ref[rows, :] = low
        du_ref[rows, :] += product(low, w1_ref[here, :])
        return db + jnp.sum(dz.reshape(tile // 8, 8, -1), axis=0)

    db = lax.fori_loop(0, e_ref.shape[0] // tile, step, jnp.zeros((8, chunk), F32))
    db_ref[...] = jnp.sum(db, axis=0, keepdims=True)
    dw2_ref[...] = product_over_rows(act_ref[...], e_ref[...]).astype(BF16)
    dw1_ref[...] = product_over_rows(f_ref[...], u_ref[...]).astype(BF16)


def feed_backward(e, u, base, act, slope, firsts, seconds, chunk=512, tile=1024):
    tokens, width = u.shape
    count = len(firsts)
    units = count * firsts[0].shape[0]
    acts = lambda: pl.BlockSpec((tokens, chunk), lambda c: (0, c))
    grads = lambda: pl.BlockSpec((chunk, width), lambda c: (c, 0))
    far = [pl.BlockSpec(memory_space=pl.ANY)] * (2 * count)
    return pl.pallas_call(
        functools.partial(backward_kernel, tile=tile, count=count, chunk=chunk),
        grid=(units // chunk,),
        in_specs=[
            whole_block((tokens, width)),
            whole_block((tokens, width)),
            pl.BlockSpec(memory_space=pl.ANY),
            acts(),
            acts(),
        ]
        + far,
        out_specs=[
            grads(),
            grads(),
            pl.BlockSpec((1, chunk), lambda c: (0, c)),
            pl.BlockSpec((tokens, width), lambda c: (0, 0)),
        ],
        out_shape=[
            jax.ShapeDtypeStruct((units, width), BF16),
            jax.ShapeDtypeStruct((units, width), BF16),
            jax.ShapeDtypeStruct((1, units), F32),
            jax.ShapeDtypeStruct((tokens, width), F32),
        ],
        scratch_shapes=[
            pltpu.VMEM((units, width), BF16),
            pltpu.VMEM((units, width), BF16),
            pltpu.VMEM((tokens, chunk), BF16),
            pltpu.VMEM((width, chunk), BF16),
            pltpu.SemaphoreType.DMA((count,)),
            pltpu.SemaphoreType.DMA((count,)),
            pltpu.SemaphoreType.DMA((1,)),
        ],
        compiler_params=pltpu.CompilerParams(vmem_limit_bytes=VMEM_BYTES),
        cost_estimate=pl.CostEstimate(
            flops=8 * tokens * units * width, transcendentals=0, bytes_accessed=60 << 20
        ),
        name="feed_backward",
    )(e, u, base, act, slope, *firsts, *seconds)


def table_pair(points, scale=None):
    numbers = jnp.arange(points, dtype=jnp.int32)
    coarse = 32 * jnp.arange(points // 32, dtype=jnp.int32)
    fine = jnp.arange(32, dtype=jnp.int32)

    def waves(rows):
        angles = (rows[:, None] * numbers[None, :] % points).astype(F32) * (2.0 * math.pi / points)
        return jnp.cos(angles), jnp.sin(angles)

    factor = 1.0 / math.sqrt(points)
    if points <= 64:
        cosine, sine = waves(numbers)
    else:
        coarse_cos, coarse_sin = waves(coarse)
        fine_cos, fine_sin = waves(fine)
        coarse_cos, coarse_sin, fine_cos, fine_sin = lax.optimization_barrier(
            (coarse_cos, coarse_sin, fine_cos, fine_sin)
        )
        coarse_cos, coarse_sin = coarse_cos[:, None], coarse_sin[:, None]
        fine_cos, fine_sin = fine_cos[None], fine_sin[None]
        cosine = (coarse_cos * fine_cos - coarse_sin * fine_sin).reshape(points, points)
        sine = (coarse_sin * fine_cos + coarse_cos * fine_sin).reshape(points, points)
    return (cosine * factor).astype(BF16), (sine * factor).astype(BF16)


def twiddles():
    row_index = jnp.arange(L1, dtype=jnp.int32)[None, :]
    col_index = jnp.arange(L2, dtype=jnp.int32)[:, None]
    angles = (row_index * col_index % L).astype(F32) * (2.0 * math.pi / L)
    return jnp.cos(angles)[:, :, None], jnp.sin(angles)[:, :, None]


def swap(values, step):
    axis, mask = step
    size = lax.axis_size(axis)
    return lax.ppermute(values, axis, [(i, i ^ mask) for i in range(size)])


def bits(size):
    masks = []
    mask = size // 2
    while mask >= 1:
        masks.append(mask)
        mask //= 2
    return masks


def widen(held, step):
    return jnp.concatenate([held, swap(held, step)], axis=0)


def widen_codes(codes, steps, groups):
    for axis, mask in steps:
        code = mask if axis == "seq" else mask * groups
        codes = codes + [held ^ code for held in codes]
    return codes


def spread(plane, steps_batch):
    pieces = [plane]
    for step in steps_batch:
        pieces = pieces + [swap(piece, step) for piece in pieces]
    return pieces


def spread_core(pieces, step_core):
    whole = []
    for piece in pieces:
        whole += [piece, swap(piece, step_core)]
    return whole


def fold(held, names, step, kind):
    axis = names.index(step)
    keep = lax.index_in_dim(held, 0, axis, keepdims=False)
    send = lax.index_in_dim(held, 1, axis, keepdims=False)
    total = keep.astype(F32) + swap(send.astype(kind), step).astype(F32)
    return total, names[:axis] + names[axis + 1 :]


def fold_all(held, names, steps, kind):
    for step in steps:
        held, names = fold(held, names, step, kind)
    return held, names


def arrange(rows):
    return with_layout_constraint(rows.transpose(0, 2, 1, 3), Layout(major_to_minor=(0, 1, 2, 3)))


def exchange(rows):
    order = Layout(major_to_minor=(0, 1, 2, 3))
    rows = with_layout_constraint(rows, order)
    rows = lax.all_to_all(rows, "seq", split_axis=0, concat_axis=0, tiled=True)
    return with_layout_constraint(rows, order)


def body(tokens, lengths, labels, picked, cotangent, w_in, b_in, w_out, shifts, norm_gains):
    groups = lax.axis_size("seq")
    me = lax.axis_index("seq")
    here = lax.axis_index("batch") * groups + me
    columns = tokens.shape[2]
    share = w_in.shape[2]
    part = shifts.shape[2]
    blocks = groups * lax.axis_size("batch")

    steps_plane = [("seq", mask) for mask in bits(groups)[:-1]]
    steps_batch = [("batch", mask) for mask in bits(lax.axis_size("batch"))]
    step_core = ("seq", 1)
    numbers = jnp.arange(blocks, dtype=jnp.int32)

    codes = []
    for code in widen_codes([0], steps_batch, groups):
        codes += widen_codes(widen_codes([code], steps_plane, groups), [step_core], groups)
    owner = jnp.array(codes, dtype=jnp.int32) ^ here
    one_hot = (owner[:, None] == numbers[None, :]).astype(F32)

    steps_small = [steps_plane[-1], step_core] + steps_batch + steps_plane[:-1]
    small_codes = widen_codes([0], steps_small, groups)
    small_owner = jnp.array(small_codes, dtype=jnp.int32) ^ here
    small_hot = (small_owner[:, None] == numbers[None, :]).astype(F32)
    small = jnp.concatenate([b_in[0], shifts[0].reshape(-1), norm_gains[0].reshape(-1)])
    small = small.astype(F32)[None]
    for step in steps_small:
        small = widen(small, step)

    marks = jnp.where(picked > 0, labels, -1).astype(F32).transpose(0, 2, 1)
    marks = marks.reshape(groups, columns * L1)
    seats = jnp.arange(groups, dtype=jnp.int32)
    seat_hot = ((seats ^ me)[:, None] == seats[None, :]).astype(F32)
    marks = jnp.sum(seat_hot[:, :, None] * marks[None], axis=1)
    masks = bits(groups)
    marks = marks.reshape((2,) * len(masks) + (columns * L1,))
    for axis, mask in enumerate(masks):
        keep = lax.slice_in_dim(marks, 0, 1, axis=axis)
        send = lax.slice_in_dim(marks, 1, 2, axis=axis)
        marks = jnp.concatenate([keep, swap(send, ("seq", mask))], axis=axis)
    marks = marks.reshape(groups, columns * L1)

    first_held = w_in[0].T[None]
    second_held = w_out[0][None]
    for step in steps_plane[:-1]:
        first_held = widen(first_held, step)
        second_held = widen(second_held, step)
    tokens_late, late_cotangent, small, marks, first_held, second_held = lax.optimization_barrier(
        (arrange(tokens), arrange(cotangent), small, marks, first_held, second_held)
    )
    marks = jnp.sum(seat_hot[:, :, None] * marks[None], axis=1)
    first_held = widen(first_held, steps_plane[-1])
    second_held = widen(second_held, steps_plane[-1])

    wide_cos, wide_sin = table_pair(D)
    wide = jnp.stack([wide_cos, -wide_sin])
    twiddle_cos, twiddle_sin = twiddles()
    first_held, second_held, wide, twiddle_cos, twiddle_sin = lax.optimization_barrier(
        (first_held, second_held, wide, twiddle_cos, twiddle_sin)
    )
    firsts = spread(first_held, steps_batch)
    seconds = spread(second_held, steps_batch)
    places = jnp.array([small_codes.index(code) for code in codes], dtype=jnp.int32)
    place_hot = (places[:, None] == numbers[None, :]).astype(F32)
    b_first = jnp.sum(place_hot[:, :, None] * small[None, :, :share], axis=1)
    b_first = b_first.reshape(1, blocks * share)
    rows = jnp.sum(small_hot[:, :, None] * small[:, None, share:], axis=0)
    rows = rows.reshape(blocks, 5, part).transpose(1, 0, 2).reshape(5, D)
    shifts_f = rows[:3]
    gains_f = rows[3:]

    short_cos, short_sin = table_pair(L1)
    long_cos, long_sin = table_pair(L2)
    short_table = jnp.concatenate([short_cos, short_sin], axis=0)
    long_table = jnp.stack([jnp.stack([long_cos, -long_sin]), jnp.stack([long_sin, long_cos])])
    both = jnp.eye(2, dtype=BF16)
    pair_table = jnp.einsum("qukm,bc->qkbcum", long_table, both).reshape(4 * L2, 4 * L2)

    x_all = exchange(tokens_late)
    x_all, late_cotangent = lax.optimization_barrier((x_all, late_cotangent))
    g_all = exchange(late_cotangent)

    length = lengths[me]
    spots = (
        L2 * jnp.arange(L1, dtype=jnp.int32)[None, :] + jnp.arange(L2, dtype=jnp.int32)[:, None]
    )
    valid = spots < length
    x_rows = x_all.reshape(L2, L1, D)
    x_rows = jnp.where(valid[:, :, None], x_rows, jnp.zeros_like(x_rows))

    first = jnp.einsum("kn,mnd->mkd", short_table, x_rows, preferred_element_type=F32)
    first_cos, first_sin = first[:, :L1], first[:, L1:]
    turned_cos = (first_cos * twiddle_cos - first_sin * twiddle_sin).astype(BF16)
    turned_sin = (first_cos * twiddle_sin + first_sin * twiddle_cos).astype(BF16)
    turned = jnp.stack([turned_cos, turned_sin]).reshape(2, L2, 2, L2, D)
    turned = turned.transpose(3, 2, 0, 1, 4).reshape(L2, 4 * L2, D)
    spectrum = jnp.einsum("rk,lkd->lrd", pair_table, turned, preferred_element_type=F32)
    spectrum = spectrum.astype(BF16).reshape(L2, 2, L1, D)
    mixed = jnp.einsum("lund,ude->lne", spectrum, wide, preferred_element_type=F32)
    mixed, firsts, seconds = lax.optimization_barrier((mixed, firsts, seconds))
    flat = lambda pieces: [piece.reshape(-1, D) for piece in spread_core(pieces, step_core)]
    firsts, seconds = flat(firsts), flat(seconds)
    residual = (x_rows.astype(F32) + mixed).reshape(L, D)

    normed = layer_norm(residual, gains_f[0], shifts_f[1])
    normed_low = normed.astype(BF16)
    act_low, slope, summed = feed_forward(
        normed_low, normed + shifts_f[0], firsts, b_first, seconds
    )
    layer_out = layer_norm(summed, gains_f[1], shifts_f[2]).astype(BF16)
    out_rows = exchange(layer_out.reshape(groups, columns, L1, D))
    current = out_rows.transpose(0, 2, 1, 3)

    logits = layer_out.astype(F32)
    label_rows = marks.reshape(L).astype(jnp.int32)
    highest = jnp.max(logits, axis=-1, keepdims=True)
    powers = jnp.exp(logits - highest)
    denominator = jnp.sum(powers, axis=-1)
    features = jnp.arange(D, dtype=jnp.int32)
    top = jnp.sum(jnp.where(features == label_rows[:, None], powers, 0.0), axis=-1)
    weight = jnp.where(valid.reshape(L) & (label_rows >= 0), 1.0, 0.0)
    sums = jnp.stack([jnp.sum(weight * (top / denominator)), jnp.sum(weight)])

    grad_out = g_all.reshape(L, D).astype(F32)
    unused, pull_second = jax.vjp(layer_norm, summed, gains_f[1], shifts_f[2])
    grad_summed, grad_gain_two, grad_shift_two = pull_second(grad_out)
    grad_bias_two = jnp.sum(grad_summed, axis=0)
    summed_low = grad_summed.astype(BF16)
    grad_first, grad_second, grad_b_first, grad_normed = feed_backward(
        summed_low, normed_low, grad_summed, act_low, slope, firsts, seconds
    )
    names = steps_batch[::-1] + [step_core] + steps_plane[::-1]
    shape = (2,) * len(names) + (share,)
    grad_first = grad_first.reshape(shape + (D,))
    grad_second = grad_second.reshape(shape + (D,))
    steps_second = [step_core, steps_plane[-1]] + steps_batch[::-1] + steps_plane[:-1][::-1]
    steps_first = [step_core] + steps_batch[::-1] + steps_plane[::-1]
    grad_second, names_second = fold_all(grad_second, names, steps_second[:2], BF16)
    early_first = 1 + len(steps_batch)
    grad_first, names_first = fold_all(grad_first, names, steps_first[:early_first], BF16)
    normed_again, pull_first = jax.vjp(layer_norm, residual, gains_f[0], shifts_f[1])
    grad_residual, grad_gain_one, grad_shift_one = pull_first(grad_normed)
    residual_low = grad_residual.astype(BF16).reshape(L2, L1, D)
    grad_spectrum = jnp.einsum("lne,ude->lund", residual_low, wide, preferred_element_type=F32)
    grad_spectrum = grad_spectrum.astype(BF16).reshape(L2, 4 * L2, D)
    grad_turned = jnp.einsum("rk,lrd->lkd", pair_table, grad_spectrum, preferred_element_type=F32)
    grad_turned = grad_turned.astype(BF16).reshape(L2, 2, 2, L2, D).transpose(2, 3, 1, 0, 4)
    grad_turned = grad_turned.reshape(2, L2, L1, D)
    grad_cos, grad_sin = grad_turned[0], grad_turned[1]
    back_cos = grad_cos * twiddle_cos + grad_sin * twiddle_sin
    back_sin = grad_sin * twiddle_cos - grad_cos * twiddle_sin
    stacked = jnp.concatenate([back_cos, back_sin], axis=1).astype(BF16)
    grad_x = residual_low.astype(F32) + jnp.einsum(
        "kn,mkd->mnd", short_table, stacked, preferred_element_type=F32
    )
    grad_x = jnp.where(valid[:, :, None], grad_x, 0.0).astype(BF16)
    grad_x = grad_x.reshape(groups, columns, L1, D)
    grad_x, grad_first, grad_second = lax.optimization_barrier((grad_x, grad_first, grad_second))
    input_grad = exchange(grad_x).transpose(0, 2, 1, 3)
    norms = jnp.stack(
        [grad_bias_two, grad_shift_one, grad_shift_two, grad_gain_one, grad_gain_two]
    )
    norms = norms.reshape(5, blocks, part).transpose(1, 0, 2).reshape(blocks, 5 * part)
    norms = jnp.sum(one_hot[:, :, None] * norms[None], axis=1)
    sums = jnp.broadcast_to(sums[None], (blocks, 2))
    small_grads = jnp.concatenate([grad_b_first.reshape(blocks, share), norms, sums], axis=1)
    small_grads = small_grads.reshape(shape[:-1] + (-1,))
    small_grads, names_small = fold_all(small_grads, names, steps_first[:early_first], F32)
    rest_first, rest_second = steps_first[early_first:], steps_second[2:]
    while rest_second:
        count = len(rest_second) - len(rest_first) + 1
        small_grads, grad_first, grad_second = lax.optimization_barrier(
            (small_grads, grad_first, grad_second)
        )
        small_grads, names_small = fold_all(small_grads, names_small, rest_first[:1], F32)
        grad_first, names_first = fold_all(grad_first, names_first, rest_first[:1], BF16)
        grad_second, names_second = fold_all(grad_second, names_second, rest_second[:count], BF16)
        rest_first, rest_second = rest_first[1:], rest_second[count:]
    norms = small_grads[share:-2].reshape(5, part)
    match_rate = D * small_grads[-2] / jnp.maximum(small_grads[-1], 1.0)
    return (
        current,
        input_grad,
        grad_first.T[None],
        small_grads[:share][None],
        grad_second[None],
        norms[:3][None],
        norms[3:][None],
        match_rate,
    )


def solution(mesh):
    in_specs = (
        P("batch", None, "seq", None),
        P("batch"),
        P("batch", None, "seq"),
        P("batch", None, "seq"),
        P("batch", None, "seq", None),
        P(None, None, ("batch", "seq")),
        P(None, ("batch", "seq")),
        P(None, ("batch", "seq"), None),
        P(None, None, ("batch", "seq")),
        P(None, None, ("batch", "seq")),
    )
    out_specs = (
        P("batch", None, "seq", None),
        P("batch", None, "seq", None),
        P(None, None, ("batch", "seq")),
        P(None, ("batch", "seq")),
        P(None, ("batch", "seq"), None),
        P(None, None, ("batch", "seq")),
        P(None, None, ("batch", "seq")),
        P(),
    )
    return jax.shard_map(body, mesh=mesh, in_specs=in_specs, out_specs=out_specs, check_vma=False)
```

```python
import functools
import math

import jax
import jax.numpy as jnp
from jax import lax
from jax.experimental import pallas as pl
from jax.experimental.layout import Layout, with_layout_constraint
from jax.experimental.pallas import tpu as pltpu
from jax.sharding import PartitionSpec as P

D = 768
L1 = 64
L2 = 32
L = 2048

EPSILON = 1e-12
ROOT_TWO_PI = 0.7978845608028654
CUBIC = ROOT_TWO_PI * 0.044715
F32 = jnp.float32
BF16 = jnp.bfloat16
VMEM_BYTES = 60 << 20


def layer_norm(values, gain_rows, shift_rows):
    center = values - jnp.mean(values, axis=-1, keepdims=True)
    spread = jnp.mean(center * center, axis=-1, keepdims=True)
    return center * lax.rsqrt(spread + EPSILON) * gain_rows + shift_rows


def product(left, right):
    return lax.dot_general(left, right, (((1,), (0,)), ((), ())), preferred_element_type=F32)


def product_over_rows(left, right):
    return lax.dot_general(left, right, (((0,), (0,)), ((), ())), preferred_element_type=F32)


def fetch_weights(pieces, holder, sems, chunk):
    rows = pieces[0].shape[0]
    step = pl.program_id(0)
    copies = [
        pltpu.make_async_copy(piece, holder.at[pl.ds(i * rows, rows), :], sems.at[i])
        for i, piece in enumerate(pieces)
    ]

    @pl.when(step == 0)
    def _():
        for copy in copies:
            copy.start()

    for number in range(rows * len(pieces) // chunk):
        needed = [copy for i, copy in enumerate(copies) if i * rows // chunk == number]
        if needed:

            @pl.when(step == number)
            def _():
                for copy in needed:
                    copy.wait()


def forward_kernel(*refs, tile, counts, chunk):
    u_ref, base_ref, b_ref = refs[:3]
    split = sum(counts)
    firsts, seconds = refs[3 : 3 + counts[0]], refs[3 + counts[0] : 3 + split]
    act_ref, slope_ref, y_ref, w1_ref, w2_ref, turn_ref, sem1, sem2, sem3 = refs[3 + split :]
    start = pltpu.make_async_copy(base_ref, y_ref, sem3.at[0])

    @pl.when(pl.program_id(0) == 0)
    def _():
        start.start()

    fetch_weights(firsts, w1_ref, sem1, chunk)
    fetch_weights(seconds, w2_ref, sem2, chunk)
    here = pl.ds(pl.multiple_of(pl.program_id(0) * chunk, chunk), chunk)

    @pl.when(pl.program_id(0) == 0)
    def _():
        start.wait()

    turn_ref[...] = w1_ref[here, :].T

    def step(i, carry):
        rows = pl.ds(pl.multiple_of(i * tile, tile), tile)
        z = product(u_ref[rows, :], turn_ref[...]) + b_ref[...]
        square = z * z
        t = jnp.tanh(z * (ROOT_TWO_PI + CUBIC * square))
        half = 0.5 + 0.5 * t
        a = z * half
        low = a.astype(BF16)
        act_ref[rows, :] = low
        slope = half + (a - a * t) * (ROOT_TWO_PI + (3.0 * CUBIC) * square)
        slope_ref[rows, :] = slope.astype(BF16)
        y_ref[rows, :] += product(low, w2_ref[here, :])
        return carry

    lax.fori_loop(0, u_ref.shape[0] // tile, step, 0)


def whole_block(shape, buffers=1):
    return pl.BlockSpec(shape, lambda c: (0, 0), pipeline_mode=pl.Buffered(buffers))


def feed_forward(u, base, firsts, b, seconds, chunk=768, tile=1024):
    tokens, width = u.shape
    counts = (len(firsts), len(seconds))
    units = b.shape[1]
    acts = lambda: pl.BlockSpec((tokens, chunk), lambda c: (0, c))
    far = [pl.BlockSpec(memory_space=pl.ANY)] * sum(counts)
    return pl.pallas_call(
        functools.partial(forward_kernel, tile=tile, counts=counts, chunk=chunk),
        grid=(units // chunk,),
        in_specs=[
            whole_block((tokens, width)),
            pl.BlockSpec(memory_space=pl.ANY),
            pl.BlockSpec((1, chunk), lambda c: (0, c)),
        ]
        + far,
        out_specs=[acts(), acts(), pl.BlockSpec((tokens, width), lambda c: (0, 0))],
        out_shape=[
            jax.ShapeDtypeStruct((tokens, units), BF16),
            jax.ShapeDtypeStruct((tokens, units), BF16),
            jax.ShapeDtypeStruct((tokens, width), F32),
        ],
        scratch_shapes=[
            pltpu.VMEM((units, width), BF16),
            pltpu.VMEM((units, width), BF16),
            pltpu.VMEM((width, chunk), BF16),
            pltpu.SemaphoreType.DMA((counts[0],)),
            pltpu.SemaphoreType.DMA((counts[1],)),
            pltpu.SemaphoreType.DMA((1,)),
        ],
        compiler_params=pltpu.CompilerParams(vmem_limit_bytes=VMEM_BYTES),
        cost_estimate=pl.CostEstimate(
            flops=4 * tokens * units * width, transcendentals=tokens * units, bytes_accessed=60 << 20
        ),
        name="feed_forward",
    )(u, base, b, *firsts, *seconds)


def backward_kernel(*refs, tile, counts, chunk):
    e_ref, u_ref, base_ref, act_ref, slope_ref = refs[:5]
    split = sum(counts)
    firsts, seconds = refs[5 : 5 + counts[0]], refs[5 + counts[0] : 5 + split]
    keep1_ref, keep2_ref, send1_ref, send2_ref, db_ref, du_ref = refs[5 + split : 11 + split]
    w1_ref, w2_ref, f_ref, turn_ref, sem1, sem2, sem3 = refs[11 + split :]
    start = pltpu.make_async_copy(base_ref, du_ref, sem3.at[0])

    @pl.when(pl.program_id(0) == 0)
    def _():
        start.start()

    fetch_weights(firsts, w1_ref, sem1, chunk)
    fetch_weights(seconds, w2_ref, sem2, chunk)
    here = pl.ds(pl.multiple_of(pl.program_id(0) * chunk, chunk), chunk)

    @pl.when(pl.program_id(0) == 0)
    def _():
        start.wait()

    turn_ref[...] = w2_ref[here, :].T

    def step(i, db):
        rows = pl.ds(pl.multiple_of(i * tile, tile), tile)
        dz = product(e_ref[rows, :], turn_ref[...]) * slope_ref[rows, :].astype(F32)
        low = dz.astype(BF16)
        f_ref[rows, :] = low
        du_ref[rows, :] += product(low, w1_ref[here, :])
        return db + jnp.sum(dz.reshape(tile // 8, 8, -1), axis=0)

    db = lax.fori_loop(0, e_ref.shape[0] // tile, step, jnp.zeros((8, chunk), F32))
    db_ref[...] = jnp.sum(db, axis=0, keepdims=True)
    dw2 = product_over_rows(act_ref[...], e_ref[...]).astype(BF16)
    dw1 = product_over_rows(f_ref[...], u_ref[...]).astype(BF16)
    half = pl.num_programs(0) // 2

    @pl.when(pl.program_id(0) < half)
    def _():
        keep1_ref[...] = dw1
        keep2_ref[...] = dw2

    @pl.when(pl.program_id(0) >= half)
    def _():
        send1_ref[...] = dw1
        send2_ref[...] = dw2


def feed_backward(e, u, base, act, slope, firsts, seconds, chunk=768, tile=512):
    tokens, width = u.shape
    counts = (len(firsts), len(seconds))
    units = act.shape[1]
    half = units // chunk // 2
    acts = lambda: pl.BlockSpec((tokens, chunk), lambda c: (0, c))
    keep = lambda: pl.BlockSpec((chunk, width), lambda c: (jnp.minimum(c, half - 1), 0))
    send = lambda: pl.BlockSpec((chunk, width), lambda c: (jnp.maximum(c - half, 0), 0))
    far = lambda number: [pl.BlockSpec(memory_space=pl.ANY)] * number
    grads = jax.ShapeDtypeStruct((units // 2, width), BF16)
    return pl.pallas_call(
        functools.partial(backward_kernel, tile=tile, counts=counts, chunk=chunk),
        grid=(units // chunk,),
        in_specs=[whole_block((tokens, width)), whole_block((tokens, width))]
        + far(1)
        + [acts(), acts()]
        + far(sum(counts)),
        out_specs=[
            keep(),
            keep(),
            send(),
            send(),
            pl.BlockSpec((1, chunk), lambda c: (0, c)),
            whole_block((tokens, width)),
        ],
        out_shape=[grads] * 4
        + [
            jax.ShapeDtypeStruct((1, units), F32),
            jax.ShapeDtypeStruct((tokens, width), F32),
        ],
        scratch_shapes=[
            pltpu.VMEM((units, width), BF16),
            pltpu.VMEM((units, width), BF16),
            pltpu.VMEM((tokens, chunk), BF16),
            pltpu.VMEM((width, chunk), BF16),
            pltpu.SemaphoreType.DMA((counts[0],)),
            pltpu.SemaphoreType.DMA((counts[1],)),
            pltpu.SemaphoreType.DMA((1,)),
        ],
        compiler_params=pltpu.CompilerParams(vmem_limit_bytes=VMEM_BYTES),
        cost_estimate=pl.CostEstimate(
            flops=8 * tokens * units * width, transcendentals=0, bytes_accessed=60 << 20
        ),
        name="feed_backward",
    )(e, u, base, act, slope, *firsts, *seconds)


def table_pair(points, scale=None):
    numbers = jnp.arange(points, dtype=jnp.int32)
    coarse = 32 * jnp.arange(points // 32, dtype=jnp.int32)
    fine = jnp.arange(32, dtype=jnp.int32)

    def waves(rows):
        angles = (rows[:, None] * numbers[None, :] % points).astype(F32) * (2.0 * math.pi / points)
        return jnp.cos(angles), jnp.sin(angles)

    factor = 1.0 / math.sqrt(points)
    if points <= 64:
        cosine, sine = waves(numbers)
    else:
        coarse_cos, coarse_sin = waves(coarse)
        fine_cos, fine_sin = waves(fine)
        coarse_cos, coarse_sin, fine_cos, fine_sin = lax.optimization_barrier(
            (coarse_cos, coarse_sin, fine_cos, fine_sin)
        )
        coarse_cos, coarse_sin = coarse_cos[:, None], coarse_sin[:, None]
        fine_cos, fine_sin = fine_cos[None], fine_sin[None]
        cosine = (coarse_cos * fine_cos - coarse_sin * fine_sin).reshape(points, points)
        sine = (coarse_sin * fine_cos + coarse_cos * fine_sin).reshape(points, points)
    return (cosine * factor).astype(BF16), (sine * factor).astype(BF16)


def twiddles():
    row_index = jnp.arange(L1, dtype=jnp.int32)[None, :]
    col_index = jnp.arange(L2, dtype=jnp.int32)[:, None]
    angles = (row_index * col_index % L).astype(F32) * (2.0 * math.pi / L)
    return jnp.cos(angles)[:, :, None], jnp.sin(angles)[:, :, None]


def swap(values, step):
    axis, mask = step
    size = lax.axis_size(axis)
    return lax.ppermute(values, axis, [(i, i ^ mask) for i in range(size)])


def bits(size):
    masks = []
    mask = size // 2
    while mask >= 1:
        masks.append(mask)
        mask //= 2
    return masks


def widen(held, step):
    return jnp.concatenate([held, swap(held, step)], axis=0)


def widen_codes(codes, steps, groups):
    for axis, mask in steps:
        code = mask if axis == "seq" else mask * groups
        codes = codes + [held ^ code for held in codes]
    return codes


def spread(pieces, steps):
    for step in steps:
        pieces = pieces + [swap(piece, step) for piece in pieces]
    return pieces


def spread_core(pieces, step_core):
    return pieces + [swap(piece, step_core) for piece in pieces]


def fold(held, names, step, kind):
    axis = names.index(step)
    keep = lax.index_in_dim(held, 0, axis, keepdims=False)
    send = lax.index_in_dim(held, 1, axis, keepdims=False)
    total = keep.astype(F32) + swap(send.astype(kind), step).astype(F32)
    return total, names[:axis] + names[axis + 1 :]


def fold_all(held, names, steps, kind):
    for step in steps:
        held, names = fold(held, names, step, kind)
    return held, names


def arrange(rows):
    return with_layout_constraint(rows.transpose(0, 2, 1, 3), Layout(major_to_minor=(0, 1, 2, 3)))


def exchange(rows):
    order = Layout(major_to_minor=(0, 1, 2, 3))
    rows = with_layout_constraint(rows, order)
    rows = lax.all_to_all(rows, "seq", split_axis=0, concat_axis=0, tiled=True)
    return with_layout_constraint(rows, order)


def body(tokens, lengths, labels, picked, cotangent, w_in, b_in, w_out, shifts, norm_gains):
    groups = lax.axis_size("seq")
    me = lax.axis_index("seq")
    here = lax.axis_index("batch") * groups + me
    columns = tokens.shape[2]
    share = w_in.shape[2]
    part = shifts.shape[2]
    blocks = groups * lax.axis_size("batch")

    steps_plane = [("seq", mask) for mask in bits(groups)[:-1]]
    steps_batch = [("batch", mask) for mask in bits(lax.axis_size("batch"))]
    step_core = ("seq", 1)
    numbers = jnp.arange(blocks, dtype=jnp.int32)

    codes = widen_codes([0], steps_plane + steps_batch + [step_core], groups)
    owner = jnp.array(codes, dtype=jnp.int32) ^ here
    one_hot = (owner[:, None] == numbers[None, :]).astype(F32)

    steps_small = [steps_plane[-1], step_core] + steps_batch + steps_plane[:-1]
    small_codes = widen_codes([0], steps_small, groups)
    small_owner = jnp.array(small_codes, dtype=jnp.int32) ^ here
    small_hot = (small_owner[:, None] == numbers[None, :]).astype(F32)
    small = jnp.concatenate([b_in[0], shifts[0].reshape(-1), norm_gains[0].reshape(-1)])
    small = small.astype(F32)[None]
    for step in steps_small:
        small = widen(small, step)

    first_held = w_in[0].T[None]
    second_held = w_out[0][None]
    for step in steps_plane[:-1]:
        first_held = widen(first_held, step)
        second_held = widen(second_held, step)
    tokens_late, late_cotangent, small, first_held, second_held = lax.optimization_barrier(
        (arrange(tokens), arrange(cotangent), small, first_held, second_held)
    )
    first_held = widen(first_held, steps_plane[-1])
    seconds = []
    for piece in spread([second_held], steps_batch):
        seconds += [piece, swap(piece, steps_plane[-1])]

    wide_cos, wide_sin = table_pair(D)
    wide = jnp.stack([wide_cos, -wide_sin])
    twiddle_cos, twiddle_sin = twiddles()
    first_held, wide, twiddle_cos, twiddle_sin = lax.optimization_barrier(
        (first_held, wide, twiddle_cos, twiddle_sin)
    )
    firsts = spread([first_held], steps_batch)
    places = jnp.array([small_codes.index(code) for code in codes], dtype=jnp.int32)
    place_hot = (places[:, None] == numbers[None, :]).astype(F32)
    b_first = jnp.sum(place_hot[:, :, None] * small[None, :, :share], axis=1)
    b_first = b_first.reshape(1, blocks * share)
    rows = jnp.sum(small_hot[:, :, None] * small[:, None, share:], axis=0)
    rows = rows.reshape(blocks, 5, part).transpose(1, 0, 2).reshape(5, D)
    shifts_f = rows[:3]
    gains_f = rows[3:]

    short_cos, short_sin = table_pair(L1)
    long_cos, long_sin = table_pair(L2)
    short_table = jnp.concatenate([short_cos, short_sin], axis=0)
    long_table = jnp.stack([jnp.stack([long_cos, -long_sin]), jnp.stack([long_sin, long_cos])])
    both = jnp.eye(2, dtype=BF16)
    pair_table = jnp.einsum("qukm,bc->qkbcum", long_table, both).reshape(4 * L2, 4 * L2)

    x_all = exchange(tokens_late)
    x_all, late_cotangent = lax.optimization_barrier((x_all, late_cotangent))
    g_all = exchange(late_cotangent)

    length = lengths[me]
    spots = (
        L2 * jnp.arange(L1, dtype=jnp.int32)[None, :] + jnp.arange(L2, dtype=jnp.int32)[:, None]
    )
    valid = spots < length
    x_rows = x_all.reshape(L2, L1, D)
    x_rows = jnp.where(valid[:, :, None], x_rows, jnp.zeros_like(x_rows))

    first = jnp.einsum("kn,mnd->mkd", short_table, x_rows, preferred_element_type=F32)
    first_cos, first_sin = first[:, :L1], first[:, L1:]
    turned_cos = (first_cos * twiddle_cos - first_sin * twiddle_sin).astype(BF16)
    turned_sin = (first_cos * twiddle_sin + first_sin * twiddle_cos).astype(BF16)
    turned = jnp.stack([turned_cos, turned_sin]).reshape(2, L2, 2, L2, D)
    turned = turned.transpose(3, 2, 0, 1, 4).reshape(L2, 4 * L2, D)
    spectrum = jnp.einsum("rk,lkd->lrd", pair_table, turned, preferred_element_type=F32)
    spectrum = spectrum.astype(BF16).reshape(L2, 2, L1, D)
    mixed = jnp.einsum("lund,ude->lne", spectrum, wide, preferred_element_type=F32)
    mixed, firsts, seconds = lax.optimization_barrier((mixed, firsts, seconds))
    flat = lambda pieces: [piece.reshape(-1, D) for piece in spread_core(pieces, step_core)]
    firsts, seconds = flat(firsts), flat(seconds)
    residual = (x_rows.astype(F32) + mixed).reshape(L, D)

    normed = layer_norm(residual, gains_f[0], shifts_f[1])
    normed_low = normed.astype(BF16)
    act_low, slope, summed = feed_forward(
        normed_low, normed + shifts_f[0], firsts, b_first, seconds
    )
    layer_out = layer_norm(summed, gains_f[1], shifts_f[2]).astype(BF16)
    out_rows = exchange(layer_out.reshape(groups, columns, L1, D))
    current = out_rows.transpose(0, 2, 1, 3)

    grad_out = g_all.reshape(L, D).astype(F32)
    unused, pull_second = jax.vjp(layer_norm, summed, gains_f[1], shifts_f[2])
    grad_summed, grad_gain_two, grad_shift_two = pull_second(grad_out)
    grad_bias_two = jnp.sum(grad_summed, axis=0)
    summed_low = grad_summed.astype(BF16)
    keep_first, keep_second, send_first, send_second, grad_b_first, grad_normed = feed_backward(
        summed_low, normed_low, grad_summed, act_low, slope, firsts, seconds
    )
    names = steps_batch[::-1] + steps_plane[::-1]
    shape = (2,) * len(names) + (share,)
    normed_again, pull_first = jax.vjp(layer_norm, residual, gains_f[0], shifts_f[1])
    grad_residual, grad_gain_one, grad_shift_one = pull_first(grad_normed)
    residual_low = grad_residual.astype(BF16).reshape(L2, L1, D)
    grad_spectrum = jnp.einsum("lne,ude->lund", residual_low, wide, preferred_element_type=F32)
    grad_spectrum = grad_spectrum.astype(BF16).reshape(L2, 4 * L2, D)
    grad_turned = jnp.einsum("rk,lrd->lkd", pair_table, grad_spectrum, preferred_element_type=F32)
    grad_turned = grad_turned.astype(BF16).reshape(L2, 2, 2, L2, D).transpose(2, 3, 1, 0, 4)
    grad_turned = grad_turned.reshape(2, L2, L1, D)
    grad_cos, grad_sin = grad_turned[0], grad_turned[1]
    back_cos = grad_cos * twiddle_cos + grad_sin * twiddle_sin
    back_sin = grad_sin * twiddle_cos - grad_cos * twiddle_sin
    stacked = jnp.concatenate([back_cos, back_sin], axis=1).astype(BF16)
    grad_x = residual_low.astype(F32) + jnp.einsum(
        "kn,mkd->mnd", short_table, stacked, preferred_element_type=F32
    )
    grad_x = jnp.where(valid[:, :, None], grad_x, 0.0).astype(BF16)
    grad_x = grad_x.reshape(groups, columns, L1, D)
    input_grad = exchange(grad_x).transpose(0, 2, 1, 3)

    shift_of = jnp.arange(columns, dtype=jnp.int32) + me * columns
    place_of = L2 * jnp.arange(L1, dtype=jnp.int32)[None, :] + shift_of[:, None]
    out_rows, grad_x = lax.optimization_barrier((out_rows, grad_x))
    logits = out_rows.astype(F32)
    highest = jnp.max(logits, axis=-1, keepdims=True)
    powers = jnp.exp(logits - highest)
    denominator = jnp.sum(powers, axis=-1)
    features = jnp.arange(D, dtype=jnp.int32)
    label_rows = labels.transpose(0, 2, 1)
    top = jnp.sum(jnp.where(features == label_rows[..., None], powers, 0.0), axis=-1)
    counted = (picked.transpose(0, 2, 1) > 0) & (place_of[None] < lengths[:, None, None])
    weight = jnp.where(counted, 1.0, 0.0)
    sums = jnp.stack([jnp.sum(weight * (top / denominator)), jnp.sum(weight)])

    def fold_core(keep, send):
        return keep.astype(F32) + swap(send, step_core).astype(F32)

    grad_first = fold_core(keep_first, send_first).reshape(shape + (D,))
    grad_second = fold_core(keep_second, send_second).reshape(shape + (D,))
    steps_first = steps_batch[::-1] + steps_plane[::-1]
    steps_second = [steps_plane[-1]] + steps_batch[::-1] + steps_plane[:-1][::-1]
    early = len(steps_batch)
    grad_first, names_first = fold_all(grad_first, names, steps_first[:early], BF16)
    grad_second, names_second = fold_all(grad_second, names, steps_second[:1], BF16)
    norms = jnp.stack(
        [grad_bias_two, grad_shift_one, grad_shift_two, grad_gain_one, grad_gain_two]
    )
    norms = norms.reshape(5, blocks, part).transpose(1, 0, 2).reshape(blocks, 5 * part)
    norms = jnp.sum(one_hot[:, :, None] * norms[None], axis=1)
    sums = jnp.broadcast_to(sums[None], (blocks, 2))
    small_grads = jnp.concatenate([grad_b_first.reshape(blocks, share), norms, sums], axis=1)
    half = blocks // 2
    small_grads = fold_core(small_grads[:half], small_grads[half:])
    small_grads = small_grads.reshape(shape[:-1] + (-1,))
    small_grads, names_small = fold_all(small_grads, names, steps_first[:early], F32)
    small_grads, current = lax.optimization_barrier(
        (small_grads, with_layout_constraint(current, Layout(major_to_minor=(0, 1, 2, 3))))
    )
    rest_first, rest_second = steps_first[early:], steps_second[1:]
    while rest_second:
        count = len(rest_second) - len(rest_first) + 1
        small_grads, grad_first, grad_second = lax.optimization_barrier(
            (small_grads, grad_first, grad_second)
        )
        small_grads, names_small = fold_all(small_grads, names_small, rest_first[:1], F32)
        grad_first, names_first = fold_all(grad_first, names_first, rest_first[:1], BF16)
        grad_second, names_second = fold_all(grad_second, names_second, rest_second[:count], BF16)
        rest_first, rest_second = rest_first[1:], rest_second[count:]
    norms = small_grads[share:-2].reshape(5, part)
    match_rate = D * small_grads[-2] / jnp.maximum(small_grads[-1], 1.0)
    return (
        current,
        input_grad,
        grad_first.T[None],
        small_grads[:share][None],
        grad_second[None],
        norms[:3][None],
        norms[3:][None],
        match_rate,
    )


def solution(mesh):
    in_specs = (
        P("batch", None, "seq", None),
        P("batch"),
        P("batch", None, "seq"),
        P("batch", None, "seq"),
        P("batch", None, "seq", None),
        P(None, None, ("batch", "seq")),
        P(None, ("batch", "seq")),
        P(None, ("batch", "seq"), None),
        P(None, None, ("batch", "seq")),
        P(None, None, ("batch", "seq")),
    )
    out_specs = (
        P("batch", None, "seq", None),
        P("batch", None, "seq", None),
        P(None, None, ("batch", "seq")),
        P(None, ("batch", "seq")),
        P(None, ("batch", "seq"), None),
        P(None, None, ("batch", "seq")),
        P(None, None, ("batch", "seq")),
        P(),
    )
    return jax.shard_map(body, mesh=mesh, in_specs=in_specs, out_specs=out_specs, check_vma=False)
```

```python
import functools
import math

import jax
import jax.numpy as jnp
from jax import lax
from jax.experimental import pallas as pl
from jax.experimental.layout import Layout, with_layout_constraint
from jax.experimental.pallas import tpu as pltpu
from jax.sharding import PartitionSpec as P

D = 768
L1 = 64
L2 = 32
L = 2048

EPSILON = 1e-12
ROOT_TWO_PI = 0.7978845608028654
CUBIC = ROOT_TWO_PI * 0.044715
F32 = jnp.float32
BF16 = jnp.bfloat16
VMEM_BYTES = 60 << 20


def layer_norm(values, gain_rows, shift_rows):
    center = values - jnp.mean(values, axis=-1, keepdims=True)
    spread = jnp.mean(center * center, axis=-1, keepdims=True)
    return center * lax.rsqrt(spread + EPSILON) * gain_rows + shift_rows


def product(left, right):
    return lax.dot_general(left, right, (((1,), (0,)), ((), ())), preferred_element_type=F32)


def product_over_rows(left, right):
    return lax.dot_general(left, right, (((0,), (0,)), ((), ())), preferred_element_type=F32)


def fetch_weights(pieces, holder, sems, chunk):
    rows = pieces[0].shape[0]
    step = pl.program_id(0)
    copies = [
        pltpu.make_async_copy(piece, holder.at[pl.ds(i * rows, rows), :], sems.at[i])
        for i, piece in enumerate(pieces)
    ]

    @pl.when(step == 0)
    def _():
        for copy in copies:
            copy.start()

    for number in range(rows * len(pieces) // chunk):
        needed = [copy for i, copy in enumerate(copies) if i * rows // chunk == number]
        if needed:

            @pl.when(step == number)
            def _():
                for copy in needed:
                    copy.wait()


def forward_kernel(*refs, tile, counts, chunk):
    u_ref, base_ref, b_ref = refs[:3]
    split = sum(counts)
    firsts, seconds = refs[3 : 3 + counts[0]], refs[3 + counts[0] : 3 + split]
    act_ref, slope_ref, y_ref, w1_ref, w2_ref, turn_ref, sem1, sem2, sem3 = refs[3 + split :]
    start = pltpu.make_async_copy(base_ref, y_ref, sem3.at[0])

    @pl.when(pl.program_id(0) == 0)
    def _():
        start.start()

    fetch_weights(firsts, w1_ref, sem1, chunk)
    fetch_weights(seconds, w2_ref, sem2, chunk)
    here = pl.ds(pl.multiple_of(pl.program_id(0) * chunk, chunk), chunk)

    @pl.when(pl.program_id(0) == 0)
    def _():
        start.wait()

    turn_ref[...] = w1_ref[here, :].T

    def step(i, carry):
        rows = pl.ds(pl.multiple_of(i * tile, tile), tile)
        z = product(u_ref[rows, :], turn_ref[...]) + b_ref[...]
        square = z * z
        t = jnp.tanh(z * (ROOT_TWO_PI + CUBIC * square))
        half = 0.5 + 0.5 * t
        a = z * half
        low = a.astype(BF16)
        act_ref[rows, :] = low
        slope = half + (a - a * t) * (ROOT_TWO_PI + (3.0 * CUBIC) * square)
        slope_ref[rows, :] = slope.astype(BF16)
        y_ref[rows, :] += product(low, w2_ref[here, :])
        return carry

    lax.fori_loop(0, u_ref.shape[0] // tile, step, 0)


def whole_block(shape, buffers=1):
    return pl.BlockSpec(shape, lambda c: (0, 0), pipeline_mode=pl.Buffered(buffers))


def feed_forward(u, base, firsts, b, seconds, chunk=768, tile=1024):
    tokens, width = u.shape
    counts = (len(firsts), len(seconds))
    units = b.shape[1]
    acts = lambda: pl.BlockSpec((tokens, chunk), lambda c: (0, c))
    far = [pl.BlockSpec(memory_space=pl.ANY)] * sum(counts)
    return pl.pallas_call(
        functools.partial(forward_kernel, tile=tile, counts=counts, chunk=chunk),
        grid=(units // chunk,),
        in_specs=[
            whole_block((tokens, width)),
            pl.BlockSpec(memory_space=pl.ANY),
            pl.BlockSpec((1, chunk), lambda c: (0, c)),
        ]
        + far,
        out_specs=[acts(), acts(), pl.BlockSpec((tokens, width), lambda c: (0, 0))],
        out_shape=[
            jax.ShapeDtypeStruct((tokens, units), BF16),
            jax.ShapeDtypeStruct((tokens, units), BF16),
            jax.ShapeDtypeStruct((tokens, width), F32),
        ],
        scratch_shapes=[
            pltpu.VMEM((units, width), BF16),
            pltpu.VMEM((units, width), BF16),
            pltpu.VMEM((width, chunk), BF16),
            pltpu.SemaphoreType.DMA((counts[0],)),
            pltpu.SemaphoreType.DMA((counts[1],)),
            pltpu.SemaphoreType.DMA((1,)),
        ],
        compiler_params=pltpu.CompilerParams(vmem_limit_bytes=VMEM_BYTES),
        cost_estimate=pl.CostEstimate(
            flops=4 * tokens * units * width, transcendentals=tokens * units, bytes_accessed=60 << 20
        ),
        name="feed_forward",
    )(u, base, b, *firsts, *seconds)


def backward_kernel(*refs, tile, counts, chunk):
    e_ref, u_ref, base_ref, act_ref, slope_ref = refs[:5]
    split = sum(counts)
    firsts, seconds = refs[5 : 5 + counts[0]], refs[5 + counts[0] : 5 + split]
    keep1_ref, keep2_ref, send1_ref, send2_ref, db_ref, du_ref = refs[5 + split : 11 + split]
    w1_ref, w2_ref, f_ref, turn_ref, sem1, sem2, sem3 = refs[11 + split :]
    start = pltpu.make_async_copy(base_ref, du_ref, sem3.at[0])

    @pl.when(pl.program_id(0) == 0)
    def _():
        start.start()

    fetch_weights(firsts, w1_ref, sem1, chunk)
    fetch_weights(seconds, w2_ref, sem2, chunk)
    here = pl.ds(pl.multiple_of(pl.program_id(0) * chunk, chunk), chunk)

    @pl.when(pl.program_id(0) == 0)
    def _():
        start.wait()

    turn_ref[...] = w2_ref[here, :].T

    def step(i, db):
        rows = pl.ds(pl.multiple_of(i * tile, tile), tile)
        dz = product(e_ref[rows, :], turn_ref[...]) * slope_ref[rows, :].astype(F32)
        low = dz.astype(BF16)
        f_ref[rows, :] = low
        du_ref[rows, :] += product(low, w1_ref[here, :])
        return db + jnp.sum(dz.reshape(tile // 8, 8, -1), axis=0)

    db = lax.fori_loop(0, e_ref.shape[0] // tile, step, jnp.zeros((8, chunk), F32))
    db_ref[...] = jnp.sum(db, axis=0, keepdims=True)
    dw2 = product_over_rows(act_ref[...], e_ref[...]).astype(BF16)
    dw1 = product_over_rows(f_ref[...], u_ref[...]).astype(BF16)
    half = pl.num_programs(0) // 2

    @pl.when(pl.program_id(0) < half)
    def _():
        keep1_ref[...] = dw1
        keep2_ref[...] = dw2

    @pl.when(pl.program_id(0) >= half)
    def _():
        send1_ref[...] = dw1
        send2_ref[...] = dw2


def feed_backward(e, u, base, act, slope, firsts, seconds, chunk=512, tile=1024):
    tokens, width = u.shape
    counts = (len(firsts), len(seconds))
    units = act.shape[1]
    half = units // chunk // 2
    acts = lambda: pl.BlockSpec((tokens, chunk), lambda c: (0, c))
    keep = lambda: pl.BlockSpec((chunk, width), lambda c: (jnp.minimum(c, half - 1), 0))
    send = lambda: pl.BlockSpec((chunk, width), lambda c: (jnp.maximum(c - half, 0), 0))
    far = lambda number: [pl.BlockSpec(memory_space=pl.ANY)] * number
    grads = jax.ShapeDtypeStruct((units // 2, width), BF16)
    return pl.pallas_call(
        functools.partial(backward_kernel, tile=tile, counts=counts, chunk=chunk),
        grid=(units // chunk,),
        in_specs=[whole_block((tokens, width)), whole_block((tokens, width))]
        + far(1)
        + [acts(), acts()]
        + far(sum(counts)),
        out_specs=[
            keep(),
            keep(),
            send(),
            send(),
            pl.BlockSpec((1, chunk), lambda c: (0, c)),
            whole_block((tokens, width)),
        ],
        out_shape=[grads] * 4
        + [
            jax.ShapeDtypeStruct((1, units), F32),
            jax.ShapeDtypeStruct((tokens, width), F32),
        ],
        scratch_shapes=[
            pltpu.VMEM((units, width), BF16),
            pltpu.VMEM((units, width), BF16),
            pltpu.VMEM((tokens, chunk), BF16),
            pltpu.VMEM((width, chunk), BF16),
            pltpu.SemaphoreType.DMA((counts[0],)),
            pltpu.SemaphoreType.DMA((counts[1],)),
            pltpu.SemaphoreType.DMA((1,)),
        ],
        compiler_params=pltpu.CompilerParams(vmem_limit_bytes=VMEM_BYTES),
        cost_estimate=pl.CostEstimate(
            flops=8 * tokens * units * width, transcendentals=0, bytes_accessed=60 << 20
        ),
        name="feed_backward",
    )(e, u, base, act, slope, *firsts, *seconds)


def table_pair(points, scale=None):
    numbers = jnp.arange(points, dtype=jnp.int32)
    coarse = 32 * jnp.arange(points // 32, dtype=jnp.int32)
    fine = jnp.arange(32, dtype=jnp.int32)

    def waves(rows):
        angles = (rows[:, None] * numbers[None, :] % points).astype(F32) * (2.0 * math.pi / points)
        return jnp.cos(angles), jnp.sin(angles)

    factor = 1.0 / math.sqrt(points)
    if points <= 64:
        cosine, sine = waves(numbers)
    else:
        coarse_cos, coarse_sin = waves(coarse)
        fine_cos, fine_sin = waves(fine)
        coarse_cos, coarse_sin, fine_cos, fine_sin = lax.optimization_barrier(
            (coarse_cos, coarse_sin, fine_cos, fine_sin)
        )
        coarse_cos, coarse_sin = coarse_cos[:, None], coarse_sin[:, None]
        fine_cos, fine_sin = fine_cos[None], fine_sin[None]
        cosine = (coarse_cos * fine_cos - coarse_sin * fine_sin).reshape(points, points)
        sine = (coarse_sin * fine_cos + coarse_cos * fine_sin).reshape(points, points)
    return (cosine * factor).astype(BF16), (sine * factor).astype(BF16)


def twiddles():
    row_index = jnp.arange(L1, dtype=jnp.int32)[None, :]
    col_index = jnp.arange(L2, dtype=jnp.int32)[:, None]
    angles = (row_index * col_index % L).astype(F32) * (2.0 * math.pi / L)
    return jnp.cos(angles)[:, :, None], jnp.sin(angles)[:, :, None]


def swap(values, step):
    axis, mask = step
    size = lax.axis_size(axis)
    return lax.ppermute(values, axis, [(i, i ^ mask) for i in range(size)])


def bits(size):
    masks = []
    mask = size // 2
    while mask >= 1:
        masks.append(mask)
        mask //= 2
    return masks


def widen(held, step):
    return jnp.concatenate([held, swap(held, step)], axis=0)


def widen_codes(codes, steps, groups):
    for axis, mask in steps:
        code = mask if axis == "seq" else mask * groups
        codes = codes + [held ^ code for held in codes]
    return codes


def spread(pieces, steps):
    for step in steps:
        pieces = pieces + [swap(piece, step) for piece in pieces]
    return pieces


def spread_core(pieces, step_core):
    return pieces + [swap(piece, step_core) for piece in pieces]


def fold(held, names, step, kind):
    axis = names.index(step)
    keep = lax.index_in_dim(held, 0, axis, keepdims=False)
    send = lax.index_in_dim(held, 1, axis, keepdims=False)
    total = keep.astype(F32) + swap(send.astype(kind), step).astype(F32)
    return total, names[:axis] + names[axis + 1 :]


def fold_all(held, names, steps, kind):
    for step in steps:
        held, names = fold(held, names, step, kind)
    return held, names


def arrange(rows):
    return with_layout_constraint(rows.transpose(0, 2, 1, 3), Layout(major_to_minor=(0, 1, 2, 3)))


def exchange(rows):
    order = Layout(major_to_minor=(0, 1, 2, 3))
    rows = with_layout_constraint(rows, order)
    rows = lax.all_to_all(rows, "seq", split_axis=0, concat_axis=0, tiled=True)
    return with_layout_constraint(rows, order)


def body(tokens, lengths, labels, picked, cotangent, w_in, b_in, w_out, shifts, norm_gains):
    groups = lax.axis_size("seq")
    me = lax.axis_index("seq")
    here = lax.axis_index("batch") * groups + me
    columns = tokens.shape[2]
    share = w_in.shape[2]
    part = shifts.shape[2]
    blocks = groups * lax.axis_size("batch")

    steps_plane = [("seq", mask) for mask in bits(groups)[:-1]]
    steps_batch = [("batch", mask) for mask in bits(lax.axis_size("batch"))]
    step_core = ("seq", 1)
    numbers = jnp.arange(blocks, dtype=jnp.int32)

    codes = widen_codes([0], steps_plane + steps_batch + [step_core], groups)
    owner = jnp.array(codes, dtype=jnp.int32) ^ here
    one_hot = (owner[:, None] == numbers[None, :]).astype(F32)

    steps_small = [steps_plane[-1], step_core] + steps_batch + steps_plane[:-1]
    small_codes = widen_codes([0], steps_small, groups)
    small_owner = jnp.array(small_codes, dtype=jnp.int32) ^ here
    small_hot = (small_owner[:, None] == numbers[None, :]).astype(F32)
    small = jnp.concatenate([b_in[0], shifts[0].reshape(-1), norm_gains[0].reshape(-1)])
    small = small.astype(F32)[None]
    for step in steps_small:
        small = widen(small, step)

    first_held = w_in[0].T[None]
    second_held = w_out[0][None]
    for step in steps_plane[:-1]:
        first_held = widen(first_held, step)
        second_held = widen(second_held, step)
    tokens_late, late_cotangent, small, first_held, second_held = lax.optimization_barrier(
        (arrange(tokens), arrange(cotangent), small, first_held, second_held)
    )
    first_held = widen(first_held, steps_plane[-1])
    seconds = []
    for piece in spread([second_held], steps_batch):
        seconds += [piece, swap(piece, steps_plane[-1])]

    wide_cos, wide_sin = table_pair(D)
    wide = jnp.stack([wide_cos, -wide_sin])
    twiddle_cos, twiddle_sin = twiddles()
    first_held, wide, twiddle_cos, twiddle_sin = lax.optimization_barrier(
        (first_held, wide, twiddle_cos, twiddle_sin)
    )
    firsts = spread([first_held], steps_batch)
    places = jnp.array([small_codes.index(code) for code in codes], dtype=jnp.int32)
    place_hot = (places[:, None] == numbers[None, :]).astype(F32)
    b_first = jnp.sum(place_hot[:, :, None] * small[None, :, :share], axis=1)
    b_first = b_first.reshape(1, blocks * share)
    rows = jnp.sum(small_hot[:, :, None] * small[:, None, share:], axis=0)
    rows = rows.reshape(blocks, 5, part).transpose(1, 0, 2).reshape(5, D)
    shifts_f = rows[:3]
    gains_f = rows[3:]

    short_cos, short_sin = table_pair(L1)
    long_cos, long_sin = table_pair(L2)
    short_table = jnp.concatenate([short_cos, short_sin], axis=0)
    long_table = jnp.stack([jnp.stack([long_cos, -long_sin]), jnp.stack([long_sin, long_cos])])
    both = jnp.eye(2, dtype=BF16)
    pair_table = jnp.einsum("qukm,bc->qkbcum", long_table, both).reshape(4 * L2, 4 * L2)

    x_all = exchange(tokens_late)
    x_all, late_cotangent = lax.optimization_barrier((x_all, late_cotangent))
    g_all = exchange(late_cotangent)

    length = lengths[me]
    spots = (
        L2 * jnp.arange(L1, dtype=jnp.int32)[None, :] + jnp.arange(L2, dtype=jnp.int32)[:, None]
    )
    valid = spots < length
    x_rows = x_all.reshape(L2, L1, D)
    x_rows = jnp.where(valid[:, :, None], x_rows, jnp.zeros_like(x_rows))

    first = jnp.einsum("kn,mnd->mkd", short_table, x_rows, preferred_element_type=F32)
    first_cos, first_sin = first[:, :L1], first[:, L1:]
    turned_cos = (first_cos * twiddle_cos - first_sin * twiddle_sin).astype(BF16)
    turned_sin = (first_cos * twiddle_sin + first_sin * twiddle_cos).astype(BF16)
    turned = jnp.stack([turned_cos, turned_sin]).reshape(2, L2, 2, L2, D)
    turned = turned.transpose(3, 2, 0, 1, 4).reshape(L2, 4 * L2, D)
    spectrum = jnp.einsum("rk,lkd->lrd", pair_table, turned, preferred_element_type=F32)
    spectrum = spectrum.astype(BF16).reshape(L2, 2, L1, D)
    mixed = jnp.einsum("lund,ude->lne", spectrum, wide, preferred_element_type=F32)
    mixed, firsts, seconds = lax.optimization_barrier((mixed, firsts, seconds))
    flat = lambda pieces: [piece.reshape(-1, D) for piece in spread_core(pieces, step_core)]
    firsts, seconds = flat(firsts), flat(seconds)
    residual = (x_rows.astype(F32) + mixed).reshape(L, D)

    normed = layer_norm(residual, gains_f[0], shifts_f[1])
    normed_low = normed.astype(BF16)
    act_low, slope, summed = feed_forward(
        normed_low, normed + shifts_f[0], firsts, b_first, seconds
    )
    layer_out = layer_norm(summed, gains_f[1], shifts_f[2]).astype(BF16)
    out_rows = exchange(layer_out.reshape(groups, columns, L1, D))

    grad_out = g_all.reshape(L, D).astype(F32)
    unused, pull_second = jax.vjp(layer_norm, summed, gains_f[1], shifts_f[2])
    grad_summed, grad_gain_two, grad_shift_two = pull_second(grad_out)
    grad_bias_two = jnp.sum(grad_summed, axis=0)
    summed_low = grad_summed.astype(BF16)
    keep_first, keep_second, send_first, send_second, grad_b_first, grad_normed = feed_backward(
        summed_low, normed_low, grad_summed, act_low, slope, firsts, seconds
    )
    names = steps_batch[::-1] + steps_plane[::-1]
    shape = (2,) * len(names) + (share,)
    normed_again, pull_first = jax.vjp(layer_norm, residual, gains_f[0], shifts_f[1])
    grad_residual, grad_gain_one, grad_shift_one = pull_first(grad_normed)
    residual_low = grad_residual.astype(BF16).reshape(L2, L1, D)

    def fold_core(keep, send):
        return keep.astype(F32) + swap(send, step_core).astype(F32)

    grad_first = fold_core(keep_first, send_first).reshape(shape + (D,))
    grad_second = fold_core(keep_second, send_second).reshape(shape + (D,))
    residual_low, grad_first, grad_second, out_rows = lax.optimization_barrier(
        (residual_low, grad_first, grad_second, out_rows)
    )
    grad_spectrum = jnp.einsum("lne,ude->lund", residual_low, wide, preferred_element_type=F32)
    grad_spectrum = grad_spectrum.astype(BF16).reshape(L2, 4 * L2, D)
    grad_turned = jnp.einsum("rk,lrd->lkd", pair_table, grad_spectrum, preferred_element_type=F32)
    grad_turned = grad_turned.astype(BF16).reshape(L2, 2, 2, L2, D).transpose(2, 3, 1, 0, 4)
    grad_turned = grad_turned.reshape(2, L2, L1, D)
    grad_cos, grad_sin = grad_turned[0], grad_turned[1]
    back_cos = grad_cos * twiddle_cos + grad_sin * twiddle_sin
    back_sin = grad_sin * twiddle_cos - grad_cos * twiddle_sin
    stacked = jnp.concatenate([back_cos, back_sin], axis=1).astype(BF16)
    grad_x = residual_low.astype(F32) + jnp.einsum(
        "kn,mkd->mnd", short_table, stacked, preferred_element_type=F32
    )
    grad_x = jnp.where(valid[:, :, None], grad_x, 0.0).astype(BF16)
    grad_x = grad_x.reshape(groups, columns, L1, D)
    input_grad = exchange(grad_x).transpose(0, 2, 1, 3)

    shift_of = jnp.arange(columns, dtype=jnp.int32) + me * columns
    place_of = L2 * jnp.arange(L1, dtype=jnp.int32)[None, :] + shift_of[:, None]
    steps_fold = steps_batch[::-1] + steps_plane[::-1]
    out_rows, grad_x = lax.optimization_barrier((out_rows, grad_x))
    logits = out_rows.astype(F32)
    highest = jnp.max(logits, axis=-1, keepdims=True)
    powers = jnp.exp(logits - highest)
    denominator = jnp.sum(powers, axis=-1)
    features = jnp.arange(D, dtype=jnp.int32)
    label_rows = labels.transpose(0, 2, 1)
    top = jnp.sum(jnp.where(features == label_rows[..., None], powers, 0.0), axis=-1)
    counted = (picked.transpose(0, 2, 1) > 0) & (place_of[None] < lengths[:, None, None])
    weight = jnp.where(counted, 1.0, 0.0)
    sums = jnp.stack([jnp.sum(weight * (top / denominator)), jnp.sum(weight)])

    norms = jnp.stack(
        [grad_bias_two, grad_shift_one, grad_shift_two, grad_gain_one, grad_gain_two]
    )
    norms = norms.reshape(5, blocks, part).transpose(1, 0, 2).reshape(blocks, 5 * part)
    norms = jnp.sum(one_hot[:, :, None] * norms[None], axis=1)
    sums = jnp.broadcast_to(sums[None], (blocks, 2))
    small_grads = jnp.concatenate([grad_b_first.reshape(blocks, share), norms, sums], axis=1)
    half = blocks // 2
    small_grads = fold_core(small_grads[:half], small_grads[half:])
    small_grads = small_grads.reshape(shape[:-1] + (-1,))
    grad_first, done = fold_all(grad_first, names, steps_fold, BF16)
    early = len(steps_batch)
    grad_second, names_second = fold_all(grad_second, names, steps_fold[:early], BF16)
    small_grads, names_small = fold_all(small_grads, names, steps_fold[:early], F32)
    small_grads, out_rows = lax.optimization_barrier((small_grads, out_rows))
    current = out_rows.transpose(0, 2, 1, 3)
    for step in steps_fold[early:]:
        small_grads, grad_second = lax.optimization_barrier((small_grads, grad_second))
        small_grads, names_small = fold(small_grads, names_small, step, F32)
        grad_second, names_second = fold(grad_second, names_second, step, BF16)
    norms = small_grads[share:-2].reshape(5, part)
    match_rate = D * small_grads[-2] / jnp.maximum(small_grads[-1], 1.0)
    return (
        current,
        input_grad,
        grad_first.T[None],
        small_grads[:share][None],
        grad_second[None],
        norms[:3][None],
        norms[3:][None],
        match_rate,
    )


def solution(mesh):
    in_specs = (
        P("batch", None, "seq", None),
        P("batch"),
        P("batch", None, "seq"),
        P("batch", None, "seq"),
        P("batch", None, "seq", None),
        P(None, None, ("batch", "seq")),
        P(None, ("batch", "seq")),
        P(None, ("batch", "seq"), None),
        P(None, None, ("batch", "seq")),
        P(None, None, ("batch", "seq")),
    )
    out_specs = (
        P("batch", None, "seq", None),
        P("batch", None, "seq", None),
        P(None, None, ("batch", "seq")),
        P(None, ("batch", "seq")),
        P(None, ("batch", "seq"), None),
        P(None, None, ("batch", "seq")),
        P(None, None, ("batch", "seq")),
        P(),
    )
    return jax.shard_map(body, mesh=mesh, in_specs=in_specs, out_specs=out_specs, check_vma=False)
```

```python
import functools
import math

import jax
import jax.numpy as jnp
from jax import lax
from jax.experimental import pallas as pl
from jax.experimental.layout import Layout, with_layout_constraint
from jax.experimental.pallas import tpu as pltpu
from jax.sharding import PartitionSpec as P

D = 768
L1 = 64
L2 = 32
L = 2048
LANES = 128
PAIR = 4 * L2
STRIDE = PAIR + 1

EPSILON = 1e-12
ROOT_TWO_PI = 0.7978845608028654
CUBIC = ROOT_TWO_PI * 0.044715
F32 = jnp.float32
BF16 = jnp.bfloat16
VMEM_BYTES = 60 << 20
FAR = pl.BlockSpec(memory_space=pl.ANY)


def product(left, right):
    return lax.dot_general(left, right, (((1,), (0,)), ((), ())), preferred_element_type=F32)


def product_over_rows(left, right):
    return lax.dot_general(left, right, (((0,), (0,)), ((), ())), preferred_element_type=F32)


def lanes(column):
    return jnp.concatenate([column] * (D // LANES), axis=1)


def rows_of_eight(values):
    return jnp.sum(values.reshape(-1, 8, values.shape[-1]), axis=0)


def average(values):
    return jnp.mean(values, axis=1, keepdims=True)


def norm_back(grad, x_hat, scale, gain):
    q = grad * gain
    return lanes(scale) * (q - average(q) - x_hat * average(q * x_hat))


def whole_block(shape):
    return pl.BlockSpec(shape, lambda c: (0,) * len(shape), pipeline_mode=pl.Buffered(1))


def params():
    return pltpu.CompilerParams(vmem_limit_bytes=VMEM_BYTES)


def cost(flops, transcendentals, size):
    return pl.CostEstimate(flops=flops, transcendentals=transcendentals, bytes_accessed=size)


def scatter(refs, start, value):
    for j, ref in enumerate(refs):
        ref[pl.ds(start, L2, stride=STRIDE), :] = value[:, j * LANES : (j + 1) * LANES]


def gather(refs, block):
    return jnp.concatenate([ref[pl.ds(block * STRIDE, PAIR), :] for ref in refs], axis=1)


def middle_scratch():
    return [pltpu.VMEM((L2 * STRIDE, LANES), F32)] * (D // LANES)


def transform_kernel(
    length_ref, x_ref, short_ref, pair_ref, cos_ref, sin_ref, vec_ref, wide_hbm,
    u_ref, base_ref, hat_ref, scale_ref, spec_ref, wide_ref, sem, *middle, group
):
    length = length_ref[0]
    step = pl.program_id(0)
    load = pltpu.make_async_copy(wide_hbm, wide_ref, sem.at[0])

    @pl.when(step == 0)
    def _():
        load.start()

        def first(m, carry):
            spots = L2 * lax.broadcasted_iota(jnp.int32, (L1, D), 0) + m
            x = jnp.where(spots < length, x_ref[m].astype(F32), 0.0).astype(BF16)
            y = product(short_ref[...], x)
            real, imag = y[:L1], y[L1:]
            cosine, sine = lanes(cos_ref[m]), lanes(sin_ref[m])
            turned = (real * cosine - imag * sine, real * sine + imag * cosine)
            for b in range(2):
                for part in range(2):
                    scatter(middle, (b * 2 + part) * L2 + m, turned[part][b * L2 : (b + 1) * L2])
            return carry

        lax.fori_loop(0, L2, first, 0, unroll=4)
        load.wait()

    for j in range(group):
        turned = gather(middle, step * group + j).astype(BF16)
        q = product(pair_ref[...], turned).astype(BF16)
        spec_ref[j * L1 : (j + 1) * L1, :D] = q[:L1]
        spec_ref[j * L1 : (j + 1) * L1, D:] = q[L1:]
    mixed = product(spec_ref[...], wide_ref[...])
    number = lax.broadcasted_iota(jnp.int32, (group * L1, D), 0)
    spots = L2 * (number % L1) + step * group + number // L1
    x = x_ref[pl.ds(step * group, group)].reshape(group * L1, D).astype(F32)
    h = jnp.where(spots < length, x, 0.0) + mixed
    center = h - average(h)
    scale = lax.rsqrt(average(center * center) + EPSILON)
    hat = center * scale
    u = hat * vec_ref[0:1, :] + vec_ref[1:2, :]
    u_ref[...] = u.astype(BF16)
    base_ref[...] = u + vec_ref[2:3, :]
    hat_ref[...] = hat.astype(BF16)
    scale_ref[...] = jnp.broadcast_to(scale, scale_ref.shape)


def transform(length, x, short, pair, cosine, sine, vec, wide, group=8):
    out = lambda width: pl.BlockSpec((group * L1, width), lambda c: (c, 0))
    return pl.pallas_call(
        functools.partial(transform_kernel, group=group),
        grid=(L2 // group,),
        in_specs=[pl.BlockSpec(memory_space=pltpu.SMEM)]
        + [whole_block(values.shape) for values in (x, short, pair, cosine, sine, vec)]
        + [FAR],
        out_specs=[out(D), out(D), out(D), out(LANES)],
        out_shape=[
            jax.ShapeDtypeStruct((L, D), BF16),
            jax.ShapeDtypeStruct((L, D), F32),
            jax.ShapeDtypeStruct((L, D), BF16),
            jax.ShapeDtypeStruct((L, LANES), F32),
        ],
        scratch_shapes=[
            pltpu.VMEM((group * L1, 2 * D), BF16),
            pltpu.VMEM((2 * D, D), BF16),
            pltpu.SemaphoreType.DMA((1,)),
        ]
        + middle_scratch(),
        compiler_params=params(),
        cost_estimate=cost(7 << 30, L, 24 << 20),
        name="transform",
    )(length, x, short, pair, cosine, sine, vec, wide)


def back_kernel(
    length_ref, du_ref, hat_ref, scale_ref, short_ref, pair_ref, cos_ref, sin_ref, vec_ref, wide_ref,
    dx_ref, sums_ref, rh_ref, spec_ref, *middle, group
):
    length = length_ref[0]
    step = pl.program_id(0)
    steps = L2 // group

    @pl.when(step == 0)
    def _():
        sums_ref[...] = jnp.zeros_like(sums_ref)

    @pl.when(step < steps)
    def _():
        du = du_ref[...]
        hat = hat_ref[...].astype(F32)
        rh = norm_back(du, hat, scale_ref[...], vec_ref[0:1, :]).astype(BF16)
        rh_ref[pl.ds(pl.multiple_of(step * group * L1, group * L1), group * L1), :] = rh
        sums_ref[0:8, :] += rows_of_eight(du * hat)
        sums_ref[8:16, :] += rows_of_eight(du)
        real = product(rh, wide_ref[:D, :]).astype(BF16)
        imag = product(rh, wide_ref[D:, :]).astype(BF16)
        for j in range(group):
            spec_ref[j, :L1, :] = real[j * L1 : (j + 1) * L1]
            spec_ref[j, L1:, :] = imag[j * L1 : (j + 1) * L1]
            turned = product(pair_ref[...], spec_ref[j]).astype(BF16).astype(F32)
            for b in range(2):
                for part in range(2):
                    start = (b * 2 + part) * L2
                    spot = part * L1 + b * L2 + step * group + j
                    scatter(middle, spot, turned[start : start + L2])

    @pl.when(step >= steps)
    def _():
        def second(i, carry):
            m = (step - steps) * group + i
            turned = gather(middle, m)
            real, imag = turned[:L1], turned[L1:]
            cosine, sine = lanes(cos_ref[m]), lanes(sin_ref[m])
            back = jnp.concatenate(
                [
                    (real * cosine + imag * sine).astype(BF16),
                    (imag * cosine - real * sine).astype(BF16),
                ],
                axis=0,
            )
            rh = rh_ref[pl.ds(pl.multiple_of(m * L1, L1), L1), :].astype(F32)
            dx = rh + product(short_ref[...], back)
            spots = L2 * lax.broadcasted_iota(jnp.int32, (L1, D), 0) + m
            dx_ref[i] = jnp.where(spots < length, dx, 0.0).astype(BF16)
            return carry

        lax.fori_loop(0, group, second, 0, unroll=4)


def transform_back(length, du, hat, scale, short, pair, cosine, sine, vec, wide, group=8):
    steps = L2 // group
    rows = lambda width: pl.BlockSpec((group * L1, width), lambda c: (jnp.minimum(c, steps - 1), 0))
    return pl.pallas_call(
        functools.partial(back_kernel, group=group),
        grid=(2 * steps,),
        in_specs=[pl.BlockSpec(memory_space=pltpu.SMEM), rows(D), rows(D), rows(LANES)]
        + [whole_block(values.shape) for values in (short, pair, cosine, sine, vec, wide)],
        out_specs=[
            pl.BlockSpec((group, L1, D), lambda c: (jnp.maximum(c - steps, 0), 0, 0)),
            pl.BlockSpec((16, D), lambda c: (0, 0)),
        ],
        out_shape=[
            jax.ShapeDtypeStruct((L2, L1, D), BF16),
            jax.ShapeDtypeStruct((16, D), F32),
        ],
        scratch_shapes=[pltpu.VMEM((L, D), BF16), pltpu.VMEM((group, 2 * L1, D), BF16)]
        + middle_scratch(),
        compiler_params=params(),
        cost_estimate=cost(7 << 30, 0, 20 << 20),
        name="transform_back",
    )(length, du, hat, scale, short, pair, cosine, sine, vec, wide)


def fetch_weights(pieces, holder, sems, chunk):
    rows = pieces[0].shape[0]
    step = pl.program_id(0)
    copies = [
        pltpu.make_async_copy(piece, holder.at[pl.ds(i * rows, rows), :], sems.at[i])
        for i, piece in enumerate(pieces)
    ]

    @pl.when(step == 0)
    def _():
        for copy in copies:
            copy.start()

    for number in range(rows * len(pieces) // chunk):
        needed = [copy for i, copy in enumerate(copies) if i * rows // chunk == number]
        if needed:

            @pl.when(step == number)
            def _():
                for copy in needed:
                    copy.wait()


def forward_kernel(*refs, tile, counts, chunk):
    u_ref, base_ref, b_ref, vec_ref = refs[:4]
    split = 4 + sum(counts)
    firsts, seconds = refs[4 : 4 + counts[0]], refs[4 + counts[0] : split]
    act_ref, slope_ref, out_ref, hat_ref, scale_ref = refs[split : split + 5]
    y_ref, w1_ref, w2_ref, turn_ref, sem1, sem2, sem3 = refs[split + 5 :]
    start = pltpu.make_async_copy(base_ref, y_ref, sem3.at[0])
    tiles = u_ref.shape[0] // tile

    @pl.when(pl.program_id(0) == 0)
    def _():
        start.start()

    fetch_weights(firsts, w1_ref, sem1, chunk)
    fetch_weights(seconds, w2_ref, sem2, chunk)
    here = pl.ds(pl.multiple_of(pl.program_id(0) * chunk, chunk), chunk)

    @pl.when(pl.program_id(0) == 0)
    def _():
        start.wait()

    turn_ref[...] = w1_ref[here, :].T

    def step(i, carry):
        rows = pl.ds(pl.multiple_of(i * tile, tile), tile)
        z = product(u_ref[rows, :], turn_ref[...]) + b_ref[...]
        square = z * z
        t = jnp.tanh(z * (ROOT_TWO_PI + CUBIC * square))
        half = 0.5 + 0.5 * t
        a = z * half
        low = a.astype(BF16)
        act_ref[rows, :] = low
        slope = half + (a - a * t) * (ROOT_TWO_PI + (3.0 * CUBIC) * square)
        slope_ref[rows, :] = slope.astype(BF16)
        y_ref[rows, :] += product(low, w2_ref[here, :])
        return carry

    lax.fori_loop(0, tiles, step, 0)

    @pl.when(pl.program_id(0) == pl.num_programs(0) - 1)
    def _():
        small = 256

        def finish(i, carry):
            rows = pl.ds(pl.multiple_of(i * small, small), small)
            y = y_ref[rows, :]
            center = y - average(y)
            scale = lax.rsqrt(average(center * center) + EPSILON)
            hat = center * scale
            out_ref[rows, :] = (hat * vec_ref[0:1, :] + vec_ref[1:2, :]).astype(BF16)
            hat_ref[rows, :] = hat.astype(BF16)
            scale_ref[rows, :] = jnp.broadcast_to(scale, (small, LANES))
            return carry

        lax.fori_loop(0, u_ref.shape[0] // small, finish, 0)


def feed_forward(u, base, b, vec, firsts, seconds, chunk=768, tile=1024):
    tokens, width = u.shape
    counts = (len(firsts), len(seconds))
    units = b.shape[1]
    acts = lambda: pl.BlockSpec((tokens, chunk), lambda c: (0, c))
    return pl.pallas_call(
        functools.partial(forward_kernel, tile=tile, counts=counts, chunk=chunk),
        grid=(units // chunk,),
        in_specs=[
            whole_block((tokens, width)),
            FAR,
            pl.BlockSpec((1, chunk), lambda c: (0, c)),
            whole_block(vec.shape),
        ]
        + [FAR] * sum(counts),
        out_specs=[
            acts(),
            acts(),
            whole_block((tokens, width)),
            whole_block((tokens, width)),
            whole_block((tokens, LANES)),
        ],
        out_shape=[
            jax.ShapeDtypeStruct((tokens, units), BF16),
            jax.ShapeDtypeStruct((tokens, units), BF16),
            jax.ShapeDtypeStruct((tokens, width), BF16),
            jax.ShapeDtypeStruct((tokens, width), BF16),
            jax.ShapeDtypeStruct((tokens, LANES), F32),
        ],
        scratch_shapes=[
            pltpu.VMEM((tokens, width), F32),
            pltpu.VMEM((units, width), BF16),
            pltpu.VMEM((units, width), BF16),
            pltpu.VMEM((width, chunk), BF16),
            pltpu.SemaphoreType.DMA((counts[0],)),
            pltpu.SemaphoreType.DMA((counts[1],)),
            pltpu.SemaphoreType.DMA((1,)),
        ],
        compiler_params=params(),
        cost_estimate=cost(4 * tokens * units * width, tokens * units, 50 << 20),
        name="feed_forward",
    )(u, base, b, vec, *firsts, *seconds)


def backward_kernel(*refs, tile, counts, chunk):
    g_ref, hat_ref, scale_ref, vec_ref, u_ref, act_ref, slope_ref = refs[:7]
    split = 7 + sum(counts)
    firsts, seconds = refs[7 : 7 + counts[0]], refs[7 + counts[0] : split]
    keep1_ref, keep2_ref, send1_ref, send2_ref, db_ref, du_ref, sums_ref = refs[split : split + 7]
    e_ref, w1_ref, w2_ref, f_ref, turn_ref, sem1, sem2 = refs[split + 7 :]
    fetch_weights(firsts, w1_ref, sem1, chunk)
    fetch_weights(seconds, w2_ref, sem2, chunk)
    here = pl.ds(pl.multiple_of(pl.program_id(0) * chunk, chunk), chunk)

    @pl.when(pl.program_id(0) == 0)
    def _():
        small = 256
        sums_ref[...] = jnp.zeros_like(sums_ref)

        def begin(i, carry):
            rows = pl.ds(pl.multiple_of(i * small, small), small)
            g = g_ref[rows, :].astype(F32)
            hat = hat_ref[rows, :].astype(F32)
            dy = norm_back(g, hat, scale_ref[rows, :], vec_ref[0:1, :])
            du_ref[rows, :] = dy
            e_ref[rows, :] = dy.astype(BF16)
            sums_ref[0:8, :] += rows_of_eight(dy)
            sums_ref[8:16, :] += rows_of_eight(g * hat)
            sums_ref[16:24, :] += rows_of_eight(g)
            return carry

        lax.fori_loop(0, u_ref.shape[0] // small, begin, 0)

    turn_ref[...] = w2_ref[here, :].T

    def step(i, db):
        rows = pl.ds(pl.multiple_of(i * tile, tile), tile)
        dz = product(e_ref[rows, :], turn_ref[...]) * slope_ref[rows, :].astype(F32)
        low = dz.astype(BF16)
        f_ref[rows, :] = low
        du_ref[rows, :] += product(low, w1_ref[here, :])
        return db + rows_of_eight(dz)

    db = lax.fori_loop(0, u_ref.shape[0] // tile, step, jnp.zeros((8, chunk), F32))
    db_ref[...] = jnp.sum(db, axis=0, keepdims=True)
    dw2 = product_over_rows(act_ref[...], e_ref[...]).astype(BF16)
    dw1 = product_over_rows(f_ref[...], u_ref[...]).astype(BF16)
    half = pl.num_programs(0) // 2

    @pl.when(pl.program_id(0) < half)
    def _():
        keep1_ref[...] = dw1
        keep2_ref[...] = dw2

    @pl.when(pl.program_id(0) >= half)
    def _():
        send1_ref[...] = dw1
        send2_ref[...] = dw2


def feed_backward(g, hat, scale, vec, u, act, slope, firsts, seconds, chunk=512, tile=1024):
    tokens, width = u.shape
    counts = (len(firsts), len(seconds))
    units = act.shape[1]
    half = units // chunk // 2
    acts = lambda: pl.BlockSpec((tokens, chunk), lambda c: (0, c))
    keep = lambda: pl.BlockSpec((chunk, width), lambda c: (jnp.minimum(c, half - 1), 0))
    send = lambda: pl.BlockSpec((chunk, width), lambda c: (jnp.maximum(c - half, 0), 0))
    grads = jax.ShapeDtypeStruct((units // 2, width), BF16)
    return pl.pallas_call(
        functools.partial(backward_kernel, tile=tile, counts=counts, chunk=chunk),
        grid=(units // chunk,),
        in_specs=[whole_block(values.shape) for values in (g, hat, scale, vec, u)]
        + [acts(), acts()]
        + [FAR] * sum(counts),
        out_specs=[
            keep(),
            keep(),
            send(),
            send(),
            pl.BlockSpec((1, chunk), lambda c: (0, c)),
            whole_block((tokens, width)),
            whole_block((24, width)),
        ],
        out_shape=[grads] * 4
        + [
            jax.ShapeDtypeStruct((1, units), F32),
            jax.ShapeDtypeStruct((tokens, width), F32),
            jax.ShapeDtypeStruct((24, width), F32),
        ],
        scratch_shapes=[
            pltpu.VMEM((tokens, width), BF16),
            pltpu.VMEM((units, width), BF16),
            pltpu.VMEM((units, width), BF16),
            pltpu.VMEM((tokens, chunk), BF16),
            pltpu.VMEM((width, chunk), BF16),
            pltpu.SemaphoreType.DMA((counts[0],)),
            pltpu.SemaphoreType.DMA((counts[1],)),
        ],
        compiler_params=params(),
        cost_estimate=cost(8 * tokens * units * width, 0, 60 << 20),
        name="feed_backward",
    )(g, hat, scale, vec, u, act, slope, *firsts, *seconds)


def table_pair(points):
    numbers = jnp.arange(points, dtype=jnp.int32)
    coarse = 32 * jnp.arange(points // 32, dtype=jnp.int32)
    fine = jnp.arange(32, dtype=jnp.int32)

    def waves(rows):
        angles = (rows[:, None] * numbers[None, :] % points).astype(F32) * (2.0 * math.pi / points)
        return jnp.cos(angles), jnp.sin(angles)

    factor = 1.0 / math.sqrt(points)
    if points <= 64:
        cosine, sine = waves(numbers)
    else:
        coarse_cos, coarse_sin = waves(coarse)
        fine_cos, fine_sin = waves(fine)
        coarse_cos, coarse_sin, fine_cos, fine_sin = lax.optimization_barrier(
            (coarse_cos, coarse_sin, fine_cos, fine_sin)
        )
        coarse_cos, coarse_sin = coarse_cos[:, None], coarse_sin[:, None]
        fine_cos, fine_sin = fine_cos[None], fine_sin[None]
        cosine = (coarse_cos * fine_cos - coarse_sin * fine_sin).reshape(points, points)
        sine = (coarse_sin * fine_cos + coarse_cos * fine_sin).reshape(points, points)
    return (cosine * factor).astype(BF16), (sine * factor).astype(BF16)


def twiddles():
    row_index = jnp.arange(L1, dtype=jnp.int32)[None, :]
    col_index = jnp.arange(L2, dtype=jnp.int32)[:, None]
    angles = (row_index * col_index % L).astype(F32) * (2.0 * math.pi / L)
    wave = jnp.cos(angles), jnp.sin(angles)
    return [jnp.broadcast_to(values[:, :, None], (L2, L1, LANES)) for values in wave]


def swap(values, step):
    axis, mask = step
    size = lax.axis_size(axis)
    return lax.ppermute(values, axis, [(i, i ^ mask) for i in range(size)])


def bits(size):
    masks = []
    mask = size // 2
    while mask >= 1:
        masks.append(mask)
        mask //= 2
    return masks


def widen(held, step):
    return jnp.concatenate([held, swap(held, step)], axis=0)


def widen_codes(codes, steps, groups):
    for axis, mask in steps:
        code = mask if axis == "seq" else mask * groups
        codes = codes + [held ^ code for held in codes]
    return codes


def spread(pieces, steps):
    for step in steps:
        pieces = pieces + [swap(piece, step) for piece in pieces]
    return pieces


def spread_core(pieces, step_core):
    return pieces + [swap(piece, step_core) for piece in pieces]


def total(addends):
    return sum(addends[1:], addends[0].astype(F32))


def half_of(addends, axis, number):
    return [lax.index_in_dim(held, number, axis, keepdims=False) for held in addends]


def fold(addends, names, step, kind):
    axis = names.index(step)
    send = total(half_of(addends, axis, 1)).astype(kind)
    arrived = swap(send, step)
    return half_of(addends, axis, 0) + [arrived], names[:axis] + names[axis + 1 :]


def fold_all(addends, names, steps, kind):
    for step in steps:
        addends, names = fold(addends, names, step, kind)
    return addends, names


def arrange(rows):
    return with_layout_constraint(rows.transpose(0, 2, 1, 3), Layout(major_to_minor=(0, 1, 2, 3)))


def exchange(rows):
    order = Layout(major_to_minor=(0, 1, 2, 3))
    rows = with_layout_constraint(rows, order)
    rows = lax.all_to_all(rows, "seq", split_axis=0, concat_axis=0, tiled=True)
    return with_layout_constraint(rows, order)


def body(tokens, lengths, labels, picked, cotangent, w_in, b_in, w_out, shifts, norm_gains):
    groups = lax.axis_size("seq")
    me = lax.axis_index("seq")
    here = lax.axis_index("batch") * groups + me
    columns = tokens.shape[2]
    share = w_in.shape[2]
    part = shifts.shape[2]
    blocks = groups * lax.axis_size("batch")

    steps_plane = [("seq", mask) for mask in bits(groups)[:-1]]
    steps_batch = [("batch", mask) for mask in bits(lax.axis_size("batch"))]
    step_core = ("seq", 1)
    numbers = jnp.arange(blocks, dtype=jnp.int32)

    codes = widen_codes([0], steps_plane + steps_batch + [step_core], groups)
    owner = jnp.array(codes, dtype=jnp.int32) ^ here
    one_hot = (owner[:, None] == numbers[None, :]).astype(F32)

    steps_small = [steps_plane[-1], step_core] + steps_batch + steps_plane[:-1]
    small_codes = widen_codes([0], steps_small, groups)
    small_owner = jnp.array(small_codes, dtype=jnp.int32) ^ here
    small_hot = (small_owner[:, None] == numbers[None, :]).astype(F32)
    small = jnp.concatenate([b_in[0], shifts[0].reshape(-1), norm_gains[0].reshape(-1)])
    small = small.astype(F32)[None]
    for step in steps_small:
        small = widen(small, step)

    first_held = w_in[0].T[None]
    second_held = w_out[0][None]
    for step in steps_plane[:-1]:
        first_held = widen(first_held, step)
        second_held = widen(second_held, step)
    tokens_late, late_cotangent, small, first_held, second_held = lax.optimization_barrier(
        (arrange(tokens), arrange(cotangent), small, first_held, second_held)
    )
    first_held = widen(first_held, steps_plane[-1])
    seconds = []
    for piece in spread([second_held], steps_batch):
        seconds += [piece, swap(piece, steps_plane[-1])]

    wide_cos, wide_sin = table_pair(D)
    wide = jnp.concatenate([wide_cos, -wide_sin], axis=0)
    twiddle_cos, twiddle_sin = twiddles()
    firsts = [first_held]
    places = jnp.array([small_codes.index(code) for code in codes], dtype=jnp.int32)
    place_hot = (places[:, None] == numbers[None, :]).astype(F32)
    b_first = jnp.sum(place_hot[:, :, None] * small[None, :, :share], axis=1)
    b_first = b_first.reshape(1, blocks * share)
    rows = jnp.sum(small_hot[:, :, None] * small[:, None, share:], axis=0)
    rows = rows.reshape(blocks, 5, part).transpose(1, 0, 2).reshape(5, D)
    shifts_f = rows[:3]
    gains_f = rows[3:]

    short_cos, short_sin = table_pair(L1)
    long_cos, long_sin = table_pair(L2)
    short_table = jnp.concatenate([short_cos, short_sin], axis=0)
    long_table = jnp.stack([jnp.stack([long_cos, -long_sin]), jnp.stack([long_sin, long_cos])])
    both = jnp.eye(2, dtype=BF16)
    pair_table = jnp.einsum("qukm,bc->qkbcum", long_table, both).reshape(4 * L2, 4 * L2)

    length = lax.dynamic_slice_in_dim(lengths, me, 1)
    blank = jnp.zeros((5, D), F32)
    vec_one = jnp.concatenate([gains_f[0:1], shifts_f[1:2], shifts_f[0:1], blank])
    vec_two = jnp.concatenate([gains_f[1:2], shifts_f[2:3], blank, blank[:1]])
    x_all = exchange(tokens_late)
    early = (wide, twiddle_cos, twiddle_sin, short_table, pair_table, vec_one, vec_two, b_first)
    x_all, late_cotangent, firsts, seconds, early = lax.optimization_barrier(
        (x_all, late_cotangent, firsts, seconds, early)
    )
    wide, twiddle_cos, twiddle_sin, short_table, pair_table, vec_one, vec_two, b_first = early
    firsts = spread(firsts, steps_batch)
    g_all = exchange(late_cotangent)

    x_rows = x_all.reshape(L2, L1, D)
    u, base, hat_one, scale_one = transform(
        length, x_rows, short_table, pair_table, twiddle_cos, twiddle_sin, vec_one, wide
    )
    u, firsts, seconds = lax.optimization_barrier((u, firsts, seconds))
    flat = lambda pieces: [piece.reshape(-1, D) for piece in spread_core(pieces, step_core)]
    firsts, seconds = flat(firsts), flat(seconds)
    act, slope, layer_out, hat_two, scale_two = feed_forward(
        u, base, b_first, vec_two, firsts, seconds
    )
    out_rows = exchange(layer_out.reshape(groups, columns, L1, D))

    keep_first, keep_second, send_first, send_second, grad_b_first, grad_u, sums_two = feed_backward(
        g_all.reshape(L, D), hat_two, scale_two, vec_two, u, act, slope, firsts, seconds
    )
    names = steps_batch[::-1] + steps_plane[::-1]
    shape = (2,) * len(names) + (share,)
    came_first = swap(send_first, step_core)
    came_second = swap(send_second, step_core)
    grad_x, sums_one = transform_back(
        length, grad_u, hat_one, scale_one, short_table.T, pair_table.T,
        twiddle_cos, twiddle_sin, vec_one, wide
    )
    grad_x, came_first, came_second, out_rows = lax.optimization_barrier(
        (grad_x, came_first, came_second, out_rows)
    )
    grad_first = [values.reshape(shape + (D,)) for values in (keep_first, came_first)]
    grad_second = [values.reshape(shape + (D,)) for values in (keep_second, came_second)]
    sums_two = jnp.sum(sums_two.reshape(3, 8, D), axis=1)
    sums_one = jnp.sum(sums_one.reshape(2, 8, D), axis=1)
    grad_x = grad_x.reshape(groups, columns, L1, D)
    input_grad = exchange(grad_x).transpose(0, 2, 1, 3)

    shift_of = jnp.arange(columns, dtype=jnp.int32) + me * columns
    place_of = L2 * jnp.arange(L1, dtype=jnp.int32)[None, :] + shift_of[:, None]
    steps_fold = steps_batch[::-1] + steps_plane[::-1]
    out_rows, grad_x = lax.optimization_barrier((out_rows, grad_x))
    logits = out_rows.astype(F32)
    highest = jnp.max(logits, axis=-1, keepdims=True)
    powers = jnp.exp(logits - highest)
    denominator = jnp.sum(powers, axis=-1)
    features = jnp.arange(D, dtype=jnp.int32)
    label_rows = labels.transpose(0, 2, 1)
    top = jnp.sum(jnp.where(features == label_rows[..., None], powers, 0.0), axis=-1)
    counted = (picked.transpose(0, 2, 1) > 0) & (place_of[None] < lengths[:, None, None])
    weight = jnp.where(counted, 1.0, 0.0)
    sums = jnp.stack([jnp.sum(weight * (top / denominator)), jnp.sum(weight)])

    norms = jnp.stack([sums_two[0], sums_one[1], sums_two[2], sums_one[0], sums_two[1]])
    norms = norms.reshape(5, blocks, part).transpose(1, 0, 2).reshape(blocks, 5 * part)
    norms = jnp.sum(one_hot[:, :, None] * norms[None], axis=1)
    sums = jnp.broadcast_to(sums[None], (blocks, 2))
    small_grads = jnp.concatenate([grad_b_first.reshape(blocks, share), norms, sums], axis=1)
    half = blocks // 2
    arrived = swap(small_grads[half:], step_core)
    small = [values.reshape(shape[:-1] + (-1,)) for values in (small_grads[:half], arrived)]
    early = len(steps_batch)
    grad_first, done = fold_all(grad_first, names, steps_fold, BF16)
    grad_second, names_second = fold_all(grad_second, names, steps_fold[:early], BF16)
    small, names_small = fold_all(small, names, steps_fold[:early], F32)
    small, out_rows = lax.optimization_barrier((small, out_rows))
    current = out_rows.transpose(0, 2, 1, 3)
    for step in steps_fold[early:]:
        small, grad_second = lax.optimization_barrier((small, grad_second))
        small, names_small = fold(small, names_small, step, F32)
        grad_second, names_second = fold(grad_second, names_second, step, BF16)
    small_grads, grad_first, grad_second = total(small), total(grad_first), total(grad_second)
    norms = small_grads[share:-2].reshape(5, part)
    match_rate = D * small_grads[-2] / jnp.maximum(small_grads[-1], 1.0)
    return (
        current,
        input_grad,
        grad_first.T[None],
        small_grads[:share][None],
        grad_second[None],
        norms[:3][None],
        norms[3:][None],
        match_rate,
    )


def solution(mesh):
    in_specs = (
        P("batch", None, "seq", None),
        P("batch"),
        P("batch", None, "seq"),
        P("batch", None, "seq"),
        P("batch", None, "seq", None),
        P(None, None, ("batch", "seq")),
        P(None, ("batch", "seq")),
        P(None, ("batch", "seq"), None),
        P(None, None, ("batch", "seq")),
        P(None, None, ("batch", "seq")),
    )
    out_specs = (
        P("batch", None, "seq", None),
        P("batch", None, "seq", None),
        P(None, None, ("batch", "seq")),
        P(None, ("batch", "seq")),
        P(None, ("batch", "seq"), None),
        P(None, None, ("batch", "seq")),
        P(None, None, ("batch", "seq")),
        P(),
    )
    return jax.shard_map(body, mesh=mesh, in_specs=in_specs, out_specs=out_specs, check_vma=False)
```

```python
import functools
import math

import jax
import jax.numpy as jnp
from jax import lax
from jax.experimental import pallas as pl
from jax.experimental.layout import Layout, with_layout_constraint
from jax.experimental.pallas import tpu as pltpu
from jax.sharding import PartitionSpec as P

D = 768
L1 = 64
L2 = 32
L = 2048
LANES = 128
PAIR = 4 * L2
STRIDE = PAIR + 1

EPSILON = 1e-12
ROOT_TWO_PI = 0.7978845608028654
CUBIC = ROOT_TWO_PI * 0.044715
F32 = jnp.float32
BF16 = jnp.bfloat16
VMEM_BYTES = 60 << 20
FAR = pl.BlockSpec(memory_space=pl.ANY)


def product(left, right):
    return lax.dot_general(left, right, (((1,), (0,)), ((), ())), preferred_element_type=F32)


def product_over_rows(left, right):
    return lax.dot_general(left, right, (((0,), (0,)), ((), ())), preferred_element_type=F32)


def lanes(column):
    return jnp.concatenate([column] * (D // LANES), axis=1)


def rows_of_eight(values):
    return jnp.sum(values.reshape(-1, 8, values.shape[-1]), axis=0)


def average(values):
    return jnp.mean(values, axis=1, keepdims=True)


def norm_back(grad, x_hat, scale, gain):
    q = grad * gain
    return lanes(scale) * (q - average(q) - x_hat * average(q * x_hat))


def whole_block(shape):
    return pl.BlockSpec(shape, lambda c: (0,) * len(shape), pipeline_mode=pl.Buffered(1))


def params():
    return pltpu.CompilerParams(vmem_limit_bytes=VMEM_BYTES)


def cost(flops, transcendentals, size):
    return pl.CostEstimate(flops=flops, transcendentals=transcendentals, bytes_accessed=size)


def scatter(refs, start, value):
    for j, ref in enumerate(refs):
        ref[pl.ds(start, L2, stride=STRIDE), :] = value[:, j * LANES : (j + 1) * LANES]


def gather(refs, block):
    return jnp.concatenate([ref[pl.ds(block * STRIDE, PAIR), :] for ref in refs], axis=1)


def middle_scratch():
    return [pltpu.VMEM((L2 * STRIDE, LANES), F32)] * (D // LANES)


def transform_kernel(
    length_ref, x_ref, short_ref, pair_ref, cos_ref, sin_ref, vec_ref, wide_hbm,
    u_ref, base_ref, hat_ref, scale_ref, spec_ref, wide_ref, sem, *middle, group
):
    length = length_ref[0]
    step = pl.program_id(0)
    load = pltpu.make_async_copy(wide_hbm, wide_ref, sem.at[0])

    @pl.when(step == 0)
    def _():
        load.start()

        def first(m, carry):
            spots = L2 * lax.broadcasted_iota(jnp.int32, (L1, D), 0) + m
            x = jnp.where(spots < length, x_ref[m].astype(F32), 0.0).astype(BF16)
            y = product(short_ref[...], x)
            real, imag = y[:L1], y[L1:]
            cosine, sine = lanes(cos_ref[m]), lanes(sin_ref[m])
            turned = (real * cosine - imag * sine, real * sine + imag * cosine)
            for b in range(2):
                for part in range(2):
                    scatter(middle, (b * 2 + part) * L2 + m, turned[part][b * L2 : (b + 1) * L2])
            return carry

        lax.fori_loop(0, L2, first, 0, unroll=4)
        load.wait()

    for j in range(group):
        turned = gather(middle, step * group + j).astype(BF16)
        q = product(pair_ref[...], turned).astype(BF16)
        spec_ref[j * L1 : (j + 1) * L1, :D] = q[:L1]
        spec_ref[j * L1 : (j + 1) * L1, D:] = q[L1:]
    mixed = product(spec_ref[...], wide_ref[...])
    number = lax.broadcasted_iota(jnp.int32, (group * L1, D), 0)
    spots = L2 * (number % L1) + step * group + number // L1
    x = x_ref[pl.ds(step * group, group)].reshape(group * L1, D).astype(F32)
    h = jnp.where(spots < length, x, 0.0) + mixed
    center = h - average(h)
    scale = lax.rsqrt(average(center * center) + EPSILON)
    hat = center * scale
    u = hat * vec_ref[0:1, :] + vec_ref[1:2, :]
    u_ref[...] = u.astype(BF16)
    base_ref[...] = u + vec_ref[2:3, :]
    hat_ref[...] = hat.astype(BF16)
    scale_ref[...] = jnp.broadcast_to(scale, scale_ref.shape)


def transform(length, x, short, pair, cosine, sine, vec, wide, group=8):
    out = lambda width: pl.BlockSpec((group * L1, width), lambda c: (c, 0))
    return pl.pallas_call(
        functools.partial(transform_kernel, group=group),
        grid=(L2 // group,),
        in_specs=[pl.BlockSpec(memory_space=pltpu.SMEM)]
        + [whole_block(values.shape) for values in (x, short, pair, cosine, sine, vec)]
        + [FAR],
        out_specs=[out(D), out(D), out(D), out(LANES)],
        out_shape=[
            jax.ShapeDtypeStruct((L, D), BF16),
            jax.ShapeDtypeStruct((L, D), F32),
            jax.ShapeDtypeStruct((L, D), BF16),
            jax.ShapeDtypeStruct((L, LANES), F32),
        ],
        scratch_shapes=[
            pltpu.VMEM((group * L1, 2 * D), BF16),
            pltpu.VMEM((2 * D, D), BF16),
            pltpu.SemaphoreType.DMA((1,)),
        ]
        + middle_scratch(),
        compiler_params=params(),
        cost_estimate=cost(7 << 30, L, 24 << 20),
        name="transform",
    )(length, x, short, pair, cosine, sine, vec, wide)


def back_kernel(
    length_ref, du_ref, hat_ref, scale_ref, short_ref, pair_ref, cos_ref, sin_ref, vec_ref, wide_ref,
    dx_ref, sums_ref, rh_ref, spec_ref, *middle, group
):
    length = length_ref[0]
    step = pl.program_id(0)
    steps = L2 // group

    @pl.when(step == 0)
    def _():
        sums_ref[...] = jnp.zeros_like(sums_ref)

    @pl.when(step < steps)
    def _():
        du = du_ref[...]
        hat = hat_ref[...].astype(F32)
        rh = norm_back(du, hat, scale_ref[...], vec_ref[0:1, :]).astype(BF16)
        rh_ref[pl.ds(pl.multiple_of(step * group * L1, group * L1), group * L1), :] = rh
        sums_ref[0:8, :] += rows_of_eight(du * hat)
        sums_ref[8:16, :] += rows_of_eight(du)
        real = product(rh, wide_ref[:D, :]).astype(BF16)
        imag = product(rh, wide_ref[D:, :]).astype(BF16)
        for j in range(group):
            spec_ref[j, :L1, :] = real[j * L1 : (j + 1) * L1]
            spec_ref[j, L1:, :] = imag[j * L1 : (j + 1) * L1]
            turned = product(pair_ref[...], spec_ref[j]).astype(BF16).astype(F32)
            for b in range(2):
                for part in range(2):
                    start = (b * 2 + part) * L2
                    spot = part * L1 + b * L2 + step * group + j
                    scatter(middle, spot, turned[start : start + L2])

    @pl.when(step >= steps)
    def _():
        def second(i, carry):
            m = (step - steps) * group + i
            turned = gather(middle, m)
            real, imag = turned[:L1], turned[L1:]
            cosine, sine = lanes(cos_ref[m]), lanes(sin_ref[m])
            back = jnp.concatenate(
                [
                    (real * cosine + imag * sine).astype(BF16),
                    (imag * cosine - real * sine).astype(BF16),
                ],
                axis=0,
            )
            rh = rh_ref[pl.ds(pl.multiple_of(m * L1, L1), L1), :].astype(F32)
            dx = rh + product(short_ref[...], back)
            spots = L2 * lax.broadcasted_iota(jnp.int32, (L1, D), 0) + m
            dx_ref[i] = jnp.where(spots < length, dx, 0.0).astype(BF16)
            return carry

        lax.fori_loop(0, group, second, 0, unroll=4)


def transform_back(length, du, hat, scale, short, pair, cosine, sine, vec, wide, group=8):
    steps = L2 // group
    rows = lambda width: pl.BlockSpec((group * L1, width), lambda c: (jnp.minimum(c, steps - 1), 0))
    return pl.pallas_call(
        functools.partial(back_kernel, group=group),
        grid=(2 * steps,),
        in_specs=[pl.BlockSpec(memory_space=pltpu.SMEM), rows(D), rows(D), rows(LANES)]
        + [whole_block(values.shape) for values in (short, pair, cosine, sine, vec, wide)],
        out_specs=[
            pl.BlockSpec((group, L1, D), lambda c: (jnp.maximum(c - steps, 0), 0, 0)),
            pl.BlockSpec((16, D), lambda c: (0, 0)),
        ],
        out_shape=[
            jax.ShapeDtypeStruct((L2, L1, D), BF16),
            jax.ShapeDtypeStruct((16, D), F32),
        ],
        scratch_shapes=[pltpu.VMEM((L, D), BF16), pltpu.VMEM((group, 2 * L1, D), BF16)]
        + middle_scratch(),
        compiler_params=params(),
        cost_estimate=cost(7 << 30, 0, 20 << 20),
        name="transform_back",
    )(length, du, hat, scale, short, pair, cosine, sine, vec, wide)


def fetch_weights(pieces, holder, sems, chunk):
    rows = pieces[0].shape[0]
    step = pl.program_id(0)
    copies = [
        pltpu.make_async_copy(piece, holder.at[pl.ds(i * rows, rows), :], sems.at[i])
        for i, piece in enumerate(pieces)
    ]

    @pl.when(step == 0)
    def _():
        for copy in copies:
            copy.start()

    for number in range(rows * len(pieces) // chunk):
        needed = [copy for i, copy in enumerate(copies) if i * rows // chunk == number]
        if needed:

            @pl.when(step == number)
            def _():
                for copy in needed:
                    copy.wait()


def forward_kernel(*refs, tile, counts, chunk):
    u_ref, base_ref, b_ref, vec_ref = refs[:4]
    split = 4 + sum(counts)
    firsts, seconds = refs[4 : 4 + counts[0]], refs[4 + counts[0] : split]
    act_ref, slope_ref, out_ref, hat_ref, scale_ref = refs[split : split + 5]
    y_ref, w1_ref, w2_ref, turn_ref, sem1, sem2, sem3 = refs[split + 5 :]
    start = pltpu.make_async_copy(base_ref, y_ref, sem3.at[0])
    tiles = u_ref.shape[0] // tile

    @pl.when(pl.program_id(0) == 0)
    def _():
        start.start()

    fetch_weights(firsts, w1_ref, sem1, chunk)
    fetch_weights(seconds, w2_ref, sem2, chunk)
    here = pl.ds(pl.multiple_of(pl.program_id(0) * chunk, chunk), chunk)

    @pl.when(pl.program_id(0) == 0)
    def _():
        start.wait()

    turn_ref[...] = w1_ref[here, :].T

    def step(i, carry):
        rows = pl.ds(pl.multiple_of(i * tile, tile), tile)
        z = product(u_ref[rows, :], turn_ref[...]) + b_ref[...]
        square = z * z
        t = jnp.tanh(z * (ROOT_TWO_PI + CUBIC * square))
        half = 0.5 + 0.5 * t
        a = z * half
        low = a.astype(BF16)
        act_ref[rows, :] = low
        slope = half + (a - a * t) * (ROOT_TWO_PI + (3.0 * CUBIC) * square)
        slope_ref[rows, :] = slope.astype(BF16)
        y_ref[rows, :] += product(low, w2_ref[here, :])
        return carry

    lax.fori_loop(0, tiles, step, 0)

    @pl.when(pl.program_id(0) == pl.num_programs(0) - 1)
    def _():
        small = 256

        def finish(i, carry):
            rows = pl.ds(pl.multiple_of(i * small, small), small)
            y = y_ref[rows, :]
            center = y - average(y)
            scale = lax.rsqrt(average(center * center) + EPSILON)
            hat = center * scale
            out_ref[rows, :] = (hat * vec_ref[0:1, :] + vec_ref[1:2, :]).astype(BF16)
            hat_ref[rows, :] = hat.astype(BF16)
            scale_ref[rows, :] = jnp.broadcast_to(scale, (small, LANES))
            return carry

        lax.fori_loop(0, u_ref.shape[0] // small, finish, 0)


def feed_forward(u, base, b, vec, firsts, seconds, chunk=768, tile=1024):
    tokens, width = u.shape
    counts = (len(firsts), len(seconds))
    units = b.shape[1]
    acts = lambda: pl.BlockSpec((tokens, chunk), lambda c: (0, c))
    return pl.pallas_call(
        functools.partial(forward_kernel, tile=tile, counts=counts, chunk=chunk),
        grid=(units // chunk,),
        in_specs=[
            whole_block((tokens, width)),
            FAR,
            pl.BlockSpec((1, chunk), lambda c: (0, c)),
            whole_block(vec.shape),
        ]
        + [FAR] * sum(counts),
        out_specs=[
            acts(),
            acts(),
            whole_block((tokens, width)),
            whole_block((tokens, width)),
            whole_block((tokens, LANES)),
        ],
        out_shape=[
            jax.ShapeDtypeStruct((tokens, units), BF16),
            jax.ShapeDtypeStruct((tokens, units), BF16),
            jax.ShapeDtypeStruct((tokens, width), BF16),
            jax.ShapeDtypeStruct((tokens, width), BF16),
            jax.ShapeDtypeStruct((tokens, LANES), F32),
        ],
        scratch_shapes=[
            pltpu.VMEM((tokens, width), F32),
            pltpu.VMEM((units, width), BF16),
            pltpu.VMEM((units, width), BF16),
            pltpu.VMEM((width, chunk), BF16),
            pltpu.SemaphoreType.DMA((counts[0],)),
            pltpu.SemaphoreType.DMA((counts[1],)),
            pltpu.SemaphoreType.DMA((1,)),
        ],
        compiler_params=params(),
        cost_estimate=cost(4 * tokens * units * width, tokens * units, 50 << 20),
        name="feed_forward",
    )(u, base, b, vec, *firsts, *seconds)


def backward_kernel(*refs, tile, counts, chunk):
    g_ref, hat_ref, scale_ref, vec_ref, u_ref, act_ref, slope_ref = refs[:7]
    split = 7 + sum(counts)
    firsts, seconds = refs[7 : 7 + counts[0]], refs[7 + counts[0] : split]
    keep1_ref, keep2_ref, send1_ref, send2_ref, db_ref, du_ref, sums_ref = refs[split : split + 7]
    e_ref, w1_ref, w2_ref, f_ref, turn_ref, sem1, sem2 = refs[split + 7 :]
    fetch_weights(firsts, w1_ref, sem1, chunk)
    fetch_weights(seconds, w2_ref, sem2, chunk)
    here = pl.ds(pl.multiple_of(pl.program_id(0) * chunk, chunk), chunk)

    @pl.when(pl.program_id(0) == 0)
    def _():
        small = 256
        sums_ref[...] = jnp.zeros_like(sums_ref)

        def begin(i, carry):
            rows = pl.ds(pl.multiple_of(i * small, small), small)
            g = g_ref[rows, :].astype(F32)
            hat = hat_ref[rows, :].astype(F32)
            dy = norm_back(g, hat, scale_ref[rows, :], vec_ref[0:1, :])
            du_ref[rows, :] = dy
            e_ref[rows, :] = dy.astype(BF16)
            sums_ref[0:8, :] += rows_of_eight(dy)
            sums_ref[8:16, :] += rows_of_eight(g * hat)
            sums_ref[16:24, :] += rows_of_eight(g)
            return carry

        lax.fori_loop(0, u_ref.shape[0] // small, begin, 0)

    turn_ref[...] = w2_ref[here, :].T

    def step(i, db):
        rows = pl.ds(pl.multiple_of(i * tile, tile), tile)
        dz = product(e_ref[rows, :], turn_ref[...]) * slope_ref[rows, :].astype(F32)
        low = dz.astype(BF16)
        f_ref[rows, :] = low
        du_ref[rows, :] += product(low, w1_ref[here, :])
        return db + rows_of_eight(dz)

    db = lax.fori_loop(0, u_ref.shape[0] // tile, step, jnp.zeros((8, chunk), F32))
    db_ref[...] = jnp.sum(db, axis=0, keepdims=True)
    dw2 = product_over_rows(act_ref[...], e_ref[...]).astype(BF16)
    dw1 = product_over_rows(f_ref[...], u_ref[...]).astype(BF16)
    half = pl.num_programs(0) // 2

    @pl.when(pl.program_id(0) < half)
    def _():
        keep1_ref[...] = dw1
        keep2_ref[...] = dw2

    @pl.when(pl.program_id(0) >= half)
    def _():
        send1_ref[...] = dw1
        send2_ref[...] = dw2


def feed_backward(g, hat, scale, vec, u, act, slope, firsts, seconds, chunk=512, tile=2048):
    tokens, width = u.shape
    counts = (len(firsts), len(seconds))
    units = act.shape[1]
    half = units // chunk // 2
    acts = lambda: pl.BlockSpec((tokens, chunk), lambda c: (0, c))
    keep = lambda: pl.BlockSpec((chunk, width), lambda c: (jnp.minimum(c, half - 1), 0))
    send = lambda: pl.BlockSpec((chunk, width), lambda c: (jnp.maximum(c - half, 0), 0))
    grads = jax.ShapeDtypeStruct((units // 2, width), BF16)
    return pl.pallas_call(
        functools.partial(backward_kernel, tile=tile, counts=counts, chunk=chunk),
        grid=(units // chunk,),
        in_specs=[whole_block(values.shape) for values in (g, hat, scale, vec, u)]
        + [acts(), acts()]
        + [FAR] * sum(counts),
        out_specs=[
            keep(),
            keep(),
            send(),
            send(),
            pl.BlockSpec((1, chunk), lambda c: (0, c)),
            whole_block((tokens, width)),
            whole_block((24, width)),
        ],
        out_shape=[grads] * 4
        + [
            jax.ShapeDtypeStruct((1, units), F32),
            jax.ShapeDtypeStruct((tokens, width), F32),
            jax.ShapeDtypeStruct((24, width), F32),
        ],
        scratch_shapes=[
            pltpu.VMEM((tokens, width), BF16),
            pltpu.VMEM((units, width), BF16),
            pltpu.VMEM((units, width), BF16),
            pltpu.VMEM((tokens, chunk), BF16),
            pltpu.VMEM((width, chunk), BF16),
            pltpu.SemaphoreType.DMA((counts[0],)),
            pltpu.SemaphoreType.DMA((counts[1],)),
        ],
        compiler_params=params(),
        cost_estimate=cost(8 * tokens * units * width, 0, 60 << 20),
        name="feed_backward",
    )(g, hat, scale, vec, u, act, slope, *firsts, *seconds)


def table_pair(points):
    numbers = jnp.arange(points, dtype=jnp.int32)
    coarse = 32 * jnp.arange(points // 32, dtype=jnp.int32)
    fine = jnp.arange(32, dtype=jnp.int32)

    def waves(rows):
        angles = (rows[:, None] * numbers[None, :] % points).astype(F32) * (2.0 * math.pi / points)
        return jnp.cos(angles), jnp.sin(angles)

    factor = 1.0 / math.sqrt(points)
    if points <= 64:
        cosine, sine = waves(numbers)
    else:
        coarse_cos, coarse_sin = waves(coarse)
        fine_cos, fine_sin = waves(fine)
        coarse_cos, coarse_sin, fine_cos, fine_sin = lax.optimization_barrier(
            (coarse_cos, coarse_sin, fine_cos, fine_sin)
        )
        coarse_cos, coarse_sin = coarse_cos[:, None], coarse_sin[:, None]
        fine_cos, fine_sin = fine_cos[None], fine_sin[None]
        cosine = (coarse_cos * fine_cos - coarse_sin * fine_sin).reshape(points, points)
        sine = (coarse_sin * fine_cos + coarse_cos * fine_sin).reshape(points, points)
    return (cosine * factor).astype(BF16), (sine * factor).astype(BF16)


def twiddles():
    row_index = jnp.arange(L1, dtype=jnp.int32)[None, :]
    col_index = jnp.arange(L2, dtype=jnp.int32)[:, None]
    angles = (row_index * col_index % L).astype(F32) * (2.0 * math.pi / L)
    wave = jnp.cos(angles), jnp.sin(angles)
    return [jnp.broadcast_to(values[:, :, None], (L2, L1, LANES)) for values in wave]


def swap(values, step):
    axis, mask = step
    size = lax.axis_size(axis)
    return lax.ppermute(values, axis, [(i, i ^ mask) for i in range(size)])


def bits(size):
    masks = []
    mask = size // 2
    while mask >= 1:
        masks.append(mask)
        mask //= 2
    return masks


def widen(held, step):
    return jnp.concatenate([held, swap(held, step)], axis=0)


def widen_codes(codes, steps, groups):
    for axis, mask in steps:
        code = mask if axis == "seq" else mask * groups
        codes = codes + [held ^ code for held in codes]
    return codes


def spread(pieces, steps):
    for step in steps:
        pieces = pieces + [swap(piece, step) for piece in pieces]
    return pieces


def spread_core(pieces, step_core):
    return pieces + [swap(piece, step_core) for piece in pieces]


def total(addends):
    return sum(addends[1:], addends[0].astype(F32))


def half_of(addends, axis, number):
    return [lax.index_in_dim(held, number, axis, keepdims=False) for held in addends]


def fold(addends, names, step, kind):
    axis = names.index(step)
    send = total(half_of(addends, axis, 1)).astype(kind)
    arrived = swap(send, step)
    return half_of(addends, axis, 0) + [arrived], names[:axis] + names[axis + 1 :]


def fold_all(addends, names, steps, kind):
    for step in steps:
        addends, names = fold(addends, names, step, kind)
    return addends, names


def arrange(rows):
    return with_layout_constraint(rows.transpose(0, 2, 1, 3), Layout(major_to_minor=(0, 1, 2, 3)))


def exchange(rows):
    order = Layout(major_to_minor=(0, 1, 2, 3))
    rows = with_layout_constraint(rows, order)
    rows = lax.all_to_all(rows, "seq", split_axis=0, concat_axis=0, tiled=True)
    return with_layout_constraint(rows, order)


def body(tokens, lengths, labels, picked, cotangent, w_in, b_in, w_out, shifts, norm_gains):
    groups = lax.axis_size("seq")
    me = lax.axis_index("seq")
    here = lax.axis_index("batch") * groups + me
    columns = tokens.shape[2]
    share = w_in.shape[2]
    part = shifts.shape[2]
    blocks = groups * lax.axis_size("batch")

    masks = bits(groups)[:-1]
    steps_plane = [("seq", mask) for mask in masks[:1] + masks[:0:-1]]
    steps_seq = [("seq", mask) for mask in masks[::-1]]
    steps_batch = [("batch", mask) for mask in bits(lax.axis_size("batch"))]
    step_core = ("seq", 1)
    numbers = jnp.arange(blocks, dtype=jnp.int32)

    codes = widen_codes([0], steps_plane + steps_batch + [step_core], groups)
    owner = jnp.array(codes, dtype=jnp.int32) ^ here
    one_hot = (owner[:, None] == numbers[None, :]).astype(F32)

    small = jnp.concatenate([b_in[0], shifts[0].reshape(-1), norm_gains[0].reshape(-1)])
    small = small.astype(F32)[None]
    first_held = w_in[0].T[None]
    second_held = w_out[0][None]
    tokens_late, late_cotangent = arrange(tokens), arrange(cotangent)
    for number, step in enumerate(steps_plane[:-1]):
        first_held = widen(first_held, step)
        second_held = widen(second_held, step)
        small = widen(small, step)
        small, first_held, second_held = lax.optimization_barrier(
            (small, first_held, second_held)
        )
        if number == 0:
            tokens_late, small = lax.optimization_barrier((tokens_late, small))
    small, first_held = lax.optimization_barrier((small, first_held))
    first_held = widen(first_held, steps_plane[-1])
    for step in steps_plane[-1:] + steps_batch + [step_core]:
        small = widen(small, step)
    seconds = []
    for piece in spread([second_held], steps_batch):
        seconds += [piece, swap(piece, steps_plane[-1])]

    wide_cos, wide_sin = table_pair(D)
    wide = jnp.concatenate([wide_cos, -wide_sin], axis=0)
    twiddle_cos, twiddle_sin = twiddles()
    firsts = [first_held]
    b_first = small[:, :share].reshape(1, blocks * share)
    rows = jnp.sum(one_hot[:, :, None] * small[:, None, share:], axis=0)
    rows = rows.reshape(blocks, 5, part).transpose(1, 0, 2).reshape(5, D)
    shifts_f = rows[:3]
    gains_f = rows[3:]

    short_cos, short_sin = table_pair(L1)
    long_cos, long_sin = table_pair(L2)
    short_table = jnp.concatenate([short_cos, short_sin], axis=0)
    long_table = jnp.stack([jnp.stack([long_cos, -long_sin]), jnp.stack([long_sin, long_cos])])
    both = jnp.eye(2, dtype=BF16)
    pair_table = jnp.einsum("qukm,bc->qkbcum", long_table, both).reshape(4 * L2, 4 * L2)

    length = lax.dynamic_slice_in_dim(lengths, me, 1)
    blank = jnp.zeros((5, D), F32)
    vec_one = jnp.concatenate([gains_f[0:1], shifts_f[1:2], shifts_f[0:1], blank])
    vec_two = jnp.concatenate([gains_f[1:2], shifts_f[2:3], blank, blank[:1]])
    x_all = exchange(tokens_late)
    early = (wide, twiddle_cos, twiddle_sin, short_table, pair_table, vec_one, vec_two, b_first)
    x_all, early = lax.optimization_barrier((x_all, early))
    x_all, late_cotangent, firsts, seconds = lax.optimization_barrier(
        (x_all, late_cotangent, firsts, seconds)
    )
    wide, twiddle_cos, twiddle_sin, short_table, pair_table, vec_one, vec_two, b_first = early
    firsts = spread(firsts, steps_batch)
    g_all = exchange(late_cotangent)

    x_rows = x_all.reshape(L2, L1, D)
    u, base, hat_one, scale_one = transform(
        length, x_rows, short_table, pair_table, twiddle_cos, twiddle_sin, vec_one, wide
    )
    u, firsts, seconds = lax.optimization_barrier((u, firsts, seconds))
    flat = lambda pieces: [piece.reshape(-1, D) for piece in spread_core(pieces, step_core)]
    firsts, seconds = flat(firsts), flat(seconds)
    act, slope, layer_out, hat_two, scale_two = feed_forward(
        u, base, b_first, vec_two, firsts, seconds
    )
    out_rows = exchange(layer_out.reshape(groups, columns, L1, D))

    keep_first, keep_second, send_first, send_second, grad_b_first, grad_u, sums_two = feed_backward(
        g_all.reshape(L, D), hat_two, scale_two, vec_two, u, act, slope, firsts, seconds
    )
    names = steps_batch[::-1] + steps_plane[::-1]
    shape = (2,) * len(names) + (share,)
    came_first = swap(send_first, step_core)
    came_second = swap(send_second, step_core)
    grad_x, sums_one = transform_back(
        length, grad_u, hat_one, scale_one, short_table.T, pair_table.T,
        twiddle_cos, twiddle_sin, vec_one, wide
    )
    grad_x, came_first, came_second, out_rows = lax.optimization_barrier(
        (grad_x, came_first, came_second, out_rows)
    )
    grad_first = [values.reshape(shape + (D,)) for values in (keep_first, came_first)]
    grad_second = [values.reshape(shape + (D,)) for values in (keep_second, came_second)]
    grad_x = grad_x.reshape(groups, columns, L1, D)
    input_grad = exchange(grad_x).transpose(0, 2, 1, 3)

    shift_of = jnp.arange(columns, dtype=jnp.int32) + me * columns
    place_of = L2 * jnp.arange(L1, dtype=jnp.int32)[None, :] + shift_of[:, None]
    steps_fold = steps_batch[::-1] + steps_seq
    early = len(steps_batch)
    grad_first, names_first = fold_all(grad_first, names, steps_fold[:early], BF16)
    grad_second, names_second = fold_all(grad_second, names, steps_fold[:early], BF16)
    out_rows, sums_one, sums_two, grad_b_first, grad_first = lax.optimization_barrier(
        (out_rows, sums_one, sums_two, grad_b_first, grad_first)
    )
    logits = out_rows.astype(F32)
    highest = jnp.max(logits, axis=-1, keepdims=True)
    powers = jnp.exp(logits - highest)
    denominator = jnp.sum(powers, axis=-1)
    features = jnp.arange(D, dtype=jnp.int32)
    label_rows = labels.transpose(0, 2, 1)
    top = jnp.sum(jnp.where(features == label_rows[..., None], powers, 0.0), axis=-1)
    counted = (picked.transpose(0, 2, 1) > 0) & (place_of[None] < lengths[:, None, None])
    weight = jnp.where(counted, 1.0, 0.0)
    sums = jnp.stack([jnp.sum(weight * (top / denominator)), jnp.sum(weight)])

    sums_two = jnp.sum(sums_two.reshape(3, 8, D), axis=1)
    sums_one = jnp.sum(sums_one.reshape(2, 8, D), axis=1)
    norms = jnp.stack([sums_two[0], sums_one[1], sums_two[2], sums_one[0], sums_two[1]])
    norms = norms.reshape(5, blocks, part).transpose(1, 0, 2).reshape(blocks, 5 * part)
    norms = jnp.sum(one_hot[:, :, None] * norms[None], axis=1)
    sums = jnp.broadcast_to(sums[None], (blocks, 2))
    small_grads = jnp.concatenate([grad_b_first.reshape(blocks, share), norms, sums], axis=1)
    half = blocks // 2
    arrived = swap(small_grads[half:], step_core)
    small = [values.reshape(shape[:-1] + (-1,)) for values in (small_grads[:half], arrived)]
    small, names_small = fold_all(small, names, steps_fold[:early], F32)
    small, out_rows = lax.optimization_barrier((small, out_rows))
    grad_first, names_first = fold_all(grad_first, names_first, steps_fold[early:], BF16)
    for step in steps_fold[early:]:
        small, grad_second = lax.optimization_barrier((small, grad_second))
        small, names_small = fold(small, names_small, step, F32)
        grad_second, names_second = fold(grad_second, names_second, step, BF16)
    current = out_rows.transpose(0, 2, 1, 3)
    small_grads, grad_first, grad_second = total(small), total(grad_first), total(grad_second)
    norms = small_grads[share:-2].reshape(5, part)
    match_rate = D * small_grads[-2] / jnp.maximum(small_grads[-1], 1.0)
    return (
        current,
        input_grad,
        grad_first.T[None],
        small_grads[:share][None],
        grad_second[None],
        norms[:3][None],
        norms[3:][None],
        match_rate,
    )


def solution(mesh):
    in_specs = (
        P("batch", None, "seq", None),
        P("batch"),
        P("batch", None, "seq"),
        P("batch", None, "seq"),
        P("batch", None, "seq", None),
        P(None, None, ("batch", "seq")),
        P(None, ("batch", "seq")),
        P(None, ("batch", "seq"), None),
        P(None, None, ("batch", "seq")),
        P(None, None, ("batch", "seq")),
    )
    out_specs = (
        P("batch", None, "seq", None),
        P("batch", None, "seq", None),
        P(None, None, ("batch", "seq")),
        P(None, ("batch", "seq")),
        P(None, ("batch", "seq"), None),
        P(None, None, ("batch", "seq")),
        P(None, None, ("batch", "seq")),
        P(),
    )
    return jax.shard_map(body, mesh=mesh, in_specs=in_specs, out_specs=out_specs, check_vma=False)
```

```python
import functools
import math

import jax
import jax.numpy as jnp
from jax import lax
from jax.experimental import pallas as pl
from jax.experimental.layout import Layout, with_layout_constraint
from jax.experimental.pallas import tpu as pltpu
from jax.sharding import PartitionSpec as P

D = 768
L1 = 64
L2 = 32
L = 2048
LANES = 128
PAIR = 4 * L2
STRIDE = PAIR + 1

EPSILON = 1e-12
ROOT_TWO_PI = 0.7978845608028654
CUBIC = ROOT_TWO_PI * 0.044715
F32 = jnp.float32
BF16 = jnp.bfloat16
VMEM_BYTES = 60 << 20
FAR = pl.BlockSpec(memory_space=pl.ANY)


def product(left, right):
    return lax.dot_general(left, right, (((1,), (0,)), ((), ())), preferred_element_type=F32)


def product_over_rows(left, right):
    return lax.dot_general(left, right, (((0,), (0,)), ((), ())), preferred_element_type=F32)


def lanes(column):
    return jnp.concatenate([column] * (D // LANES), axis=1)


def rows_of_eight(values):
    return jnp.sum(values.reshape(-1, 8, values.shape[-1]), axis=0)


def average(values):
    return jnp.mean(values, axis=1, keepdims=True)


def norm_back(grad, x_hat, scale, gain):
    q = grad * gain
    return lanes(scale) * (q - average(q) - x_hat * average(q * x_hat))


def whole_block(shape):
    return pl.BlockSpec(shape, lambda c: (0,) * len(shape), pipeline_mode=pl.Buffered(1))


def params():
    return pltpu.CompilerParams(vmem_limit_bytes=VMEM_BYTES)


def cost(flops, transcendentals, size):
    return pl.CostEstimate(flops=flops, transcendentals=transcendentals, bytes_accessed=size)


def scatter(refs, start, value):
    for j, ref in enumerate(refs):
        ref[pl.ds(start, L2, stride=STRIDE), :] = value[:, j * LANES : (j + 1) * LANES]


def gather(refs, block):
    return jnp.concatenate([ref[pl.ds(block * STRIDE, PAIR), :] for ref in refs], axis=1)


def middle_scratch():
    return [pltpu.VMEM((L2 * STRIDE, LANES), F32)] * (D // LANES)


def transform_kernel(
    length_ref, x_ref, short_ref, pair_ref, cos_ref, sin_ref, wide_hbm,
    hat_ref, scale_ref, spec_ref, wide_ref, sem, *middle, group
):
    length = length_ref[0]
    step = pl.program_id(0)
    load = pltpu.make_async_copy(wide_hbm, wide_ref, sem.at[0])

    @pl.when(step == 0)
    def _():
        load.start()

        def first(m, carry):
            spots = L2 * lax.broadcasted_iota(jnp.int32, (L1, D), 0) + m
            x = jnp.where(spots < length, x_ref[m].astype(F32), 0.0).astype(BF16)
            y = product(short_ref[...], x)
            real, imag = y[:L1], y[L1:]
            cosine, sine = lanes(cos_ref[m]), lanes(sin_ref[m])
            turned = (real * cosine - imag * sine, real * sine + imag * cosine)
            for b in range(2):
                for part in range(2):
                    scatter(middle, (b * 2 + part) * L2 + m, turned[part][b * L2 : (b + 1) * L2])
            return carry

        lax.fori_loop(0, L2, first, 0, unroll=4)
        load.wait()

    for j in range(group):
        turned = gather(middle, step * group + j).astype(BF16)
        q = product(pair_ref[...], turned).astype(BF16)
        spec_ref[j * L1 : (j + 1) * L1, :D] = q[:L1]
        spec_ref[j * L1 : (j + 1) * L1, D:] = q[L1:]
    mixed = product(spec_ref[...], wide_ref[...])
    number = lax.broadcasted_iota(jnp.int32, (group * L1, D), 0)
    spots = L2 * (number % L1) + step * group + number // L1
    x = x_ref[pl.ds(step * group, group)].reshape(group * L1, D).astype(F32)
    h = jnp.where(spots < length, x, 0.0) + mixed
    center = h - average(h)
    scale = lax.rsqrt(average(center * center) + EPSILON)
    hat_ref[...] = center * scale
    scale_ref[...] = jnp.broadcast_to(scale, scale_ref.shape)


def transform(length, x, short, pair, cosine, sine, wide, group=8):
    out = lambda width: pl.BlockSpec((group * L1, width), lambda c: (c, 0))
    return pl.pallas_call(
        functools.partial(transform_kernel, group=group),
        grid=(L2 // group,),
        in_specs=[pl.BlockSpec(memory_space=pltpu.SMEM)]
        + [whole_block(values.shape) for values in (x, short, pair, cosine, sine)]
        + [FAR],
        out_specs=[out(D), out(LANES)],
        out_shape=[
            jax.ShapeDtypeStruct((L, D), F32),
            jax.ShapeDtypeStruct((L, LANES), F32),
        ],
        scratch_shapes=[
            pltpu.VMEM((group * L1, 2 * D), BF16),
            pltpu.VMEM((2 * D, D), BF16),
            pltpu.SemaphoreType.DMA((1,)),
        ]
        + middle_scratch(),
        compiler_params=params(),
        cost_estimate=cost(7 << 30, L, 24 << 20),
        name="transform",
    )(length, x, short, pair, cosine, sine, wide)


def back_kernel(
    length_ref, du_ref, hat_ref, scale_ref, short_ref, pair_ref, cos_ref, sin_ref, vec_ref, wide_ref,
    dx_ref, sums_ref, rh_ref, spec_ref, *middle, group
):
    length = length_ref[0]
    step = pl.program_id(0)
    steps = L2 // group

    @pl.when(step == 0)
    def _():
        sums_ref[...] = jnp.zeros_like(sums_ref)

    @pl.when(step < steps)
    def _():
        du = du_ref[...]
        hat = hat_ref[...]
        rh = norm_back(du, hat, scale_ref[...], vec_ref[0:1, :]).astype(BF16)
        rh_ref[pl.ds(pl.multiple_of(step * group * L1, group * L1), group * L1), :] = rh
        sums_ref[0:8, :] += rows_of_eight(du * hat)
        sums_ref[8:16, :] += rows_of_eight(du)
        real = product(rh, wide_ref[:D, :]).astype(BF16)
        imag = product(rh, wide_ref[D:, :]).astype(BF16)
        for j in range(group):
            spec_ref[j, :L1, :] = real[j * L1 : (j + 1) * L1]
            spec_ref[j, L1:, :] = imag[j * L1 : (j + 1) * L1]
            turned = product(pair_ref[...], spec_ref[j]).astype(BF16).astype(F32)
            for b in range(2):
                for part in range(2):
                    start = (b * 2 + part) * L2
                    spot = part * L1 + b * L2 + step * group + j
                    scatter(middle, spot, turned[start : start + L2])

    @pl.when(step >= steps)
    def _():
        def second(i, carry):
            m = (step - steps) * group + i
            turned = gather(middle, m)
            real, imag = turned[:L1], turned[L1:]
            cosine, sine = lanes(cos_ref[m]), lanes(sin_ref[m])
            back = jnp.concatenate(
                [
                    (real * cosine + imag * sine).astype(BF16),
                    (imag * cosine - real * sine).astype(BF16),
                ],
                axis=0,
            )
            rh = rh_ref[pl.ds(pl.multiple_of(m * L1, L1), L1), :].astype(F32)
            dx = rh + product(short_ref[...], back)
            spots = L2 * lax.broadcasted_iota(jnp.int32, (L1, D), 0) + m
            dx_ref[i] = jnp.where(spots < length, dx, 0.0).astype(BF16)
            return carry

        lax.fori_loop(0, group, second, 0, unroll=4)


def transform_back(length, du, hat, scale, short, pair, cosine, sine, vec, wide, group=8):
    steps = L2 // group
    rows = lambda width: pl.BlockSpec((group * L1, width), lambda c: (jnp.minimum(c, steps - 1), 0))
    return pl.pallas_call(
        functools.partial(back_kernel, group=group),
        grid=(2 * steps,),
        in_specs=[pl.BlockSpec(memory_space=pltpu.SMEM), rows(D), rows(D), rows(LANES)]
        + [whole_block(values.shape) for values in (short, pair, cosine, sine, vec, wide)],
        out_specs=[
            pl.BlockSpec((group, L1, D), lambda c: (jnp.maximum(c - steps, 0), 0, 0)),
            pl.BlockSpec((16, D), lambda c: (0, 0)),
        ],
        out_shape=[
            jax.ShapeDtypeStruct((L2, L1, D), BF16),
            jax.ShapeDtypeStruct((16, D), F32),
        ],
        scratch_shapes=[pltpu.VMEM((L, D), BF16), pltpu.VMEM((group, 2 * L1, D), BF16)]
        + middle_scratch(),
        compiler_params=params(),
        cost_estimate=cost(7 << 30, 0, 20 << 20),
        name="transform_back",
    )(length, du, hat, scale, short, pair, cosine, sine, vec, wide)


def fetch_weights(pieces, holder, sems, chunk):
    rows = holder.shape[0] // len(pieces)
    step = pl.program_id(0)
    copies = [
        pltpu.make_async_copy(
            piece.at[pl.ds(0, rows), :], holder.at[pl.ds(i * rows, rows), :], sems.at[i]
        )
        for i, piece in enumerate(pieces)
    ]

    @pl.when(step == 0)
    def _():
        for copy in copies:
            copy.start()

    for number in range(holder.shape[0] // chunk):
        needed = [copy for i, copy in enumerate(copies) if i * rows // chunk == number]
        if needed:

            @pl.when(step == number)
            def _():
                for copy in needed:
                    copy.wait()


def forward_kernel(*refs, tile, counts, chunk):
    first_hat_ref, b_ref, vec_ref = refs[:3]
    split = 3 + sum(counts)
    firsts, seconds = refs[3 : 3 + counts[0]], refs[3 + counts[0] : split]
    act_ref, slope_ref, out_ref, hat_ref, scale_ref, u_ref = refs[split : split + 6]
    y_ref, w1_ref, w2_ref, turn_ref, sem1, sem2, sem3 = refs[split + 6 :]
    start = pltpu.make_async_copy(first_hat_ref, y_ref, sem3.at[0])
    tiles = u_ref.shape[0] // tile

    @pl.when(pl.program_id(0) == 0)
    def _():
        start.start()

    fetch_weights(firsts, w1_ref, sem1, chunk)
    fetch_weights(seconds, w2_ref, sem2, chunk)
    here = pl.ds(pl.multiple_of(pl.program_id(0) * chunk, chunk), chunk)

    @pl.when(pl.program_id(0) == 0)
    def _():
        start.wait()
        small = 256

        def begin(i, carry):
            rows = pl.ds(pl.multiple_of(i * small, small), small)
            u = y_ref[rows, :] * vec_ref[2:3, :] + vec_ref[3:4, :]
            u_ref[rows, :] = u.astype(BF16)
            y_ref[rows, :] = u + vec_ref[4:5, :]
            return carry

        lax.fori_loop(0, u_ref.shape[0] // small, begin, 0)

    turn_ref[...] = w1_ref[here, :].T

    def step(i, carry):
        rows = pl.ds(pl.multiple_of(i * tile, tile), tile)
        z = product(u_ref[rows, :], turn_ref[...]) + b_ref[...]
        square = z * z
        t = jnp.tanh(z * (ROOT_TWO_PI + CUBIC * square))
        half = 0.5 + 0.5 * t
        a = z * half
        low = a.astype(BF16)
        act_ref[rows, :] = low
        slope = half + (a - a * t) * (ROOT_TWO_PI + (3.0 * CUBIC) * square)
        slope_ref[rows, :] = slope.astype(BF16)
        y_ref[rows, :] += product(low, w2_ref[here, :])
        return carry

    lax.fori_loop(0, tiles, step, 0)

    @pl.when(pl.program_id(0) == pl.num_programs(0) - 1)
    def _():
        small = 256

        def finish(i, carry):
            rows = pl.ds(pl.multiple_of(i * small, small), small)
            y = y_ref[rows, :]
            center = y - average(y)
            scale = lax.rsqrt(average(center * center) + EPSILON)
            hat = center * scale
            out_ref[rows, :] = (hat * vec_ref[0:1, :] + vec_ref[1:2, :]).astype(BF16)
            hat_ref[rows, :] = hat.astype(BF16)
            scale_ref[rows, :] = jnp.broadcast_to(scale, (small, LANES))
            return carry

        lax.fori_loop(0, u_ref.shape[0] // small, finish, 0)


def feed_forward(hat, b, vec, firsts, seconds, chunk=768, tile=1024):
    tokens, width = hat.shape
    counts = (len(firsts), len(seconds))
    units = b.shape[1]
    acts = lambda: pl.BlockSpec((tokens, chunk), lambda c: (0, c))
    return pl.pallas_call(
        functools.partial(forward_kernel, tile=tile, counts=counts, chunk=chunk),
        grid=(units // chunk,),
        in_specs=[
            FAR,
            pl.BlockSpec((1, chunk), lambda c: (0, c)),
            whole_block(vec.shape),
        ]
        + [FAR] * sum(counts),
        out_specs=[
            acts(),
            acts(),
            whole_block((tokens, width)),
            whole_block((tokens, width)),
            whole_block((tokens, LANES)),
            whole_block((tokens, width)),
        ],
        out_shape=[
            jax.ShapeDtypeStruct((tokens, units), BF16),
            jax.ShapeDtypeStruct((tokens, units), BF16),
            jax.ShapeDtypeStruct((tokens, width), BF16),
            jax.ShapeDtypeStruct((tokens, width), BF16),
            jax.ShapeDtypeStruct((tokens, LANES), F32),
            jax.ShapeDtypeStruct((tokens, width), BF16),
        ],
        scratch_shapes=[
            pltpu.VMEM((tokens, width), F32),
            pltpu.VMEM((units, width), BF16),
            pltpu.VMEM((units, width), BF16),
            pltpu.VMEM((width, chunk), BF16),
            pltpu.SemaphoreType.DMA((counts[0],)),
            pltpu.SemaphoreType.DMA((counts[1],)),
            pltpu.SemaphoreType.DMA((1,)),
        ],
        compiler_params=params(),
        cost_estimate=cost(4 * tokens * units * width, tokens * units, 50 << 20),
        name="feed_forward",
    )(hat, b, vec, *firsts, *seconds)


def backward_kernel(*refs, tile, counts, chunk):
    g_ref, hat_ref, scale_ref, vec_ref, u_ref, act_ref, slope_ref = refs[:7]
    split = 7 + sum(counts)
    firsts, seconds = refs[7 : 7 + counts[0]], refs[7 + counts[0] : split]
    keep1_ref, keep2_ref, send1_ref, send2_ref, db_ref, du_ref, sums_ref = refs[split : split + 7]
    e_ref, w1_ref, w2_ref, f_ref, turn_ref, sem1, sem2 = refs[split + 7 :]
    fetch_weights(firsts, w1_ref, sem1, chunk)
    fetch_weights(seconds, w2_ref, sem2, chunk)
    here = pl.ds(pl.multiple_of(pl.program_id(0) * chunk, chunk), chunk)

    @pl.when(pl.program_id(0) == 0)
    def _():
        small = 256
        sums_ref[...] = jnp.zeros_like(sums_ref)

        def begin(i, carry):
            rows = pl.ds(pl.multiple_of(i * small, small), small)
            g = g_ref[rows, :].astype(F32)
            hat = hat_ref[rows, :].astype(F32)
            dy = norm_back(g, hat, scale_ref[rows, :], vec_ref[0:1, :])
            du_ref[rows, :] = dy
            e_ref[rows, :] = dy.astype(BF16)
            sums_ref[0:8, :] += rows_of_eight(dy)
            sums_ref[8:16, :] += rows_of_eight(g * hat)
            sums_ref[16:24, :] += rows_of_eight(g)
            return carry

        lax.fori_loop(0, u_ref.shape[0] // small, begin, 0)

    turn_ref[...] = w2_ref[here, :].T

    def step(i, db):
        rows = pl.ds(pl.multiple_of(i * tile, tile), tile)
        dz = product(e_ref[rows, :], turn_ref[...]) * slope_ref[rows, :].astype(F32)
        low = dz.astype(BF16)
        f_ref[rows, :] = low
        du_ref[rows, :] += product(low, w1_ref[here, :])
        return db + rows_of_eight(dz)

    db = lax.fori_loop(0, u_ref.shape[0] // tile, step, jnp.zeros((8, chunk), F32))
    db_ref[...] = jnp.sum(db, axis=0, keepdims=True)
    dw2 = product_over_rows(act_ref[...], e_ref[...]).astype(BF16)
    dw1 = product_over_rows(f_ref[...], u_ref[...]).astype(BF16)
    half = pl.num_programs(0) // 2

    @pl.when(pl.program_id(0) < half)
    def _():
        keep1_ref[...] = dw1
        keep2_ref[...] = dw2

    @pl.when(pl.program_id(0) >= half)
    def _():
        send1_ref[...] = dw1
        send2_ref[...] = dw2


def feed_backward(g, hat, scale, vec, u, act, slope, firsts, seconds, chunk=512, tile=2048):
    tokens, width = u.shape
    counts = (len(firsts), len(seconds))
    units = act.shape[1]
    half = units // chunk // 2
    acts = lambda: pl.BlockSpec((tokens, chunk), lambda c: (0, c))
    keep = lambda: pl.BlockSpec((chunk, width), lambda c: (jnp.minimum(c, half - 1), 0))
    send = lambda: pl.BlockSpec((chunk, width), lambda c: (jnp.maximum(c - half, 0), 0))
    grads = jax.ShapeDtypeStruct((units // 2, width), BF16)
    return pl.pallas_call(
        functools.partial(backward_kernel, tile=tile, counts=counts, chunk=chunk),
        grid=(units // chunk,),
        in_specs=[whole_block(values.shape) for values in (g, hat, scale, vec, u)]
        + [acts(), acts()]
        + [FAR] * sum(counts),
        out_specs=[
            keep(),
            keep(),
            send(),
            send(),
            pl.BlockSpec((1, chunk), lambda c: (0, c)),
            whole_block((tokens, width)),
            whole_block((24, width)),
        ],
        out_shape=[grads] * 4
        + [
            jax.ShapeDtypeStruct((1, units), F32),
            jax.ShapeDtypeStruct((tokens, width), F32),
            jax.ShapeDtypeStruct((24, width), F32),
        ],
        scratch_shapes=[
            pltpu.VMEM((tokens, width), BF16),
            pltpu.VMEM((units, width), BF16),
            pltpu.VMEM((units, width), BF16),
            pltpu.VMEM((tokens, chunk), BF16),
            pltpu.VMEM((width, chunk), BF16),
            pltpu.SemaphoreType.DMA((counts[0],)),
            pltpu.SemaphoreType.DMA((counts[1],)),
        ],
        compiler_params=params(),
        cost_estimate=cost(8 * tokens * units * width, 0, 60 << 20),
        name="feed_backward",
    )(g, hat, scale, vec, u, act, slope, *firsts, *seconds)


def table_pair(points):
    numbers = jnp.arange(points, dtype=jnp.int32)
    coarse = 32 * jnp.arange(points // 32, dtype=jnp.int32)
    fine = jnp.arange(32, dtype=jnp.int32)

    def waves(rows):
        angles = (rows[:, None] * numbers[None, :] % points).astype(F32) * (2.0 * math.pi / points)
        return jnp.cos(angles), jnp.sin(angles)

    factor = 1.0 / math.sqrt(points)
    if points <= 64:
        cosine, sine = waves(numbers)
    else:
        coarse_cos, coarse_sin = waves(coarse)
        fine_cos, fine_sin = waves(fine)
        coarse_cos, coarse_sin, fine_cos, fine_sin = lax.optimization_barrier(
            (coarse_cos, coarse_sin, fine_cos, fine_sin)
        )
        coarse_cos, coarse_sin = coarse_cos[:, None], coarse_sin[:, None]
        fine_cos, fine_sin = fine_cos[None], fine_sin[None]
        cosine = (coarse_cos * fine_cos - coarse_sin * fine_sin).reshape(points, points)
        sine = (coarse_sin * fine_cos + coarse_cos * fine_sin).reshape(points, points)
    return (cosine * factor).astype(BF16), (sine * factor).astype(BF16)


def twiddles():
    row_index = jnp.arange(L1, dtype=jnp.int32)[None, :]
    col_index = jnp.arange(L2, dtype=jnp.int32)[:, None]
    angles = (row_index * col_index % L).astype(F32) * (2.0 * math.pi / L)
    wave = jnp.cos(angles), jnp.sin(angles)
    return [jnp.broadcast_to(values[:, :, None], (L2, L1, LANES)) for values in wave]


def swap(values, step):
    axis, mask = step
    size = lax.axis_size(axis)
    return lax.ppermute(values, axis, [(i, i ^ mask) for i in range(size)])


def bits(size):
    masks = []
    mask = size // 2
    while mask >= 1:
        masks.append(mask)
        mask //= 2
    return masks


def widen(held, step):
    return jnp.concatenate([held, swap(held, step)], axis=0)


def widen_codes(codes, steps, groups):
    for axis, mask in steps:
        code = mask if axis == "seq" else mask * groups
        codes = codes + [held ^ code for held in codes]
    return codes


def spread(pieces, steps):
    for step in steps:
        pieces = pieces + [swap(piece, step) for piece in pieces]
    return pieces


def spread_core(pieces, step_core):
    return pieces + [swap(piece, step_core) for piece in pieces]


def total(addends):
    return sum(addends[1:], addends[0].astype(F32))


def half_of(addends, axis, number):
    return [lax.index_in_dim(held, number, axis, keepdims=False) for held in addends]


def fold(addends, names, step, kind):
    axis = names.index(step)
    send = total(half_of(addends, axis, 1)).astype(kind)
    arrived = swap(send, step)
    return half_of(addends, axis, 0) + [arrived], names[:axis] + names[axis + 1 :]


def fold_all(addends, names, steps, kind):
    for step in steps:
        addends, names = fold(addends, names, step, kind)
    return addends, names


def arrange(rows):
    return with_layout_constraint(rows.transpose(0, 2, 1, 3), Layout(major_to_minor=(0, 1, 2, 3)))


def exchange(rows):
    order = Layout(major_to_minor=(0, 1, 2, 3))
    rows = with_layout_constraint(rows, order)
    rows = lax.all_to_all(rows, "seq", split_axis=0, concat_axis=0, tiled=True)
    return with_layout_constraint(rows, order)


def body(tokens, lengths, labels, picked, cotangent, w_in, b_in, w_out, shifts, norm_gains):
    groups = lax.axis_size("seq")
    me = lax.axis_index("seq")
    here = lax.axis_index("batch") * groups + me
    columns = tokens.shape[2]
    share = w_in.shape[2]
    part = shifts.shape[2]
    blocks = groups * lax.axis_size("batch")

    masks = bits(groups)[:-1]
    steps_plane = [("seq", mask) for mask in masks[:1] + masks[:0:-1]]
    steps_seq = [("seq", mask) for mask in masks[::-1]]
    steps_batch = [("batch", mask) for mask in bits(lax.axis_size("batch"))]
    step_core = ("seq", 1)
    numbers = jnp.arange(blocks, dtype=jnp.int32)

    codes = widen_codes([0], steps_plane + steps_batch + [step_core], groups)
    owner = jnp.array(codes, dtype=jnp.int32) ^ here
    one_hot = (owner[:, None] == numbers[None, :]).astype(F32)

    wide_cos, wide_sin = table_pair(D)
    wide = jnp.concatenate([wide_cos, -wide_sin], axis=0)
    twiddle_cos, twiddle_sin = twiddles()
    short_cos, short_sin = table_pair(L1)
    long_cos, long_sin = table_pair(L2)
    short_table = jnp.concatenate([short_cos, short_sin], axis=0)
    long_table = jnp.stack([jnp.stack([long_cos, -long_sin]), jnp.stack([long_sin, long_cos])])
    both = jnp.eye(2, dtype=BF16)
    pair_table = jnp.einsum("qukm,bc->qkbcum", long_table, both).reshape(4 * L2, 4 * L2)

    length = lax.dynamic_slice_in_dim(lengths, me, 1)
    small = jnp.concatenate([b_in[0], shifts[0].reshape(-1), norm_gains[0].reshape(-1)])
    small = small.astype(F32)[None]
    first_held = w_in[0].T[None]
    second_held = w_out[0][None]
    tokens_late = arrange(tokens)
    for number, step in enumerate(steps_plane[:-1]):
        first_held = widen(first_held, step)
        second_held = widen(second_held, step)
        small = widen(small, step)
        if number == 0:
            tokens_late, small, first_held, second_held = lax.optimization_barrier(
                (tokens_late, small, first_held, second_held)
            )
            x_all = exchange(tokens_late)
    early = (wide, twiddle_cos, twiddle_sin, short_table, pair_table, arrange(cotangent))
    small, first_held, second_held, early = lax.optimization_barrier(
        (small, first_held, second_held, early)
    )
    wide, twiddle_cos, twiddle_sin, short_table, pair_table, late_cotangent = early
    first_held = widen(first_held, steps_plane[-1])
    seconds = []
    for piece in spread([second_held], steps_batch):
        seconds += [piece, swap(piece, steps_plane[-1])]
    steps_small = steps_plane[:-1] + steps_batch + [step_core] + steps_plane[-1:]
    small_codes = widen_codes([0], steps_small, groups)
    for step in steps_batch + [step_core]:
        small = widen(small, step)
    small, first_held = lax.optimization_barrier((small, first_held))
    small = widen(small, steps_plane[-1])
    places = jnp.array([small_codes.index(code) for code in codes], dtype=jnp.int32)
    place_hot = (places[:, None] == numbers[None, :]).astype(F32)
    small = jnp.sum(place_hot[:, :, None] * small[None], axis=1)
    b_first = small[:, :share].reshape(1, blocks * share)
    rows = jnp.sum(one_hot[:, :, None] * small[:, None, share:], axis=0)
    rows = rows.reshape(blocks, 5, part).transpose(1, 0, 2).reshape(5, D)
    shifts_f = rows[:3]
    gains_f = rows[3:]
    blank = jnp.zeros((3, D), F32)
    vec = jnp.concatenate(
        [gains_f[1:2], shifts_f[2:3], gains_f[0:1], shifts_f[1:2], shifts_f[0:1], blank]
    )
    vec_one = vec[2:]
    vec_one = jnp.concatenate([vec_one, blank[:2]])
    firsts = spread([first_held], steps_batch)
    x_all, late_cotangent, firsts, seconds, vec, vec_one, b_first = lax.optimization_barrier(
        (x_all, late_cotangent, firsts, seconds, vec, vec_one, b_first)
    )
    g_all = exchange(late_cotangent)

    x_rows = x_all.reshape(L2, L1, D)
    hat_one, scale_one = transform(
        length, x_rows, short_table, pair_table, twiddle_cos, twiddle_sin, wide
    )
    hat_one, firsts, seconds = lax.optimization_barrier((hat_one, firsts, seconds))
    flat = lambda pieces: [piece.reshape(-1, D) for piece in spread_core(pieces, step_core)]
    firsts, seconds = flat(firsts), flat(seconds)
    act, slope, layer_out, hat_two, scale_two, u = feed_forward(
        hat_one, b_first, vec, firsts, seconds
    )
    out_rows = exchange(layer_out.reshape(groups, columns, L1, D))

    keep_first, keep_second, send_first, send_second, grad_b_first, grad_u, sums_two = feed_backward(
        g_all.reshape(L, D), hat_two, scale_two, vec, u, act, slope, firsts, seconds
    )
    names = steps_batch[::-1] + steps_plane[::-1]
    shape = (2,) * len(names) + (share,)
    came_first = swap(send_first, step_core)
    came_second = swap(send_second, step_core)
    grad_x, sums_one = transform_back(
        length, grad_u, hat_one, scale_one, short_table.T, pair_table.T,
        twiddle_cos, twiddle_sin, vec_one, wide
    )
    grad_x, came_first, came_second, out_rows = lax.optimization_barrier(
        (grad_x, came_first, came_second, out_rows)
    )
    grad_first = [values.reshape(shape + (D,)) for values in (keep_first, came_first)]
    grad_second = [values.reshape(shape + (D,)) for values in (keep_second, came_second)]
    grad_x = grad_x.reshape(groups, columns, L1, D)
    input_grad = exchange(grad_x).transpose(0, 2, 1, 3)

    shift_of = jnp.arange(columns, dtype=jnp.int32) + me * columns
    place_of = L2 * jnp.arange(L1, dtype=jnp.int32)[None, :] + shift_of[:, None]
    steps_fold = steps_batch[::-1] + steps_seq
    early = len(steps_batch)
    grad_first, names_first = fold_all(grad_first, names, steps_fold[:early], BF16)
    grad_second, names_second = fold_all(grad_second, names, steps_fold[:early], BF16)
    out_rows, sums_one, sums_two, grad_b_first, grad_first = lax.optimization_barrier(
        (out_rows, sums_one, sums_two, grad_b_first, grad_first)
    )
    logits = out_rows.astype(F32)
    highest = jnp.max(logits, axis=-1, keepdims=True)
    powers = jnp.exp(logits - highest)
    denominator = jnp.sum(powers, axis=-1)
    features = jnp.arange(D, dtype=jnp.int32)
    label_rows = labels.transpose(0, 2, 1)
    top = jnp.sum(jnp.where(features == label_rows[..., None], powers, 0.0), axis=-1)
    counted = (picked.transpose(0, 2, 1) > 0) & (place_of[None] < lengths[:, None, None])
    weight = jnp.where(counted, 1.0, 0.0)
    sums = jnp.stack([jnp.sum(weight * (top / denominator)), jnp.sum(weight)])

    sums_two = jnp.sum(sums_two.reshape(3, 8, D), axis=1)
    sums_one = jnp.sum(sums_one.reshape(2, 8, D), axis=1)
    norms = jnp.stack([sums_two[0], sums_one[1], sums_two[2], sums_one[0], sums_two[1]])
    norms = norms.reshape(5, blocks, part).transpose(1, 0, 2).reshape(blocks, 5 * part)
    norms = jnp.sum(one_hot[:, :, None] * norms[None], axis=1)
    sums = jnp.broadcast_to(sums[None], (blocks, 2))
    small_grads = jnp.concatenate([grad_b_first.reshape(blocks, share), norms, sums], axis=1)
    half = blocks // 2
    arrived = swap(small_grads[half:], step_core)
    small = [values.reshape(shape[:-1] + (-1,)) for values in (small_grads[:half], arrived)]
    small, names_small = fold_all(small, names, steps_fold[:early], F32)
    small, out_rows = lax.optimization_barrier((small, out_rows))
    grad_first, names_first = fold_all(grad_first, names_first, steps_fold[early:], BF16)
    for step in steps_fold[early:]:
        small, grad_second = lax.optimization_barrier((small, grad_second))
        small, names_small = fold(small, names_small, step, F32)
        grad_second, names_second = fold(grad_second, names_second, step, BF16)
    current = out_rows.transpose(0, 2, 1, 3)
    small_grads, grad_first, grad_second = total(small), total(grad_first), total(grad_second)
    norms = small_grads[share:-2].reshape(5, part)
    match_rate = D * small_grads[-2] / jnp.maximum(small_grads[-1], 1.0)
    return (
        current,
        input_grad,
        grad_first.T[None],
        small_grads[:share][None],
        grad_second[None],
        norms[:3][None],
        norms[3:][None],
        match_rate,
    )


def solution(mesh):
    in_specs = (
        P("batch", None, "seq", None),
        P("batch"),
        P("batch", None, "seq"),
        P("batch", None, "seq"),
        P("batch", None, "seq", None),
        P(None, None, ("batch", "seq")),
        P(None, ("batch", "seq")),
        P(None, ("batch", "seq"), None),
        P(None, None, ("batch", "seq")),
        P(None, None, ("batch", "seq")),
    )
    out_specs = (
        P("batch", None, "seq", None),
        P("batch", None, "seq", None),
        P(None, None, ("batch", "seq")),
        P(None, ("batch", "seq")),
        P(None, ("batch", "seq"), None),
        P(None, None, ("batch", "seq")),
        P(None, None, ("batch", "seq")),
        P(),
    )
    return jax.shard_map(body, mesh=mesh, in_specs=in_specs, out_specs=out_specs, check_vma=False)
```

```python
import functools
import math

import jax
import jax.numpy as jnp
from jax import lax
from jax.experimental import pallas as pl
from jax.experimental.layout import Layout, with_layout_constraint
from jax.experimental.pallas import tpu as pltpu
from jax.sharding import PartitionSpec as P

D = 768
L1 = 64
L2 = 32
L = 2048
LANES = 128
PAIR = 4 * L2
STRIDE = PAIR + 1

EPSILON = 1e-12
ROOT_TWO_PI = 0.7978845608028654
CUBIC = ROOT_TWO_PI * 0.044715
F32 = jnp.float32
BF16 = jnp.bfloat16
VMEM_BYTES = 60 << 20
FAR = pl.BlockSpec(memory_space=pl.ANY)


def product(left, right):
    return lax.dot_general(left, right, (((1,), (0,)), ((), ())), preferred_element_type=F32)


def product_turned(left, right):
    return lax.dot_general(left, right, (((1,), (1,)), ((), ())), preferred_element_type=F32)


def product_over_rows(left, right):
    return lax.dot_general(left, right, (((0,), (0,)), ((), ())), preferred_element_type=F32)


def lanes(column):
    return jnp.concatenate([column] * (D // LANES), axis=1)


def rows_of_eight(values):
    return jnp.sum(values.reshape(-1, 8, values.shape[-1]), axis=0)


def average(values):
    return jnp.mean(values, axis=1, keepdims=True)


def norm_back(grad, x_hat, scale, gain):
    q = grad * gain
    return lanes(scale) * (q - average(q) - x_hat * average(q * x_hat))


def whole_block(shape):
    return pl.BlockSpec(shape, lambda c: (0,) * len(shape), pipeline_mode=pl.Buffered(1))


def params():
    return pltpu.CompilerParams(vmem_limit_bytes=VMEM_BYTES)


def cost(flops, transcendentals, size):
    return pl.CostEstimate(flops=flops, transcendentals=transcendentals, bytes_accessed=size)


def scatter(refs, start, value):
    for j, ref in enumerate(refs):
        ref[pl.ds(start, L2, stride=STRIDE), :] = value[:, j * LANES : (j + 1) * LANES]


def gather(refs, block):
    return jnp.concatenate([ref[pl.ds(block * STRIDE, PAIR), :] for ref in refs], axis=1)


def middle_scratch():
    return [pltpu.VMEM((L2 * STRIDE, LANES), F32)] * (D // LANES)


def transform_kernel(
    length_ref, x_ref, short_ref, pair_ref, cos_ref, sin_ref, wide_hbm,
    hat_ref, scale_ref, spec_ref, wide_ref, sem, *middle, group
):
    length = length_ref[0]
    step = pl.program_id(0)
    load = pltpu.make_async_copy(wide_hbm, wide_ref, sem.at[0])

    @pl.when(step == 0)
    def _():
        load.start()

        def first(m, carry):
            spots = L2 * lax.broadcasted_iota(jnp.int32, (L1, D), 0) + m
            x = jnp.where(spots < length, x_ref[m].astype(F32), 0.0).astype(BF16)
            y = product(short_ref[...], x)
            real, imag = y[:L1], y[L1:]
            cosine, sine = lanes(cos_ref[m]), lanes(sin_ref[m])
            turned = (real * cosine - imag * sine, real * sine + imag * cosine)
            for b in range(2):
                for part in range(2):
                    scatter(middle, (b * 2 + part) * L2 + m, turned[part][b * L2 : (b + 1) * L2])
            return carry

        lax.fori_loop(0, L2, first, 0, unroll=4)
        load.wait()

    for j in range(group):
        turned = gather(middle, step * group + j).astype(BF16)
        q = product(pair_ref[...], turned).astype(BF16)
        spec_ref[j * L1 : (j + 1) * L1, :D] = q[:L1]
        spec_ref[j * L1 : (j + 1) * L1, D:] = q[L1:]
    mixed = product(spec_ref[...], wide_ref[...])
    number = lax.broadcasted_iota(jnp.int32, (group * L1, D), 0)
    spots = L2 * (number % L1) + step * group + number // L1
    x = x_ref[pl.ds(step * group, group)].reshape(group * L1, D).astype(F32)
    h = jnp.where(spots < length, x, 0.0) + mixed
    center = h - average(h)
    scale = lax.rsqrt(average(center * center) + EPSILON)
    hat_ref[...] = center * scale
    scale_ref[...] = jnp.broadcast_to(scale, scale_ref.shape)


def transform(length, x, short, pair, cosine, sine, wide, group=8):
    out = lambda width: pl.BlockSpec((group * L1, width), lambda c: (c, 0))
    return pl.pallas_call(
        functools.partial(transform_kernel, group=group),
        grid=(L2 // group,),
        in_specs=[pl.BlockSpec(memory_space=pltpu.SMEM)]
        + [whole_block(values.shape) for values in (x, short, pair, cosine, sine)]
        + [FAR],
        out_specs=[out(D), out(LANES)],
        out_shape=[
            jax.ShapeDtypeStruct((L, D), F32),
            jax.ShapeDtypeStruct((L, LANES), F32),
        ],
        scratch_shapes=[
            pltpu.VMEM((group * L1, 2 * D), BF16),
            pltpu.VMEM((2 * D, D), BF16),
            pltpu.SemaphoreType.DMA((1,)),
        ]
        + middle_scratch(),
        compiler_params=params(),
        cost_estimate=cost(7 << 30, L, 24 << 20),
        name="transform",
    )(length, x, short, pair, cosine, sine, wide)


def back_kernel(
    length_ref, du_ref, hat_ref, scale_ref, short_ref, pair_ref, cos_ref, sin_ref, vec_ref, wide_ref,
    dx_ref, sums_ref, rh_ref, spec_ref, *middle, group
):
    length = length_ref[0]
    step = pl.program_id(0)
    steps = L2 // group

    @pl.when(step == 0)
    def _():
        sums_ref[...] = jnp.zeros_like(sums_ref)

    @pl.when(step < steps)
    def _():
        du = du_ref[...]
        hat = hat_ref[...]
        rh = norm_back(du, hat, scale_ref[...], vec_ref[0:1, :]).astype(BF16)
        rh_ref[pl.ds(pl.multiple_of(step * group * L1, group * L1), group * L1), :] = rh
        sums_ref[0:8, :] += rows_of_eight(du * hat)
        sums_ref[8:16, :] += rows_of_eight(du)
        real = product(rh, wide_ref[:D, :]).astype(BF16)
        imag = product(rh, wide_ref[D:, :]).astype(BF16)
        for j in range(group):
            spec_ref[j, :L1, :] = real[j * L1 : (j + 1) * L1]
            spec_ref[j, L1:, :] = imag[j * L1 : (j + 1) * L1]
            turned = product(pair_ref[...], spec_ref[j]).astype(BF16).astype(F32)
            for b in range(2):
                for part in range(2):
                    start = (b * 2 + part) * L2
                    spot = part * L1 + b * L2 + step * group + j
                    scatter(middle, spot, turned[start : start + L2])

    @pl.when(step >= steps)
    def _():
        def second(i, carry):
            m = (step - steps) * group + i
            turned = gather(middle, m)
            real, imag = turned[:L1], turned[L1:]
            cosine, sine = lanes(cos_ref[m]), lanes(sin_ref[m])
            back = jnp.concatenate(
                [
                    (real * cosine + imag * sine).astype(BF16),
                    (imag * cosine - real * sine).astype(BF16),
                ],
                axis=0,
            )
            rh = rh_ref[pl.ds(pl.multiple_of(m * L1, L1), L1), :].astype(F32)
            dx = rh + product(short_ref[...], back)
            spots = L2 * lax.broadcasted_iota(jnp.int32, (L1, D), 0) + m
            dx_ref[i] = jnp.where(spots < length, dx, 0.0).astype(BF16)
            return carry

        lax.fori_loop(0, group, second, 0, unroll=4)


def transform_back(length, du, hat, scale, short, pair, cosine, sine, vec, wide, group=8):
    steps = L2 // group
    rows = lambda width: pl.BlockSpec((group * L1, width), lambda c: (jnp.minimum(c, steps - 1), 0))
    return pl.pallas_call(
        functools.partial(back_kernel, group=group),
        grid=(2 * steps,),
        in_specs=[pl.BlockSpec(memory_space=pltpu.SMEM), rows(D), rows(D), rows(LANES)]
        + [whole_block(values.shape) for values in (short, pair, cosine, sine, vec, wide)],
        out_specs=[
            pl.BlockSpec((group, L1, D), lambda c: (jnp.maximum(c - steps, 0), 0, 0)),
            pl.BlockSpec((16, D), lambda c: (0, 0)),
        ],
        out_shape=[
            jax.ShapeDtypeStruct((L2, L1, D), BF16),
            jax.ShapeDtypeStruct((16, D), F32),
        ],
        scratch_shapes=[pltpu.VMEM((L, D), BF16), pltpu.VMEM((group, 2 * L1, D), BF16)]
        + middle_scratch(),
        compiler_params=params(),
        cost_estimate=cost(7 << 30, 0, 20 << 20),
        name="transform_back",
    )(length, du, hat, scale, short, pair, cosine, sine, vec, wide)


def fetch_weights(pieces, holder, sems, chunk):
    rows = holder.shape[0] // len(pieces)
    step = pl.program_id(0)
    copies = [
        pltpu.make_async_copy(
            piece.at[pl.ds(0, rows), :], holder.at[pl.ds(i * rows, rows), :], sems.at[i]
        )
        for i, piece in enumerate(pieces)
    ]

    @pl.when(step == 0)
    def _():
        for copy in copies:
            copy.start()

    for number in range(holder.shape[0] // chunk):
        needed = [copy for i, copy in enumerate(copies) if i * rows // chunk == number]
        if needed:

            @pl.when(step == number)
            def _():
                for copy in needed:
                    copy.wait()


def forward_kernel(*refs, tile, counts, chunk):
    first_hat_ref, b_ref, vec_ref = refs[:3]
    split = 3 + sum(counts)
    firsts, seconds = refs[3 : 3 + counts[0]], refs[3 + counts[0] : split]
    act_ref, slope_ref, out_far, hat_far, scale_far, u_far = refs[split : split + 6]
    y_ref, w1_ref, w2_ref, out_ref, hat_ref, scale_ref, u_ref, sem1, sem2, sem3 = refs[split + 6 :]
    parts = 4
    part = u_ref.shape[0] // parts
    tiles = u_ref.shape[0] // tile
    loads, stores = [], []
    for i in range(parts):
        rows = pl.ds(i * part, part)
        pairs = ((u_ref, u_far), (out_ref, out_far), (hat_ref, hat_far), (scale_ref, scale_far))
        loads.append(
            pltpu.make_async_copy(first_hat_ref.at[rows, :], y_ref.at[rows, :], sem3.at[i, 0])
        )
        stores.append(
            [
                pltpu.make_async_copy(near.at[rows, :], far.at[rows, :], sem3.at[i, 1 + j])
                for j, (near, far) in enumerate(pairs)
            ]
        )

    @pl.when(pl.program_id(0) == 0)
    def _():
        for load in loads:
            load.start()

    fetch_weights(firsts, w1_ref, sem1, chunk)
    fetch_weights(seconds, w2_ref, sem2, chunk)
    here = pl.ds(pl.multiple_of(pl.program_id(0) * chunk, chunk), chunk)

    @pl.when(pl.program_id(0) == 0)
    def _():
        small = 256

        def begin(i, carry):
            rows = pl.ds(pl.multiple_of(i * small, small), small)
            u = y_ref[rows, :] * vec_ref[2:3, :] + vec_ref[3:4, :]
            u_ref[rows, :] = u.astype(BF16)
            y_ref[rows, :] = u + vec_ref[4:5, :]
            return carry

        for i in range(parts):
            loads[i].wait()
            lax.fori_loop(i * part // small, (i + 1) * part // small, begin, 0)
            stores[i][0].start()


    def step(i, carry):
        rows = pl.ds(pl.multiple_of(i * tile, tile), tile)
        z = product_turned(u_ref[rows, :], w1_ref[here, :]) + b_ref[...]
        square = z * z
        t = jnp.tanh(z * (ROOT_TWO_PI + CUBIC * square))
        half = 0.5 + 0.5 * t
        a = z * half
        low = a.astype(BF16)
        act_ref[rows, :] = low
        slope = half + (a - a * t) * (ROOT_TWO_PI + (3.0 * CUBIC) * square)
        slope_ref[rows, :] = slope.astype(BF16)
        y_ref[rows, :] += product(low, w2_ref[here, :])
        return carry

    lax.fori_loop(0, tiles, step, 0)

    @pl.when(pl.program_id(0) == pl.num_programs(0) - 1)
    def _():
        small = 256

        def finish(i, carry):
            rows = pl.ds(pl.multiple_of(i * small, small), small)
            y = y_ref[rows, :]
            center = y - average(y)
            scale = lax.rsqrt(average(center * center) + EPSILON)
            hat = center * scale
            out_ref[rows, :] = (hat * vec_ref[0:1, :] + vec_ref[1:2, :]).astype(BF16)
            hat_ref[rows, :] = hat.astype(BF16)
            scale_ref[rows, :] = jnp.broadcast_to(scale, (small, LANES))
            return carry

        for i in range(parts):
            lax.fori_loop(i * part // small, (i + 1) * part // small, finish, 0)
            for copy in stores[i][1:]:
                copy.start()
        for store in stores:
            for copy in store:
                copy.wait()


def feed_forward(hat, b, vec, firsts, seconds, chunk=1024, tile=1024):
    tokens, width = hat.shape
    counts = (len(firsts), len(seconds))
    units = b.shape[1]
    acts = lambda: pl.BlockSpec((tokens, chunk), lambda c: (0, c))
    return pl.pallas_call(
        functools.partial(forward_kernel, tile=tile, counts=counts, chunk=chunk),
        grid=(units // chunk,),
        in_specs=[
            FAR,
            pl.BlockSpec((1, chunk), lambda c: (0, c)),
            whole_block(vec.shape),
        ]
        + [FAR] * sum(counts),
        out_specs=[acts(), acts()] + [FAR] * 4,
        out_shape=[
            jax.ShapeDtypeStruct((tokens, units), BF16),
            jax.ShapeDtypeStruct((tokens, units), BF16),
            jax.ShapeDtypeStruct((tokens, width), BF16),
            jax.ShapeDtypeStruct((tokens, width), BF16),
            jax.ShapeDtypeStruct((tokens, LANES), F32),
            jax.ShapeDtypeStruct((tokens, width), BF16),
        ],
        scratch_shapes=[
            pltpu.VMEM((tokens, width), F32),
            pltpu.VMEM((units, width), BF16),
            pltpu.VMEM((units, width), BF16),
            pltpu.VMEM((tokens, width), BF16),
            pltpu.VMEM((tokens, width), BF16),
            pltpu.VMEM((tokens, LANES), F32),
            pltpu.VMEM((tokens, width), BF16),
            pltpu.SemaphoreType.DMA((counts[0],)),
            pltpu.SemaphoreType.DMA((counts[1],)),
            pltpu.SemaphoreType.DMA((4, 5)),
        ],
        compiler_params=params(),
        cost_estimate=cost(4 * tokens * units * width, tokens * units, 50 << 20),
        name="feed_forward",
    )(hat, b, vec, *firsts, *seconds)


def backward_kernel(*refs, tile, counts, chunk):
    g_far, hat_far, scale_far, u_far, vec_ref, act_ref, slope_ref = refs[:7]
    split = 7 + sum(counts)
    firsts, seconds = refs[7 : 7 + counts[0]], refs[7 + counts[0] : split]
    keep1_ref, keep2_ref, send1_ref, send2_ref, db_ref, du_far, sums_ref = refs[split : split + 7]
    e_ref, w1_ref, w2_ref, f_ref, g_ref, hat_ref, scale_ref, u_ref, du_ref = refs[
        split + 7 : split + 16
    ]
    sem1, sem2, sem3, sem4 = refs[split + 16 :]
    parts = 4
    part = u_ref.shape[0] // parts
    loads = []
    for i in range(parts):
        rows = pl.ds(i * part, part)
        loads.append(
            [
                pltpu.make_async_copy(far.at[rows, :], near.at[rows, :], sem3.at[i, j])
                for j, (far, near) in enumerate(
                    ((g_far, g_ref), (hat_far, hat_ref), (scale_far, scale_ref))
                )
            ]
        )
    load_u = pltpu.make_async_copy(u_far, u_ref, sem4.at[0])
    store_du = pltpu.make_async_copy(du_ref, du_far, sem4.at[1])

    @pl.when(pl.program_id(0) == 0)
    def _():
        for load in loads:
            for copy in load:
                copy.start()

    fetch_weights(seconds, w2_ref, sem2, chunk)
    fetch_weights(firsts, w1_ref, sem1, chunk)
    here = pl.ds(pl.multiple_of(pl.program_id(0) * chunk, chunk), chunk)

    @pl.when(pl.program_id(0) == 0)
    def _():
        small = 256
        sums_ref[...] = jnp.zeros_like(sums_ref)

        def begin(i, carry):
            rows = pl.ds(pl.multiple_of(i * small, small), small)
            g = g_ref[rows, :].astype(F32)
            hat = hat_ref[rows, :].astype(F32)
            dy = norm_back(g, hat, scale_ref[rows, :], vec_ref[0:1, :])
            du_ref[rows, :] = dy
            e_ref[rows, :] = dy.astype(BF16)
            sums_ref[0:8, :] += rows_of_eight(dy)
            sums_ref[8:16, :] += rows_of_eight(g * hat)
            sums_ref[16:24, :] += rows_of_eight(g)
            return carry

        load_u.start()
        for i in range(parts):
            for copy in loads[i]:
                copy.wait()
            lax.fori_loop(i * part // small, (i + 1) * part // small, begin, 0)
        load_u.wait()


    def step(i, db):
        rows = pl.ds(pl.multiple_of(i * tile, tile), tile)
        dz = product_turned(e_ref[rows, :], w2_ref[here, :]) * slope_ref[rows, :].astype(F32)
        low = dz.astype(BF16)
        f_ref[rows, :] = low
        du_ref[rows, :] += product(low, w1_ref[here, :])
        return db + rows_of_eight(dz)

    db = lax.fori_loop(0, u_ref.shape[0] // tile, step, jnp.zeros((8, chunk), F32))
    db_ref[...] = jnp.sum(db, axis=0, keepdims=True)

    @pl.when(pl.program_id(0) == pl.num_programs(0) - 1)
    def _():
        store_du.start()

    dw2 = product_over_rows(act_ref[...], e_ref[...]).astype(BF16)
    dw1 = product_over_rows(f_ref[...], u_ref[...]).astype(BF16)
    half = pl.num_programs(0) // 2

    @pl.when(pl.program_id(0) < half)
    def _():
        keep1_ref[...] = dw1
        keep2_ref[...] = dw2

    @pl.when(pl.program_id(0) >= half)
    def _():
        send1_ref[...] = dw1
        send2_ref[...] = dw2

    @pl.when(pl.program_id(0) == pl.num_programs(0) - 1)
    def _():
        store_du.wait()


def feed_backward(g, hat, scale, vec, u, act, slope, firsts, seconds, chunk=512, tile=2048):
    tokens, width = u.shape
    counts = (len(firsts), len(seconds))
    units = act.shape[1]
    half = units // chunk // 2
    acts = lambda: pl.BlockSpec((tokens, chunk), lambda c: (0, c))
    keep = lambda: pl.BlockSpec((chunk, width), lambda c: (jnp.minimum(c, half - 1), 0))
    send = lambda: pl.BlockSpec((chunk, width), lambda c: (jnp.maximum(c - half, 0), 0))
    grads = jax.ShapeDtypeStruct((units // 2, width), BF16)
    return pl.pallas_call(
        functools.partial(backward_kernel, tile=tile, counts=counts, chunk=chunk),
        grid=(units // chunk,),
        in_specs=[FAR] * 4
        + [whole_block(vec.shape), acts(), acts()]
        + [FAR] * sum(counts),
        out_specs=[
            keep(),
            keep(),
            send(),
            send(),
            pl.BlockSpec((1, chunk), lambda c: (0, c)),
            FAR,
            whole_block((24, width)),
        ],
        out_shape=[grads] * 4
        + [
            jax.ShapeDtypeStruct((1, units), F32),
            jax.ShapeDtypeStruct((tokens, width), F32),
            jax.ShapeDtypeStruct((24, width), F32),
        ],
        scratch_shapes=[
            pltpu.VMEM((tokens, width), BF16),
            pltpu.VMEM((units, width), BF16),
            pltpu.VMEM((units, width), BF16),
            pltpu.VMEM((tokens, chunk), BF16),
            pltpu.VMEM((tokens, width), BF16),
            pltpu.VMEM((tokens, width), BF16),
            pltpu.VMEM((tokens, LANES), F32),
            pltpu.VMEM((tokens, width), BF16),
            pltpu.VMEM((tokens, width), F32),
            pltpu.SemaphoreType.DMA((counts[0],)),
            pltpu.SemaphoreType.DMA((counts[1],)),
            pltpu.SemaphoreType.DMA((4, 3)),
            pltpu.SemaphoreType.DMA((2,)),
        ],
        compiler_params=params(),
        cost_estimate=cost(8 * tokens * units * width, 0, 60 << 20),
        name="feed_backward",
    )(g, hat, scale, u, vec, act, slope, *firsts, *seconds)


def table_pair(points):
    numbers = jnp.arange(points, dtype=jnp.int32)
    coarse = 32 * jnp.arange(points // 32, dtype=jnp.int32)
    fine = jnp.arange(32, dtype=jnp.int32)

    def waves(rows):
        angles = (rows[:, None] * numbers[None, :] % points).astype(F32) * (2.0 * math.pi / points)
        return jnp.cos(angles), jnp.sin(angles)

    factor = 1.0 / math.sqrt(points)
    if points <= 64:
        cosine, sine = waves(numbers)
    else:
        coarse_cos, coarse_sin = waves(coarse)
        fine_cos, fine_sin = waves(fine)
        coarse_cos, coarse_sin, fine_cos, fine_sin = lax.optimization_barrier(
            (coarse_cos, coarse_sin, fine_cos, fine_sin)
        )
        coarse_cos, coarse_sin = coarse_cos[:, None], coarse_sin[:, None]
        fine_cos, fine_sin = fine_cos[None], fine_sin[None]
        cosine = (coarse_cos * fine_cos - coarse_sin * fine_sin).reshape(points, points)
        sine = (coarse_sin * fine_cos + coarse_cos * fine_sin).reshape(points, points)
    return (cosine * factor).astype(BF16), (sine * factor).astype(BF16)


def twiddles():
    row_index = jnp.arange(L1, dtype=jnp.int32)[None, :]
    col_index = jnp.arange(L2, dtype=jnp.int32)[:, None]
    angles = (row_index * col_index % L).astype(F32) * (2.0 * math.pi / L)
    wave = jnp.cos(angles), jnp.sin(angles)
    return [jnp.broadcast_to(values[:, :, None], (L2, L1, LANES)) for values in wave]


def swap(values, step):
    axis, mask = step
    size = lax.axis_size(axis)
    return lax.ppermute(values, axis, [(i, i ^ mask) for i in range(size)])


def bits(size):
    masks = []
    mask = size // 2
    while mask >= 1:
        masks.append(mask)
        mask //= 2
    return masks


def widen(held, step):
    return jnp.concatenate([held, swap(held, step)], axis=0)


def widen_codes(codes, steps, groups):
    for axis, mask in steps:
        code = mask if axis == "seq" else mask * groups
        codes = codes + [held ^ code for held in codes]
    return codes


def spread(pieces, steps):
    for step in steps:
        pieces = pieces + [swap(piece, step) for piece in pieces]
    return pieces


def spread_core(pieces, step_core):
    return pieces + [swap(piece, step_core) for piece in pieces]


def total(addends):
    return sum(addends[1:], addends[0].astype(F32))


def half_of(addends, axis, number):
    return [lax.index_in_dim(held, number, axis, keepdims=False) for held in addends]


def fold(addends, names, step, kind):
    axis = names.index(step)
    send = total(half_of(addends, axis, 1)).astype(kind)
    arrived = swap(send, step)
    return half_of(addends, axis, 0) + [arrived], names[:axis] + names[axis + 1 :]


def fold_all(addends, names, steps, kind):
    for step in steps:
        addends, names = fold(addends, names, step, kind)
    return addends, names


def arrange(rows):
    return with_layout_constraint(rows.transpose(0, 2, 1, 3), Layout(major_to_minor=(0, 1, 2, 3)))


def exchange(rows):
    order = Layout(major_to_minor=(0, 1, 2, 3))
    rows = with_layout_constraint(rows, order)
    rows = lax.all_to_all(rows, "seq", split_axis=0, concat_axis=0, tiled=True)
    return with_layout_constraint(rows, order)


def body(tokens, lengths, labels, picked, cotangent, w_in, b_in, w_out, shifts, norm_gains):
    groups = lax.axis_size("seq")
    me = lax.axis_index("seq")
    here = lax.axis_index("batch") * groups + me
    columns = tokens.shape[2]
    share = w_in.shape[2]
    part = shifts.shape[2]
    blocks = groups * lax.axis_size("batch")

    masks = bits(groups)[:-1]
    steps_plane = [("seq", mask) for mask in masks[:1] + masks[:0:-1]]
    steps_seq = [("seq", mask) for mask in masks[::-1]]
    steps_batch = [("batch", mask) for mask in bits(lax.axis_size("batch"))]
    step_core = ("seq", 1)
    numbers = jnp.arange(blocks, dtype=jnp.int32)

    codes = widen_codes([0], steps_plane + steps_batch + [step_core], groups)
    owner = jnp.array(codes, dtype=jnp.int32) ^ here
    one_hot = (owner[:, None] == numbers[None, :]).astype(F32)

    wide_cos, wide_sin = table_pair(D)
    wide = jnp.concatenate([wide_cos, -wide_sin], axis=0)
    twiddle_cos, twiddle_sin = twiddles()
    short_cos, short_sin = table_pair(L1)
    long_cos, long_sin = table_pair(L2)
    short_table = jnp.concatenate([short_cos, short_sin], axis=0)
    long_table = jnp.stack([jnp.stack([long_cos, -long_sin]), jnp.stack([long_sin, long_cos])])
    both = jnp.eye(2, dtype=BF16)
    pair_table = jnp.einsum("qukm,bc->qkbcum", long_table, both).reshape(4 * L2, 4 * L2)

    length = lax.dynamic_slice_in_dim(lengths, me, 1)
    small = jnp.concatenate([b_in[0], shifts[0].reshape(-1), norm_gains[0].reshape(-1)])
    small = small.astype(F32)[None]
    first_held = w_in[0].T[None]
    second_held = w_out[0][None]
    tokens_late = arrange(tokens)
    for number, step in enumerate(steps_plane[:-1]):
        first_held = widen(first_held, step)
        second_held = widen(second_held, step)
        small = widen(small, step)
        if number == 0:
            tokens_late, small, first_held, second_held = lax.optimization_barrier(
                (tokens_late, small, first_held, second_held)
            )
            x_all = exchange(tokens_late)
    early = (wide, twiddle_cos, twiddle_sin, short_table, pair_table, arrange(cotangent))
    small, first_held, second_held, early = lax.optimization_barrier(
        (small, first_held, second_held, early)
    )
    wide, twiddle_cos, twiddle_sin, short_table, pair_table, late_cotangent = early
    first_held = widen(first_held, steps_plane[-1])
    seconds = []
    for piece in spread([second_held], steps_batch):
        seconds += [piece, swap(piece, steps_plane[-1])]
    steps_small = steps_plane[:-1] + steps_batch + [step_core] + steps_plane[-1:]
    small_codes = widen_codes([0], steps_small, groups)
    for step in steps_batch + [step_core]:
        small = widen(small, step)
    small, first_held = lax.optimization_barrier((small, first_held))
    small = widen(small, steps_plane[-1])
    places = jnp.array([small_codes.index(code) for code in codes], dtype=jnp.int32)
    place_hot = (places[:, None] == numbers[None, :]).astype(F32)
    small = jnp.sum(place_hot[:, :, None] * small[None], axis=1)
    b_first = small[:, :share].reshape(1, blocks * share)
    rows = jnp.sum(one_hot[:, :, None] * small[:, None, share:], axis=0)
    rows = rows.reshape(blocks, 5, part).transpose(1, 0, 2).reshape(5, D)
    shifts_f = rows[:3]
    gains_f = rows[3:]
    blank = jnp.zeros((3, D), F32)
    vec = jnp.concatenate(
        [gains_f[1:2], shifts_f[2:3], gains_f[0:1], shifts_f[1:2], shifts_f[0:1], blank]
    )
    vec_one = vec[2:]
    vec_one = jnp.concatenate([vec_one, blank[:2]])
    firsts = spread([first_held], steps_batch)
    x_rows = x_all.reshape(L2, L1, D)
    hat_one, scale_one = transform(
        length, x_rows, short_table, pair_table, twiddle_cos, twiddle_sin, wide
    )
    hat_one, late_cotangent, firsts, seconds, vec, vec_one, b_first = lax.optimization_barrier(
        (hat_one, late_cotangent, firsts, seconds, vec, vec_one, b_first)
    )
    g_all = exchange(late_cotangent)
    flat = lambda pieces: [piece.reshape(-1, D) for piece in spread_core(pieces, step_core)]
    firsts, seconds = flat(firsts), flat(seconds)
    act, slope, layer_out, hat_two, scale_two, u = feed_forward(
        hat_one, b_first, vec, firsts, seconds
    )
    out_rows = exchange(layer_out.reshape(groups, columns, L1, D))

    keep_first, keep_second, send_first, send_second, grad_b_first, grad_u, sums_two = feed_backward(
        g_all.reshape(L, D), hat_two, scale_two, vec, u, act, slope, firsts, seconds
    )
    names = steps_batch[::-1] + steps_plane[::-1]
    shape = (2,) * len(names) + (share,)
    came_first = swap(send_first, step_core)
    came_second = swap(send_second, step_core)
    grad_x, sums_one = transform_back(
        length, grad_u, hat_one, scale_one, short_table.T, pair_table.T,
        twiddle_cos, twiddle_sin, vec_one, wide
    )
    grad_x, came_first, came_second, out_rows = lax.optimization_barrier(
        (grad_x, came_first, came_second, out_rows)
    )
    grad_first = [values.reshape(shape + (D,)) for values in (keep_first, came_first)]
    grad_second = [values.reshape(shape + (D,)) for values in (keep_second, came_second)]
    grad_x = grad_x.reshape(groups, columns, L1, D)
    input_grad = exchange(grad_x).transpose(0, 2, 1, 3)

    shift_of = jnp.arange(columns, dtype=jnp.int32) + me * columns
    place_of = L2 * jnp.arange(L1, dtype=jnp.int32)[None, :] + shift_of[:, None]
    steps_fold = steps_batch[::-1] + steps_seq
    early = len(steps_batch)
    grad_first, names_first = fold_all(grad_first, names, steps_fold[:early], BF16)
    grad_second, names_second = fold_all(grad_second, names, steps_fold[:early], BF16)
    out_rows, sums_one, sums_two, grad_b_first, grad_first[-1] = lax.optimization_barrier(
        (out_rows, sums_one, sums_two, grad_b_first, grad_first[-1])
    )
    logits = out_rows.astype(F32)
    highest = jnp.max(logits, axis=-1, keepdims=True)
    powers = jnp.exp(logits - highest)
    denominator = jnp.sum(powers, axis=-1)
    features = jnp.arange(D, dtype=jnp.int32)
    label_rows = labels.transpose(0, 2, 1)
    top = jnp.sum(jnp.where(features == label_rows[..., None], powers, 0.0), axis=-1)
    counted = (picked.transpose(0, 2, 1) > 0) & (place_of[None] < lengths[:, None, None])
    weight = jnp.where(counted, 1.0, 0.0)
    sums = jnp.stack([jnp.sum(weight * (top / denominator)), jnp.sum(weight)])

    sums_two = jnp.sum(sums_two.reshape(3, 8, D), axis=1)
    sums_one = jnp.sum(sums_one.reshape(2, 8, D), axis=1)
    norms = jnp.stack([sums_two[0], sums_one[1], sums_two[2], sums_one[0], sums_two[1]])
    norms = norms.reshape(5, blocks, part).transpose(1, 0, 2).reshape(blocks, 5 * part)
    norms = jnp.sum(one_hot[:, :, None] * norms[None], axis=1)
    sums = jnp.broadcast_to(sums[None], (blocks, 2))
    small_grads = jnp.concatenate([grad_b_first.reshape(blocks, share), norms, sums], axis=1)
    half = blocks // 2
    arrived = swap(small_grads[half:], step_core)
    small = [values.reshape(shape[:-1] + (-1,)) for values in (small_grads[:half], arrived)]
    small, names_small = fold_all(small, names, steps_fold[:early], F32)
    small[-1], out_rows = lax.optimization_barrier((small[-1], out_rows))
    grad_first, names_first = fold_all(grad_first, names_first, steps_fold[early:], BF16)
    for step in steps_fold[early:]:
        small[-1], grad_second[-1] = lax.optimization_barrier((small[-1], grad_second[-1]))
        small, names_small = fold(small, names_small, step, F32)
        grad_second, names_second = fold(grad_second, names_second, step, BF16)
    current = out_rows.transpose(0, 2, 1, 3)
    small_grads, grad_first, grad_second = total(small), total(grad_first), total(grad_second)
    norms = small_grads[share:-2].reshape(5, part)
    match_rate = D * small_grads[-2] / jnp.maximum(small_grads[-1], 1.0)
    return (
        current,
        input_grad,
        grad_first.T[None],
        small_grads[:share][None],
        grad_second[None],
        norms[:3][None],
        norms[3:][None],
        match_rate,
    )


def solution(mesh):
    in_specs = (
        P("batch", None, "seq", None),
        P("batch"),
        P("batch", None, "seq"),
        P("batch", None, "seq"),
        P("batch", None, "seq", None),
        P(None, None, ("batch", "seq")),
        P(None, ("batch", "seq")),
        P(None, ("batch", "seq"), None),
        P(None, None, ("batch", "seq")),
        P(None, None, ("batch", "seq")),
    )
    out_specs = (
        P("batch", None, "seq", None),
        P("batch", None, "seq", None),
        P(None, None, ("batch", "seq")),
        P(None, ("batch", "seq")),
        P(None, ("batch", "seq"), None),
        P(None, None, ("batch", "seq")),
        P(None, None, ("batch", "seq")),
        P(),
    )
    return jax.shard_map(body, mesh=mesh, in_specs=in_specs, out_specs=out_specs, check_vma=False)
```

```python
import functools
import math

import jax
import jax.numpy as jnp
from jax import lax
from jax.experimental import pallas as pl
from jax.experimental.layout import Layout, with_layout_constraint
from jax.experimental.pallas import tpu as pltpu
from jax.sharding import PartitionSpec as P

D = 768
L1 = 64
L2 = 32
L = 2048
LANES = 128
PAIR = 4 * L2
STRIDE = PAIR + 1

EPSILON = 1e-12
ROOT_TWO_PI = 0.7978845608028654
CUBIC = ROOT_TWO_PI * 0.044715
F32 = jnp.float32
BF16 = jnp.bfloat16
VMEM_BYTES = 60 << 20
FAR = pl.BlockSpec(memory_space=pl.ANY)


def product(left, right):
    return lax.dot_general(left, right, (((1,), (0,)), ((), ())), preferred_element_type=F32)


def product_turned(left, right):
    return lax.dot_general(left, right, (((1,), (1,)), ((), ())), preferred_element_type=F32)


def product_over_rows(left, right):
    return lax.dot_general(left, right, (((0,), (0,)), ((), ())), preferred_element_type=F32)


def lanes(column):
    return jnp.concatenate([column] * (D // LANES), axis=1)


def rows_of_eight(values):
    return jnp.sum(values.reshape(-1, 8, values.shape[-1]), axis=0)


def average(values):
    return jnp.mean(values, axis=1, keepdims=True)


def norm_back(grad, x_hat, scale, gain):
    q = grad * gain
    return lanes(scale) * (q - average(q) - x_hat * average(q * x_hat))


def whole_block(shape):
    return pl.BlockSpec(shape, lambda c: (0,) * len(shape), pipeline_mode=pl.Buffered(1))


def params():
    return pltpu.CompilerParams(vmem_limit_bytes=VMEM_BYTES)


def cost(flops, transcendentals, size):
    return pl.CostEstimate(flops=flops, transcendentals=transcendentals, bytes_accessed=size)


def scatter(refs, start, value):
    for j, ref in enumerate(refs):
        ref[pl.ds(start, L2, stride=STRIDE), :] = value[:, j * LANES : (j + 1) * LANES]


def gather(refs, block):
    return jnp.concatenate([ref[pl.ds(block * STRIDE, PAIR), :] for ref in refs], axis=1)


def middle_scratch():
    return [pltpu.VMEM((L2 * STRIDE, LANES), F32)] * (D // LANES)


def transform_kernel(
    length_ref, x_ref, short_ref, pair_ref, cos_ref, sin_ref, wide_hbm,
    hat_ref, scale_ref, spec_ref, wide_ref, sem, *middle, group
):
    length = length_ref[0]
    step = pl.program_id(0)
    load = pltpu.make_async_copy(wide_hbm, wide_ref, sem.at[0])

    @pl.when(step == 0)
    def _():
        load.start()

        def first(m, carry):
            spots = L2 * lax.broadcasted_iota(jnp.int32, (L1, D), 0) + m
            x = jnp.where(spots < length, x_ref[m].astype(F32), 0.0).astype(BF16)
            y = product(short_ref[...], x)
            real, imag = y[:L1], y[L1:]
            cosine, sine = lanes(cos_ref[m]), lanes(sin_ref[m])
            turned = (real * cosine - imag * sine, real * sine + imag * cosine)
            for b in range(2):
                for part in range(2):
                    scatter(middle, (b * 2 + part) * L2 + m, turned[part][b * L2 : (b + 1) * L2])
            return carry

        lax.fori_loop(0, L2, first, 0, unroll=4)
        load.wait()

    for j in range(group):
        turned = gather(middle, step * group + j).astype(BF16)
        q = product(pair_ref[...], turned).astype(BF16)
        spec_ref[j * L1 : (j + 1) * L1, :D] = q[:L1]
        spec_ref[j * L1 : (j + 1) * L1, D:] = q[L1:]
    mixed = product(spec_ref[...], wide_ref[...])
    number = lax.broadcasted_iota(jnp.int32, (group * L1, D), 0)
    spots = L2 * (number % L1) + step * group + number // L1
    x = x_ref[pl.ds(step * group, group)].reshape(group * L1, D).astype(F32)
    h = jnp.where(spots < length, x, 0.0) + mixed
    center = h - average(h)
    scale = lax.rsqrt(average(center * center) + EPSILON)
    hat_ref[...] = center * scale
    scale_ref[...] = jnp.broadcast_to(scale, scale_ref.shape)


def transform(length, x, short, pair, cosine, sine, wide, group=8):
    out = lambda width: pl.BlockSpec((group * L1, width), lambda c: (c, 0))
    return pl.pallas_call(
        functools.partial(transform_kernel, group=group),
        grid=(L2 // group,),
        in_specs=[pl.BlockSpec(memory_space=pltpu.SMEM)]
        + [whole_block(values.shape) for values in (x, short, pair, cosine, sine)]
        + [FAR],
        out_specs=[out(D), out(LANES)],
        out_shape=[
            jax.ShapeDtypeStruct((L, D), F32),
            jax.ShapeDtypeStruct((L, LANES), F32),
        ],
        scratch_shapes=[
            pltpu.VMEM((group * L1, 2 * D), BF16),
            pltpu.VMEM((2 * D, D), BF16),
            pltpu.SemaphoreType.DMA((1,)),
        ]
        + middle_scratch(),
        compiler_params=params(),
        cost_estimate=cost(7 << 30, L, 24 << 20),
        name="transform",
    )(length, x, short, pair, cosine, sine, wide)


def back_kernel(
    length_ref, du_ref, hat_ref, scale_ref, short_ref, pair_ref, cos_ref, sin_ref, vec_ref, wide_ref,
    dx_ref, sums_ref, rh_ref, spec_ref, *middle, group
):
    length = length_ref[0]
    step = pl.program_id(0)
    steps = L2 // group

    @pl.when(step == 0)
    def _():
        sums_ref[...] = jnp.zeros_like(sums_ref)

    @pl.when(step < steps)
    def _():
        du = du_ref[...]
        hat = hat_ref[...]
        rh = norm_back(du, hat, scale_ref[...], vec_ref[0:1, :]).astype(BF16)
        rh_ref[pl.ds(pl.multiple_of(step * group * L1, group * L1), group * L1), :] = rh
        sums_ref[0:8, :] += rows_of_eight(du * hat)
        sums_ref[8:16, :] += rows_of_eight(du)
        real = product(rh, wide_ref[:D, :]).astype(BF16)
        imag = product(rh, wide_ref[D:, :]).astype(BF16)
        for j in range(group):
            spec_ref[j, :L1, :] = real[j * L1 : (j + 1) * L1]
            spec_ref[j, L1:, :] = imag[j * L1 : (j + 1) * L1]
            turned = product(pair_ref[...], spec_ref[j]).astype(BF16).astype(F32)
            for b in range(2):
                for part in range(2):
                    start = (b * 2 + part) * L2
                    spot = part * L1 + b * L2 + step * group + j
                    scatter(middle, spot, turned[start : start + L2])

    @pl.when(step >= steps)
    def _():
        def second(i, carry):
            m = (step - steps) * group + i
            turned = gather(middle, m)
            real, imag = turned[:L1], turned[L1:]
            cosine, sine = lanes(cos_ref[m]), lanes(sin_ref[m])
            back = jnp.concatenate(
                [
                    (real * cosine + imag * sine).astype(BF16),
                    (imag * cosine - real * sine).astype(BF16),
                ],
                axis=0,
            )
            rh = rh_ref[pl.ds(pl.multiple_of(m * L1, L1), L1), :].astype(F32)
            dx = rh + product(short_ref[...], back)
            spots = L2 * lax.broadcasted_iota(jnp.int32, (L1, D), 0) + m
            dx_ref[i] = jnp.where(spots < length, dx, 0.0).astype(BF16)
            return carry

        lax.fori_loop(0, group, second, 0, unroll=4)


def transform_back(length, du, hat, scale, short, pair, cosine, sine, vec, wide, group=8):
    steps = L2 // group
    rows = lambda width: pl.BlockSpec((group * L1, width), lambda c: (jnp.minimum(c, steps - 1), 0))
    return pl.pallas_call(
        functools.partial(back_kernel, group=group),
        grid=(2 * steps,),
        in_specs=[pl.BlockSpec(memory_space=pltpu.SMEM), rows(D), rows(D), rows(LANES)]
        + [whole_block(values.shape) for values in (short, pair, cosine, sine, vec, wide)],
        out_specs=[
            pl.BlockSpec((group, L1, D), lambda c: (jnp.maximum(c - steps, 0), 0, 0)),
            pl.BlockSpec((16, D), lambda c: (0, 0)),
        ],
        out_shape=[
            jax.ShapeDtypeStruct((L2, L1, D), BF16),
            jax.ShapeDtypeStruct((16, D), F32),
        ],
        scratch_shapes=[pltpu.VMEM((L, D), BF16), pltpu.VMEM((group, 2 * L1, D), BF16)]
        + middle_scratch(),
        compiler_params=params(),
        cost_estimate=cost(7 << 30, 0, 20 << 20),
        name="transform_back",
    )(length, du, hat, scale, short, pair, cosine, sine, vec, wide)


def fetch_weights(pieces, holder, sems, chunk):
    rows = holder.shape[0] // len(pieces)
    step = pl.program_id(0)
    copies = [
        pltpu.make_async_copy(
            piece.at[pl.ds(0, rows), :], holder.at[pl.ds(i * rows, rows), :], sems.at[i]
        )
        for i, piece in enumerate(pieces)
    ]

    @pl.when(step == 0)
    def _():
        for copy in copies:
            copy.start()

    for number in range(holder.shape[0] // chunk):
        needed = [copy for i, copy in enumerate(copies) if i * rows // chunk == number]
        if needed:

            @pl.when(step == number)
            def _():
                for copy in needed:
                    copy.wait()


def forward_kernel(*refs, tile, counts, chunk):
    first_hat_ref, b_ref, vec_ref = refs[:3]
    split = 3 + sum(counts)
    firsts, seconds = refs[3 : 3 + counts[0]], refs[3 + counts[0] : split]
    act_ref, slope_ref, out_far, hat_far, scale_far, u_far = refs[split : split + 6]
    y_ref, w1_ref, w2_ref, out_ref, hat_ref, scale_ref, u_ref, sem1, sem2, sem3 = refs[split + 6 :]
    parts = 4
    part = u_ref.shape[0] // parts
    tiles = u_ref.shape[0] // tile
    loads, stores = [], []
    for i in range(parts):
        rows = pl.ds(i * part, part)
        pairs = ((u_ref, u_far), (out_ref, out_far), (hat_ref, hat_far), (scale_ref, scale_far))
        loads.append(
            pltpu.make_async_copy(first_hat_ref.at[rows, :], y_ref.at[rows, :], sem3.at[i, 0])
        )
        stores.append(
            [
                pltpu.make_async_copy(near.at[rows, :], far.at[rows, :], sem3.at[i, 1 + j])
                for j, (near, far) in enumerate(pairs)
            ]
        )

    @pl.when(pl.program_id(0) == 0)
    def _():
        for load in loads:
            load.start()

    fetch_weights(firsts, w1_ref, sem1, chunk)
    fetch_weights(seconds, w2_ref, sem2, chunk)
    here = pl.ds(pl.multiple_of(pl.program_id(0) * chunk, chunk), chunk)

    @pl.when(pl.program_id(0) == 0)
    def _():
        small = 256

        def begin(i, carry):
            rows = pl.ds(pl.multiple_of(i * small, small), small)
            u = y_ref[rows, :] * vec_ref[2:3, :] + vec_ref[3:4, :]
            u_ref[rows, :] = u.astype(BF16)
            y_ref[rows, :] = u + vec_ref[4:5, :]
            return carry

        for i in range(parts):
            loads[i].wait()
            lax.fori_loop(i * part // small, (i + 1) * part // small, begin, 0)
            stores[i][0].start()


    def step(i, carry):
        rows = pl.ds(pl.multiple_of(i * tile, tile), tile)
        z = product_turned(u_ref[rows, :], w1_ref[here, :]) + b_ref[...]
        square = z * z
        t = jnp.tanh(z * (ROOT_TWO_PI + CUBIC * square))
        half = 0.5 + 0.5 * t
        a = z * half
        low = a.astype(BF16)
        act_ref[rows, :] = low
        slope = half + (a - a * t) * (ROOT_TWO_PI + (3.0 * CUBIC) * square)
        slope_ref[rows, :] = slope.astype(BF16)
        y_ref[rows, :] += product(low, w2_ref[here, :])
        return carry

    lax.fori_loop(0, tiles, step, 0)

    @pl.when(pl.program_id(0) == pl.num_programs(0) - 1)
    def _():
        small = 256

        def finish(i, carry):
            rows = pl.ds(pl.multiple_of(i * small, small), small)
            y = y_ref[rows, :]
            center = y - average(y)
            scale = lax.rsqrt(average(center * center) + EPSILON)
            hat = center * scale
            out_ref[rows, :] = (hat * vec_ref[0:1, :] + vec_ref[1:2, :]).astype(BF16)
            hat_ref[rows, :] = hat.astype(BF16)
            scale_ref[rows, :] = jnp.broadcast_to(scale, (small, LANES))
            return carry

        for i in range(parts):
            lax.fori_loop(i * part // small, (i + 1) * part // small, finish, 0)
            for copy in stores[i][1:]:
                copy.start()
        for store in stores:
            for copy in store:
                copy.wait()


def feed_forward(hat, b, vec, firsts, seconds, chunk=1024, tile=1024):
    tokens, width = hat.shape
    counts = (len(firsts), len(seconds))
    units = b.shape[1]
    acts = lambda: pl.BlockSpec((tokens, chunk), lambda c: (0, c))
    return pl.pallas_call(
        functools.partial(forward_kernel, tile=tile, counts=counts, chunk=chunk),
        grid=(units // chunk,),
        in_specs=[
            FAR,
            pl.BlockSpec((1, chunk), lambda c: (0, c)),
            whole_block(vec.shape),
        ]
        + [FAR] * sum(counts),
        out_specs=[acts(), acts()] + [FAR] * 4,
        out_shape=[
            jax.ShapeDtypeStruct((tokens, units), BF16),
            jax.ShapeDtypeStruct((tokens, units), BF16),
            jax.ShapeDtypeStruct((tokens, width), BF16),
            jax.ShapeDtypeStruct((tokens, width), BF16),
            jax.ShapeDtypeStruct((tokens, LANES), F32),
            jax.ShapeDtypeStruct((tokens, width), BF16),
        ],
        scratch_shapes=[
            pltpu.VMEM((tokens, width), F32),
            pltpu.VMEM((units, width), BF16),
            pltpu.VMEM((units, width), BF16),
            pltpu.VMEM((tokens, width), BF16),
            pltpu.VMEM((tokens, width), BF16),
            pltpu.VMEM((tokens, LANES), F32),
            pltpu.VMEM((tokens, width), BF16),
            pltpu.SemaphoreType.DMA((counts[0],)),
            pltpu.SemaphoreType.DMA((counts[1],)),
            pltpu.SemaphoreType.DMA((4, 5)),
        ],
        compiler_params=params(),
        cost_estimate=cost(4 * tokens * units * width, tokens * units, 50 << 20),
        name="feed_forward",
    )(hat, b, vec, *firsts, *seconds)


def backward_kernel(*refs, tile, counts, chunk):
    g_far, hat_far, scale_far, u_far, vec_ref, act_ref, slope_ref = refs[:7]
    split = 7 + sum(counts)
    firsts, seconds = refs[7 : 7 + counts[0]], refs[7 + counts[0] : split]
    keep1_ref, keep2_ref, send1_ref, send2_ref, db_ref, du_far, sums_ref = refs[split : split + 7]
    e_ref, w1_ref, w2_ref, f_ref, g_ref, hat_ref, scale_ref, u_ref, du_ref = refs[
        split + 7 : split + 16
    ]
    sem1, sem2, sem3, sem4 = refs[split + 16 :]
    parts = 4
    part = u_ref.shape[0] // parts
    loads = []
    for i in range(parts):
        rows = pl.ds(i * part, part)
        loads.append(
            [
                pltpu.make_async_copy(far.at[rows, :], near.at[rows, :], sem3.at[i, j])
                for j, (far, near) in enumerate(
                    ((g_far, g_ref), (hat_far, hat_ref), (scale_far, scale_ref))
                )
            ]
        )
    load_u = pltpu.make_async_copy(u_far, u_ref, sem4.at[0])
    store_du = pltpu.make_async_copy(du_ref, du_far, sem4.at[1])

    @pl.when(pl.program_id(0) == 0)
    def _():
        for load in loads:
            for copy in load:
                copy.start()

    fetch_weights(seconds, w2_ref, sem2, chunk)
    fetch_weights(firsts, w1_ref, sem1, chunk)
    here = pl.ds(pl.multiple_of(pl.program_id(0) * chunk, chunk), chunk)

    @pl.when(pl.program_id(0) == 0)
    def _():
        small = 256
        sums_ref[...] = jnp.zeros_like(sums_ref)

        def begin(i, carry):
            rows = pl.ds(pl.multiple_of(i * small, small), small)
            g = g_ref[rows, :].astype(F32)
            hat = hat_ref[rows, :].astype(F32)
            dy = norm_back(g, hat, scale_ref[rows, :], vec_ref[0:1, :])
            du_ref[rows, :] = dy
            e_ref[rows, :] = dy.astype(BF16)
            sums_ref[0:8, :] += rows_of_eight(dy)
            sums_ref[8:16, :] += rows_of_eight(g * hat)
            sums_ref[16:24, :] += rows_of_eight(g)
            return carry

        load_u.start()
        for i in range(parts):
            for copy in loads[i]:
                copy.wait()
            lax.fori_loop(i * part // small, (i + 1) * part // small, begin, 0)
        load_u.wait()


    def step(i, db):
        rows = pl.ds(pl.multiple_of(i * tile, tile), tile)
        dz = product_turned(e_ref[rows, :], w2_ref[here, :]) * slope_ref[rows, :].astype(F32)
        low = dz.astype(BF16)
        f_ref[rows, :] = low
        du_ref[rows, :] += product(low, w1_ref[here, :])
        return db + rows_of_eight(dz)

    db = lax.fori_loop(0, u_ref.shape[0] // tile, step, jnp.zeros((8, chunk), F32))
    db_ref[...] = jnp.sum(db, axis=0, keepdims=True)

    @pl.when(pl.program_id(0) == pl.num_programs(0) - 1)
    def _():
        store_du.start()

    dw2 = product_over_rows(act_ref[...], e_ref[...]).astype(BF16)
    dw1 = product_over_rows(f_ref[...], u_ref[...]).astype(BF16)
    half = pl.num_programs(0) // 2

    @pl.when(pl.program_id(0) < half)
    def _():
        keep1_ref[...] = dw1
        keep2_ref[...] = dw2

    @pl.when(pl.program_id(0) >= half)
    def _():
        send1_ref[...] = dw1
        send2_ref[...] = dw2

    @pl.when(pl.program_id(0) == pl.num_programs(0) - 1)
    def _():
        store_du.wait()


def feed_backward(g, hat, scale, vec, u, act, slope, firsts, seconds, chunk=512, tile=2048):
    tokens, width = u.shape
    counts = (len(firsts), len(seconds))
    units = act.shape[1]
    half = units // chunk // 2
    acts = lambda: pl.BlockSpec((tokens, chunk), lambda c: (0, c))
    keep = lambda: pl.BlockSpec((chunk, width), lambda c: (jnp.minimum(c, half - 1), 0))
    send = lambda: pl.BlockSpec((chunk, width), lambda c: (jnp.maximum(c - half, 0), 0))
    grads = jax.ShapeDtypeStruct((units // 2, width), BF16)
    return pl.pallas_call(
        functools.partial(backward_kernel, tile=tile, counts=counts, chunk=chunk),
        grid=(units // chunk,),
        in_specs=[FAR] * 4
        + [whole_block(vec.shape), acts(), acts()]
        + [FAR] * sum(counts),
        out_specs=[
            keep(),
            keep(),
            send(),
            send(),
            pl.BlockSpec((1, chunk), lambda c: (0, c)),
            FAR,
            whole_block((24, width)),
        ],
        out_shape=[grads] * 4
        + [
            jax.ShapeDtypeStruct((1, units), F32),
            jax.ShapeDtypeStruct((tokens, width), F32),
            jax.ShapeDtypeStruct((24, width), F32),
        ],
        scratch_shapes=[
            pltpu.VMEM((tokens, width), BF16),
            pltpu.VMEM((units, width), BF16),
            pltpu.VMEM((units, width), BF16),
            pltpu.VMEM((tokens, chunk), BF16),
            pltpu.VMEM((tokens, width), BF16),
            pltpu.VMEM((tokens, width), BF16),
            pltpu.VMEM((tokens, LANES), F32),
            pltpu.VMEM((tokens, width), BF16),
            pltpu.VMEM((tokens, width), F32),
            pltpu.SemaphoreType.DMA((counts[0],)),
            pltpu.SemaphoreType.DMA((counts[1],)),
            pltpu.SemaphoreType.DMA((4, 3)),
            pltpu.SemaphoreType.DMA((2,)),
        ],
        compiler_params=params(),
        cost_estimate=cost(8 * tokens * units * width, 0, 60 << 20),
        name="feed_backward",
    )(g, hat, scale, u, vec, act, slope, *firsts, *seconds)


def table_pair(points):
    numbers = jnp.arange(points, dtype=jnp.int32)
    coarse = 32 * jnp.arange(points // 32, dtype=jnp.int32)
    fine = jnp.arange(32, dtype=jnp.int32)

    def waves(rows):
        angles = (rows[:, None] * numbers[None, :] % points).astype(F32) * (2.0 * math.pi / points)
        return jnp.cos(angles), jnp.sin(angles)

    factor = 1.0 / math.sqrt(points)
    if points <= 64:
        cosine, sine = waves(numbers)
    else:
        coarse_cos, coarse_sin = waves(coarse)
        fine_cos, fine_sin = waves(fine)
        coarse_cos, coarse_sin, fine_cos, fine_sin = lax.optimization_barrier(
            (coarse_cos, coarse_sin, fine_cos, fine_sin)
        )
        coarse_cos, coarse_sin = coarse_cos[:, None], coarse_sin[:, None]
        fine_cos, fine_sin = fine_cos[None], fine_sin[None]
        cosine = (coarse_cos * fine_cos - coarse_sin * fine_sin).reshape(points, points)
        sine = (coarse_sin * fine_cos + coarse_cos * fine_sin).reshape(points, points)
    return (cosine * factor).astype(BF16), (sine * factor).astype(BF16)


def twiddles():
    row_index = jnp.arange(L1, dtype=jnp.int32)[None, :]
    col_index = jnp.arange(L2, dtype=jnp.int32)[:, None]
    angles = (row_index * col_index % L).astype(F32) * (2.0 * math.pi / L)
    wave = jnp.cos(angles), jnp.sin(angles)
    return [jnp.broadcast_to(values[:, :, None], (L2, L1, LANES)) for values in wave]


def swap(values, step):
    axis, mask = step
    size = lax.axis_size(axis)
    return lax.ppermute(values, axis, [(i, i ^ mask) for i in range(size)])


def bits(size):
    masks = []
    mask = size // 2
    while mask >= 1:
        masks.append(mask)
        mask //= 2
    return masks


def widen(held, step):
    return jnp.concatenate([held, swap(held, step)], axis=0)


def widen_codes(codes, steps, groups):
    for axis, mask in steps:
        code = mask if axis == "seq" else mask * groups
        codes = codes + [held ^ code for held in codes]
    return codes


def spread(pieces, steps):
    for step in steps:
        pieces = pieces + [swap(piece, step) for piece in pieces]
    return pieces


def spread_core(pieces, step_core):
    return pieces + [swap(piece, step_core) for piece in pieces]


def total(addends):
    return sum(addends[1:], addends[0].astype(F32))


def half_of(addends, axis, number):
    return [lax.index_in_dim(held, number, axis, keepdims=False) for held in addends]


def fold(addends, names, step, kind):
    axis = names.index(step)
    send = total(half_of(addends, axis, 1)).astype(kind)
    arrived = swap(send, step)
    return half_of(addends, axis, 0) + [arrived], names[:axis] + names[axis + 1 :]


def fold_all(addends, names, steps, kind):
    for step in steps:
        addends, names = fold(addends, names, step, kind)
    return addends, names


def arrange(rows):
    return with_layout_constraint(rows.transpose(0, 2, 1, 3), Layout(major_to_minor=(0, 1, 2, 3)))


def exchange(rows):
    order = Layout(major_to_minor=(0, 1, 2, 3))
    rows = with_layout_constraint(rows, order)
    rows = lax.all_to_all(rows, "seq", split_axis=0, concat_axis=0, tiled=True)
    return with_layout_constraint(rows, order)


def body(tokens, lengths, labels, picked, cotangent, w_in, b_in, w_out, shifts, norm_gains):
    groups = lax.axis_size("seq")
    me = lax.axis_index("seq")
    here = lax.axis_index("batch") * groups + me
    columns = tokens.shape[2]
    share = w_in.shape[2]
    part = shifts.shape[2]
    blocks = groups * lax.axis_size("batch")

    masks = bits(groups)[:-1]
    steps_plane = [("seq", mask) for mask in masks[:1] + masks[:0:-1]]
    steps_seq = [("seq", mask) for mask in masks[::-1]]
    steps_batch = [("batch", mask) for mask in bits(lax.axis_size("batch"))]
    step_core = ("seq", 1)
    numbers = jnp.arange(blocks, dtype=jnp.int32)

    codes = widen_codes([0], steps_plane + steps_batch + [step_core], groups)
    owner = jnp.array(codes, dtype=jnp.int32) ^ here
    one_hot = (owner[:, None] == numbers[None, :]).astype(F32)

    wide_cos, wide_sin = table_pair(D)
    wide = jnp.concatenate([wide_cos, -wide_sin], axis=0)
    twiddle_cos, twiddle_sin = twiddles()
    short_cos, short_sin = table_pair(L1)
    long_cos, long_sin = table_pair(L2)
    short_table = jnp.concatenate([short_cos, short_sin], axis=0)
    long_table = jnp.stack([jnp.stack([long_cos, -long_sin]), jnp.stack([long_sin, long_cos])])
    both = jnp.eye(2, dtype=BF16)
    pair_table = jnp.einsum("qukm,bc->qkbcum", long_table, both).reshape(4 * L2, 4 * L2)

    length = lax.dynamic_slice_in_dim(lengths, me, 1)
    small = jnp.concatenate([b_in[0], shifts[0].reshape(-1), norm_gains[0].reshape(-1)])
    small = small.astype(F32)[None]
    first_held = w_in[0].T[None]
    second_held = w_out[0][None]
    tokens_late = arrange(tokens)
    for number, step in enumerate(steps_plane[:-1]):
        first_held = widen(first_held, step)
        second_held = widen(second_held, step)
        small = widen(small, step)
        if number == 0:
            tokens_late, small, first_held, second_held = lax.optimization_barrier(
                (tokens_late, small, first_held, second_held)
            )
            x_all = exchange(tokens_late)
    early = (wide, twiddle_cos, twiddle_sin, short_table, pair_table, arrange(cotangent))
    small, first_held, second_held, early = lax.optimization_barrier(
        (small, first_held, second_held, early)
    )
    wide, twiddle_cos, twiddle_sin, short_table, pair_table, late_cotangent = early
    first_held = widen(first_held, steps_plane[-1])
    seconds = []
    for piece in spread([second_held], steps_batch):
        seconds += [piece, swap(piece, steps_plane[-1])]
    steps_small = steps_plane[:-1] + steps_batch + [step_core] + steps_plane[-1:]
    small_codes = widen_codes([0], steps_small, groups)
    for step in steps_batch + [step_core]:
        small = widen(small, step)
    small, first_held = lax.optimization_barrier((small, first_held))
    small = widen(small, steps_plane[-1])
    places = jnp.array([small_codes.index(code) for code in codes], dtype=jnp.int32)
    place_hot = (places[:, None] == numbers[None, :]).astype(F32)
    small = jnp.sum(place_hot[:, :, None] * small[None], axis=1)
    b_first = small[:, :share].reshape(1, blocks * share)
    rows = jnp.sum(one_hot[:, :, None] * small[:, None, share:], axis=0)
    rows = rows.reshape(blocks, 5, part).transpose(1, 0, 2).reshape(5, D)
    shifts_f = rows[:3]
    gains_f = rows[3:]
    blank = jnp.zeros((3, D), F32)
    vec = jnp.concatenate(
        [gains_f[1:2], shifts_f[2:3], gains_f[0:1], shifts_f[1:2], shifts_f[0:1], blank]
    )
    vec_one = vec[2:]
    vec_one = jnp.concatenate([vec_one, blank[:2]])
    firsts = spread([first_held], steps_batch)
    x_rows = x_all.reshape(L2, L1, D)
    hat_one, scale_one = transform(
        length, x_rows, short_table, pair_table, twiddle_cos, twiddle_sin, wide
    )
    hat_one, late_cotangent, firsts, seconds, vec, vec_one, b_first = lax.optimization_barrier(
        (hat_one, late_cotangent, firsts, seconds, vec, vec_one, b_first)
    )
    g_all = exchange(late_cotangent)
    flat = lambda pieces: [piece.reshape(-1, D) for piece in spread_core(pieces, step_core)]
    firsts, seconds = flat(firsts), flat(seconds)
    act, slope, layer_out, hat_two, scale_two, u = feed_forward(
        hat_one, b_first, vec, firsts, seconds
    )
    out_rows = exchange(layer_out.reshape(groups, columns, L1, D))

    keep_first, keep_second, send_first, send_second, grad_b_first, grad_u, sums_two = feed_backward(
        g_all.reshape(L, D), hat_two, scale_two, vec, u, act, slope, firsts, seconds
    )
    names = steps_batch[::-1] + steps_plane[::-1]
    shape = (2,) * len(names) + (share,)
    grad_x, sums_one = transform_back(
        length, grad_u, hat_one, scale_one, short_table.T, pair_table.T,
        twiddle_cos, twiddle_sin, vec_one, wide
    )
    grad_x, send_first, send_second, out_rows = lax.optimization_barrier(
        (grad_x, send_first, send_second, out_rows)
    )
    came_first = swap(send_first, step_core)
    came_second = swap(send_second, step_core)
    grad_first = [values.reshape(shape + (D,)) for values in (keep_first, came_first)]
    grad_second = [values.reshape(shape + (D,)) for values in (keep_second, came_second)]
    grad_x = grad_x.reshape(groups, columns, L1, D)
    input_grad = arrange(exchange(grad_x))

    shift_of = jnp.arange(columns, dtype=jnp.int32) + me * columns
    place_of = L2 * jnp.arange(L1, dtype=jnp.int32)[None, :] + shift_of[:, None]
    steps_fold = steps_batch[::-1] + steps_seq
    early = len(steps_batch)
    grad_first, names_first = fold_all(grad_first, names, steps_fold[:early], BF16)
    grad_second, names_second = fold_all(grad_second, names, steps_fold[:early], BF16)
    out_rows, sums_one, sums_two, grad_b_first, grad_first[-1] = lax.optimization_barrier(
        (out_rows, sums_one, sums_two, grad_b_first, grad_first[-1])
    )
    logits = out_rows.astype(F32)
    highest = jnp.max(logits, axis=-1, keepdims=True)
    powers = jnp.exp(logits - highest)
    denominator = jnp.sum(powers, axis=-1)
    features = jnp.arange(D, dtype=jnp.int32)
    label_rows = labels.transpose(0, 2, 1)
    top = jnp.sum(jnp.where(features == label_rows[..., None], powers, 0.0), axis=-1)
    counted = (picked.transpose(0, 2, 1) > 0) & (place_of[None] < lengths[:, None, None])
    weight = jnp.where(counted, 1.0, 0.0)
    sums = jnp.stack([jnp.sum(weight * (top / denominator)), jnp.sum(weight)])

    sums_two = jnp.sum(sums_two.reshape(3, 8, D), axis=1)
    sums_one = jnp.sum(sums_one.reshape(2, 8, D), axis=1)
    norms = jnp.stack([sums_two[0], sums_one[1], sums_two[2], sums_one[0], sums_two[1]])
    norms = norms.reshape(5, blocks, part).transpose(1, 0, 2).reshape(blocks, 5 * part)
    norms = jnp.sum(one_hot[:, :, None] * norms[None], axis=1)
    sums = jnp.broadcast_to(sums[None], (blocks, 2))
    small_grads = jnp.concatenate([grad_b_first.reshape(blocks, share), norms, sums], axis=1)
    half = blocks // 2
    arrived = swap(small_grads[half:], step_core)
    small = [values.reshape(shape[:-1] + (-1,)) for values in (small_grads[:half], arrived)]
    small, names_small = fold_all(small, names, steps_fold[:early], F32)
    small[-1], out_rows = lax.optimization_barrier((small[-1], out_rows))
    grad_first, names_first = fold_all(grad_first, names_first, steps_fold[early:], BF16)
    for step in steps_fold[early:]:
        small[-1], grad_second[-1] = lax.optimization_barrier((small[-1], grad_second[-1]))
        if step == steps_fold[-1]:
            input_grad, small[-1], grad_second[-1] = lax.optimization_barrier(
                (input_grad, small[-1], grad_second[-1])
            )
        small, names_small = fold(small, names_small, step, F32)
        grad_second, names_second = fold(grad_second, names_second, step, BF16)
    current = out_rows.transpose(0, 2, 1, 3)
    small_grads, grad_first, grad_second = total(small), total(grad_first), total(grad_second)
    norms = small_grads[share:-2].reshape(5, part)
    match_rate = D * small_grads[-2] / jnp.maximum(small_grads[-1], 1.0)
    return (
        current,
        input_grad,
        grad_first.T[None],
        small_grads[:share][None],
        grad_second[None],
        norms[:3][None],
        norms[3:][None],
        match_rate,
    )


def solution(mesh):
    in_specs = (
        P("batch", None, "seq", None),
        P("batch"),
        P("batch", None, "seq"),
        P("batch", None, "seq"),
        P("batch", None, "seq", None),
        P(None, None, ("batch", "seq")),
        P(None, ("batch", "seq")),
        P(None, ("batch", "seq"), None),
        P(None, None, ("batch", "seq")),
        P(None, None, ("batch", "seq")),
    )
    out_specs = (
        P("batch", None, "seq", None),
        P("batch", None, "seq", None),
        P(None, None, ("batch", "seq")),
        P(None, ("batch", "seq")),
        P(None, ("batch", "seq"), None),
        P(None, None, ("batch", "seq")),
        P(None, None, ("batch", "seq")),
        P(),
    )
    return jax.shard_map(body, mesh=mesh, in_specs=in_specs, out_specs=out_specs, check_vma=False)
```

```python
import functools
import math

import jax
import jax.numpy as jnp
from jax import lax
from jax.experimental import pallas as pl
from jax.experimental.layout import Layout, with_layout_constraint
from jax.experimental.pallas import tpu as pltpu
from jax.sharding import PartitionSpec as P

D = 768
L1 = 64
L2 = 32
L = 2048
LANES = 128
PAIR = 4 * L2
STRIDE = PAIR + 1

EPSILON = 1e-12
ROOT_TWO_PI = 0.7978845608028654
CUBIC = ROOT_TWO_PI * 0.044715
F32 = jnp.float32
BF16 = jnp.bfloat16
VMEM_BYTES = 60 << 20
FAR = pl.BlockSpec(memory_space=pl.ANY)


def product(left, right):
    return lax.dot_general(left, right, (((1,), (0,)), ((), ())), preferred_element_type=F32)


def product_turned(left, right):
    return lax.dot_general(left, right, (((1,), (1,)), ((), ())), preferred_element_type=F32)


def product_over_rows(left, right):
    return lax.dot_general(left, right, (((0,), (0,)), ((), ())), preferred_element_type=F32)


def lanes(column):
    return jnp.concatenate([column] * (D // LANES), axis=1)


def rows_of_eight(values):
    return jnp.sum(values.reshape(-1, 8, values.shape[-1]), axis=0)


def average(values):
    return jnp.mean(values, axis=1, keepdims=True)


def norm_back(grad, x_hat, scale, gain):
    q = grad * gain
    return lanes(scale) * (q - average(q) - x_hat * average(q * x_hat))


def whole_block(shape):
    return pl.BlockSpec(shape, lambda c: (0,) * len(shape), pipeline_mode=pl.Buffered(1))


def params():
    return pltpu.CompilerParams(vmem_limit_bytes=VMEM_BYTES)


def cost(flops, transcendentals, size):
    return pl.CostEstimate(flops=flops, transcendentals=transcendentals, bytes_accessed=size)


def scatter(refs, start, value):
    for j, ref in enumerate(refs):
        ref[pl.ds(start, L2, stride=STRIDE), :] = value[:, j * LANES : (j + 1) * LANES]


def gather(refs, block):
    return jnp.concatenate([ref[pl.ds(block * STRIDE, PAIR), :] for ref in refs], axis=1)


def middle_scratch():
    return [pltpu.VMEM((L2 * STRIDE, LANES), F32)] * (D // LANES)


def transform_kernel(
    length_ref, x_ref, short_ref, pair_ref, cos_ref, sin_ref, wide_hbm,
    hat_ref, scale_ref, spec_ref, wide_ref, sem, *middle, group
):
    length = length_ref[0]
    step = pl.program_id(0)
    load = pltpu.make_async_copy(wide_hbm, wide_ref, sem.at[0])

    @pl.when(step == 0)
    def _():
        load.start()

        def first(m, carry):
            spots = L2 * lax.broadcasted_iota(jnp.int32, (L1, D), 0) + m
            x = jnp.where(spots < length, x_ref[m].astype(F32), 0.0).astype(BF16)
            y = product(short_ref[...], x)
            real, imag = y[:L1], y[L1:]
            cosine, sine = lanes(cos_ref[m]), lanes(sin_ref[m])
            turned = (real * cosine - imag * sine, real * sine + imag * cosine)
            for b in range(2):
                for part in range(2):
                    scatter(middle, (b * 2 + part) * L2 + m, turned[part][b * L2 : (b + 1) * L2])
            return carry

        lax.fori_loop(0, L2, first, 0, unroll=4)
        load.wait()

    for j in range(group):
        turned = gather(middle, step * group + j).astype(BF16)
        q = product(pair_ref[...], turned).astype(BF16)
        spec_ref[j * L1 : (j + 1) * L1, :D] = q[:L1]
        spec_ref[j * L1 : (j + 1) * L1, D:] = q[L1:]
    mixed = product(spec_ref[...], wide_ref[...])
    number = lax.broadcasted_iota(jnp.int32, (group * L1, D), 0)
    spots = L2 * (number % L1) + step * group + number // L1
    x = x_ref[pl.ds(step * group, group)].reshape(group * L1, D).astype(F32)
    h = jnp.where(spots < length, x, 0.0) + mixed
    center = h - average(h)
    scale = lax.rsqrt(average(center * center) + EPSILON)
    hat_ref[...] = center * scale
    scale_ref[...] = jnp.broadcast_to(scale, scale_ref.shape)


def transform(length, x, short, pair, cosine, sine, wide, group=8):
    out = lambda width: pl.BlockSpec((group * L1, width), lambda c: (c, 0))
    return pl.pallas_call(
        functools.partial(transform_kernel, group=group),
        grid=(L2 // group,),
        in_specs=[pl.BlockSpec(memory_space=pltpu.SMEM)]
        + [whole_block(values.shape) for values in (x, short, pair, cosine, sine)]
        + [FAR],
        out_specs=[out(D), out(LANES)],
        out_shape=[
            jax.ShapeDtypeStruct((L, D), F32),
            jax.ShapeDtypeStruct((L, LANES), F32),
        ],
        scratch_shapes=[
            pltpu.VMEM((group * L1, 2 * D), BF16),
            pltpu.VMEM((2 * D, D), BF16),
            pltpu.SemaphoreType.DMA((1,)),
        ]
        + middle_scratch(),
        compiler_params=params(),
        cost_estimate=cost(7 << 30, L, 24 << 20),
        name="transform",
    )(length, x, short, pair, cosine, sine, wide)


def back_kernel(
    length_ref, du_ref, hat_ref, scale_ref, short_ref, pair_ref, cos_ref, sin_ref, vec_ref, wide_ref,
    dx_ref, sums_ref, rh_ref, spec_ref, *middle, group
):
    length = length_ref[0]
    step = pl.program_id(0)
    steps = L2 // group

    @pl.when(step == 0)
    def _():
        sums_ref[...] = jnp.zeros_like(sums_ref)

    @pl.when(step < steps)
    def _():
        du = du_ref[...]
        hat = hat_ref[...]
        rh = norm_back(du, hat, scale_ref[...], vec_ref[0:1, :]).astype(BF16)
        rh_ref[pl.ds(pl.multiple_of(step * group * L1, group * L1), group * L1), :] = rh
        sums_ref[0:8, :] += rows_of_eight(du * hat)
        sums_ref[8:16, :] += rows_of_eight(du)
        real = product(rh, wide_ref[:D, :]).astype(BF16)
        imag = product(rh, wide_ref[D:, :]).astype(BF16)
        for j in range(group):
            spec_ref[j, :L1, :] = real[j * L1 : (j + 1) * L1]
            spec_ref[j, L1:, :] = imag[j * L1 : (j + 1) * L1]
            turned = product(pair_ref[...], spec_ref[j]).astype(BF16).astype(F32)
            for b in range(2):
                for part in range(2):
                    start = (b * 2 + part) * L2
                    spot = part * L1 + b * L2 + step * group + j
                    scatter(middle, spot, turned[start : start + L2])

    @pl.when(step >= steps)
    def _():
        def second(i, carry):
            m = (step - steps) * group + i
            turned = gather(middle, m)
            real, imag = turned[:L1], turned[L1:]
            cosine, sine = lanes(cos_ref[m]), lanes(sin_ref[m])
            back = jnp.concatenate(
                [
                    (real * cosine + imag * sine).astype(BF16),
                    (imag * cosine - real * sine).astype(BF16),
                ],
                axis=0,
            )
            rh = rh_ref[pl.ds(pl.multiple_of(m * L1, L1), L1), :].astype(F32)
            dx = rh + product(short_ref[...], back)
            spots = L2 * lax.broadcasted_iota(jnp.int32, (L1, D), 0) + m
            dx_ref[i] = jnp.where(spots < length, dx, 0.0).astype(BF16)
            return carry

        lax.fori_loop(0, group, second, 0, unroll=4)


def transform_back(length, du, hat, scale, short, pair, cosine, sine, vec, wide, group=8):
    steps = L2 // group
    rows = lambda width: pl.BlockSpec((group * L1, width), lambda c: (jnp.minimum(c, steps - 1), 0))
    return pl.pallas_call(
        functools.partial(back_kernel, group=group),
        grid=(2 * steps,),
        in_specs=[pl.BlockSpec(memory_space=pltpu.SMEM), rows(D), rows(D), rows(LANES)]
        + [whole_block(values.shape) for values in (short, pair, cosine, sine, vec, wide)],
        out_specs=[
            pl.BlockSpec((group, L1, D), lambda c: (jnp.maximum(c - steps, 0), 0, 0)),
            pl.BlockSpec((16, D), lambda c: (0, 0)),
        ],
        out_shape=[
            jax.ShapeDtypeStruct((L2, L1, D), BF16),
            jax.ShapeDtypeStruct((16, D), F32),
        ],
        scratch_shapes=[pltpu.VMEM((L, D), BF16), pltpu.VMEM((group, 2 * L1, D), BF16)]
        + middle_scratch(),
        compiler_params=params(),
        cost_estimate=cost(7 << 30, 0, 20 << 20),
        name="transform_back",
    )(length, du, hat, scale, short, pair, cosine, sine, vec, wide)


def fetch_weights(pieces, holder, sems, chunk):
    rows = holder.shape[0] // len(pieces)
    step = pl.program_id(0)
    copies = [
        pltpu.make_async_copy(
            piece.at[pl.ds(0, rows), :], holder.at[pl.ds(i * rows, rows), :], sems.at[i]
        )
        for i, piece in enumerate(pieces)
    ]

    @pl.when(step == 0)
    def _():
        for copy in copies:
            copy.start()

    for number in range(holder.shape[0] // chunk):
        needed = [copy for i, copy in enumerate(copies) if i * rows // chunk == number]
        if needed:

            @pl.when(step == number)
            def _():
                for copy in needed:
                    copy.wait()


def forward_kernel(*refs, tile, counts, chunk):
    first_hat_ref, b_ref, vec_ref = refs[:3]
    split = 3 + sum(counts)
    firsts, seconds = refs[3 : 3 + counts[0]], refs[3 + counts[0] : split]
    act_ref, slope_ref, out_far, hat_far, scale_far, u_far = refs[split : split + 6]
    y_ref, w1_ref, w2_ref, out_ref, hat_ref, scale_ref, u_ref, sem1, sem2, sem3 = refs[split + 6 :]
    parts = 4
    part = u_ref.shape[0] // parts
    tiles = u_ref.shape[0] // tile
    loads, stores = [], []
    for i in range(parts):
        rows = pl.ds(i * part, part)
        pairs = ((u_ref, u_far), (out_ref, out_far), (hat_ref, hat_far), (scale_ref, scale_far))
        loads.append(
            pltpu.make_async_copy(first_hat_ref.at[rows, :], y_ref.at[rows, :], sem3.at[i, 0])
        )
        stores.append(
            [
                pltpu.make_async_copy(near.at[rows, :], far.at[rows, :], sem3.at[i, 1 + j])
                for j, (near, far) in enumerate(pairs)
            ]
        )

    @pl.when(pl.program_id(0) == 0)
    def _():
        for load in loads:
            load.start()

    fetch_weights(firsts, w1_ref, sem1, chunk)
    fetch_weights(seconds, w2_ref, sem2, chunk)
    here = pl.ds(pl.multiple_of(pl.program_id(0) * chunk, chunk), chunk)

    @pl.when(pl.program_id(0) == 0)
    def _():
        small = 256

        def begin(i, carry):
            rows = pl.ds(pl.multiple_of(i * small, small), small)
            u = y_ref[rows, :] * vec_ref[2:3, :] + vec_ref[3:4, :]
            u_ref[rows, :] = u.astype(BF16)
            y_ref[rows, :] = u + vec_ref[4:5, :]
            return carry

        for i in range(parts):
            loads[i].wait()
            lax.fori_loop(i * part // small, (i + 1) * part // small, begin, 0)
            stores[i][0].start()


    def step(i, carry):
        rows = pl.ds(pl.multiple_of(i * tile, tile), tile)
        z = product_turned(u_ref[rows, :], w1_ref[here, :]) + b_ref[...]
        square = z * z
        t = jnp.tanh(z * (ROOT_TWO_PI + CUBIC * square))
        half = 0.5 + 0.5 * t
        a = z * half
        low = a.astype(BF16)
        act_ref[rows, :] = low
        slope = half + (a - a * t) * (ROOT_TWO_PI + (3.0 * CUBIC) * square)
        slope_ref[rows, :] = slope.astype(BF16)
        y_ref[rows, :] += product(low, w2_ref[here, :])
        return carry

    lax.fori_loop(0, tiles, step, 0)

    @pl.when(pl.program_id(0) == pl.num_programs(0) - 1)
    def _():
        small = 256

        def finish(i, carry):
            rows = pl.ds(pl.multiple_of(i * small, small), small)
            y = y_ref[rows, :]
            center = y - average(y)
            scale = lax.rsqrt(average(center * center) + EPSILON)
            hat = center * scale
            out_ref[rows, :] = (hat * vec_ref[0:1, :] + vec_ref[1:2, :]).astype(BF16)
            hat_ref[rows, :] = hat.astype(BF16)
            scale_ref[rows, :] = jnp.broadcast_to(scale, (small, LANES))
            return carry

        for i in range(parts):
            lax.fori_loop(i * part // small, (i + 1) * part // small, finish, 0)
            for copy in stores[i][1:]:
                copy.start()
        for store in stores:
            for copy in store:
                copy.wait()


def feed_forward(hat, b, vec, firsts, seconds, chunk=1024, tile=1024):
    tokens, width = hat.shape
    counts = (len(firsts), len(seconds))
    units = b.shape[1]
    acts = lambda: pl.BlockSpec((tokens, chunk), lambda c: (0, c))
    return pl.pallas_call(
        functools.partial(forward_kernel, tile=tile, counts=counts, chunk=chunk),
        grid=(units // chunk,),
        in_specs=[
            FAR,
            pl.BlockSpec((1, chunk), lambda c: (0, c)),
            whole_block(vec.shape),
        ]
        + [FAR] * sum(counts),
        out_specs=[acts(), acts()] + [FAR] * 4,
        out_shape=[
            jax.ShapeDtypeStruct((tokens, units), BF16),
            jax.ShapeDtypeStruct((tokens, units), BF16),
            jax.ShapeDtypeStruct((tokens, width), BF16),
            jax.ShapeDtypeStruct((tokens, width), BF16),
            jax.ShapeDtypeStruct((tokens, LANES), F32),
            jax.ShapeDtypeStruct((tokens, width), BF16),
        ],
        scratch_shapes=[
            pltpu.VMEM((tokens, width), F32),
            pltpu.VMEM((units, width), BF16),
            pltpu.VMEM((units, width), BF16),
            pltpu.VMEM((tokens, width), BF16),
            pltpu.VMEM((tokens, width), BF16),
            pltpu.VMEM((tokens, LANES), F32),
            pltpu.VMEM((tokens, width), BF16),
            pltpu.SemaphoreType.DMA((counts[0],)),
            pltpu.SemaphoreType.DMA((counts[1],)),
            pltpu.SemaphoreType.DMA((4, 5)),
        ],
        compiler_params=params(),
        cost_estimate=cost(4 * tokens * units * width, tokens * units, 50 << 20),
        name="feed_forward",
    )(hat, b, vec, *firsts, *seconds)


def backward_kernel(*refs, tile, counts, chunk):
    g_far, hat_far, scale_far, u_far, vec_ref, act_ref, slope_ref = refs[:7]
    split = 7 + sum(counts)
    firsts, seconds = refs[7 : 7 + counts[0]], refs[7 + counts[0] : split]
    keep1_ref, keep2_ref, send1_ref, send2_ref, db_ref, du_far, sums_ref = refs[split : split + 7]
    e_ref, w1_ref, w2_ref, f_ref, g_ref, hat_ref, scale_ref, u_ref, du_ref = refs[
        split + 7 : split + 16
    ]
    sem1, sem2, sem3, sem4 = refs[split + 16 :]
    parts = 4
    part = u_ref.shape[0] // parts
    loads = []
    for i in range(parts):
        rows = pl.ds(i * part, part)
        loads.append(
            [
                pltpu.make_async_copy(far.at[rows, :], near.at[rows, :], sem3.at[i, j])
                for j, (far, near) in enumerate(
                    ((g_far, g_ref), (hat_far, hat_ref), (scale_far, scale_ref))
                )
            ]
        )
    load_u = pltpu.make_async_copy(u_far, u_ref, sem4.at[0])
    store_du = pltpu.make_async_copy(du_ref, du_far, sem4.at[1])

    @pl.when(pl.program_id(0) == 0)
    def _():
        for load in loads:
            for copy in load:
                copy.start()

    fetch_weights(seconds, w2_ref, sem2, chunk)
    fetch_weights(firsts, w1_ref, sem1, chunk)
    here = pl.ds(pl.multiple_of(pl.program_id(0) * chunk, chunk), chunk)

    @pl.when(pl.program_id(0) == 0)
    def _():
        small = 256
        sums_ref[...] = jnp.zeros_like(sums_ref)

        def begin(i, carry):
            rows = pl.ds(pl.multiple_of(i * small, small), small)
            g = g_ref[rows, :].astype(F32)
            hat = hat_ref[rows, :].astype(F32)
            dy = norm_back(g, hat, scale_ref[rows, :], vec_ref[0:1, :])
            du_ref[rows, :] = dy
            e_ref[rows, :] = dy.astype(BF16)
            sums_ref[0:8, :] += rows_of_eight(dy)
            sums_ref[8:16, :] += rows_of_eight(g * hat)
            sums_ref[16:24, :] += rows_of_eight(g)
            return carry

        load_u.start()
        for i in range(parts):
            for copy in loads[i]:
                copy.wait()
            lax.fori_loop(i * part // small, (i + 1) * part // small, begin, 0)
        load_u.wait()


    def step(i, db):
        rows = pl.ds(pl.multiple_of(i * tile, tile), tile)
        dz = product_turned(e_ref[rows, :], w2_ref[here, :]) * slope_ref[rows, :].astype(F32)
        low = dz.astype(BF16)
        f_ref[rows, :] = low
        du_ref[rows, :] += product(low, w1_ref[here, :])
        return db + rows_of_eight(dz)

    db = lax.fori_loop(0, u_ref.shape[0] // tile, step, jnp.zeros((8, chunk), F32))
    db_ref[...] = jnp.sum(db, axis=0, keepdims=True)

    @pl.when(pl.program_id(0) == pl.num_programs(0) - 1)
    def _():
        store_du.start()

    dw2 = product_over_rows(act_ref[...], e_ref[...]).astype(BF16)
    dw1 = product_over_rows(f_ref[...], u_ref[...]).astype(BF16)
    half = pl.num_programs(0) // 2

    @pl.when(pl.program_id(0) < half)
    def _():
        keep1_ref[...] = dw1
        keep2_ref[...] = dw2

    @pl.when(pl.program_id(0) >= half)
    def _():
        send1_ref[...] = dw1
        send2_ref[...] = dw2

    @pl.when(pl.program_id(0) == pl.num_programs(0) - 1)
    def _():
        store_du.wait()


def feed_backward(g, hat, scale, vec, u, act, slope, firsts, seconds, chunk=512, tile=2048):
    tokens, width = u.shape
    counts = (len(firsts), len(seconds))
    units = act.shape[1]
    half = units // chunk // 2
    acts = lambda: pl.BlockSpec((tokens, chunk), lambda c: (0, c))
    keep = lambda: pl.BlockSpec((chunk, width), lambda c: (jnp.minimum(c, half - 1), 0))
    send = lambda: pl.BlockSpec((chunk, width), lambda c: (jnp.maximum(c - half, 0), 0))
    grads = jax.ShapeDtypeStruct((units // 2, width), BF16)
    return pl.pallas_call(
        functools.partial(backward_kernel, tile=tile, counts=counts, chunk=chunk),
        grid=(units // chunk,),
        in_specs=[FAR] * 4
        + [whole_block(vec.shape), acts(), acts()]
        + [FAR] * sum(counts),
        out_specs=[
            keep(),
            keep(),
            send(),
            send(),
            pl.BlockSpec((1, chunk), lambda c: (0, c)),
            FAR,
            whole_block((24, width)),
        ],
        out_shape=[grads] * 4
        + [
            jax.ShapeDtypeStruct((1, units), F32),
            jax.ShapeDtypeStruct((tokens, width), F32),
            jax.ShapeDtypeStruct((24, width), F32),
        ],
        scratch_shapes=[
            pltpu.VMEM((tokens, width), BF16),
            pltpu.VMEM((units, width), BF16),
            pltpu.VMEM((units, width), BF16),
            pltpu.VMEM((tokens, chunk), BF16),
            pltpu.VMEM((tokens, width), BF16),
            pltpu.VMEM((tokens, width), BF16),
            pltpu.VMEM((tokens, LANES), F32),
            pltpu.VMEM((tokens, width), BF16),
            pltpu.VMEM((tokens, width), F32),
            pltpu.SemaphoreType.DMA((counts[0],)),
            pltpu.SemaphoreType.DMA((counts[1],)),
            pltpu.SemaphoreType.DMA((4, 3)),
            pltpu.SemaphoreType.DMA((2,)),
        ],
        compiler_params=params(),
        cost_estimate=cost(8 * tokens * units * width, 0, 60 << 20),
        name="feed_backward",
    )(g, hat, scale, u, vec, act, slope, *firsts, *seconds)


def table_pair(points):
    numbers = jnp.arange(points, dtype=jnp.int32)
    coarse = 32 * jnp.arange(points // 32, dtype=jnp.int32)
    fine = jnp.arange(32, dtype=jnp.int32)

    def waves(rows):
        angles = (rows[:, None] * numbers[None, :] % points).astype(F32) * (2.0 * math.pi / points)
        return jnp.cos(angles), jnp.sin(angles)

    factor = 1.0 / math.sqrt(points)
    if points <= 64:
        cosine, sine = waves(numbers)
    else:
        coarse_cos, coarse_sin = waves(coarse)
        fine_cos, fine_sin = waves(fine)
        coarse_cos, coarse_sin, fine_cos, fine_sin = lax.optimization_barrier(
            (coarse_cos, coarse_sin, fine_cos, fine_sin)
        )
        coarse_cos, coarse_sin = coarse_cos[:, None], coarse_sin[:, None]
        fine_cos, fine_sin = fine_cos[None], fine_sin[None]
        cosine = (coarse_cos * fine_cos - coarse_sin * fine_sin).reshape(points, points)
        sine = (coarse_sin * fine_cos + coarse_cos * fine_sin).reshape(points, points)
    return (cosine * factor).astype(BF16), (sine * factor).astype(BF16)


def twiddles():
    row_index = jnp.arange(L1, dtype=jnp.int32)[None, :]
    col_index = jnp.arange(L2, dtype=jnp.int32)[:, None]
    angles = (row_index * col_index % L).astype(F32) * (2.0 * math.pi / L)
    wave = jnp.cos(angles), jnp.sin(angles)
    return [jnp.broadcast_to(values[:, :, None], (L2, L1, LANES)) for values in wave]


def swap(values, step):
    axis, mask = step
    size = lax.axis_size(axis)
    return lax.ppermute(values, axis, [(i, i ^ mask) for i in range(size)])


def bits(size):
    masks = []
    mask = size // 2
    while mask >= 1:
        masks.append(mask)
        mask //= 2
    return masks


def widen(held, step):
    return jnp.concatenate([held, swap(held, step)], axis=0)


def widen_codes(codes, steps, groups):
    for axis, mask in steps:
        code = mask if axis == "seq" else mask * groups
        codes = codes + [held ^ code for held in codes]
    return codes


def spread(pieces, steps):
    for step in steps:
        pieces = pieces + [swap(piece, step) for piece in pieces]
    return pieces


def spread_core(pieces, step_core):
    return pieces + [swap(piece, step_core) for piece in pieces]


def pick(addend, extra):
    values, names, fixed = addend
    chosen = {**fixed, **extra}
    return values[tuple(chosen.get(name, slice(None)) for name in names)]


def total(addends, extra={}):
    parts = [pick(addend, extra) for addend in addends]
    return sum(parts[1:], parts[0].astype(F32))


def settle(addends, send, step):
    values, names, fixed = addends[-1]
    rest = [name for name in names if name not in fixed and name != step]
    kept = [(held, order, {**gone, step: 0}) for held, order, gone in addends]
    return kept + [(swap(send, step), rest, {})]


def fold(addends, step, kind):
    return settle(addends, total(addends, {step: 1}).astype(kind), step)


def after(addends, *others):
    values, names, fixed = addends[-1]
    results = lax.optimization_barrier((values,) + others)
    return (addends[:-1] + [(results[0], names, fixed)],) + tuple(results[1:])


def arrange(rows):
    return with_layout_constraint(rows.transpose(0, 2, 1, 3), Layout(major_to_minor=(0, 1, 2, 3)))


def exchange(rows):
    order = Layout(major_to_minor=(0, 1, 2, 3))
    rows = with_layout_constraint(rows, order)
    rows = lax.all_to_all(rows, "seq", split_axis=0, concat_axis=0, tiled=True)
    return with_layout_constraint(rows, order)


def body(tokens, lengths, labels, picked, cotangent, w_in, b_in, w_out, shifts, norm_gains):
    groups = lax.axis_size("seq")
    me = lax.axis_index("seq")
    here = lax.axis_index("batch") * groups + me
    columns = tokens.shape[2]
    share = w_in.shape[2]
    part = shifts.shape[2]
    blocks = groups * lax.axis_size("batch")

    masks = bits(groups)[:-1]
    steps_plane = [("seq", mask) for mask in masks[:1] + masks[:0:-1]]
    steps_seq = [("seq", mask) for mask in masks[::-1]]
    steps_batch = [("batch", mask) for mask in bits(lax.axis_size("batch"))]
    step_core = ("seq", 1)
    numbers = jnp.arange(blocks, dtype=jnp.int32)

    codes = widen_codes([0], steps_plane + steps_batch + [step_core], groups)
    owner = jnp.array(codes, dtype=jnp.int32) ^ here
    one_hot = (owner[:, None] == numbers[None, :]).astype(F32)

    wide_cos, wide_sin = table_pair(D)
    wide = jnp.concatenate([wide_cos, -wide_sin], axis=0)
    twiddle_cos, twiddle_sin = twiddles()
    short_cos, short_sin = table_pair(L1)
    long_cos, long_sin = table_pair(L2)
    short_table = jnp.concatenate([short_cos, short_sin], axis=0)
    long_table = jnp.stack([jnp.stack([long_cos, -long_sin]), jnp.stack([long_sin, long_cos])])
    both = jnp.eye(2, dtype=BF16)
    pair_table = jnp.einsum("qukm,bc->qkbcum", long_table, both).reshape(4 * L2, 4 * L2)

    length = lax.dynamic_slice_in_dim(lengths, me, 1)
    small = jnp.concatenate([b_in[0], shifts[0].reshape(-1), norm_gains[0].reshape(-1)])
    small = small.astype(F32)[None]
    first_held = w_in[0].T[None]
    second_held = w_out[0][None]
    tokens_late = arrange(tokens)
    for number, step in enumerate(steps_plane[:-1]):
        first_held = widen(first_held, step)
        second_held = widen(second_held, step)
        small = widen(small, step)
        if number == 0:
            tokens_late, small, first_held, second_held = lax.optimization_barrier(
                (tokens_late, small, first_held, second_held)
            )
            x_all = exchange(tokens_late)
    early = (wide, twiddle_cos, twiddle_sin, short_table, pair_table, arrange(cotangent))
    small, first_held, second_held, early = lax.optimization_barrier(
        (small, first_held, second_held, early)
    )
    wide, twiddle_cos, twiddle_sin, short_table, pair_table, late_cotangent = early
    first_held = widen(first_held, steps_plane[-1])
    seconds = []
    for piece in spread([second_held], steps_batch):
        seconds += [piece, swap(piece, steps_plane[-1])]
    steps_small = steps_plane[:-1] + steps_batch + [step_core] + steps_plane[-1:]
    small_codes = widen_codes([0], steps_small, groups)
    for step in steps_batch + [step_core]:
        small = widen(small, step)
    small, first_held = lax.optimization_barrier((small, first_held))
    small = widen(small, steps_plane[-1])
    places = jnp.array([small_codes.index(code) for code in codes], dtype=jnp.int32)
    place_hot = (places[:, None] == numbers[None, :]).astype(F32)
    small = jnp.sum(place_hot[:, :, None] * small[None], axis=1)
    b_first = small[:, :share].reshape(1, blocks * share)
    rows = jnp.sum(one_hot[:, :, None] * small[:, None, share:], axis=0)
    rows = rows.reshape(blocks, 5, part).transpose(1, 0, 2).reshape(5, D)
    shifts_f = rows[:3]
    gains_f = rows[3:]
    blank = jnp.zeros((3, D), F32)
    vec = jnp.concatenate(
        [gains_f[1:2], shifts_f[2:3], gains_f[0:1], shifts_f[1:2], shifts_f[0:1], blank]
    )
    vec_one = vec[2:]
    vec_one = jnp.concatenate([vec_one, blank[:2]])
    firsts = spread([first_held], steps_batch)
    x_rows = x_all.reshape(L2, L1, D)
    hat_one, scale_one = transform(
        length, x_rows, short_table, pair_table, twiddle_cos, twiddle_sin, wide
    )
    hat_one, late_cotangent, firsts, seconds, vec, vec_one, b_first = lax.optimization_barrier(
        (hat_one, late_cotangent, firsts, seconds, vec, vec_one, b_first)
    )
    g_all = exchange(late_cotangent)
    flat = lambda pieces: [piece.reshape(-1, D) for piece in spread_core(pieces, step_core)]
    firsts, seconds = flat(firsts), flat(seconds)
    act, slope, layer_out, hat_two, scale_two, u = feed_forward(
        hat_one, b_first, vec, firsts, seconds
    )
    out_rows = exchange(layer_out.reshape(groups, columns, L1, D))

    keep_first, keep_second, send_first, send_second, grad_b_first, grad_u, sums_two = feed_backward(
        g_all.reshape(L, D), hat_two, scale_two, vec, u, act, slope, firsts, seconds
    )
    names = steps_batch[::-1] + steps_plane[::-1]
    shape = (2,) * len(names) + (share,)
    grad_x, sums_one = transform_back(
        length, grad_u, hat_one, scale_one, short_table.T, pair_table.T,
        twiddle_cos, twiddle_sin, vec_one, wide
    )
    grad_x, send_first, send_second, out_rows = lax.optimization_barrier(
        (grad_x, send_first, send_second, out_rows)
    )
    came_first = swap(send_first, step_core)
    came_second = swap(send_second, step_core)
    grad_first, grad_second = [
        [(values.reshape(shape + (D,)), names, {}) for values in pair]
        for pair in ((keep_first, came_first), (keep_second, came_second))
    ]
    grad_x = grad_x.reshape(groups, columns, L1, D)
    input_grad = arrange(exchange(grad_x))

    shift_of = jnp.arange(columns, dtype=jnp.int32) + me * columns
    place_of = L2 * jnp.arange(L1, dtype=jnp.int32)[None, :] + shift_of[:, None]
    for step in steps_batch[::-1]:
        grad_first = fold(grad_first, step, BF16)
        grad_second = fold(grad_second, step, BF16)
    grad_first = fold(grad_first, steps_seq[0], BF16)
    grad_first, out_rows, sums_one, sums_two, grad_b_first = after(
        grad_first, out_rows, sums_one, sums_two, grad_b_first
    )
    logits = out_rows.astype(F32)
    highest = jnp.max(logits, axis=-1, keepdims=True)
    powers = jnp.exp(logits - highest)
    denominator = jnp.sum(powers, axis=-1)
    features = jnp.arange(D, dtype=jnp.int32)
    label_rows = labels.transpose(0, 2, 1)
    top = jnp.sum(jnp.where(features == label_rows[..., None], powers, 0.0), axis=-1)
    counted = (picked.transpose(0, 2, 1) > 0) & (place_of[None] < lengths[:, None, None])
    weight = jnp.where(counted, 1.0, 0.0)
    sums = jnp.stack([jnp.sum(weight * (top / denominator)), jnp.sum(weight)])

    sums_two = jnp.sum(sums_two.reshape(3, 8, D), axis=1)
    sums_one = jnp.sum(sums_one.reshape(2, 8, D), axis=1)
    norms = jnp.stack([sums_two[0], sums_one[1], sums_two[2], sums_one[0], sums_two[1]])
    norms = norms.reshape(5, blocks, part).transpose(1, 0, 2).reshape(blocks, 5 * part)
    norms = jnp.sum(one_hot[:, :, None] * norms[None], axis=1)
    sums = jnp.broadcast_to(sums[None], (blocks, 2))
    small_grads = jnp.concatenate([grad_b_first.reshape(blocks, share), norms, sums], axis=1)
    half = blocks // 2
    arrived = swap(small_grads[half:], step_core)
    small = [
        (values.reshape(shape[:-1] + (-1,)), names, {}) for values in (small_grads[:half], arrived)
    ]
    for step in steps_batch[::-1]:
        small = fold(small, step, F32)
    small, out_rows = after(small, out_rows)
    for step in steps_seq[1:]:
        grad_first = fold(grad_first, step, BF16)
    grad_second = fold(grad_second, steps_seq[0], BF16)
    for number, step in enumerate(steps_seq[1:]):
        small, latest = after(small, grad_second[-1][0])
        grad_second = grad_second[:-1] + [(latest,) + grad_second[-1][1:]]
        if step == steps_seq[-1]:
            small, input_grad = after(small, input_grad)
        small = fold(small, steps_seq[number], F32)
        grad_second = fold(grad_second, step, BF16)
    small = fold(small, steps_seq[-1], F32)
    current = out_rows.transpose(0, 2, 1, 3)
    small_grads, grad_first, grad_second = total(small), total(grad_first), total(grad_second)
    norms = small_grads[share:-2].reshape(5, part)
    match_rate = D * small_grads[-2] / jnp.maximum(small_grads[-1], 1.0)
    return (
        current,
        input_grad,
        grad_first.T[None],
        small_grads[:share][None],
        grad_second[None],
        norms[:3][None],
        norms[3:][None],
        match_rate,
    )


def solution(mesh):
    in_specs = (
        P("batch", None, "seq", None),
        P("batch"),
        P("batch", None, "seq"),
        P("batch", None, "seq"),
        P("batch", None, "seq", None),
        P(None, None, ("batch", "seq")),
        P(None, ("batch", "seq")),
        P(None, ("batch", "seq"), None),
        P(None, None, ("batch", "seq")),
        P(None, None, ("batch", "seq")),
    )
    out_specs = (
        P("batch", None, "seq", None),
        P("batch", None, "seq", None),
        P(None, None, ("batch", "seq")),
        P(None, ("batch", "seq")),
        P(None, ("batch", "seq"), None),
        P(None, None, ("batch", "seq")),
        P(None, None, ("batch", "seq")),
        P(),
    )
    return jax.shard_map(body, mesh=mesh, in_specs=in_specs, out_specs=out_specs, check_vma=False)
```

```python
import functools
import math

import jax
import jax.numpy as jnp
from jax import lax
from jax.experimental import pallas as pl
from jax.experimental.layout import Layout, with_layout_constraint
from jax.experimental.pallas import tpu as pltpu
from jax.sharding import PartitionSpec as P

D = 768
L1 = 64
L2 = 32
L = 2048
LANES = 128
PAIR = 4 * L2
STRIDE = PAIR + 1

EPSILON = 1e-12
ROOT_TWO_PI = 0.7978845608028654
CUBIC = ROOT_TWO_PI * 0.044715
F32 = jnp.float32
BF16 = jnp.bfloat16
VMEM_BYTES = 60 << 20
FAR = pl.BlockSpec(memory_space=pl.ANY)


def product(left, right):
    return lax.dot_general(left, right, (((1,), (0,)), ((), ())), preferred_element_type=F32)


def product_turned(left, right):
    return lax.dot_general(left, right, (((1,), (1,)), ((), ())), preferred_element_type=F32)


def product_over_rows(left, right):
    return lax.dot_general(left, right, (((0,), (0,)), ((), ())), preferred_element_type=F32)


def lanes(column):
    return jnp.concatenate([column] * (D // LANES), axis=1)


def rows_of_eight(values):
    return jnp.sum(values.reshape(-1, 8, values.shape[-1]), axis=0)


def average(values):
    return jnp.mean(values, axis=1, keepdims=True)


def norm_back(grad, x_hat, scale, gain):
    q = grad * gain
    return lanes(scale) * (q - average(q) - x_hat * average(q * x_hat))


def whole_block(shape):
    return pl.BlockSpec(shape, lambda c: (0,) * len(shape), pipeline_mode=pl.Buffered(1))


def params():
    return pltpu.CompilerParams(vmem_limit_bytes=VMEM_BYTES)


def cost(flops, transcendentals, size):
    return pl.CostEstimate(flops=flops, transcendentals=transcendentals, bytes_accessed=size)


def scatter(refs, start, value):
    for j, ref in enumerate(refs):
        ref[pl.ds(start, L2, stride=STRIDE), :] = value[:, j * LANES : (j + 1) * LANES]


def gather(refs, block):
    return jnp.concatenate([ref[pl.ds(block * STRIDE, PAIR), :] for ref in refs], axis=1)


def middle_scratch():
    return [pltpu.VMEM((L2 * STRIDE, LANES), F32)] * (D // LANES)


def transform_kernel(
    length_ref, x_ref, short_ref, pair_ref, cos_ref, sin_ref, wide_hbm,
    hat_ref, scale_ref, spec_ref, wide_ref, sem, *middle, group
):
    length = length_ref[0]
    step = pl.program_id(0)
    load = pltpu.make_async_copy(wide_hbm, wide_ref, sem.at[0])

    @pl.when(step == 0)
    def _():
        load.start()

        def first(m, carry):
            spots = L2 * lax.broadcasted_iota(jnp.int32, (L1, D), 0) + m
            x = jnp.where(spots < length, x_ref[m].astype(F32), 0.0).astype(BF16)
            y = product(short_ref[...], x)
            real, imag = y[:L1], y[L1:]
            cosine, sine = lanes(cos_ref[m]), lanes(sin_ref[m])
            turned = (real * cosine - imag * sine, real * sine + imag * cosine)
            for b in range(2):
                for part in range(2):
                    scatter(middle, (b * 2 + part) * L2 + m, turned[part][b * L2 : (b + 1) * L2])
            return carry

        lax.fori_loop(0, L2, first, 0, unroll=4)
        load.wait()

    for j in range(group):
        turned = gather(middle, step * group + j).astype(BF16)
        q = product(pair_ref[...], turned).astype(BF16)
        spec_ref[j * L1 : (j + 1) * L1, :D] = q[:L1]
        spec_ref[j * L1 : (j + 1) * L1, D:] = q[L1:]
    mixed = product(spec_ref[...], wide_ref[...])
    number = lax.broadcasted_iota(jnp.int32, (group * L1, D), 0)
    spots = L2 * (number % L1) + step * group + number // L1
    x = x_ref[pl.ds(step * group, group)].reshape(group * L1, D).astype(F32)
    h = jnp.where(spots < length, x, 0.0) + mixed
    center = h - average(h)
    scale = lax.rsqrt(average(center * center) + EPSILON)
    hat_ref[...] = center * scale
    scale_ref[...] = jnp.broadcast_to(scale, scale_ref.shape)


def transform(length, x, short, pair, cosine, sine, wide, group=8):
    out = lambda width: pl.BlockSpec((group * L1, width), lambda c: (c, 0))
    return pl.pallas_call(
        functools.partial(transform_kernel, group=group),
        grid=(L2 // group,),
        in_specs=[pl.BlockSpec(memory_space=pltpu.SMEM)]
        + [whole_block(values.shape) for values in (x, short, pair, cosine, sine)]
        + [FAR],
        out_specs=[out(D), out(LANES)],
        out_shape=[
            jax.ShapeDtypeStruct((L, D), F32),
            jax.ShapeDtypeStruct((L, LANES), F32),
        ],
        scratch_shapes=[
            pltpu.VMEM((group * L1, 2 * D), BF16),
            pltpu.VMEM((2 * D, D), BF16),
            pltpu.SemaphoreType.DMA((1,)),
        ]
        + middle_scratch(),
        compiler_params=params(),
        cost_estimate=cost(7 << 30, L, 24 << 20),
        name="transform",
    )(length, x, short, pair, cosine, sine, wide)


def back_kernel(
    length_ref, du_ref, hat_ref, scale_ref, short_ref, pair_ref, cos_ref, sin_ref, vec_ref, wide_ref,
    dx_ref, sums_ref, rh_ref, spec_ref, *middle, group
):
    length = length_ref[0]
    step = pl.program_id(0)
    steps = L2 // group

    @pl.when(step == 0)
    def _():
        sums_ref[...] = jnp.zeros_like(sums_ref)

    @pl.when(step < steps)
    def _():
        du = du_ref[...]
        hat = hat_ref[...]
        rh = norm_back(du, hat, scale_ref[...], vec_ref[0:1, :]).astype(BF16)
        rh_ref[pl.ds(pl.multiple_of(step * group * L1, group * L1), group * L1), :] = rh
        sums_ref[0:8, :] += rows_of_eight(du * hat)
        sums_ref[8:16, :] += rows_of_eight(du)
        real = product(rh, wide_ref[:D, :]).astype(BF16)
        imag = product(rh, wide_ref[D:, :]).astype(BF16)
        for j in range(group):
            spec_ref[j, :L1, :] = real[j * L1 : (j + 1) * L1]
            spec_ref[j, L1:, :] = imag[j * L1 : (j + 1) * L1]
            turned = product(pair_ref[...], spec_ref[j]).astype(BF16).astype(F32)
            for b in range(2):
                for part in range(2):
                    start = (b * 2 + part) * L2
                    spot = part * L1 + b * L2 + step * group + j
                    scatter(middle, spot, turned[start : start + L2])

    @pl.when(step >= steps)
    def _():
        def second(i, carry):
            m = (step - steps) * group + i
            turned = gather(middle, m)
            real, imag = turned[:L1], turned[L1:]
            cosine, sine = lanes(cos_ref[m]), lanes(sin_ref[m])
            back = jnp.concatenate(
                [
                    (real * cosine + imag * sine).astype(BF16),
                    (imag * cosine - real * sine).astype(BF16),
                ],
                axis=0,
            )
            rh = rh_ref[pl.ds(pl.multiple_of(m * L1, L1), L1), :].astype(F32)
            dx = rh + product(short_ref[...], back)
            spots = L2 * lax.broadcasted_iota(jnp.int32, (L1, D), 0) + m
            dx_ref[i] = jnp.where(spots < length, dx, 0.0).astype(BF16)
            return carry

        lax.fori_loop(0, group, second, 0, unroll=4)


def transform_back(length, du, hat, scale, short, pair, cosine, sine, vec, wide, group=8):
    steps = L2 // group
    rows = lambda width: pl.BlockSpec((group * L1, width), lambda c: (jnp.minimum(c, steps - 1), 0))
    return pl.pallas_call(
        functools.partial(back_kernel, group=group),
        grid=(2 * steps,),
        in_specs=[pl.BlockSpec(memory_space=pltpu.SMEM), rows(D), rows(D), rows(LANES)]
        + [whole_block(values.shape) for values in (short, pair, cosine, sine, vec, wide)],
        out_specs=[
            pl.BlockSpec((group, L1, D), lambda c: (jnp.maximum(c - steps, 0), 0, 0)),
            pl.BlockSpec((16, D), lambda c: (0, 0)),
        ],
        out_shape=[
            jax.ShapeDtypeStruct((L2, L1, D), BF16),
            jax.ShapeDtypeStruct((16, D), F32),
        ],
        scratch_shapes=[pltpu.VMEM((L, D), BF16), pltpu.VMEM((group, 2 * L1, D), BF16)]
        + middle_scratch(),
        compiler_params=params(),
        cost_estimate=cost(7 << 30, 0, 20 << 20),
        name="transform_back",
    )(length, du, hat, scale, short, pair, cosine, sine, vec, wide)


def fetch_weights(pieces, holder, sems, chunk):
    rows = holder.shape[0] // len(pieces)
    step = pl.program_id(0)
    copies = [
        pltpu.make_async_copy(
            piece.at[pl.ds(0, rows), :], holder.at[pl.ds(i * rows, rows), :], sems.at[i]
        )
        for i, piece in enumerate(pieces)
    ]

    @pl.when(step == 0)
    def _():
        for copy in copies:
            copy.start()

    for number in range(holder.shape[0] // chunk):
        needed = [copy for i, copy in enumerate(copies) if i * rows // chunk == number]
        if needed:

            @pl.when(step == number)
            def _():
                for copy in needed:
                    copy.wait()


def forward_kernel(*refs, tile, counts, chunk):
    first_hat_ref, b_ref, vec_ref = refs[:3]
    split = 3 + sum(counts)
    firsts, seconds = refs[3 : 3 + counts[0]], refs[3 + counts[0] : split]
    act_ref, slope_ref, out_far, hat_far, scale_far, u_far = refs[split : split + 6]
    y_ref, w1_ref, w2_ref, out_ref, hat_ref, scale_ref, u_ref, sem1, sem2, sem3 = refs[split + 6 :]
    parts = 4
    part = u_ref.shape[0] // parts
    tiles = u_ref.shape[0] // tile
    loads, stores = [], []
    for i in range(parts):
        rows = pl.ds(i * part, part)
        pairs = ((u_ref, u_far), (out_ref, out_far), (hat_ref, hat_far), (scale_ref, scale_far))
        loads.append(
            pltpu.make_async_copy(first_hat_ref.at[rows, :], y_ref.at[rows, :], sem3.at[i, 0])
        )
        stores.append(
            [
                pltpu.make_async_copy(near.at[rows, :], far.at[rows, :], sem3.at[i, 1 + j])
                for j, (near, far) in enumerate(pairs)
            ]
        )

    @pl.when(pl.program_id(0) == 0)
    def _():
        for load in loads:
            load.start()

    fetch_weights(firsts, w1_ref, sem1, chunk)
    fetch_weights(seconds, w2_ref, sem2, chunk)
    here = pl.ds(pl.multiple_of(pl.program_id(0) * chunk, chunk), chunk)

    @pl.when(pl.program_id(0) == 0)
    def _():
        small = 256

        def begin(i, carry):
            rows = pl.ds(pl.multiple_of(i * small, small), small)
            u = y_ref[rows, :] * vec_ref[2:3, :] + vec_ref[3:4, :]
            u_ref[rows, :] = u.astype(BF16)
            y_ref[rows, :] = u + vec_ref[4:5, :]
            return carry

        for i in range(parts):
            loads[i].wait()
            lax.fori_loop(i * part // small, (i + 1) * part // small, begin, 0)
            stores[i][0].start()


    def step(i, carry):
        rows = pl.ds(pl.multiple_of(i * tile, tile), tile)
        z = product_turned(u_ref[rows, :], w1_ref[here, :]) + b_ref[...]
        square = z * z
        t = jnp.tanh(z * (ROOT_TWO_PI + CUBIC * square))
        half = 0.5 + 0.5 * t
        a = z * half
        low = a.astype(BF16)
        act_ref[rows, :] = low
        slope = half + (a - a * t) * (ROOT_TWO_PI + (3.0 * CUBIC) * square)
        slope_ref[rows, :] = slope.astype(BF16)
        y_ref[rows, :] += product(low, w2_ref[here, :])
        return carry

    lax.fori_loop(0, tiles, step, 0)

    @pl.when(pl.program_id(0) == pl.num_programs(0) - 1)
    def _():
        small = 256

        def finish(i, carry):
            rows = pl.ds(pl.multiple_of(i * small, small), small)
            y = y_ref[rows, :]
            center = y - average(y)
            scale = lax.rsqrt(average(center * center) + EPSILON)
            hat = center * scale
            out_ref[rows, :] = (hat * vec_ref[0:1, :] + vec_ref[1:2, :]).astype(BF16)
            hat_ref[rows, :] = hat.astype(BF16)
            scale_ref[rows, :] = jnp.broadcast_to(scale, (small, LANES))
            return carry

        for i in range(parts):
            lax.fori_loop(i * part // small, (i + 1) * part // small, finish, 0)
            for copy in stores[i][1:]:
                copy.start()
        for store in stores:
            for copy in store:
                copy.wait()


def feed_forward(hat, b, vec, firsts, seconds, chunk=1024, tile=1024):
    tokens, width = hat.shape
    counts = (len(firsts), len(seconds))
    units = b.shape[1]
    acts = lambda: pl.BlockSpec((tokens, chunk), lambda c: (0, c))
    return pl.pallas_call(
        functools.partial(forward_kernel, tile=tile, counts=counts, chunk=chunk),
        grid=(units // chunk,),
        in_specs=[
            FAR,
            pl.BlockSpec((1, chunk), lambda c: (0, c)),
            whole_block(vec.shape),
        ]
        + [FAR] * sum(counts),
        out_specs=[acts(), acts()] + [FAR] * 4,
        out_shape=[
            jax.ShapeDtypeStruct((tokens, units), BF16),
            jax.ShapeDtypeStruct((tokens, units), BF16),
            jax.ShapeDtypeStruct((tokens, width), BF16),
            jax.ShapeDtypeStruct((tokens, width), BF16),
            jax.ShapeDtypeStruct((tokens, LANES), F32),
            jax.ShapeDtypeStruct((tokens, width), BF16),
        ],
        scratch_shapes=[
            pltpu.VMEM((tokens, width), F32),
            pltpu.VMEM((units, width), BF16),
            pltpu.VMEM((units, width), BF16),
            pltpu.VMEM((tokens, width), BF16),
            pltpu.VMEM((tokens, width), BF16),
            pltpu.VMEM((tokens, LANES), F32),
            pltpu.VMEM((tokens, width), BF16),
            pltpu.SemaphoreType.DMA((counts[0],)),
            pltpu.SemaphoreType.DMA((counts[1],)),
            pltpu.SemaphoreType.DMA((4, 5)),
        ],
        compiler_params=params(),
        cost_estimate=cost(4 * tokens * units * width, tokens * units, 50 << 20),
        name="feed_forward",
    )(hat, b, vec, *firsts, *seconds)


def backward_kernel(*refs, tile, counts, chunk, opening):
    inputs = 7 if opening else 5
    split = inputs + sum(counts)
    firsts, seconds = refs[inputs : inputs + counts[0]], refs[inputs + counts[0] : split]
    keep1_ref, keep2_ref, send1_ref, send2_ref, db_ref, du_far = refs[split : split + 6]
    rest = refs[split + 6 :]
    if opening:
        g_far, hat_far, scale_far, u_far, vec_ref, act_ref, slope_ref = refs[:7]
        e_far, sums_ref = rest[:2]
        rest = rest[2:]
    else:
        e_far, base_far, u_far, act_ref, slope_ref = refs[:5]
    e_ref, w1_ref, w2_ref, f_ref, u_ref, du_ref, sem1, sem2, sem3, sem4 = rest[:10]
    parts = 4
    part = u_ref.shape[0] // parts
    step = pl.program_id(0)
    load_u = pltpu.make_async_copy(u_far, u_ref, sem4.at[0])
    store_du = pltpu.make_async_copy(du_ref, du_far, sem4.at[1])
    if opening:
        scale_ref = rest[10]
        pairs = ((g_far, e_ref), (hat_far, f_ref), (scale_far, scale_ref))
        store_e = pltpu.make_async_copy(e_ref, e_far, sem4.at[2])
    else:
        pairs = ((e_far, e_ref), (base_far, du_ref))
    loads = []
    for i in range(parts):
        rows = pl.ds(i * part, part)
        loads.append(
            [
                pltpu.make_async_copy(far.at[rows, :], near.at[rows, :], sem3.at[i, j])
                for j, (far, near) in enumerate(pairs)
            ]
        )

    @pl.when(step == 0)
    def _():
        for load in loads:
            for copy in load:
                copy.start()

    fetch_weights(seconds, w2_ref, sem2, chunk)
    fetch_weights(firsts, w1_ref, sem1, chunk)
    here = pl.ds(pl.multiple_of(step * chunk, chunk), chunk)

    @pl.when(step == 0)
    def _():
        load_u.start()
        if opening:
            sums_ref[...] = jnp.zeros_like(sums_ref)
        small = 256

        def begin(i, carry):
            rows = pl.ds(pl.multiple_of(i * small, small), small)
            g = e_ref[rows, :].astype(F32)
            hat = f_ref[rows, :].astype(F32)
            dy = norm_back(g, hat, scale_ref[rows, :], vec_ref[0:1, :])
            du_ref[rows, :] = dy
            e_ref[rows, :] = dy.astype(BF16)
            sums_ref[0:8, :] += rows_of_eight(dy)
            sums_ref[8:16, :] += rows_of_eight(g * hat)
            sums_ref[16:24, :] += rows_of_eight(g)
            return carry

        for i in range(parts):
            for copy in loads[i]:
                copy.wait()
            if opening:
                lax.fori_loop(i * part // small, (i + 1) * part // small, begin, 0)
        load_u.wait()
        if opening:
            store_e.start()

    def run(i, db):
        rows = pl.ds(pl.multiple_of(i * tile, tile), tile)
        dz = product_turned(e_ref[rows, :], w2_ref[here, :]) * slope_ref[rows, :].astype(F32)
        low = dz.astype(BF16)
        f_ref[rows, :] = low
        du_ref[rows, :] += product(low, w1_ref[here, :])
        return db + rows_of_eight(dz)

    db = lax.fori_loop(0, u_ref.shape[0] // tile, run, jnp.zeros((8, chunk), F32))
    db_ref[...] = jnp.sum(db, axis=0, keepdims=True)
    last = step == pl.num_programs(0) - 1

    @pl.when(last)
    def _():
        store_du.start()

    dw2 = product_over_rows(act_ref[...], e_ref[...]).astype(BF16)
    dw1 = product_over_rows(f_ref[...], u_ref[...]).astype(BF16)
    half = pl.num_programs(0) // 2

    @pl.when(step < half)
    def _():
        keep1_ref[...] = dw1
        keep2_ref[...] = dw2

    @pl.when(step >= half)
    def _():
        send1_ref[...] = dw1
        send2_ref[...] = dw2

    @pl.when(last)
    def _():
        store_du.wait()
        if opening:
            store_e.wait()


def feed_backward(rows_in, u, act, slope, firsts, seconds, start, vec=None, chunk=768, tile=1024):
    tokens, width = u.shape
    opening = vec is not None
    counts = (len(firsts), len(seconds))
    units = act.shape[1] // 2
    first = start // chunk
    half = units // chunk // 2
    acts = lambda: pl.BlockSpec((tokens, chunk), lambda c: (0, c + first))
    keep = lambda: pl.BlockSpec((chunk, width), lambda c: (jnp.minimum(c, half - 1), 0))
    send = lambda: pl.BlockSpec((chunk, width), lambda c: (jnp.maximum(c - half, 0), 0))
    grads = jax.ShapeDtypeStruct((units // 2, width), BF16)
    rows_out = [jax.ShapeDtypeStruct((tokens, width), F32)]
    scratch = [
        pltpu.VMEM((tokens, width), BF16),
        pltpu.VMEM((units, width), BF16),
        pltpu.VMEM((units, width), BF16),
        pltpu.VMEM((tokens, chunk), BF16),
        pltpu.VMEM((tokens, width), BF16),
        pltpu.VMEM((tokens, width), F32),
        pltpu.SemaphoreType.DMA((counts[0],)),
        pltpu.SemaphoreType.DMA((counts[1],)),
        pltpu.SemaphoreType.DMA((4, 3)),
        pltpu.SemaphoreType.DMA((3,)),
    ]
    specs_in, specs_out, more = [FAR] * (len(rows_in) + 1), [FAR], ()
    if opening:
        rows_out += [
            jax.ShapeDtypeStruct((tokens, width), BF16),
            jax.ShapeDtypeStruct((24, width), F32),
        ]
        specs_in += [whole_block(vec.shape)]
        specs_out += [FAR, whole_block((24, width))]
        more = (vec,)
        scratch += [pltpu.VMEM((tokens, LANES), F32)]
    return pl.pallas_call(
        functools.partial(backward_kernel, tile=tile, counts=counts, chunk=chunk, opening=opening),
        grid=(units // chunk,),
        in_specs=specs_in + [acts(), acts()] + [FAR] * sum(counts),
        out_specs=[keep(), keep(), send(), send(), pl.BlockSpec((1, chunk), lambda c: (0, c))]
        + specs_out,
        out_shape=[grads] * 4 + [jax.ShapeDtypeStruct((1, units), F32)] + rows_out,
        scratch_shapes=scratch,
        compiler_params=params(),
        cost_estimate=cost(8 * tokens * units * width, 0, 30 << 20),
        name="feed_backward",
    )(*rows_in, u, *more, act, slope, *firsts, *seconds)


def table_pair(points):
    numbers = jnp.arange(points, dtype=jnp.int32)
    coarse = 32 * jnp.arange(points // 32, dtype=jnp.int32)
    fine = jnp.arange(32, dtype=jnp.int32)

    def waves(rows):
        angles = (rows[:, None] * numbers[None, :] % points).astype(F32) * (2.0 * math.pi / points)
        return jnp.cos(angles), jnp.sin(angles)

    factor = 1.0 / math.sqrt(points)
    if points <= 64:
        cosine, sine = waves(numbers)
    else:
        coarse_cos, coarse_sin = waves(coarse)
        fine_cos, fine_sin = waves(fine)
        coarse_cos, coarse_sin, fine_cos, fine_sin = lax.optimization_barrier(
            (coarse_cos, coarse_sin, fine_cos, fine_sin)
        )
        coarse_cos, coarse_sin = coarse_cos[:, None], coarse_sin[:, None]
        fine_cos, fine_sin = fine_cos[None], fine_sin[None]
        cosine = (coarse_cos * fine_cos - coarse_sin * fine_sin).reshape(points, points)
        sine = (coarse_sin * fine_cos + coarse_cos * fine_sin).reshape(points, points)
    return (cosine * factor).astype(BF16), (sine * factor).astype(BF16)


def twiddles():
    row_index = jnp.arange(L1, dtype=jnp.int32)[None, :]
    col_index = jnp.arange(L2, dtype=jnp.int32)[:, None]
    angles = (row_index * col_index % L).astype(F32) * (2.0 * math.pi / L)
    wave = jnp.cos(angles), jnp.sin(angles)
    return [jnp.broadcast_to(values[:, :, None], (L2, L1, LANES)) for values in wave]


def swap(values, step):
    axis, mask = step
    size = lax.axis_size(axis)
    return lax.ppermute(values, axis, [(i, i ^ mask) for i in range(size)])


def bits(size):
    masks = []
    mask = size // 2
    while mask >= 1:
        masks.append(mask)
        mask //= 2
    return masks


def widen(held, step):
    return jnp.concatenate([held, swap(held, step)], axis=0)


def widen_codes(codes, steps, groups):
    for axis, mask in steps:
        code = mask if axis == "seq" else mask * groups
        codes = codes + [held ^ code for held in codes]
    return codes


def spread(pieces, steps):
    for step in steps:
        pieces = pieces + [swap(piece, step) for piece in pieces]
    return pieces


def spread_core(pieces, step_core):
    twins = [swap(piece, step_core) for piece in pieces]
    half = len(pieces) // 2
    return pieces[:half] + twins[:half] + pieces[half:] + twins[half:]


def pick(addend, extra):
    values, names, fixed = addend
    chosen = {**fixed, **extra}
    return values[tuple(chosen.get(name, slice(None)) for name in names)]


def total(addends, extra={}):
    parts = [pick(addend, extra) for addend in addends]
    return sum(parts[1:], parts[0].astype(F32))


def settle(addends, send, step):
    values, names, fixed = addends[-1]
    rest = [name for name in names if name not in fixed and name != step]
    kept = [(held, order, {**gone, step: 0}) for held, order, gone in addends]
    return kept + [(swap(send, step), rest, {})]


def fold(addends, step, kind):
    return settle(addends, total(addends, {step: 1}).astype(kind), step)


def after(addends, *others):
    values, names, fixed = addends[-1]
    results = lax.optimization_barrier((values,) + others)
    return (addends[:-1] + [(results[0], names, fixed)],) + tuple(results[1:])


def arrange(rows):
    return with_layout_constraint(rows.transpose(0, 2, 1, 3), Layout(major_to_minor=(0, 1, 2, 3)))


def exchange(rows):
    order = Layout(major_to_minor=(0, 1, 2, 3))
    rows = with_layout_constraint(rows, order)
    rows = lax.all_to_all(rows, "seq", split_axis=0, concat_axis=0, tiled=True)
    return with_layout_constraint(rows, order)


def body(tokens, lengths, labels, picked, cotangent, w_in, b_in, w_out, shifts, norm_gains):
    groups = lax.axis_size("seq")
    me = lax.axis_index("seq")
    here = lax.axis_index("batch") * groups + me
    columns = tokens.shape[2]
    share = w_in.shape[2]
    part = shifts.shape[2]
    blocks = groups * lax.axis_size("batch")

    masks = bits(groups)[:-1]
    steps_plane = [("seq", mask) for mask in masks[:1] + masks[:0:-1]]
    steps_seq = [("seq", mask) for mask in masks[::-1]]
    steps_batch = [("batch", mask) for mask in bits(lax.axis_size("batch"))]
    step_core = ("seq", 1)
    numbers = jnp.arange(blocks, dtype=jnp.int32)

    codes = widen_codes(
        [0], steps_plane + steps_batch[:-1] + [step_core] + steps_batch[-1:], groups
    )
    owner = jnp.array(codes, dtype=jnp.int32) ^ here
    one_hot = (owner[:, None] == numbers[None, :]).astype(F32)

    wide_cos, wide_sin = table_pair(D)
    wide = jnp.concatenate([wide_cos, -wide_sin], axis=0)
    twiddle_cos, twiddle_sin = twiddles()
    short_cos, short_sin = table_pair(L1)
    long_cos, long_sin = table_pair(L2)
    short_table = jnp.concatenate([short_cos, short_sin], axis=0)
    long_table = jnp.stack([jnp.stack([long_cos, -long_sin]), jnp.stack([long_sin, long_cos])])
    both = jnp.eye(2, dtype=BF16)
    pair_table = jnp.einsum("qukm,bc->qkbcum", long_table, both).reshape(4 * L2, 4 * L2)

    length = lax.dynamic_slice_in_dim(lengths, me, 1)
    small = jnp.concatenate([b_in[0], shifts[0].reshape(-1), norm_gains[0].reshape(-1)])
    small = small.astype(F32)[None]
    first_held = w_in[0].T[None]
    second_held = w_out[0][None]
    tokens_late = arrange(tokens)
    for number, step in enumerate(steps_plane[:-1]):
        first_held = widen(first_held, step)
        second_held = widen(second_held, step)
        small = widen(small, step)
        if number == 0:
            tokens_late, small, first_held, second_held = lax.optimization_barrier(
                (tokens_late, small, first_held, second_held)
            )
            x_all = exchange(tokens_late)
    early = (wide, twiddle_cos, twiddle_sin, short_table, pair_table, arrange(cotangent))
    small, first_held, second_held, early = lax.optimization_barrier(
        (small, first_held, second_held, early)
    )
    wide, twiddle_cos, twiddle_sin, short_table, pair_table, late_cotangent = early
    first_held = widen(first_held, steps_plane[-1])
    seconds = []
    for piece in spread([second_held], steps_batch):
        seconds += [piece, swap(piece, steps_plane[-1])]
    steps_small = steps_plane[:-1] + steps_batch + [step_core] + steps_plane[-1:]
    small_codes = widen_codes([0], steps_small, groups)
    for step in steps_batch + [step_core]:
        small = widen(small, step)
    small, first_held = lax.optimization_barrier((small, first_held))
    small = widen(small, steps_plane[-1])
    places = jnp.array([small_codes.index(code) for code in codes], dtype=jnp.int32)
    place_hot = (places[:, None] == numbers[None, :]).astype(F32)
    small = jnp.sum(place_hot[:, :, None] * small[None], axis=1)
    b_first = small[:, :share].reshape(1, blocks * share)
    rows = jnp.sum(one_hot[:, :, None] * small[:, None, share:], axis=0)
    rows = rows.reshape(blocks, 5, part).transpose(1, 0, 2).reshape(5, D)
    shifts_f = rows[:3]
    gains_f = rows[3:]
    blank = jnp.zeros((3, D), F32)
    vec = jnp.concatenate(
        [gains_f[1:2], shifts_f[2:3], gains_f[0:1], shifts_f[1:2], shifts_f[0:1], blank]
    )
    vec_one = vec[2:]
    vec_one = jnp.concatenate([vec_one, blank[:2]])
    firsts = spread([first_held], steps_batch)
    x_rows = x_all.reshape(L2, L1, D)
    hat_one, scale_one = transform(
        length, x_rows, short_table, pair_table, twiddle_cos, twiddle_sin, wide
    )
    hat_one, late_cotangent, firsts, seconds, vec, vec_one, b_first = lax.optimization_barrier(
        (hat_one, late_cotangent, firsts, seconds, vec, vec_one, b_first)
    )
    g_all = exchange(late_cotangent)
    flat = lambda pieces: [piece.reshape(-1, D) for piece in spread_core(pieces, step_core)]
    firsts, seconds = flat(firsts), flat(seconds)
    act, slope, layer_out, hat_two, scale_two, u = feed_forward(
        hat_one, b_first, vec, firsts, seconds
    )
    out_rows = exchange(layer_out.reshape(groups, columns, L1, D))

    parts = [(held[: len(held) // 2], held[len(held) // 2 :]) for held in (firsts, seconds)]
    units = blocks * share
    upper = feed_backward(
        (g_all.reshape(L, D), hat_two, scale_two),
        u, act, slope, parts[0][1], parts[1][1], units // 2, vec=vec
    )
    grad_u, low_e, sums_two = upper[5:]
    lower = feed_backward((low_e, grad_u), u, act, slope, parts[0][0], parts[1][0], 0)
    grad_u = lower[5]
    grad_b_first = jnp.concatenate([lower[4], upper[4]], axis=1)
    names = steps_batch[:-1][::-1] + steps_plane[::-1]
    shape = (2,) * len(names) + (share,)

    def fold_core(keep, send):
        return (keep.astype(F32) + swap(send, step_core).astype(F32)).astype(BF16)

    send_first, send_second = fold_core(upper[0], upper[2]), fold_core(upper[1], upper[3])
    grad_u, send_first, send_second = lax.optimization_barrier((grad_u, send_first, send_second))
    came_first, came_second = swap(send_first, steps_batch[-1]), swap(send_second, steps_batch[-1])
    grad_x, sums_one = transform_back(
        length, grad_u, hat_one, scale_one, short_table.T, pair_table.T,
        twiddle_cos, twiddle_sin, vec_one, wide
    )
    grad_x, out_rows, other_first, other_second, came_first = lax.optimization_barrier(
        (grad_x, out_rows, lower[2], lower[3], came_first)
    )
    other_first, other_second = swap(other_first, step_core), swap(other_second, step_core)
    grad_first, grad_second = [
        [(values.reshape(shape + (D,)), names, {}) for values in held]
        for held in (
            (lower[0], other_first, came_first),
            (lower[1], other_second, came_second),
        )
    ]
    grad_x = grad_x.reshape(groups, columns, L1, D)
    input_grad = arrange(exchange(grad_x))

    shift_of = jnp.arange(columns, dtype=jnp.int32) + me * columns
    place_of = L2 * jnp.arange(L1, dtype=jnp.int32)[None, :] + shift_of[:, None]
    for step in steps_batch[:-1][::-1]:
        grad_first = fold(grad_first, step, BF16)
        grad_second = fold(grad_second, step, BF16)
    grad_first = fold(grad_first, steps_seq[0], BF16)
    grad_first, out_rows, sums_one, sums_two, grad_b_first = after(
        grad_first, out_rows, sums_one, sums_two, grad_b_first
    )
    logits = out_rows.astype(F32)
    highest = jnp.max(logits, axis=-1, keepdims=True)
    powers = jnp.exp(logits - highest)
    denominator = jnp.sum(powers, axis=-1)
    features = jnp.arange(D, dtype=jnp.int32)
    label_rows = labels.transpose(0, 2, 1)
    top = jnp.sum(jnp.where(features == label_rows[..., None], powers, 0.0), axis=-1)
    counted = (picked.transpose(0, 2, 1) > 0) & (place_of[None] < lengths[:, None, None])
    weight = jnp.where(counted, 1.0, 0.0)
    sums = jnp.stack([jnp.sum(weight * (top / denominator)), jnp.sum(weight)])

    sums_two = jnp.sum(sums_two.reshape(3, 8, D), axis=1)
    sums_one = jnp.sum(sums_one.reshape(2, 8, D), axis=1)
    norms = jnp.stack([sums_two[0], sums_one[1], sums_two[2], sums_one[0], sums_two[1]])
    norms = norms.reshape(5, blocks, part).transpose(1, 0, 2).reshape(blocks, 5 * part)
    norms = jnp.sum(one_hot[:, :, None] * norms[None], axis=1)
    sums = jnp.broadcast_to(sums[None], (blocks, 2))
    small_grads = jnp.concatenate([grad_b_first.reshape(blocks, share), norms, sums], axis=1)
    names_small = steps_batch[-1:] + [step_core] + names
    small_grads = small_grads.reshape((2, 2) + shape[:-1] + (-1,))
    small = [(small_grads, names_small, {})]
    for step in [step_core] + steps_batch[::-1]:
        small = fold(small, step, F32)
    small, out_rows = after(small, out_rows)
    for step in steps_seq[1:]:
        grad_first = fold(grad_first, step, BF16)
    grad_second = fold(grad_second, steps_seq[0], BF16)
    for number, step in enumerate(steps_seq[1:]):
        small, latest = after(small, grad_second[-1][0])
        grad_second = grad_second[:-1] + [(latest,) + grad_second[-1][1:]]
        if step == steps_seq[-1]:
            small, input_grad = after(small, input_grad)
        small = fold(small, steps_seq[number], F32)
        grad_second = fold(grad_second, step, BF16)
    small = fold(small, steps_seq[-1], F32)
    current = out_rows.transpose(0, 2, 1, 3)
    small_grads, grad_first, grad_second = total(small), total(grad_first), total(grad_second)
    norms = small_grads[share:-2].reshape(5, part)
    match_rate = D * small_grads[-2] / jnp.maximum(small_grads[-1], 1.0)
    return (
        current,
        input_grad,
        grad_first.T[None],
        small_grads[:share][None],
        grad_second[None],
        norms[:3][None],
        norms[3:][None],
        match_rate,
    )


def solution(mesh):
    in_specs = (
        P("batch", None, "seq", None),
        P("batch"),
        P("batch", None, "seq"),
        P("batch", None, "seq"),
        P("batch", None, "seq", None),
        P(None, None, ("batch", "seq")),
        P(None, ("batch", "seq")),
        P(None, ("batch", "seq"), None),
        P(None, None, ("batch", "seq")),
        P(None, None, ("batch", "seq")),
    )
    out_specs = (
        P("batch", None, "seq", None),
        P("batch", None, "seq", None),
        P(None, None, ("batch", "seq")),
        P(None, ("batch", "seq")),
        P(None, ("batch", "seq"), None),
        P(None, None, ("batch", "seq")),
        P(None, None, ("batch", "seq")),
        P(),
    )
    return jax.shard_map(body, mesh=mesh, in_specs=in_specs, out_specs=out_specs, check_vma=False)
```

```python
import functools
import math

import jax
import jax.numpy as jnp
from jax import lax
from jax.experimental import pallas as pl
from jax.experimental.layout import Layout, with_layout_constraint
from jax.experimental.pallas import tpu as pltpu
from jax.sharding import PartitionSpec as P

D = 768
L1 = 64
L2 = 32
L = 2048
LANES = 128
PAIR = 4 * L2
STRIDE = PAIR + 1

EPSILON = 1e-12
ROOT_TWO_PI = 0.7978845608028654
CUBIC = ROOT_TWO_PI * 0.044715
F32 = jnp.float32
BF16 = jnp.bfloat16
VMEM_BYTES = 60 << 20
FAR = pl.BlockSpec(memory_space=pl.ANY)


def product(left, right):
    return lax.dot_general(left, right, (((1,), (0,)), ((), ())), preferred_element_type=F32)


def product_turned(left, right):
    return lax.dot_general(left, right, (((1,), (1,)), ((), ())), preferred_element_type=F32)


def product_over_rows(left, right):
    return lax.dot_general(left, right, (((0,), (0,)), ((), ())), preferred_element_type=F32)


def lanes(column):
    return jnp.concatenate([column] * (D // LANES), axis=1)


def rows_of_eight(values):
    return jnp.sum(values.reshape(-1, 8, values.shape[-1]), axis=0)


def average(values):
    return jnp.mean(values, axis=1, keepdims=True)


def norm_back(grad, x_hat, scale, gain):
    q = grad * gain
    return lanes(scale) * (q - average(q) - x_hat * average(q * x_hat))


def whole_block(shape):
    return pl.BlockSpec(shape, lambda c: (0,) * len(shape), pipeline_mode=pl.Buffered(1))


def params():
    return pltpu.CompilerParams(vmem_limit_bytes=VMEM_BYTES)


def cost(flops, transcendentals, size):
    return pl.CostEstimate(flops=flops, transcendentals=transcendentals, bytes_accessed=size)


def scatter(refs, start, value):
    for j, ref in enumerate(refs):
        ref[pl.ds(start, L2, stride=STRIDE), :] = value[:, j * LANES : (j + 1) * LANES]


def gather(refs, block):
    return jnp.concatenate([ref[pl.ds(block * STRIDE, PAIR), :] for ref in refs], axis=1)


def middle_scratch():
    return [pltpu.VMEM((L2 * STRIDE, LANES), F32)] * (D // LANES)


def transform_kernel(
    length_ref, x_ref, short_ref, pair_ref, cos_ref, sin_ref, wide_hbm,
    hat_ref, scale_ref, spec_ref, wide_ref, sem, *middle, group
):
    length = length_ref[0]
    step = pl.program_id(0)
    load = pltpu.make_async_copy(wide_hbm, wide_ref, sem.at[0])

    @pl.when(step == 0)
    def _():
        load.start()

        def first(m, carry):
            spots = L2 * lax.broadcasted_iota(jnp.int32, (L1, D), 0) + m
            x = jnp.where(spots < length, x_ref[m].astype(F32), 0.0).astype(BF16)
            y = product(short_ref[...], x)
            real, imag = y[:L1], y[L1:]
            cosine, sine = lanes(cos_ref[m]), lanes(sin_ref[m])
            turned = (real * cosine - imag * sine, real * sine + imag * cosine)
            for b in range(2):
                for part in range(2):
                    scatter(middle, (b * 2 + part) * L2 + m, turned[part][b * L2 : (b + 1) * L2])
            return carry

        lax.fori_loop(0, L2, first, 0, unroll=4)
        load.wait()

    for j in range(group):
        turned = gather(middle, step * group + j).astype(BF16)
        q = product(pair_ref[...], turned).astype(BF16)
        spec_ref[j * L1 : (j + 1) * L1, :D] = q[:L1]
        spec_ref[j * L1 : (j + 1) * L1, D:] = q[L1:]
    mixed = product(spec_ref[...], wide_ref[...])
    number = lax.broadcasted_iota(jnp.int32, (group * L1, D), 0)
    spots = L2 * (number % L1) + step * group + number // L1
    x = x_ref[pl.ds(step * group, group)].reshape(group * L1, D).astype(F32)
    h = jnp.where(spots < length, x, 0.0) + mixed
    center = h - average(h)
    scale = lax.rsqrt(average(center * center) + EPSILON)
    hat_ref[...] = center * scale
    scale_ref[...] = jnp.broadcast_to(scale, scale_ref.shape)


def transform(length, x, short, pair, cosine, sine, wide, group=8):
    out = lambda width: pl.BlockSpec((group * L1, width), lambda c: (c, 0))
    return pl.pallas_call(
        functools.partial(transform_kernel, group=group),
        grid=(L2 // group,),
        in_specs=[pl.BlockSpec(memory_space=pltpu.SMEM)]
        + [whole_block(values.shape) for values in (x, short, pair, cosine, sine)]
        + [FAR],
        out_specs=[out(D), out(LANES)],
        out_shape=[
            jax.ShapeDtypeStruct((L, D), F32),
            jax.ShapeDtypeStruct((L, LANES), F32),
        ],
        scratch_shapes=[
            pltpu.VMEM((group * L1, 2 * D), BF16),
            pltpu.VMEM((2 * D, D), BF16),
            pltpu.SemaphoreType.DMA((1,)),
        ]
        + middle_scratch(),
        compiler_params=params(),
        cost_estimate=cost(7 << 30, L, 24 << 20),
        name="transform",
    )(length, x, short, pair, cosine, sine, wide)


def back_kernel(
    length_ref, du_ref, hat_ref, scale_ref, short_ref, pair_ref, cos_ref, sin_ref, vec_ref, wide_ref,
    dx_ref, sums_ref, rh_ref, spec_ref, *middle, group
):
    length = length_ref[0]
    step = pl.program_id(0)
    steps = L2 // group

    @pl.when(step == 0)
    def _():
        sums_ref[...] = jnp.zeros_like(sums_ref)

    @pl.when(step < steps)
    def _():
        du = du_ref[...]
        hat = hat_ref[...]
        rh = norm_back(du, hat, scale_ref[...], vec_ref[0:1, :]).astype(BF16)
        rh_ref[pl.ds(pl.multiple_of(step * group * L1, group * L1), group * L1), :] = rh
        sums_ref[0:8, :] += rows_of_eight(du * hat)
        sums_ref[8:16, :] += rows_of_eight(du)
        real = product(rh, wide_ref[:D, :]).astype(BF16)
        imag = product(rh, wide_ref[D:, :]).astype(BF16)
        for j in range(group):
            spec_ref[j, :L1, :] = real[j * L1 : (j + 1) * L1]
            spec_ref[j, L1:, :] = imag[j * L1 : (j + 1) * L1]
            turned = product(pair_ref[...], spec_ref[j]).astype(BF16).astype(F32)
            for b in range(2):
                for part in range(2):
                    start = (b * 2 + part) * L2
                    spot = part * L1 + b * L2 + step * group + j
                    scatter(middle, spot, turned[start : start + L2])

    @pl.when(step >= steps)
    def _():
        def second(i, carry):
            m = (step - steps) * group + i
            turned = gather(middle, m)
            real, imag = turned[:L1], turned[L1:]
            cosine, sine = lanes(cos_ref[m]), lanes(sin_ref[m])
            back = jnp.concatenate(
                [
                    (real * cosine + imag * sine).astype(BF16),
                    (imag * cosine - real * sine).astype(BF16),
                ],
                axis=0,
            )
            rh = rh_ref[pl.ds(pl.multiple_of(m * L1, L1), L1), :].astype(F32)
            dx = rh + product(short_ref[...], back)
            spots = L2 * lax.broadcasted_iota(jnp.int32, (L1, D), 0) + m
            dx_ref[i] = jnp.where(spots < length, dx, 0.0).astype(BF16)
            return carry

        lax.fori_loop(0, group, second, 0, unroll=4)


def transform_back(length, du, hat, scale, short, pair, cosine, sine, vec, wide, group=8):
    steps = L2 // group
    rows = lambda width: pl.BlockSpec((group * L1, width), lambda c: (jnp.minimum(c, steps - 1), 0))
    return pl.pallas_call(
        functools.partial(back_kernel, group=group),
        grid=(2 * steps,),
        in_specs=[pl.BlockSpec(memory_space=pltpu.SMEM), rows(D), rows(D), rows(LANES)]
        + [whole_block(values.shape) for values in (short, pair, cosine, sine, vec, wide)],
        out_specs=[
            pl.BlockSpec((group, L1, D), lambda c: (jnp.maximum(c - steps, 0), 0, 0)),
            pl.BlockSpec((16, D), lambda c: (0, 0)),
        ],
        out_shape=[
            jax.ShapeDtypeStruct((L2, L1, D), BF16),
            jax.ShapeDtypeStruct((16, D), F32),
        ],
        scratch_shapes=[pltpu.VMEM((L, D), BF16), pltpu.VMEM((group, 2 * L1, D), BF16)]
        + middle_scratch(),
        compiler_params=params(),
        cost_estimate=cost(7 << 30, 0, 20 << 20),
        name="transform_back",
    )(length, du, hat, scale, short, pair, cosine, sine, vec, wide)


def fetch_weights(pieces, holder, sems, chunk):
    rows = holder.shape[0] // len(pieces)
    step = pl.program_id(0)
    copies = [
        pltpu.make_async_copy(
            piece.at[pl.ds(0, rows), :], holder.at[pl.ds(i * rows, rows), :], sems.at[i]
        )
        for i, piece in enumerate(pieces)
    ]

    @pl.when(step == 0)
    def _():
        for copy in copies:
            copy.start()

    for number in range(holder.shape[0] // chunk):
        needed = [copy for i, copy in enumerate(copies) if i * rows // chunk == number]
        if needed:

            @pl.when(step == number)
            def _():
                for copy in needed:
                    copy.wait()


def forward_kernel(*refs, tile, counts, chunk):
    first_hat_ref, b_ref, vec_ref = refs[:3]
    split = 3 + sum(counts)
    firsts, seconds = refs[3 : 3 + counts[0]], refs[3 + counts[0] : split]
    act_ref, slope_ref, out_far, hat_far, scale_far, u_far = refs[split : split + 6]
    y_ref, w1_ref, w2_ref, out_ref, hat_ref, scale_ref, u_ref, sem1, sem2, sem3 = refs[split + 6 :]
    parts = 4
    part = u_ref.shape[0] // parts
    tiles = u_ref.shape[0] // tile
    loads, stores = [], []
    for i in range(parts):
        rows = pl.ds(i * part, part)
        pairs = ((u_ref, u_far), (out_ref, out_far), (hat_ref, hat_far), (scale_ref, scale_far))
        loads.append(
            pltpu.make_async_copy(first_hat_ref.at[rows, :], y_ref.at[rows, :], sem3.at[i, 0])
        )
        stores.append(
            [
                pltpu.make_async_copy(near.at[rows, :], far.at[rows, :], sem3.at[i, 1 + j])
                for j, (near, far) in enumerate(pairs)
            ]
        )

    @pl.when(pl.program_id(0) == 0)
    def _():
        for load in loads:
            load.start()

    fetch_weights(firsts, w1_ref, sem1, chunk)
    fetch_weights(seconds, w2_ref, sem2, chunk)
    here = pl.ds(pl.multiple_of(pl.program_id(0) * chunk, chunk), chunk)

    @pl.when(pl.program_id(0) == 0)
    def _():
        small = 256

        def begin(i, carry):
            rows = pl.ds(pl.multiple_of(i * small, small), small)
            u = y_ref[rows, :] * vec_ref[2:3, :] + vec_ref[3:4, :]
            u_ref[rows, :] = u.astype(BF16)
            y_ref[rows, :] = u + vec_ref[4:5, :]
            return carry

        for i in range(parts):
            loads[i].wait()
            lax.fori_loop(i * part // small, (i + 1) * part // small, begin, 0)
            stores[i][0].start()


    def step(i, carry):
        rows = pl.ds(pl.multiple_of(i * tile, tile), tile)
        z = product_turned(u_ref[rows, :], w1_ref[here, :]) + b_ref[...]
        square = z * z
        t = jnp.tanh(z * (ROOT_TWO_PI + CUBIC * square))
        half = 0.5 + 0.5 * t
        a = z * half
        low = a.astype(BF16)
        act_ref[rows, :] = low
        slope = half + (a - a * t) * (ROOT_TWO_PI + (3.0 * CUBIC) * square)
        slope_ref[rows, :] = slope.astype(BF16)
        y_ref[rows, :] += product(low, w2_ref[here, :])
        return carry

    lax.fori_loop(0, tiles, step, 0)

    @pl.when(pl.program_id(0) == pl.num_programs(0) - 1)
    def _():
        small = 256

        def finish(i, carry):
            rows = pl.ds(pl.multiple_of(i * small, small), small)
            y = y_ref[rows, :]
            center = y - average(y)
            scale = lax.rsqrt(average(center * center) + EPSILON)
            hat = center * scale
            out_ref[rows, :] = (hat * vec_ref[0:1, :] + vec_ref[1:2, :]).astype(BF16)
            hat_ref[rows, :] = hat.astype(BF16)
            scale_ref[rows, :] = jnp.broadcast_to(scale, (small, LANES))
            return carry

        for i in range(parts):
            lax.fori_loop(i * part // small, (i + 1) * part // small, finish, 0)
            for copy in stores[i][1:]:
                copy.start()
        for store in stores:
            for copy in store:
                copy.wait()


def feed_forward(hat, b, vec, firsts, seconds, chunk=1024, tile=1024):
    tokens, width = hat.shape
    counts = (len(firsts), len(seconds))
    units = b.shape[1]
    acts = lambda: pl.BlockSpec((tokens, chunk), lambda c: (0, c))
    return pl.pallas_call(
        functools.partial(forward_kernel, tile=tile, counts=counts, chunk=chunk),
        grid=(units // chunk,),
        in_specs=[
            FAR,
            pl.BlockSpec((1, chunk), lambda c: (0, c)),
            whole_block(vec.shape),
        ]
        + [FAR] * sum(counts),
        out_specs=[acts(), acts()] + [FAR] * 4,
        out_shape=[
            jax.ShapeDtypeStruct((tokens, units), BF16),
            jax.ShapeDtypeStruct((tokens, units), BF16),
            jax.ShapeDtypeStruct((tokens, width), BF16),
            jax.ShapeDtypeStruct((tokens, width), BF16),
            jax.ShapeDtypeStruct((tokens, LANES), F32),
            jax.ShapeDtypeStruct((tokens, width), BF16),
        ],
        scratch_shapes=[
            pltpu.VMEM((tokens, width), F32),
            pltpu.VMEM((units, width), BF16),
            pltpu.VMEM((units, width), BF16),
            pltpu.VMEM((tokens, width), BF16),
            pltpu.VMEM((tokens, width), BF16),
            pltpu.VMEM((tokens, LANES), F32),
            pltpu.VMEM((tokens, width), BF16),
            pltpu.SemaphoreType.DMA((counts[0],)),
            pltpu.SemaphoreType.DMA((counts[1],)),
            pltpu.SemaphoreType.DMA((4, 5)),
        ],
        compiler_params=params(),
        cost_estimate=cost(4 * tokens * units * width, tokens * units, 50 << 20),
        name="feed_forward",
    )(hat, b, vec, *firsts, *seconds)


def backward_kernel(*refs, tile, counts, chunk):
    g_far, hat_far, scale_far, u_far, vec_ref, act_ref, slope_ref = refs[:7]
    split = 7 + sum(counts)
    firsts, seconds = refs[7 : 7 + counts[0]], refs[7 + counts[0] : split]
    keep1_ref, keep2_ref, send1_ref, send2_ref, db_ref, du_far, sums_ref = refs[split : split + 7]
    e_ref, w1_ref, w2_ref, f_ref, g_ref, hat_ref, scale_ref, u_ref, du_ref = refs[
        split + 7 : split + 16
    ]
    sem1, sem2, sem3, sem4 = refs[split + 16 :]
    parts = 4
    part = u_ref.shape[0] // parts
    loads = []
    for i in range(parts):
        rows = pl.ds(i * part, part)
        loads.append(
            [
                pltpu.make_async_copy(far.at[rows, :], near.at[rows, :], sem3.at[i, j])
                for j, (far, near) in enumerate(
                    ((g_far, g_ref), (hat_far, hat_ref), (scale_far, scale_ref))
                )
            ]
        )
    load_u = pltpu.make_async_copy(u_far, u_ref, sem4.at[0])
    store_du = pltpu.make_async_copy(du_ref, du_far, sem4.at[1])

    @pl.when(pl.program_id(0) == 0)
    def _():
        for load in loads:
            for copy in load:
                copy.start()

    fetch_weights(seconds, w2_ref, sem2, chunk)
    fetch_weights(firsts, w1_ref, sem1, chunk)
    here = pl.ds(pl.multiple_of(pl.program_id(0) * chunk, chunk), chunk)

    @pl.when(pl.program_id(0) == 0)
    def _():
        small = 256
        sums_ref[...] = jnp.zeros_like(sums_ref)

        def begin(i, carry):
            rows = pl.ds(pl.multiple_of(i * small, small), small)
            g = g_ref[rows, :].astype(F32)
            hat = hat_ref[rows, :].astype(F32)
            dy = norm_back(g, hat, scale_ref[rows, :], vec_ref[0:1, :])
            du_ref[rows, :] = dy
            e_ref[rows, :] = dy.astype(BF16)
            sums_ref[0:8, :] += rows_of_eight(dy)
            sums_ref[8:16, :] += rows_of_eight(g * hat)
            sums_ref[16:24, :] += rows_of_eight(g)
            return carry

        load_u.start()
        for i in range(parts):
            for copy in loads[i]:
                copy.wait()
            lax.fori_loop(i * part // small, (i + 1) * part // small, begin, 0)
        load_u.wait()


    def step(i, db):
        rows = pl.ds(pl.multiple_of(i * tile, tile), tile)
        dz = product_turned(e_ref[rows, :], w2_ref[here, :]) * slope_ref[rows, :].astype(F32)
        low = dz.astype(BF16)
        f_ref[rows, :] = low
        du_ref[rows, :] += product(low, w1_ref[here, :])
        return db + rows_of_eight(dz)

    db = lax.fori_loop(0, u_ref.shape[0] // tile, step, jnp.zeros((8, chunk), F32))
    db_ref[...] = jnp.sum(db, axis=0, keepdims=True)

    @pl.when(pl.program_id(0) == pl.num_programs(0) - 1)
    def _():
        store_du.start()

    dw2 = product_over_rows(act_ref[...], e_ref[...]).astype(BF16)
    dw1 = product_over_rows(f_ref[...], u_ref[...]).astype(BF16)
    half = pl.num_programs(0) // 2

    @pl.when(pl.program_id(0) < half)
    def _():
        keep1_ref[...] = dw1
        keep2_ref[...] = dw2

    @pl.when(pl.program_id(0) >= half)
    def _():
        send1_ref[...] = dw1
        send2_ref[...] = dw2

    @pl.when(pl.program_id(0) == pl.num_programs(0) - 1)
    def _():
        store_du.wait()


def feed_backward(g, hat, scale, vec, u, act, slope, firsts, seconds, chunk=512, tile=2048):
    tokens, width = u.shape
    counts = (len(firsts), len(seconds))
    units = act.shape[1]
    half = units // chunk // 2
    acts = lambda: pl.BlockSpec((tokens, chunk), lambda c: (0, c))
    keep = lambda: pl.BlockSpec((chunk, width), lambda c: (jnp.minimum(c, half - 1), 0))
    send = lambda: pl.BlockSpec((chunk, width), lambda c: (jnp.maximum(c - half, 0), 0))
    grads = jax.ShapeDtypeStruct((units // 2, width), BF16)
    return pl.pallas_call(
        functools.partial(backward_kernel, tile=tile, counts=counts, chunk=chunk),
        grid=(units // chunk,),
        in_specs=[FAR] * 4
        + [whole_block(vec.shape), acts(), acts()]
        + [FAR] * sum(counts),
        out_specs=[
            keep(),
            keep(),
            send(),
            send(),
            pl.BlockSpec((1, chunk), lambda c: (0, c)),
            FAR,
            whole_block((24, width)),
        ],
        out_shape=[grads] * 4
        + [
            jax.ShapeDtypeStruct((1, units), F32),
            jax.ShapeDtypeStruct((tokens, width), F32),
            jax.ShapeDtypeStruct((24, width), F32),
        ],
        scratch_shapes=[
            pltpu.VMEM((tokens, width), BF16),
            pltpu.VMEM((units, width), BF16),
            pltpu.VMEM((units, width), BF16),
            pltpu.VMEM((tokens, chunk), BF16),
            pltpu.VMEM((tokens, width), BF16),
            pltpu.VMEM((tokens, width), BF16),
            pltpu.VMEM((tokens, LANES), F32),
            pltpu.VMEM((tokens, width), BF16),
            pltpu.VMEM((tokens, width), F32),
            pltpu.SemaphoreType.DMA((counts[0],)),
            pltpu.SemaphoreType.DMA((counts[1],)),
            pltpu.SemaphoreType.DMA((4, 3)),
            pltpu.SemaphoreType.DMA((2,)),
        ],
        compiler_params=params(),
        cost_estimate=cost(8 * tokens * units * width, 0, 60 << 20),
        name="feed_backward",
    )(g, hat, scale, u, vec, act, slope, *firsts, *seconds)


def table_pair(points):
    numbers = jnp.arange(points, dtype=jnp.int32)
    coarse = 32 * jnp.arange(points // 32, dtype=jnp.int32)
    fine = jnp.arange(32, dtype=jnp.int32)

    def waves(rows):
        angles = (rows[:, None] * numbers[None, :] % points).astype(F32) * (2.0 * math.pi / points)
        return jnp.cos(angles), jnp.sin(angles)

    factor = 1.0 / math.sqrt(points)
    if points <= 64:
        cosine, sine = waves(numbers)
    else:
        coarse_cos, coarse_sin = waves(coarse)
        fine_cos, fine_sin = waves(fine)
        coarse_cos, coarse_sin, fine_cos, fine_sin = lax.optimization_barrier(
            (coarse_cos, coarse_sin, fine_cos, fine_sin)
        )
        coarse_cos, coarse_sin = coarse_cos[:, None], coarse_sin[:, None]
        fine_cos, fine_sin = fine_cos[None], fine_sin[None]
        cosine = (coarse_cos * fine_cos - coarse_sin * fine_sin).reshape(points, points)
        sine = (coarse_sin * fine_cos + coarse_cos * fine_sin).reshape(points, points)
    return (cosine * factor).astype(BF16), (sine * factor).astype(BF16)


def twiddles():
    row_index = jnp.arange(L1, dtype=jnp.int32)[None, :]
    col_index = jnp.arange(L2, dtype=jnp.int32)[:, None]
    angles = (row_index * col_index % L).astype(F32) * (2.0 * math.pi / L)
    wave = jnp.cos(angles), jnp.sin(angles)
    return [jnp.broadcast_to(values[:, :, None], (L2, L1, LANES)) for values in wave]


def swap(values, step):
    axis, mask = step
    size = lax.axis_size(axis)
    return lax.ppermute(values, axis, [(i, i ^ mask) for i in range(size)])


def bits(size):
    masks = []
    mask = size // 2
    while mask >= 1:
        masks.append(mask)
        mask //= 2
    return masks


def widen(held, step):
    return jnp.concatenate([held, swap(held, step)], axis=0)


def widen_codes(codes, steps, groups):
    for axis, mask in steps:
        code = mask if axis == "seq" else mask * groups
        codes = codes + [held ^ code for held in codes]
    return codes


def spread(pieces, steps):
    for step in steps:
        pieces = pieces + [swap(piece, step) for piece in pieces]
    return pieces


def spread_core(pieces, step_core):
    return pieces + [swap(piece, step_core) for piece in pieces]


def pick(addend, extra):
    values, names, fixed = addend
    chosen = {**fixed, **extra}
    return values[tuple(chosen.get(name, slice(None)) for name in names)]


def total(addends, extra={}):
    parts = [pick(addend, extra) for addend in addends]
    return sum(parts[1:], parts[0].astype(F32))


def settle(addends, send, step):
    values, names, fixed = addends[-1]
    rest = [name for name in names if name not in fixed and name != step]
    kept = [(held, order, {**gone, step: 0}) for held, order, gone in addends]
    return kept + [(swap(send, step), rest, {})]


def fold(addends, step, kind):
    return settle(addends, total(addends, {step: 1}).astype(kind), step)


def after(addends, *others):
    values, names, fixed = addends[-1]
    results = lax.optimization_barrier((values,) + others)
    return (addends[:-1] + [(results[0], names, fixed)],) + tuple(results[1:])


def arrange(rows):
    return with_layout_constraint(rows.transpose(0, 2, 1, 3), Layout(major_to_minor=(0, 1, 2, 3)))


def exchange(rows):
    order = Layout(major_to_minor=(0, 1, 2, 3))
    rows = with_layout_constraint(rows, order)
    rows = lax.all_to_all(rows, "seq", split_axis=0, concat_axis=0, tiled=True)
    return with_layout_constraint(rows, order)


def body(tokens, lengths, labels, picked, cotangent, w_in, b_in, w_out, shifts, norm_gains):
    groups = lax.axis_size("seq")
    me = lax.axis_index("seq")
    here = lax.axis_index("batch") * groups + me
    columns = tokens.shape[2]
    share = w_in.shape[2]
    part = shifts.shape[2]
    blocks = groups * lax.axis_size("batch")

    masks = bits(groups)[:-1]
    steps_plane = [("seq", mask) for mask in masks[:1] + masks[:0:-1]]
    steps_seq = [("seq", mask) for mask in masks[::-1]]
    steps_batch = [("batch", mask) for mask in bits(lax.axis_size("batch"))]
    step_core = ("seq", 1)
    numbers = jnp.arange(blocks, dtype=jnp.int32)

    codes = widen_codes([0], steps_plane + steps_batch + [step_core], groups)
    owner = jnp.array(codes, dtype=jnp.int32) ^ here
    one_hot = (owner[:, None] == numbers[None, :]).astype(F32)

    wide_cos, wide_sin = table_pair(D)
    wide = jnp.concatenate([wide_cos, -wide_sin], axis=0)
    twiddle_cos, twiddle_sin = twiddles()
    short_cos, short_sin = table_pair(L1)
    long_cos, long_sin = table_pair(L2)
    short_table = jnp.concatenate([short_cos, short_sin], axis=0)
    long_table = jnp.stack([jnp.stack([long_cos, -long_sin]), jnp.stack([long_sin, long_cos])])
    both = jnp.eye(2, dtype=BF16)
    pair_table = jnp.einsum("qukm,bc->qkbcum", long_table, both).reshape(4 * L2, 4 * L2)

    length = lax.dynamic_slice_in_dim(lengths, me, 1)
    small = jnp.concatenate([b_in[0], shifts[0].reshape(-1), norm_gains[0].reshape(-1)])
    small = small.astype(F32)[None]
    first_held = w_in[0].T[None]
    second_held = w_out[0][None]
    tokens_late = arrange(tokens)
    for number, step in enumerate(steps_plane[:-1]):
        first_held = widen(first_held, step)
        second_held = widen(second_held, step)
        small = widen(small, step)
        if number == 0:
            tokens_late, small, first_held, second_held = lax.optimization_barrier(
                (tokens_late, small, first_held, second_held)
            )
            x_all = exchange(tokens_late)
    early = (wide, twiddle_cos, twiddle_sin, short_table, pair_table, arrange(cotangent))
    small, first_held, second_held, early = lax.optimization_barrier(
        (small, first_held, second_held, early)
    )
    wide, twiddle_cos, twiddle_sin, short_table, pair_table, late_cotangent = early
    first_held = widen(first_held, steps_plane[-1])
    seconds = []
    for piece in spread([second_held], steps_batch):
        seconds += [piece, swap(piece, steps_plane[-1])]
    steps_small = steps_plane[:-1] + steps_batch + [step_core] + steps_plane[-1:]
    small_codes = widen_codes([0], steps_small, groups)
    for step in steps_batch + [step_core]:
        small = widen(small, step)
    small, first_held = lax.optimization_barrier((small, first_held))
    small = widen(small, steps_plane[-1])
    places = jnp.array([small_codes.index(code) for code in codes], dtype=jnp.int32)
    place_hot = (places[:, None] == numbers[None, :]).astype(F32)
    small = jnp.sum(place_hot[:, :, None] * small[None], axis=1)
    b_first = small[:, :share].reshape(1, blocks * share)
    rows = jnp.sum(one_hot[:, :, None] * small[:, None, share:], axis=0)
    rows = rows.reshape(blocks, 5, part).transpose(1, 0, 2).reshape(5, D)
    shifts_f = rows[:3]
    gains_f = rows[3:]
    blank = jnp.zeros((3, D), F32)
    vec = jnp.concatenate(
        [gains_f[1:2], shifts_f[2:3], gains_f[0:1], shifts_f[1:2], shifts_f[0:1], blank]
    )
    vec_one = vec[2:]
    vec_one = jnp.concatenate([vec_one, blank[:2]])
    firsts = spread([first_held], steps_batch)
    x_rows = x_all.reshape(L2, L1, D)
    hat_one, scale_one = transform(
        length, x_rows, short_table, pair_table, twiddle_cos, twiddle_sin, wide
    )
    hat_one, late_cotangent, firsts, seconds, vec, vec_one, b_first = lax.optimization_barrier(
        (hat_one, late_cotangent, firsts, seconds, vec, vec_one, b_first)
    )
    g_all = exchange(late_cotangent)
    flat = lambda pieces: [piece.reshape(-1, D) for piece in spread_core(pieces, step_core)]
    firsts, seconds = flat(firsts), flat(seconds)
    act, slope, layer_out, hat_two, scale_two, u = feed_forward(
        hat_one, b_first, vec, firsts, seconds
    )
    out_rows = exchange(layer_out.reshape(groups, columns, L1, D))

    keep_first, keep_second, send_first, send_second, grad_b_first, grad_u, sums_two = feed_backward(
        g_all.reshape(L, D), hat_two, scale_two, vec, u, act, slope, firsts, seconds
    )
    names = steps_batch[::-1] + steps_plane[::-1]
    shape = (2,) * len(names) + (share,)
    came_first = swap(send_first, step_core)
    came_second = swap(send_second, step_core)
    grad_x, sums_one = transform_back(
        length, grad_u, hat_one, scale_one, short_table.T, pair_table.T,
        twiddle_cos, twiddle_sin, vec_one, wide
    )
    grad_x, came_first, came_second, out_rows = lax.optimization_barrier(
        (grad_x, came_first, came_second, out_rows)
    )
    grad_first, grad_second = [
        [(values.reshape(shape + (D,)), names, {}) for values in pair]
        for pair in ((keep_first, came_first), (keep_second, came_second))
    ]
    grad_x = grad_x.reshape(groups, columns, L1, D)
    input_grad = arrange(exchange(grad_x))

    shift_of = jnp.arange(columns, dtype=jnp.int32) + me * columns
    place_of = L2 * jnp.arange(L1, dtype=jnp.int32)[None, :] + shift_of[:, None]
    for step in steps_batch[::-1]:
        grad_first = fold(grad_first, step, BF16)
        grad_second = fold(grad_second, step, BF16)
    grad_first, out_rows, sums_one, sums_two, grad_b_first = after(
        grad_first, out_rows, sums_one, sums_two, grad_b_first
    )
    logits = out_rows.astype(F32)
    highest = jnp.max(logits, axis=-1, keepdims=True)
    powers = jnp.exp(logits - highest)
    denominator = jnp.sum(powers, axis=-1)
    features = jnp.arange(D, dtype=jnp.int32)
    label_rows = labels.transpose(0, 2, 1)
    top = jnp.sum(jnp.where(features == label_rows[..., None], powers, 0.0), axis=-1)
    counted = (picked.transpose(0, 2, 1) > 0) & (place_of[None] < lengths[:, None, None])
    weight = jnp.where(counted, 1.0, 0.0)
    sums = jnp.stack([jnp.sum(weight * (top / denominator)), jnp.sum(weight)])

    sums_two = jnp.sum(sums_two.reshape(3, 8, D), axis=1)
    sums_one = jnp.sum(sums_one.reshape(2, 8, D), axis=1)
    norms = jnp.stack([sums_two[0], sums_one[1], sums_two[2], sums_one[0], sums_two[1]])
    norms = norms.reshape(5, blocks, part).transpose(1, 0, 2).reshape(blocks, 5 * part)
    norms = jnp.sum(one_hot[:, :, None] * norms[None], axis=1)
    sums = jnp.broadcast_to(sums[None], (blocks, 2))
    small_grads = jnp.concatenate([grad_b_first.reshape(blocks, share), norms, sums], axis=1)
    half = blocks // 2
    arrived = swap(small_grads[half:], step_core)
    small = [
        (values.reshape(shape[:-1] + (-1,)), names, {}) for values in (small_grads[:half], arrived)
    ]
    for step in steps_batch[::-1]:
        small = fold(small, step, F32)
    small, out_rows = after(small, out_rows)
    for step in steps_seq:
        grad_first = fold(grad_first, step, BF16)
    small, latest = after(small, grad_second[-1][0])
    grad_second = grad_second[:-1] + [(latest,) + grad_second[-1][1:]]
    for number, step in enumerate(steps_seq):
        grad_second = fold(grad_second, step, BF16)
        if number == 1:
            small, input_grad = after(small, input_grad)
        small = fold(small, step, F32)
    current = out_rows.transpose(0, 2, 1, 3)
    small_grads, grad_first, grad_second = total(small), total(grad_first), total(grad_second)
    norms = small_grads[share:-2].reshape(5, part)
    match_rate = D * small_grads[-2] / jnp.maximum(small_grads[-1], 1.0)
    return (
        current,
        input_grad,
        grad_first.T[None],
        small_grads[:share][None],
        grad_second[None],
        norms[:3][None],
        norms[3:][None],
        match_rate,
    )


def solution(mesh):
    in_specs = (
        P("batch", None, "seq", None),
        P("batch"),
        P("batch", None, "seq"),
        P("batch", None, "seq"),
        P("batch", None, "seq", None),
        P(None, None, ("batch", "seq")),
        P(None, ("batch", "seq")),
        P(None, ("batch", "seq"), None),
        P(None, None, ("batch", "seq")),
        P(None, None, ("batch", "seq")),
    )
    out_specs = (
        P("batch", None, "seq", None),
        P("batch", None, "seq", None),
        P(None, None, ("batch", "seq")),
        P(None, ("batch", "seq")),
        P(None, ("batch", "seq"), None),
        P(None, None, ("batch", "seq")),
        P(None, None, ("batch", "seq")),
        P(),
    )
    return jax.shard_map(body, mesh=mesh, in_specs=in_specs, out_specs=out_specs, check_vma=False)
```

```python
import functools
import math

import jax
import jax.numpy as jnp
from jax import lax
from jax.experimental import pallas as pl
from jax.experimental.layout import Layout, with_layout_constraint
from jax.experimental.pallas import tpu as pltpu
from jax.sharding import PartitionSpec as P

D = 768
L1 = 64
L2 = 32
L = 2048
LANES = 128
PAIR = 4 * L2
STRIDE = PAIR + 1

EPSILON = 1e-12
ROOT_TWO_PI = 0.7978845608028654
CUBIC = ROOT_TWO_PI * 0.044715
F32 = jnp.float32
BF16 = jnp.bfloat16
VMEM_BYTES = 60 << 20
FAR = pl.BlockSpec(memory_space=pl.ANY)


def product(left, right):
    return lax.dot_general(left, right, (((1,), (0,)), ((), ())), preferred_element_type=F32)


def product_turned(left, right):
    return lax.dot_general(left, right, (((1,), (1,)), ((), ())), preferred_element_type=F32)


def product_over_rows(left, right):
    return lax.dot_general(left, right, (((0,), (0,)), ((), ())), preferred_element_type=F32)


def lanes(column):
    return jnp.concatenate([column] * (D // LANES), axis=1)


def rows_of_eight(values):
    return jnp.sum(values.reshape(-1, 8, values.shape[-1]), axis=0)


def average(values):
    return jnp.mean(values, axis=1, keepdims=True)


def norm_back(grad, x_hat, scale, gain):
    q = grad * gain
    return lanes(scale) * (q - average(q) - x_hat * average(q * x_hat))


def whole_block(shape):
    return pl.BlockSpec(shape, lambda c: (0,) * len(shape), pipeline_mode=pl.Buffered(1))


def params():
    return pltpu.CompilerParams(vmem_limit_bytes=VMEM_BYTES)


def cost(flops, transcendentals, size):
    return pl.CostEstimate(flops=flops, transcendentals=transcendentals, bytes_accessed=size)


def scatter(refs, start, value):
    for j, ref in enumerate(refs):
        ref[pl.ds(start, L2, stride=STRIDE), :] = value[:, j * LANES : (j + 1) * LANES]


def gather(refs, block):
    return jnp.concatenate([ref[pl.ds(block * STRIDE, PAIR), :] for ref in refs], axis=1)


def middle_scratch():
    return [pltpu.VMEM((L2 * STRIDE, LANES), F32)] * (D // LANES)


def transform_kernel(
    length_ref, x_ref, short_ref, pair_ref, cos_ref, sin_ref, wide_hbm,
    hat_ref, scale_ref, spec_ref, wide_ref, sem, *middle, group
):
    length = length_ref[0]
    step = pl.program_id(0)
    load = pltpu.make_async_copy(wide_hbm, wide_ref, sem.at[0])

    @pl.when(step == 0)
    def _():
        load.start()

        def first(m, carry):
            spots = L2 * lax.broadcasted_iota(jnp.int32, (L1, D), 0) + m
            x = jnp.where(spots < length, x_ref[m].astype(F32), 0.0).astype(BF16)
            y = product(short_ref[...], x)
            real, imag = y[:L1], y[L1:]
            cosine, sine = lanes(cos_ref[m]), lanes(sin_ref[m])
            turned = (real * cosine - imag * sine, real * sine + imag * cosine)
            for b in range(2):
                for part in range(2):
                    scatter(middle, (b * 2 + part) * L2 + m, turned[part][b * L2 : (b + 1) * L2])
            return carry

        lax.fori_loop(0, L2, first, 0, unroll=4)
        load.wait()

    for j in range(group):
        turned = gather(middle, step * group + j).astype(BF16)
        q = product(pair_ref[...], turned).astype(BF16)
        spec_ref[j * L1 : (j + 1) * L1, :D] = q[:L1]
        spec_ref[j * L1 : (j + 1) * L1, D:] = q[L1:]
    mixed = product(spec_ref[...], wide_ref[...])
    number = lax.broadcasted_iota(jnp.int32, (group * L1, D), 0)
    spots = L2 * (number % L1) + step * group + number // L1
    x = x_ref[pl.ds(step * group, group)].reshape(group * L1, D).astype(F32)
    h = jnp.where(spots < length, x, 0.0) + mixed
    center = h - average(h)
    scale = lax.rsqrt(average(center * center) + EPSILON)
    hat_ref[...] = center * scale
    scale_ref[...] = jnp.broadcast_to(scale, scale_ref.shape)


def transform(length, x, short, pair, cosine, sine, wide, group=8):
    out = lambda width: pl.BlockSpec((group * L1, width), lambda c: (c, 0))
    return pl.pallas_call(
        functools.partial(transform_kernel, group=group),
        grid=(L2 // group,),
        in_specs=[pl.BlockSpec(memory_space=pltpu.SMEM)]
        + [whole_block(values.shape) for values in (x, short, pair, cosine, sine)]
        + [FAR],
        out_specs=[out(D), out(LANES)],
        out_shape=[
            jax.ShapeDtypeStruct((L, D), F32),
            jax.ShapeDtypeStruct((L, LANES), F32),
        ],
        scratch_shapes=[
            pltpu.VMEM((group * L1, 2 * D), BF16),
            pltpu.VMEM((2 * D, D), BF16),
            pltpu.SemaphoreType.DMA((1,)),
        ]
        + middle_scratch(),
        compiler_params=params(),
        cost_estimate=cost(7 << 30, L, 24 << 20),
        name="transform",
    )(length, x, short, pair, cosine, sine, wide)


def back_kernel(
    length_ref, du_ref, hat_ref, scale_ref, short_ref, pair_ref, cos_ref, sin_ref, vec_ref, wide_ref,
    dx_ref, sums_ref, rh_ref, spec_ref, *middle, group
):
    length = length_ref[0]
    step = pl.program_id(0)
    steps = L2 // group

    @pl.when(step == 0)
    def _():
        sums_ref[...] = jnp.zeros_like(sums_ref)

    @pl.when(step < steps)
    def _():
        du = du_ref[...]
        hat = hat_ref[...]
        rh = norm_back(du, hat, scale_ref[...], vec_ref[0:1, :]).astype(BF16)
        rh_ref[pl.ds(pl.multiple_of(step * group * L1, group * L1), group * L1), :] = rh
        sums_ref[0:8, :] += rows_of_eight(du * hat)
        sums_ref[8:16, :] += rows_of_eight(du)
        real = product(rh, wide_ref[:D, :]).astype(BF16)
        imag = product(rh, wide_ref[D:, :]).astype(BF16)
        for j in range(group):
            spec_ref[j, :L1, :] = real[j * L1 : (j + 1) * L1]
            spec_ref[j, L1:, :] = imag[j * L1 : (j + 1) * L1]
            turned = product(pair_ref[...], spec_ref[j]).astype(BF16).astype(F32)
            for b in range(2):
                for part in range(2):
                    start = (b * 2 + part) * L2
                    spot = part * L1 + b * L2 + step * group + j
                    scatter(middle, spot, turned[start : start + L2])

    @pl.when(step >= steps)
    def _():
        def second(i, carry):
            m = (step - steps) * group + i
            turned = gather(middle, m)
            real, imag = turned[:L1], turned[L1:]
            cosine, sine = lanes(cos_ref[m]), lanes(sin_ref[m])
            back = jnp.concatenate(
                [
                    (real * cosine + imag * sine).astype(BF16),
                    (imag * cosine - real * sine).astype(BF16),
                ],
                axis=0,
            )
            rh = rh_ref[pl.ds(pl.multiple_of(m * L1, L1), L1), :].astype(F32)
            dx = rh + product(short_ref[...], back)
            spots = L2 * lax.broadcasted_iota(jnp.int32, (L1, D), 0) + m
            dx_ref[i] = jnp.where(spots < length, dx, 0.0).astype(BF16)
            return carry

        lax.fori_loop(0, group, second, 0, unroll=4)


def transform_back(length, du, hat, scale, short, pair, cosine, sine, vec, wide, group=8):
    steps = L2 // group
    rows = lambda width: pl.BlockSpec((group * L1, width), lambda c: (jnp.minimum(c, steps - 1), 0))
    return pl.pallas_call(
        functools.partial(back_kernel, group=group),
        grid=(2 * steps,),
        in_specs=[pl.BlockSpec(memory_space=pltpu.SMEM), rows(D), rows(D), rows(LANES)]
        + [whole_block(values.shape) for values in (short, pair, cosine, sine, vec, wide)],
        out_specs=[
            pl.BlockSpec((group, L1, D), lambda c: (jnp.maximum(c - steps, 0), 0, 0)),
            pl.BlockSpec((16, D), lambda c: (0, 0)),
        ],
        out_shape=[
            jax.ShapeDtypeStruct((L2, L1, D), BF16),
            jax.ShapeDtypeStruct((16, D), F32),
        ],
        scratch_shapes=[pltpu.VMEM((L, D), BF16), pltpu.VMEM((group, 2 * L1, D), BF16)]
        + middle_scratch(),
        compiler_params=params(),
        cost_estimate=cost(7 << 30, 0, 20 << 20),
        name="transform_back",
    )(length, du, hat, scale, short, pair, cosine, sine, vec, wide)


def fetch_weights(pieces, plan, holder, sems, chunk):
    step = pl.program_id(0)
    copies = [
        pltpu.make_async_copy(
            pieces[number].at[pl.ds(source, rows), :],
            holder.at[pl.ds(target, rows), :],
            sems.at[i],
        )
        for i, (target, number, source, rows) in enumerate(plan)
    ]

    @pl.when(step == 0)
    def _():
        for copy in copies:
            copy.start()

    for number in range(holder.shape[0] // chunk):
        needed = [copy for copy, run in zip(copies, plan) if run[0] // chunk == number]
        if needed:

            @pl.when(step == number)
            def _():
                for copy in needed:
                    copy.wait()


def runs_of(pieces_codes, codes, share):
    runs = []
    for number, own in enumerate(pieces_codes):
        spots = [codes.index(code) for code in own]
        for source, spot in enumerate(spots):
            if source and spot == spots[source - 1] + 1:
                target, piece, start, rows = runs[-1]
                runs[-1] = (target, piece, start, rows + share)
            else:
                runs.append((spot * share, number, source * share, share))
    return tuple(sorted(runs))


def forward_kernel(*refs, tile, counts, chunk, plans):
    first_hat_ref, b_ref, vec_ref = refs[:3]
    split = 3 + sum(counts)
    firsts, seconds = refs[3 : 3 + counts[0]], refs[3 + counts[0] : split]
    act_ref, slope_ref, out_far, hat_far, scale_far, u_far = refs[split : split + 6]
    y_ref, w1_ref, w2_ref, out_ref, hat_ref, scale_ref, u_ref, sem1, sem2, sem3 = refs[split + 6 :]
    parts = 4
    part = u_ref.shape[0] // parts
    tiles = u_ref.shape[0] // tile
    loads, stores = [], []
    for i in range(parts):
        rows = pl.ds(i * part, part)
        pairs = ((u_ref, u_far), (out_ref, out_far), (hat_ref, hat_far), (scale_ref, scale_far))
        loads.append(
            pltpu.make_async_copy(first_hat_ref.at[rows, :], y_ref.at[rows, :], sem3.at[i, 0])
        )
        stores.append(
            [
                pltpu.make_async_copy(near.at[rows, :], far.at[rows, :], sem3.at[i, 1 + j])
                for j, (near, far) in enumerate(pairs)
            ]
        )

    @pl.when(pl.program_id(0) == 0)
    def _():
        for load in loads:
            load.start()

    fetch_weights(firsts, plans[0], w1_ref, sem1, chunk)
    fetch_weights(seconds, plans[1], w2_ref, sem2, chunk)
    here = pl.ds(pl.multiple_of(pl.program_id(0) * chunk, chunk), chunk)

    @pl.when(pl.program_id(0) == 0)
    def _():
        small = 256

        def begin(i, carry):
            rows = pl.ds(pl.multiple_of(i * small, small), small)
            u = y_ref[rows, :] * vec_ref[2:3, :] + vec_ref[3:4, :]
            u_ref[rows, :] = u.astype(BF16)
            y_ref[rows, :] = u + vec_ref[4:5, :]
            return carry

        for i in range(parts):
            loads[i].wait()
            lax.fori_loop(i * part // small, (i + 1) * part // small, begin, 0)
            stores[i][0].start()


    def step(i, carry):
        rows = pl.ds(pl.multiple_of(i * tile, tile), tile)
        z = product_turned(u_ref[rows, :], w1_ref[here, :]) + b_ref[...]
        square = z * z
        t = jnp.tanh(z * (ROOT_TWO_PI + CUBIC * square))
        half = 0.5 + 0.5 * t
        a = z * half
        low = a.astype(BF16)
        act_ref[rows, :] = low
        slope = half + (a - a * t) * (ROOT_TWO_PI + (3.0 * CUBIC) * square)
        slope_ref[rows, :] = slope.astype(BF16)
        y_ref[rows, :] += product(low, w2_ref[here, :])
        return carry

    lax.fori_loop(0, tiles, step, 0)

    @pl.when(pl.program_id(0) == pl.num_programs(0) - 1)
    def _():
        small = 256

        def finish(i, carry):
            rows = pl.ds(pl.multiple_of(i * small, small), small)
            y = y_ref[rows, :]
            center = y - average(y)
            scale = lax.rsqrt(average(center * center) + EPSILON)
            hat = center * scale
            out_ref[rows, :] = (hat * vec_ref[0:1, :] + vec_ref[1:2, :]).astype(BF16)
            hat_ref[rows, :] = hat.astype(BF16)
            scale_ref[rows, :] = jnp.broadcast_to(scale, (small, LANES))
            return carry

        for i in range(parts):
            lax.fori_loop(i * part // small, (i + 1) * part // small, finish, 0)
            for copy in stores[i][1:]:
                copy.start()
        for store in stores:
            for copy in store:
                copy.wait()


def feed_forward(hat, b, vec, firsts, seconds, plans, chunk=1024, tile=1024):
    tokens, width = hat.shape
    counts = (len(firsts), len(seconds))
    units = b.shape[1]
    acts = lambda: pl.BlockSpec((tokens, chunk), lambda c: (0, c))
    return pl.pallas_call(
        functools.partial(forward_kernel, tile=tile, counts=counts, chunk=chunk, plans=plans),
        grid=(units // chunk,),
        in_specs=[
            FAR,
            pl.BlockSpec((1, chunk), lambda c: (0, c)),
            whole_block(vec.shape),
        ]
        + [FAR] * sum(counts),
        out_specs=[acts(), acts()] + [FAR] * 4,
        out_shape=[
            jax.ShapeDtypeStruct((tokens, units), BF16),
            jax.ShapeDtypeStruct((tokens, units), BF16),
            jax.ShapeDtypeStruct((tokens, width), BF16),
            jax.ShapeDtypeStruct((tokens, width), BF16),
            jax.ShapeDtypeStruct((tokens, LANES), F32),
            jax.ShapeDtypeStruct((tokens, width), BF16),
        ],
        scratch_shapes=[
            pltpu.VMEM((tokens, width), F32),
            pltpu.VMEM((units, width), BF16),
            pltpu.VMEM((units, width), BF16),
            pltpu.VMEM((tokens, width), BF16),
            pltpu.VMEM((tokens, width), BF16),
            pltpu.VMEM((tokens, LANES), F32),
            pltpu.VMEM((tokens, width), BF16),
            pltpu.SemaphoreType.DMA((len(plans[0]),)),
            pltpu.SemaphoreType.DMA((len(plans[1]),)),
            pltpu.SemaphoreType.DMA((4, 5)),
        ],
        compiler_params=params(),
        cost_estimate=cost(4 * tokens * units * width, tokens * units, 50 << 20),
        name="feed_forward",
    )(hat, b, vec, *firsts, *seconds)


def backward_kernel(*refs, tile, counts, chunk, plans):
    g_far, hat_far, scale_far, u_far, vec_ref, act_ref, slope_ref = refs[:7]
    split = 7 + sum(counts)
    firsts, seconds = refs[7 : 7 + counts[0]], refs[7 + counts[0] : split]
    keep1_ref, keep2_ref, send1_ref, send2_ref, db_ref, du_far, sums_ref = refs[split : split + 7]
    e_ref, w1_ref, w2_ref, f_ref, g_ref, hat_ref, scale_ref, u_ref, du_ref = refs[
        split + 7 : split + 16
    ]
    sem1, sem2, sem3, sem4 = refs[split + 16 :]
    parts = 4
    part = u_ref.shape[0] // parts
    loads = []
    for i in range(parts):
        rows = pl.ds(i * part, part)
        loads.append(
            [
                pltpu.make_async_copy(far.at[rows, :], near.at[rows, :], sem3.at[i, j])
                for j, (far, near) in enumerate(
                    ((g_far, g_ref), (hat_far, hat_ref), (scale_far, scale_ref))
                )
            ]
        )
    load_u = pltpu.make_async_copy(u_far, u_ref, sem4.at[0])
    store_du = pltpu.make_async_copy(du_ref, du_far, sem4.at[1])

    @pl.when(pl.program_id(0) == 0)
    def _():
        for load in loads:
            for copy in load:
                copy.start()

    fetch_weights(seconds, plans[1], w2_ref, sem2, chunk)
    fetch_weights(firsts, plans[0], w1_ref, sem1, chunk)
    here = pl.ds(pl.multiple_of(pl.program_id(0) * chunk, chunk), chunk)

    @pl.when(pl.program_id(0) == 0)
    def _():
        small = 256
        sums_ref[...] = jnp.zeros_like(sums_ref)

        def begin(i, carry):
            rows = pl.ds(pl.multiple_of(i * small, small), small)
            g = g_ref[rows, :].astype(F32)
            hat = hat_ref[rows, :].astype(F32)
            dy = norm_back(g, hat, scale_ref[rows, :], vec_ref[0:1, :])
            du_ref[rows, :] = dy
            e_ref[rows, :] = dy.astype(BF16)
            sums_ref[0:8, :] += rows_of_eight(dy)
            sums_ref[8:16, :] += rows_of_eight(g * hat)
            sums_ref[16:24, :] += rows_of_eight(g)
            return carry

        load_u.start()
        for i in range(parts):
            for copy in loads[i]:
                copy.wait()
            lax.fori_loop(i * part // small, (i + 1) * part // small, begin, 0)
        load_u.wait()


    def step(i, db):
        rows = pl.ds(pl.multiple_of(i * tile, tile), tile)
        dz = product_turned(e_ref[rows, :], w2_ref[here, :]) * slope_ref[rows, :].astype(F32)
        low = dz.astype(BF16)
        f_ref[rows, :] = low
        du_ref[rows, :] += product(low, w1_ref[here, :])
        return db + rows_of_eight(dz)

    db = lax.fori_loop(0, u_ref.shape[0] // tile, step, jnp.zeros((8, chunk), F32))
    db_ref[...] = jnp.sum(db, axis=0, keepdims=True)

    @pl.when(pl.program_id(0) == pl.num_programs(0) - 1)
    def _():
        store_du.start()

    dw2 = product_over_rows(act_ref[...], e_ref[...]).astype(BF16)
    dw1 = product_over_rows(f_ref[...], u_ref[...]).astype(BF16)
    half = pl.num_programs(0) // 2

    @pl.when(pl.program_id(0) < half)
    def _():
        keep1_ref[...] = dw1
        keep2_ref[...] = dw2

    @pl.when(pl.program_id(0) >= half)
    def _():
        send1_ref[...] = dw1
        send2_ref[...] = dw2

    @pl.when(pl.program_id(0) == pl.num_programs(0) - 1)
    def _():
        store_du.wait()


def feed_backward(
    g, hat, scale, vec, u, act, slope, firsts, seconds, plans, chunk=512, tile=2048
):
    tokens, width = u.shape
    counts = (len(firsts), len(seconds))
    units = act.shape[1]
    half = units // chunk // 2
    acts = lambda: pl.BlockSpec((tokens, chunk), lambda c: (0, c))
    keep = lambda: pl.BlockSpec((chunk, width), lambda c: (jnp.minimum(c, half - 1), 0))
    send = lambda: pl.BlockSpec((chunk, width), lambda c: (jnp.maximum(c - half, 0), 0))
    grads = jax.ShapeDtypeStruct((units // 2, width), BF16)
    return pl.pallas_call(
        functools.partial(backward_kernel, tile=tile, counts=counts, chunk=chunk, plans=plans),
        grid=(units // chunk,),
        in_specs=[FAR] * 4
        + [whole_block(vec.shape), acts(), acts()]
        + [FAR] * sum(counts),
        out_specs=[
            keep(),
            keep(),
            send(),
            send(),
            pl.BlockSpec((1, chunk), lambda c: (0, c)),
            FAR,
            whole_block((24, width)),
        ],
        out_shape=[grads] * 4
        + [
            jax.ShapeDtypeStruct((1, units), F32),
            jax.ShapeDtypeStruct((tokens, width), F32),
            jax.ShapeDtypeStruct((24, width), F32),
        ],
        scratch_shapes=[
            pltpu.VMEM((tokens, width), BF16),
            pltpu.VMEM((units, width), BF16),
            pltpu.VMEM((units, width), BF16),
            pltpu.VMEM((tokens, chunk), BF16),
            pltpu.VMEM((tokens, width), BF16),
            pltpu.VMEM((tokens, width), BF16),
            pltpu.VMEM((tokens, LANES), F32),
            pltpu.VMEM((tokens, width), BF16),
            pltpu.VMEM((tokens, width), F32),
            pltpu.SemaphoreType.DMA((len(plans[0]),)),
            pltpu.SemaphoreType.DMA((len(plans[1]),)),
            pltpu.SemaphoreType.DMA((4, 3)),
            pltpu.SemaphoreType.DMA((2,)),
        ],
        compiler_params=params(),
        cost_estimate=cost(8 * tokens * units * width, 0, 60 << 20),
        name="feed_backward",
    )(g, hat, scale, u, vec, act, slope, *firsts, *seconds)


def table_pair(points):
    numbers = jnp.arange(points, dtype=jnp.int32)
    coarse = 32 * jnp.arange(points // 32, dtype=jnp.int32)
    fine = jnp.arange(32, dtype=jnp.int32)

    def waves(rows):
        angles = (rows[:, None] * numbers[None, :] % points).astype(F32) * (2.0 * math.pi / points)
        return jnp.cos(angles), jnp.sin(angles)

    factor = 1.0 / math.sqrt(points)
    if points <= 64:
        cosine, sine = waves(numbers)
    else:
        coarse_cos, coarse_sin = waves(coarse)
        fine_cos, fine_sin = waves(fine)
        coarse_cos, coarse_sin, fine_cos, fine_sin = lax.optimization_barrier(
            (coarse_cos, coarse_sin, fine_cos, fine_sin)
        )
        coarse_cos, coarse_sin = coarse_cos[:, None], coarse_sin[:, None]
        fine_cos, fine_sin = fine_cos[None], fine_sin[None]
        cosine = (coarse_cos * fine_cos - coarse_sin * fine_sin).reshape(points, points)
        sine = (coarse_sin * fine_cos + coarse_cos * fine_sin).reshape(points, points)
    return (cosine * factor).astype(BF16), (sine * factor).astype(BF16)


def twiddles():
    row_index = jnp.arange(L1, dtype=jnp.int32)[None, :]
    col_index = jnp.arange(L2, dtype=jnp.int32)[:, None]
    angles = (row_index * col_index % L).astype(F32) * (2.0 * math.pi / L)
    wave = jnp.cos(angles), jnp.sin(angles)
    return [jnp.broadcast_to(values[:, :, None], (L2, L1, LANES)) for values in wave]


def swap(values, step):
    axis, mask = step
    size = lax.axis_size(axis)
    return lax.ppermute(values, axis, [(i, i ^ mask) for i in range(size)])


def bits(size):
    masks = []
    mask = size // 2
    while mask >= 1:
        masks.append(mask)
        mask //= 2
    return masks


def widen(held, step):
    return jnp.concatenate([held, swap(held, step)], axis=0)


def widen_codes(codes, steps, groups):
    for axis, mask in steps:
        code = mask if axis == "seq" else mask * groups
        codes = codes + [held ^ code for held in codes]
    return codes


def spread(pieces, steps):
    for step in steps:
        pieces = pieces + [swap(piece, step) for piece in pieces]
    return pieces


def spread_core(pieces, step_core):
    return pieces + [swap(piece, step_core) for piece in pieces]


def pick(addend, extra):
    values, names, fixed = addend
    chosen = {**fixed, **extra}
    return values[tuple(chosen.get(name, slice(None)) for name in names)]


def total(addends, extra={}):
    parts = [pick(addend, extra) for addend in addends]
    return sum(parts[1:], parts[0].astype(F32))


def settle(addends, send, step):
    values, names, fixed = addends[-1]
    rest = [name for name in names if name not in fixed and name != step]
    kept = [(held, order, {**gone, step: 0}) for held, order, gone in addends]
    return kept + [(swap(send, step), rest, {})]


def fold(addends, step, kind):
    return settle(addends, total(addends, {step: 1}).astype(kind), step)


def after(addends, *others):
    values, names, fixed = addends[-1]
    results = lax.optimization_barrier((values,) + others)
    return (addends[:-1] + [(results[0], names, fixed)],) + tuple(results[1:])


def arrange(rows):
    return with_layout_constraint(rows.transpose(0, 2, 1, 3), Layout(major_to_minor=(0, 1, 2, 3)))


def exchange(rows):
    order = Layout(major_to_minor=(0, 1, 2, 3))
    rows = with_layout_constraint(rows, order)
    rows = lax.all_to_all(rows, "seq", split_axis=0, concat_axis=0, tiled=True)
    return with_layout_constraint(rows, order)


def body(tokens, lengths, labels, picked, cotangent, w_in, b_in, w_out, shifts, norm_gains):
    groups = lax.axis_size("seq")
    me = lax.axis_index("seq")
    here = lax.axis_index("batch") * groups + me
    columns = tokens.shape[2]
    share = w_in.shape[2]
    part = shifts.shape[2]
    blocks = groups * lax.axis_size("batch")

    masks = bits(groups)[:-1]
    steps_plane = [("seq", mask) for mask in masks[:1] + masks[:0:-1]]
    steps_seq = [("seq", mask) for mask in masks[::-1]]
    steps_batch = [("batch", mask) for mask in bits(lax.axis_size("batch"))]
    step_core = ("seq", 1)
    numbers = jnp.arange(blocks, dtype=jnp.int32)

    codes = widen_codes([0], steps_plane + steps_batch + [step_core], groups)
    owner = jnp.array(codes, dtype=jnp.int32) ^ here
    one_hot = (owner[:, None] == numbers[None, :]).astype(F32)

    wide_cos, wide_sin = table_pair(D)
    wide = jnp.concatenate([wide_cos, -wide_sin], axis=0)
    twiddle_cos, twiddle_sin = twiddles()
    short_cos, short_sin = table_pair(L1)
    long_cos, long_sin = table_pair(L2)
    short_table = jnp.concatenate([short_cos, short_sin], axis=0)
    long_table = jnp.stack([jnp.stack([long_cos, -long_sin]), jnp.stack([long_sin, long_cos])])
    both = jnp.eye(2, dtype=BF16)
    pair_table = jnp.einsum("qukm,bc->qkbcum", long_table, both).reshape(4 * L2, 4 * L2)

    length = lax.dynamic_slice_in_dim(lengths, me, 1)
    small = jnp.concatenate([b_in[0], shifts[0].reshape(-1), norm_gains[0].reshape(-1)])
    small = small.astype(F32)[None]
    first_held = w_in[0].T[None]
    second_held = w_out[0][None]
    tokens_late = arrange(tokens)
    steps_second = list(steps_plane)
    if len(steps_plane) == 3 and share % 8 == 0:
        steps_second = [steps_plane[0], steps_plane[2], steps_plane[1]]
    for number, step in enumerate(steps_plane[:-1]):
        first_held = widen(first_held, step)
        second_held = widen(second_held, steps_second[number])
        small = widen(small, step)
        if number == 0:
            tokens_late, small, first_held, second_held = lax.optimization_barrier(
                (tokens_late, small, first_held, second_held)
            )
            x_all = exchange(tokens_late)
    early = (wide, twiddle_cos, twiddle_sin, short_table, pair_table, arrange(cotangent))
    small, first_held, second_held, early = lax.optimization_barrier(
        (small, first_held, second_held, early)
    )
    wide, twiddle_cos, twiddle_sin, short_table, pair_table, late_cotangent = early
    first_held = widen(first_held, steps_plane[-1])
    seconds, codes_second = [], []
    base = widen_codes([0], steps_second[:-1], groups)
    for piece, turn in zip(spread([second_held], steps_batch), widen_codes([0], steps_batch, groups)):
        seconds += [piece, swap(piece, steps_second[-1])]
        codes_second += [[code ^ turn for code in base]]
        codes_second += [[code ^ turn ^ steps_second[-1][1] for code in base]]
    steps_small = steps_plane[:-1] + steps_batch + [step_core] + steps_plane[-1:]
    small_codes = widen_codes([0], steps_small, groups)
    for step in steps_batch + [step_core]:
        small = widen(small, step)
    small, first_held = lax.optimization_barrier((small, first_held))
    small = widen(small, steps_plane[-1])
    places = jnp.array([small_codes.index(code) for code in codes], dtype=jnp.int32)
    place_hot = (places[:, None] == numbers[None, :]).astype(F32)
    small = jnp.sum(place_hot[:, :, None] * small[None], axis=1)
    b_first = small[:, :share].reshape(1, blocks * share)
    rows = jnp.sum(one_hot[:, :, None] * small[:, None, share:], axis=0)
    rows = rows.reshape(blocks, 5, part).transpose(1, 0, 2).reshape(5, D)
    shifts_f = rows[:3]
    gains_f = rows[3:]
    blank = jnp.zeros((3, D), F32)
    vec = jnp.concatenate(
        [gains_f[1:2], shifts_f[2:3], gains_f[0:1], shifts_f[1:2], shifts_f[0:1], blank]
    )
    vec_one = vec[2:]
    vec_one = jnp.concatenate([vec_one, blank[:2]])
    base = widen_codes([0], steps_plane, groups)
    half = len(base) // 2
    turn = steps_batch[0][1] * groups
    firsts = [first_held] + [swap(first_held[k : k + half], steps_batch[0]) for k in (0, half)]
    codes_first = [base] + [[code ^ turn for code in base[k : k + half]] for k in (0, half)]
    x_all, late_cotangent, firsts[0], firsts[1], seconds, vec, vec_one, b_first = (
        lax.optimization_barrier(
            (x_all, late_cotangent, firsts[0], firsts[1], seconds, vec, vec_one, b_first)
        )
    )
    g_all = exchange(late_cotangent)
    for step in steps_batch[1:]:
        firsts = spread(firsts, [step])
        codes_first = codes_first + [
            [code ^ step[1] * groups for code in own] for own in codes_first
        ]
    x_rows = x_all.reshape(L2, L1, D)
    hat_one, scale_one = transform(
        length, x_rows, short_table, pair_table, twiddle_cos, twiddle_sin, wide
    )
    hat_one, firsts, seconds = lax.optimization_barrier((hat_one, firsts, seconds))
    plans = tuple(
        runs_of(own + [[code ^ 1 for code in held] for held in own], codes, share)
        for own in (codes_first, codes_second)
    )
    flat = lambda pieces: [piece.reshape(-1, D) for piece in spread_core(pieces, step_core)]
    firsts, seconds = flat(firsts), flat(seconds)
    act, slope, layer_out, hat_two, scale_two, u = feed_forward(
        hat_one, b_first, vec, firsts, seconds, plans
    )
    out_rows = exchange(layer_out.reshape(groups, columns, L1, D))

    keep_first, keep_second, send_first, send_second, grad_b_first, grad_u, sums_two = feed_backward(
        g_all.reshape(L, D), hat_two, scale_two, vec, u, act, slope, firsts, seconds, plans
    )
    names = steps_batch[::-1] + steps_plane[::-1]
    shape = (2,) * len(names) + (share,)
    came_first = swap(send_first, step_core)
    came_second = swap(send_second, step_core)
    grad_x, sums_one = transform_back(
        length, grad_u, hat_one, scale_one, short_table.T, pair_table.T,
        twiddle_cos, twiddle_sin, vec_one, wide
    )
    grad_x, came_first, came_second, out_rows = lax.optimization_barrier(
        (grad_x, came_first, came_second, out_rows)
    )
    grad_first, grad_second = [
        [(values.reshape(shape + (D,)), names, {}) for values in pair]
        for pair in ((keep_first, came_first), (keep_second, came_second))
    ]
    grad_x = grad_x.reshape(groups, columns, L1, D)
    input_grad = arrange(exchange(grad_x))

    shift_of = jnp.arange(columns, dtype=jnp.int32) + me * columns
    place_of = L2 * jnp.arange(L1, dtype=jnp.int32)[None, :] + shift_of[:, None]
    for step in steps_batch[::-1]:
        grad_first = fold(grad_first, step, BF16)
        send = total(grad_second, {step: 1}).astype(BF16)
        send, out_rows = lax.optimization_barrier((send, out_rows))
        grad_second = settle(grad_second, send, step)
    current = arrange(out_rows)
    grad_first, out_rows, current, sums_one, sums_two, grad_b_first = after(
        grad_first, out_rows, current, sums_one, sums_two, grad_b_first
    )
    logits = out_rows.astype(F32)
    highest = jnp.max(logits, axis=-1, keepdims=True)
    powers = jnp.exp(logits - highest)
    denominator = jnp.sum(powers, axis=-1)
    features = jnp.arange(D, dtype=jnp.int32)
    label_rows = labels.transpose(0, 2, 1)
    top = jnp.sum(jnp.where(features == label_rows[..., None], powers, 0.0), axis=-1)
    counted = (picked.transpose(0, 2, 1) > 0) & (place_of[None] < lengths[:, None, None])
    weight = jnp.where(counted, 1.0, 0.0)
    sums = jnp.stack([jnp.sum(weight * (top / denominator)), jnp.sum(weight)])

    sums_two = jnp.sum(sums_two.reshape(3, 8, D), axis=1)
    sums_one = jnp.sum(sums_one.reshape(2, 8, D), axis=1)
    norms = jnp.stack([sums_two[0], sums_one[1], sums_two[2], sums_one[0], sums_two[1]])
    norms = norms.reshape(5, blocks, part).transpose(1, 0, 2).reshape(blocks, 5 * part)
    norms = jnp.sum(one_hot[:, :, None] * norms[None], axis=1)
    sums = jnp.broadcast_to(sums[None], (blocks, 2))
    small_grads = jnp.concatenate([grad_b_first.reshape(blocks, share), norms, sums], axis=1)
    half = blocks // 2
    arrived = swap(small_grads[half:], step_core)
    small = [
        (values.reshape(shape[:-1] + (-1,)), names, {}) for values in (small_grads[:half], arrived)
    ]
    for step in steps_batch[::-1]:
        small = fold(small, step, F32)
    for step in steps_seq:
        grad_first = fold(grad_first, step, BF16)
    small, latest = after(small, grad_second[-1][0])
    grad_second = grad_second[:-1] + [(latest,) + grad_second[-1][1:]]
    for number, step in enumerate(steps_seq):
        grad_second = fold(grad_second, step, BF16)
        if number == 1:
            small, input_grad = after(small, input_grad)
        small = fold(small, step, F32)
    small_grads, grad_first, grad_second = total(small), total(grad_first), total(grad_second)
    norms = small_grads[share:-2].reshape(5, part)
    match_rate = D * small_grads[-2] / jnp.maximum(small_grads[-1], 1.0)
    return (
        current,
        input_grad,
        grad_first.T[None],
        small_grads[:share][None],
        grad_second[None],
        norms[:3][None],
        norms[3:][None],
        match_rate,
    )


def solution(mesh):
    in_specs = (
        P("batch", None, "seq", None),
        P("batch"),
        P("batch", None, "seq"),
        P("batch", None, "seq"),
        P("batch", None, "seq", None),
        P(None, None, ("batch", "seq")),
        P(None, ("batch", "seq")),
        P(None, ("batch", "seq"), None),
        P(None, None, ("batch", "seq")),
        P(None, None, ("batch", "seq")),
    )
    out_specs = (
        P("batch", None, "seq", None),
        P("batch", None, "seq", None),
        P(None, None, ("batch", "seq")),
        P(None, ("batch", "seq")),
        P(None, ("batch", "seq"), None),
        P(None, None, ("batch", "seq")),
        P(None, None, ("batch", "seq")),
        P(),
    )
    return jax.shard_map(body, mesh=mesh, in_specs=in_specs, out_specs=out_specs, check_vma=False)
```

```python
import functools
import math

import jax
import jax.numpy as jnp
from jax import lax
from jax.experimental import pallas as pl
from jax.experimental.layout import Layout, with_layout_constraint
from jax.experimental.pallas import tpu as pltpu
from jax.sharding import PartitionSpec as P

D = 768
L1 = 64
L2 = 32
L = 2048
LANES = 128
PAIR = 4 * L2
STRIDE = PAIR + 1

EPSILON = 1e-12
ROOT_TWO_PI = 0.7978845608028654
CUBIC = ROOT_TWO_PI * 0.044715
F32 = jnp.float32
BF16 = jnp.bfloat16
VMEM_BYTES = 60 << 20
FAR = pl.BlockSpec(memory_space=pl.ANY)


def product(left, right):
    return lax.dot_general(left, right, (((1,), (0,)), ((), ())), preferred_element_type=F32)


def product_turned(left, right):
    return lax.dot_general(left, right, (((1,), (1,)), ((), ())), preferred_element_type=F32)


def product_over_rows(left, right):
    return lax.dot_general(left, right, (((0,), (0,)), ((), ())), preferred_element_type=F32)


def lanes(column):
    return jnp.concatenate([column] * (D // LANES), axis=1)


def rows_of_eight(values):
    return jnp.sum(values.reshape(-1, 8, values.shape[-1]), axis=0)


def average(values):
    return jnp.mean(values, axis=1, keepdims=True)


def norm_back(grad, x_hat, scale, gain):
    q = grad * gain
    return lanes(scale) * (q - average(q) - x_hat * average(q * x_hat))


def whole_block(shape):
    return pl.BlockSpec(shape, lambda c: (0,) * len(shape), pipeline_mode=pl.Buffered(1))


def params():
    return pltpu.CompilerParams(vmem_limit_bytes=VMEM_BYTES)


def cost(flops, transcendentals, size):
    return pl.CostEstimate(flops=flops, transcendentals=transcendentals, bytes_accessed=size)


def scatter(refs, start, value):
    for j, ref in enumerate(refs):
        ref[pl.ds(start, L2, stride=STRIDE), :] = value[:, j * LANES : (j + 1) * LANES]


def gather(refs, block):
    return jnp.concatenate([ref[pl.ds(block * STRIDE, PAIR), :] for ref in refs], axis=1)


def middle_scratch():
    return [pltpu.VMEM((L2 * STRIDE, LANES), F32)] * (D // LANES)


def transform_kernel(
    length_ref, x_ref, short_ref, pair_ref, cos_ref, sin_ref, wide_hbm,
    hat_ref, scale_ref, spec_ref, wide_ref, sem, *middle, group
):
    length = length_ref[0]
    step = pl.program_id(0)
    load = pltpu.make_async_copy(wide_hbm, wide_ref, sem.at[0])

    @pl.when(step == 0)
    def _():
        load.start()

        def first(m, carry):
            spots = L2 * lax.broadcasted_iota(jnp.int32, (L1, D), 0) + m
            x = jnp.where(spots < length, x_ref[m].astype(F32), 0.0).astype(BF16)
            y = product(short_ref[...], x)
            real, imag = y[:L1], y[L1:]
            cosine, sine = lanes(cos_ref[m]), lanes(sin_ref[m])
            turned = (real * cosine - imag * sine, real * sine + imag * cosine)
            for b in range(2):
                for part in range(2):
                    scatter(middle, (b * 2 + part) * L2 + m, turned[part][b * L2 : (b + 1) * L2])
            return carry

        lax.fori_loop(0, L2, first, 0, unroll=4)
        load.wait()

    for j in range(group):
        turned = gather(middle, step * group + j).astype(BF16)
        q = product(pair_ref[...], turned).astype(BF16)
        spec_ref[j * L1 : (j + 1) * L1, :D] = q[:L1]
        spec_ref[j * L1 : (j + 1) * L1, D:] = q[L1:]
    mixed = product(spec_ref[...], wide_ref[...])
    number = lax.broadcasted_iota(jnp.int32, (group * L1, D), 0)
    spots = L2 * (number % L1) + step * group + number // L1
    x = x_ref[pl.ds(step * group, group)].reshape(group * L1, D).astype(F32)
    h = jnp.where(spots < length, x, 0.0) + mixed
    center = h - average(h)
    scale = lax.rsqrt(average(center * center) + EPSILON)
    hat_ref[...] = center * scale
    scale_ref[...] = jnp.broadcast_to(scale, scale_ref.shape)


def transform(length, x, short, pair, cosine, sine, wide, group=8):
    out = lambda width: pl.BlockSpec((group * L1, width), lambda c: (c, 0))
    return pl.pallas_call(
        functools.partial(transform_kernel, group=group),
        grid=(L2 // group,),
        in_specs=[pl.BlockSpec(memory_space=pltpu.SMEM)]
        + [whole_block(values.shape) for values in (x, short, pair, cosine, sine)]
        + [FAR],
        out_specs=[out(D), out(LANES)],
        out_shape=[
            jax.ShapeDtypeStruct((L, D), F32),
            jax.ShapeDtypeStruct((L, LANES), F32),
        ],
        scratch_shapes=[
            pltpu.VMEM((group * L1, 2 * D), BF16),
            pltpu.VMEM((2 * D, D), BF16),
            pltpu.SemaphoreType.DMA((1,)),
        ]
        + middle_scratch(),
        compiler_params=params(),
        cost_estimate=cost(7 << 30, L, 24 << 20),
        name="transform",
    )(length, x, short, pair, cosine, sine, wide)


def back_kernel(
    length_ref, du_ref, hat_ref, scale_ref, short_ref, pair_ref, cos_ref, sin_ref, vec_ref, wide_ref,
    dx_ref, sums_ref, rh_ref, spec_ref, *middle, group
):
    length = length_ref[0]
    step = pl.program_id(0)
    steps = L2 // group

    @pl.when(step == 0)
    def _():
        sums_ref[...] = jnp.zeros_like(sums_ref)

    @pl.when(step < steps)
    def _():
        du = du_ref[...]
        hat = hat_ref[...]
        rh = norm_back(du, hat, scale_ref[...], vec_ref[0:1, :]).astype(BF16)
        rh_ref[pl.ds(pl.multiple_of(step * group * L1, group * L1), group * L1), :] = rh
        sums_ref[0:8, :] += rows_of_eight(du * hat)
        sums_ref[8:16, :] += rows_of_eight(du)
        real = product(rh, wide_ref[:D, :]).astype(BF16)
        imag = product(rh, wide_ref[D:, :]).astype(BF16)
        for j in range(group):
            spec_ref[j, :L1, :] = real[j * L1 : (j + 1) * L1]
            spec_ref[j, L1:, :] = imag[j * L1 : (j + 1) * L1]
            turned = product(pair_ref[...], spec_ref[j]).astype(BF16).astype(F32)
            for b in range(2):
                for part in range(2):
                    start = (b * 2 + part) * L2
                    spot = part * L1 + b * L2 + step * group + j
                    scatter(middle, spot, turned[start : start + L2])

    @pl.when(step >= steps)
    def _():
        def second(i, carry):
            m = (step - steps) * group + i
            turned = gather(middle, m)
            real, imag = turned[:L1], turned[L1:]
            cosine, sine = lanes(cos_ref[m]), lanes(sin_ref[m])
            back = jnp.concatenate(
                [
                    (real * cosine + imag * sine).astype(BF16),
                    (imag * cosine - real * sine).astype(BF16),
                ],
                axis=0,
            )
            rh = rh_ref[pl.ds(pl.multiple_of(m * L1, L1), L1), :].astype(F32)
            dx = rh + product(short_ref[...], back)
            spots = L2 * lax.broadcasted_iota(jnp.int32, (L1, D), 0) + m
            dx_ref[i] = jnp.where(spots < length, dx, 0.0).astype(BF16)
            return carry

        lax.fori_loop(0, group, second, 0, unroll=4)


def transform_back(length, du, hat, scale, short, pair, cosine, sine, vec, wide, group=8):
    steps = L2 // group
    rows = lambda width: pl.BlockSpec((group * L1, width), lambda c: (jnp.minimum(c, steps - 1), 0))
    return pl.pallas_call(
        functools.partial(back_kernel, group=group),
        grid=(2 * steps,),
        in_specs=[pl.BlockSpec(memory_space=pltpu.SMEM), rows(D), rows(D), rows(LANES)]
        + [whole_block(values.shape) for values in (short, pair, cosine, sine, vec, wide)],
        out_specs=[
            pl.BlockSpec((group, L1, D), lambda c: (jnp.maximum(c - steps, 0), 0, 0)),
            pl.BlockSpec((16, D), lambda c: (0, 0)),
        ],
        out_shape=[
            jax.ShapeDtypeStruct((L2, L1, D), BF16),
            jax.ShapeDtypeStruct((16, D), F32),
        ],
        scratch_shapes=[pltpu.VMEM((L, D), BF16), pltpu.VMEM((group, 2 * L1, D), BF16)]
        + middle_scratch(),
        compiler_params=params(),
        cost_estimate=cost(7 << 30, 0, 20 << 20),
        name="transform_back",
    )(length, du, hat, scale, short, pair, cosine, sine, vec, wide)


def fetch_weights(pieces, plan, holder, sems, chunk):
    step = pl.program_id(0)
    copies = [
        pltpu.make_async_copy(
            pieces[number].at[pl.ds(source, rows), :],
            holder.at[pl.ds(target, rows), :],
            sems.at[i],
        )
        for i, (target, number, source, rows) in enumerate(plan)
    ]

    @pl.when(step == 0)
    def _():
        for copy in copies:
            copy.start()

    for number in range(holder.shape[0] // chunk):
        needed = [copy for copy, run in zip(copies, plan) if run[0] // chunk == number]
        if needed:

            @pl.when(step == number)
            def _():
                for copy in needed:
                    copy.wait()


def runs_of(pieces_codes, codes, share):
    runs = []
    for number, own in enumerate(pieces_codes):
        spots = [codes.index(code) for code in own]
        for source, spot in enumerate(spots):
            if source and spot == spots[source - 1] + 1:
                target, piece, start, rows = runs[-1]
                runs[-1] = (target, piece, start, rows + share)
            else:
                runs.append((spot * share, number, source * share, share))
    return tuple(sorted(runs))


def forward_kernel(*refs, tile, counts, chunk, plans):
    first_hat_ref, b_ref, vec_ref = refs[:3]
    split = 3 + sum(counts)
    firsts, seconds = refs[3 : 3 + counts[0]], refs[3 + counts[0] : split]
    act_ref, slope_ref, out_far, hat_far, scale_far, u_far = refs[split : split + 6]
    y_ref, w1_ref, w2_ref, out_ref, hat_ref, scale_ref, u_ref, sem1, sem2, sem3 = refs[split + 6 :]
    parts = 4
    part = u_ref.shape[0] // parts
    tiles = u_ref.shape[0] // tile
    loads, stores = [], []
    for i in range(parts):
        rows = pl.ds(i * part, part)
        pairs = ((u_ref, u_far), (out_ref, out_far), (hat_ref, hat_far), (scale_ref, scale_far))
        loads.append(
            pltpu.make_async_copy(first_hat_ref.at[rows, :], y_ref.at[rows, :], sem3.at[i, 0])
        )
        stores.append(
            [
                pltpu.make_async_copy(near.at[rows, :], far.at[rows, :], sem3.at[i, 1 + j])
                for j, (near, far) in enumerate(pairs)
            ]
        )

    @pl.when(pl.program_id(0) == 0)
    def _():
        for load in loads:
            load.start()

    fetch_weights(firsts, plans[0], w1_ref, sem1, chunk)
    fetch_weights(seconds, plans[1], w2_ref, sem2, chunk)
    here = pl.ds(pl.multiple_of(pl.program_id(0) * chunk, chunk), chunk)

    @pl.when(pl.program_id(0) == 0)
    def _():
        small = 256

        def begin(i, carry):
            rows = pl.ds(pl.multiple_of(i * small, small), small)
            u = y_ref[rows, :] * vec_ref[2:3, :] + vec_ref[3:4, :]
            u_ref[rows, :] = u.astype(BF16)
            y_ref[rows, :] = u + vec_ref[4:5, :]
            return carry

        for i in range(parts):
            loads[i].wait()
            lax.fori_loop(i * part // small, (i + 1) * part // small, begin, 0)
            stores[i][0].start()


    def step(i, carry):
        rows = pl.ds(pl.multiple_of(i * tile, tile), tile)
        z = product_turned(u_ref[rows, :], w1_ref[here, :]) + b_ref[...]
        square = z * z
        t = jnp.tanh(z * (ROOT_TWO_PI + CUBIC * square))
        half = 0.5 + 0.5 * t
        a = z * half
        low = a.astype(BF16)
        act_ref[rows, :] = low
        slope = half + (a - a * t) * (ROOT_TWO_PI + (3.0 * CUBIC) * square)
        slope_ref[rows, :] = slope.astype(BF16)
        y_ref[rows, :] += product(low, w2_ref[here, :])
        return carry

    lax.fori_loop(0, tiles, step, 0)

    @pl.when(pl.program_id(0) == pl.num_programs(0) - 1)
    def _():
        small = 256

        def finish(i, carry):
            rows = pl.ds(pl.multiple_of(i * small, small), small)
            y = y_ref[rows, :]
            center = y - average(y)
            scale = lax.rsqrt(average(center * center) + EPSILON)
            hat = center * scale
            out_ref[rows, :] = (hat * vec_ref[0:1, :] + vec_ref[1:2, :]).astype(BF16)
            hat_ref[rows, :] = hat.astype(BF16)
            scale_ref[rows, :] = jnp.broadcast_to(scale, (small, LANES))
            return carry

        for i in range(parts):
            lax.fori_loop(i * part // small, (i + 1) * part // small, finish, 0)
            for copy in stores[i][1:]:
                copy.start()
        for store in stores:
            for copy in store:
                copy.wait()


def feed_forward(hat, b, vec, firsts, seconds, plans, chunk=1024, tile=1024):
    tokens, width = hat.shape
    counts = (len(firsts), len(seconds))
    units = b.shape[1]
    acts = lambda: pl.BlockSpec((tokens, chunk), lambda c: (0, c))
    return pl.pallas_call(
        functools.partial(forward_kernel, tile=tile, counts=counts, chunk=chunk, plans=plans),
        grid=(units // chunk,),
        in_specs=[
            FAR,
            pl.BlockSpec((1, chunk), lambda c: (0, c)),
            whole_block(vec.shape),
        ]
        + [FAR] * sum(counts),
        out_specs=[acts(), acts()] + [FAR] * 4,
        out_shape=[
            jax.ShapeDtypeStruct((tokens, units), BF16),
            jax.ShapeDtypeStruct((tokens, units), BF16),
            jax.ShapeDtypeStruct((tokens, width), BF16),
            jax.ShapeDtypeStruct((tokens, width), BF16),
            jax.ShapeDtypeStruct((tokens, LANES), F32),
            jax.ShapeDtypeStruct((tokens, width), BF16),
        ],
        scratch_shapes=[
            pltpu.VMEM((tokens, width), F32),
            pltpu.VMEM((units, width), BF16),
            pltpu.VMEM((units, width), BF16),
            pltpu.VMEM((tokens, width), BF16),
            pltpu.VMEM((tokens, width), BF16),
            pltpu.VMEM((tokens, LANES), F32),
            pltpu.VMEM((tokens, width), BF16),
            pltpu.SemaphoreType.DMA((len(plans[0]),)),
            pltpu.SemaphoreType.DMA((len(plans[1]),)),
            pltpu.SemaphoreType.DMA((4, 5)),
        ],
        compiler_params=params(),
        cost_estimate=cost(4 * tokens * units * width, tokens * units, 50 << 20),
        name="feed_forward",
    )(hat, b, vec, *firsts, *seconds)


def backward_kernel(*refs, tile, counts, chunk, plans):
    g_far, hat_far, scale_far, u_far, vec_ref, act_ref, slope_ref = refs[:7]
    split = 7 + sum(counts)
    firsts, seconds = refs[7 : 7 + counts[0]], refs[7 + counts[0] : split]
    keep1_ref, keep2_ref, send1_ref, send2_ref, db_ref, du_far, sums_ref = refs[split : split + 7]
    e_ref, w1_ref, w2_ref, f_ref, g_ref, hat_ref, scale_ref, u_ref, du_ref = refs[
        split + 7 : split + 16
    ]
    sem1, sem2, sem3, sem4 = refs[split + 16 :]
    parts = 4
    part = u_ref.shape[0] // parts
    loads = []
    for i in range(parts):
        rows = pl.ds(i * part, part)
        loads.append(
            [
                pltpu.make_async_copy(far.at[rows, :], near.at[rows, :], sem3.at[i, j])
                for j, (far, near) in enumerate(
                    ((g_far, g_ref), (hat_far, hat_ref), (scale_far, scale_ref))
                )
            ]
        )
    load_u = pltpu.make_async_copy(u_far, u_ref, sem4.at[0])
    store_du = pltpu.make_async_copy(du_ref, du_far, sem4.at[1])

    @pl.when(pl.program_id(0) == 0)
    def _():
        for load in loads:
            for copy in load:
                copy.start()

    fetch_weights(seconds, plans[1], w2_ref, sem2, chunk)
    fetch_weights(firsts, plans[0], w1_ref, sem1, chunk)
    here = pl.ds(pl.multiple_of(pl.program_id(0) * chunk, chunk), chunk)

    @pl.when(pl.program_id(0) == 0)
    def _():
        small = 256
        sums_ref[...] = jnp.zeros_like(sums_ref)

        def begin(i, carry):
            rows = pl.ds(pl.multiple_of(i * small, small), small)
            g = g_ref[rows, :].astype(F32)
            hat = hat_ref[rows, :].astype(F32)
            dy = norm_back(g, hat, scale_ref[rows, :], vec_ref[0:1, :])
            du_ref[rows, :] = dy
            e_ref[rows, :] = dy.astype(BF16)
            sums_ref[0:8, :] += rows_of_eight(dy)
            sums_ref[8:16, :] += rows_of_eight(g * hat)
            sums_ref[16:24, :] += rows_of_eight(g)
            return carry

        load_u.start()
        for i in range(parts):
            for copy in loads[i]:
                copy.wait()
            lax.fori_loop(i * part // small, (i + 1) * part // small, begin, 0)
        load_u.wait()


    def step(i, db):
        rows = pl.ds(pl.multiple_of(i * tile, tile), tile)
        dz = product_turned(e_ref[rows, :], w2_ref[here, :]) * slope_ref[rows, :].astype(F32)
        low = dz.astype(BF16)
        f_ref[rows, :] = low
        du_ref[rows, :] += product(low, w1_ref[here, :])
        return db + rows_of_eight(dz)

    db = lax.fori_loop(0, u_ref.shape[0] // tile, step, jnp.zeros((8, chunk), F32))
    db_ref[...] = jnp.sum(db, axis=0, keepdims=True)

    @pl.when(pl.program_id(0) == pl.num_programs(0) - 1)
    def _():
        store_du.start()

    dw2 = product_over_rows(act_ref[...], e_ref[...]).astype(BF16)
    dw1 = product_over_rows(f_ref[...], u_ref[...]).astype(BF16)
    half = pl.num_programs(0) // 2

    @pl.when(pl.program_id(0) < half)
    def _():
        keep1_ref[...] = dw1
        keep2_ref[...] = dw2

    @pl.when(pl.program_id(0) >= half)
    def _():
        send1_ref[...] = dw1
        send2_ref[...] = dw2

    @pl.when(pl.program_id(0) == pl.num_programs(0) - 1)
    def _():
        store_du.wait()


def feed_backward(
    g, hat, scale, vec, u, act, slope, firsts, seconds, plans, chunk=512, tile=2048
):
    tokens, width = u.shape
    counts = (len(firsts), len(seconds))
    units = act.shape[1]
    half = units // chunk // 2
    acts = lambda: pl.BlockSpec((tokens, chunk), lambda c: (0, c))
    keep = lambda: pl.BlockSpec((chunk, width), lambda c: (jnp.minimum(c, half - 1), 0))
    send = lambda: pl.BlockSpec((chunk, width), lambda c: (jnp.maximum(c - half, 0), 0))
    grads = jax.ShapeDtypeStruct((units // 2, width), BF16)
    return pl.pallas_call(
        functools.partial(backward_kernel, tile=tile, counts=counts, chunk=chunk, plans=plans),
        grid=(units // chunk,),
        in_specs=[FAR] * 4
        + [whole_block(vec.shape), acts(), acts()]
        + [FAR] * sum(counts),
        out_specs=[
            keep(),
            keep(),
            send(),
            send(),
            pl.BlockSpec((1, chunk), lambda c: (0, c)),
            FAR,
            whole_block((24, width)),
        ],
        out_shape=[grads] * 4
        + [
            jax.ShapeDtypeStruct((1, units), F32),
            jax.ShapeDtypeStruct((tokens, width), F32),
            jax.ShapeDtypeStruct((24, width), F32),
        ],
        scratch_shapes=[
            pltpu.VMEM((tokens, width), BF16),
            pltpu.VMEM((units, width), BF16),
            pltpu.VMEM((units, width), BF16),
            pltpu.VMEM((tokens, chunk), BF16),
            pltpu.VMEM((tokens, width), BF16),
            pltpu.VMEM((tokens, width), BF16),
            pltpu.VMEM((tokens, LANES), F32),
            pltpu.VMEM((tokens, width), BF16),
            pltpu.VMEM((tokens, width), F32),
            pltpu.SemaphoreType.DMA((len(plans[0]),)),
            pltpu.SemaphoreType.DMA((len(plans[1]),)),
            pltpu.SemaphoreType.DMA((4, 3)),
            pltpu.SemaphoreType.DMA((2,)),
        ],
        compiler_params=params(),
        cost_estimate=cost(8 * tokens * units * width, 0, 60 << 20),
        name="feed_backward",
    )(g, hat, scale, u, vec, act, slope, *firsts, *seconds)


def table_pair(points):
    numbers = jnp.arange(points, dtype=jnp.int32)
    coarse = 32 * jnp.arange(points // 32, dtype=jnp.int32)
    fine = jnp.arange(32, dtype=jnp.int32)

    def waves(rows):
        angles = (rows[:, None] * numbers[None, :] % points).astype(F32) * (2.0 * math.pi / points)
        return jnp.cos(angles), jnp.sin(angles)

    factor = 1.0 / math.sqrt(points)
    if points <= 64:
        cosine, sine = waves(numbers)
    else:
        coarse_cos, coarse_sin = waves(coarse)
        fine_cos, fine_sin = waves(fine)
        coarse_cos, coarse_sin, fine_cos, fine_sin = lax.optimization_barrier(
            (coarse_cos, coarse_sin, fine_cos, fine_sin)
        )
        coarse_cos, coarse_sin = coarse_cos[:, None], coarse_sin[:, None]
        fine_cos, fine_sin = fine_cos[None], fine_sin[None]
        cosine = (coarse_cos * fine_cos - coarse_sin * fine_sin).reshape(points, points)
        sine = (coarse_sin * fine_cos + coarse_cos * fine_sin).reshape(points, points)
    return (cosine * factor).astype(BF16), (sine * factor).astype(BF16)


def twiddles():
    row_index = jnp.arange(L1, dtype=jnp.int32)[None, :]
    col_index = jnp.arange(L2, dtype=jnp.int32)[:, None]
    angles = (row_index * col_index % L).astype(F32) * (2.0 * math.pi / L)
    wave = jnp.cos(angles), jnp.sin(angles)
    return [jnp.broadcast_to(values[:, :, None], (L2, L1, LANES)) for values in wave]


def swap(values, step):
    axis, mask = step
    size = lax.axis_size(axis)
    return lax.ppermute(values, axis, [(i, i ^ mask) for i in range(size)])


def bits(size):
    masks = []
    mask = size // 2
    while mask >= 1:
        masks.append(mask)
        mask //= 2
    return masks


def widen(held, step):
    return jnp.concatenate([held, swap(held, step)], axis=0)


def widen_codes(codes, steps, groups):
    for axis, mask in steps:
        code = mask if axis == "seq" else mask * groups
        codes = codes + [held ^ code for held in codes]
    return codes


def spread(pieces, steps):
    for step in steps:
        pieces = pieces + [swap(piece, step) for piece in pieces]
    return pieces


def spread_core(pieces, step_core):
    return pieces + [swap(piece, step_core) for piece in pieces]


def pick(addend, extra):
    values, names, fixed = addend
    chosen = {**fixed, **extra}
    return values[tuple(chosen.get(name, slice(None)) for name in names)]


def total(addends, extra={}):
    parts = [pick(addend, extra) for addend in addends]
    return sum(parts[1:], parts[0].astype(F32))


def settle(addends, send, step):
    values, names, fixed = addends[-1]
    rest = [name for name in names if name not in fixed and name != step]
    kept = [(held, order, {**gone, step: 0}) for held, order, gone in addends]
    return kept + [(swap(send, step), rest, {})]


def fold(addends, step, kind):
    return settle(addends, total(addends, {step: 1}).astype(kind), step)


def after(addends, *others):
    values, names, fixed = addends[-1]
    results = lax.optimization_barrier((values,) + others)
    return (addends[:-1] + [(results[0], names, fixed)],) + tuple(results[1:])


def arrange(rows):
    return with_layout_constraint(rows.transpose(0, 2, 1, 3), Layout(major_to_minor=(0, 1, 2, 3)))


def exchange(rows):
    order = Layout(major_to_minor=(0, 1, 2, 3))
    rows = with_layout_constraint(rows, order)
    rows = lax.all_to_all(rows, "seq", split_axis=0, concat_axis=0, tiled=True)
    return with_layout_constraint(rows, order)


def body(tokens, lengths, labels, picked, cotangent, w_in, b_in, w_out, shifts, norm_gains):
    groups = lax.axis_size("seq")
    me = lax.axis_index("seq")
    here = lax.axis_index("batch") * groups + me
    columns = tokens.shape[2]
    share = w_in.shape[2]
    part = shifts.shape[2]
    blocks = groups * lax.axis_size("batch")

    masks = bits(groups)[:-1]
    steps_plane = [("seq", mask) for mask in masks[:1] + masks[:0:-1]]
    steps_seq = [("seq", mask) for mask in masks[::-1]]
    steps_batch = [("batch", mask) for mask in bits(lax.axis_size("batch"))]
    step_core = ("seq", 1)
    numbers = jnp.arange(blocks, dtype=jnp.int32)

    codes = widen_codes([0], steps_plane + steps_batch + [step_core], groups)
    owner = jnp.array(codes, dtype=jnp.int32) ^ here
    one_hot = (owner[:, None] == numbers[None, :]).astype(F32)

    wide_cos, wide_sin = table_pair(D)
    wide = jnp.concatenate([wide_cos, -wide_sin], axis=0)
    twiddle_cos, twiddle_sin = twiddles()
    short_cos, short_sin = table_pair(L1)
    long_cos, long_sin = table_pair(L2)
    short_table = jnp.concatenate([short_cos, short_sin], axis=0)
    long_table = jnp.stack([jnp.stack([long_cos, -long_sin]), jnp.stack([long_sin, long_cos])])
    both = jnp.eye(2, dtype=BF16)
    pair_table = jnp.einsum("qukm,bc->qkbcum", long_table, both).reshape(4 * L2, 4 * L2)

    length = lax.dynamic_slice_in_dim(lengths, me, 1)
    small = jnp.concatenate([b_in[0], shifts[0].reshape(-1), norm_gains[0].reshape(-1)])
    small = small.astype(F32)[None]
    first_held = w_in[0].T[None]
    second_held = w_out[0][None]
    tokens_late = arrange(tokens)
    steps_second = list(steps_plane)
    if len(steps_plane) == 3 and share % 8 == 0:
        steps_second = [steps_plane[0], steps_plane[2], steps_plane[1]]
    for number, step in enumerate(steps_plane[:-1]):
        first_held = widen(first_held, step)
        second_held = widen(second_held, steps_second[number])
        small = widen(small, step)
        if number == 0:
            tokens_late, small, first_held, second_held = lax.optimization_barrier(
                (tokens_late, small, first_held, second_held)
            )
            x_all = exchange(tokens_late)
    early = (wide, twiddle_cos, twiddle_sin, short_table, pair_table, arrange(cotangent))
    small, first_held, early = lax.optimization_barrier((small, first_held, early))
    wide, twiddle_cos, twiddle_sin, short_table, pair_table, late_cotangent = early
    first_held = widen(first_held, steps_plane[-1])
    seconds, codes_second = [], []
    base = widen_codes([0], steps_second[:-1], groups)
    for piece, turn in zip(spread([second_held], steps_batch), widen_codes([0], steps_batch, groups)):
        seconds += [piece, swap(piece, steps_second[-1])]
        codes_second += [[code ^ turn for code in base]]
        codes_second += [[code ^ turn ^ steps_second[-1][1] for code in base]]
    steps_small = steps_plane[:-1] + steps_batch + [step_core] + steps_plane[-1:]
    small_codes = widen_codes([0], steps_small, groups)
    for step in steps_batch + [step_core]:
        small = widen(small, step)
    small, first_held, second_held = lax.optimization_barrier((small, first_held, second_held))
    small = widen(small, steps_plane[-1])
    places = jnp.array([small_codes.index(code) for code in codes], dtype=jnp.int32)
    place_hot = (places[:, None] == numbers[None, :]).astype(F32)
    small = jnp.sum(place_hot[:, :, None] * small[None], axis=1)
    b_first = small[:, :share].reshape(1, blocks * share)
    rows = jnp.sum(one_hot[:, :, None] * small[:, None, share:], axis=0)
    rows = rows.reshape(blocks, 5, part).transpose(1, 0, 2).reshape(5, D)
    shifts_f = rows[:3]
    gains_f = rows[3:]
    blank = jnp.zeros((3, D), F32)
    vec = jnp.concatenate(
        [gains_f[1:2], shifts_f[2:3], gains_f[0:1], shifts_f[1:2], shifts_f[0:1], blank]
    )
    vec_one = vec[2:]
    vec_one = jnp.concatenate([vec_one, blank[:2]])
    base = widen_codes([0], steps_plane, groups)
    half = len(base) // 2
    turn = steps_batch[0][1] * groups
    firsts = [first_held] + [swap(first_held[k : k + half], steps_batch[0]) for k in (0, half)]
    codes_first = [base] + [[code ^ turn for code in base[k : k + half]] for k in (0, half)]
    x_all, late_cotangent, firsts[0], firsts[1], seconds, vec, vec_one, b_first = (
        lax.optimization_barrier(
            (x_all, late_cotangent, firsts[0], firsts[1], seconds, vec, vec_one, b_first)
        )
    )
    g_all = exchange(late_cotangent)
    for step in steps_batch[1:]:
        firsts = spread(firsts, [step])
        codes_first = codes_first + [
            [code ^ step[1] * groups for code in own] for own in codes_first
        ]
    x_rows = x_all.reshape(L2, L1, D)
    hat_one, scale_one = transform(
        length, x_rows, short_table, pair_table, twiddle_cos, twiddle_sin, wide
    )
    hat_one, firsts, seconds = lax.optimization_barrier((hat_one, firsts, seconds))
    plans = tuple(
        runs_of(own + [[code ^ 1 for code in held] for held in own], codes, share)
        for own in (codes_first, codes_second)
    )
    flat = lambda pieces: [piece.reshape(-1, D) for piece in spread_core(pieces, step_core)]
    firsts, seconds = flat(firsts), flat(seconds)
    act, slope, layer_out, hat_two, scale_two, u = feed_forward(
        hat_one, b_first, vec, firsts, seconds, plans
    )
    out_rows = exchange(layer_out.reshape(groups, columns, L1, D))

    keep_first, keep_second, send_first, send_second, grad_b_first, grad_u, sums_two = feed_backward(
        g_all.reshape(L, D), hat_two, scale_two, vec, u, act, slope, firsts, seconds, plans
    )
    names = steps_batch[::-1] + steps_plane[::-1]
    shape = (2,) * len(names) + (share,)
    came_first = swap(send_first, step_core)
    came_second = swap(send_second, step_core)
    grad_x, sums_one = transform_back(
        length, grad_u, hat_one, scale_one, short_table.T, pair_table.T,
        twiddle_cos, twiddle_sin, vec_one, wide
    )
    grad_x, came_first, came_second, out_rows = lax.optimization_barrier(
        (grad_x, came_first, came_second, out_rows)
    )
    grad_first, grad_second = [
        [(values.reshape(shape + (D,)), names, {}) for values in pair]
        for pair in ((keep_first, came_first), (keep_second, came_second))
    ]
    grad_x = grad_x.reshape(groups, columns, L1, D)
    input_grad = arrange(exchange(grad_x))

    shift_of = jnp.arange(columns, dtype=jnp.int32) + me * columns
    place_of = L2 * jnp.arange(L1, dtype=jnp.int32)[None, :] + shift_of[:, None]
    for step in steps_batch[::-1]:
        grad_first = fold(grad_first, step, BF16)
        grad_second = fold(grad_second, step, BF16)
    grad_first, out_rows, sums_one, sums_two, grad_b_first = after(
        grad_first, out_rows, sums_one, sums_two, grad_b_first
    )
    logits = out_rows.astype(F32)
    highest = jnp.max(logits, axis=-1, keepdims=True)
    powers = jnp.exp(logits - highest)
    denominator = jnp.sum(powers, axis=-1)
    features = jnp.arange(D, dtype=jnp.int32)
    label_rows = labels.transpose(0, 2, 1)
    top = jnp.sum(jnp.where(features == label_rows[..., None], powers, 0.0), axis=-1)
    counted = (picked.transpose(0, 2, 1) > 0) & (place_of[None] < lengths[:, None, None])
    weight = jnp.where(counted, 1.0, 0.0)
    sums = jnp.stack([jnp.sum(weight * (top / denominator)), jnp.sum(weight)])

    sums_two = jnp.sum(sums_two.reshape(3, 8, D), axis=1)
    sums_one = jnp.sum(sums_one.reshape(2, 8, D), axis=1)
    norms = jnp.stack([sums_two[0], sums_one[1], sums_two[2], sums_one[0], sums_two[1]])
    norms = norms.reshape(5, blocks, part).transpose(1, 0, 2).reshape(blocks, 5 * part)
    norms = jnp.sum(one_hot[:, :, None] * norms[None], axis=1)
    sums = jnp.broadcast_to(sums[None], (blocks, 2))
    small_grads = jnp.concatenate([grad_b_first.reshape(blocks, share), norms, sums], axis=1)
    half = blocks // 2
    arrived = swap(small_grads[half:], step_core)
    small = [
        (values.reshape(shape[:-1] + (-1,)), names, {}) for values in (small_grads[:half], arrived)
    ]
    for step in steps_batch[::-1]:
        small = fold(small, step, F32)
    for step in steps_seq:
        grad_first = fold(grad_first, step, BF16)
    current = out_rows
    for number, step in enumerate(steps_seq):
        small, latest, current = after(small, grad_second[-1][0], current)
        grad_second = grad_second[:-1] + [(latest,) + grad_second[-1][1:]]
        send = total(grad_second, {step: 1}).astype(BF16)
        if number == 0:
            send, current = lax.optimization_barrier((send, current))
            current = arrange(current)
        grad_second = settle(grad_second, send, step)
        small = fold(small, step, F32)
    small_grads, grad_first, grad_second = total(small), total(grad_first), total(grad_second)
    norms = small_grads[share:-2].reshape(5, part)
    match_rate = D * small_grads[-2] / jnp.maximum(small_grads[-1], 1.0)
    return (
        current,
        input_grad,
        grad_first.T[None],
        small_grads[:share][None],
        grad_second[None],
        norms[:3][None],
        norms[3:][None],
        match_rate,
    )


def solution(mesh):
    in_specs = (
        P("batch", None, "seq", None),
        P("batch"),
        P("batch", None, "seq"),
        P("batch", None, "seq"),
        P("batch", None, "seq", None),
        P(None, None, ("batch", "seq")),
        P(None, ("batch", "seq")),
        P(None, ("batch", "seq"), None),
        P(None, None, ("batch", "seq")),
        P(None, None, ("batch", "seq")),
    )
    out_specs = (
        P("batch", None, "seq", None),
        P("batch", None, "seq", None),
        P(None, None, ("batch", "seq")),
        P(None, ("batch", "seq")),
        P(None, ("batch", "seq"), None),
        P(None, None, ("batch", "seq")),
        P(None, None, ("batch", "seq")),
        P(),
    )
    return jax.shard_map(body, mesh=mesh, in_specs=in_specs, out_specs=out_specs, check_vma=False)
```

```python
import functools
import math

import jax
import jax.numpy as jnp
from jax import lax
from jax.experimental import pallas as pl
from jax.experimental.layout import Layout, with_layout_constraint
from jax.experimental.pallas import tpu as pltpu
from jax.sharding import PartitionSpec as P

D = 768
L1 = 64
L2 = 32
L = 2048
LANES = 128
PAIR = 4 * L2
STRIDE = PAIR + 1

EPSILON = 1e-12
ROOT_TWO_PI = 0.7978845608028654
CUBIC = ROOT_TWO_PI * 0.044715
F32 = jnp.float32
BF16 = jnp.bfloat16
VMEM_BYTES = 60 << 20
FAR = pl.BlockSpec(memory_space=pl.ANY)


def product(left, right):
    return lax.dot_general(left, right, (((1,), (0,)), ((), ())), preferred_element_type=F32)


def product_turned(left, right):
    return lax.dot_general(left, right, (((1,), (1,)), ((), ())), preferred_element_type=F32)


def product_over_rows(left, right):
    return lax.dot_general(left, right, (((0,), (0,)), ((), ())), preferred_element_type=F32)


def lanes(column):
    return jnp.concatenate([column] * (D // LANES), axis=1)


def rows_of_eight(values):
    return jnp.sum(values.reshape(-1, 8, values.shape[-1]), axis=0)


def average(values):
    return jnp.mean(values, axis=1, keepdims=True)


def norm_back(grad, x_hat, scale, gain):
    q = grad * gain
    return lanes(scale) * (q - average(q) - x_hat * average(q * x_hat))


def whole_block(shape):
    return pl.BlockSpec(shape, lambda c: (0,) * len(shape), pipeline_mode=pl.Buffered(1))


def params():
    return pltpu.CompilerParams(vmem_limit_bytes=VMEM_BYTES)


def cost(flops, transcendentals, size):
    return pl.CostEstimate(flops=flops, transcendentals=transcendentals, bytes_accessed=size)


def scatter(refs, start, value):
    for j, ref in enumerate(refs):
        ref[pl.ds(start, L2, stride=STRIDE), :] = value[:, j * LANES : (j + 1) * LANES]


def gather(refs, block):
    return jnp.concatenate([ref[pl.ds(block * STRIDE, PAIR), :] for ref in refs], axis=1)


def middle_scratch():
    return [pltpu.VMEM((L2 * STRIDE, LANES), F32)] * (D // LANES)


def transform_kernel(
    length_ref, x_ref, short_ref, pair_ref, cos_ref, sin_ref, wide_hbm,
    hat_ref, scale_ref, spec_ref, wide_ref, sem, *middle, group
):
    length = length_ref[0]
    step = pl.program_id(0)
    load = pltpu.make_async_copy(wide_hbm, wide_ref, sem.at[0])

    @pl.when(step == 0)
    def _():
        load.start()

        def first(m, carry):
            spots = L2 * lax.broadcasted_iota(jnp.int32, (L1, D), 0) + m
            x = jnp.where(spots < length, x_ref[m].astype(F32), 0.0).astype(BF16)
            y = product(short_ref[...], x)
            real, imag = y[:L1], y[L1:]
            cosine, sine = lanes(cos_ref[m]), lanes(sin_ref[m])
            turned = (real * cosine - imag * sine, real * sine + imag * cosine)
            for b in range(2):
                for part in range(2):
                    scatter(middle, (b * 2 + part) * L2 + m, turned[part][b * L2 : (b + 1) * L2])
            return carry

        lax.fori_loop(0, L2, first, 0, unroll=4)
        load.wait()

    for j in range(group):
        turned = gather(middle, step * group + j).astype(BF16)
        q = product(pair_ref[...], turned).astype(BF16)
        spec_ref[j * L1 : (j + 1) * L1, :D] = q[:L1]
        spec_ref[j * L1 : (j + 1) * L1, D:] = q[L1:]
    mixed = product(spec_ref[...], wide_ref[...])
    number = lax.broadcasted_iota(jnp.int32, (group * L1, D), 0)
    spots = L2 * (number % L1) + step * group + number // L1
    x = x_ref[pl.ds(step * group, group)].reshape(group * L1, D).astype(F32)
    h = jnp.where(spots < length, x, 0.0) + mixed
    center = h - average(h)
    scale = lax.rsqrt(average(center * center) + EPSILON)
    hat_ref[...] = center * scale
    scale_ref[...] = jnp.broadcast_to(scale, scale_ref.shape)


def transform(length, x, short, pair, cosine, sine, wide, group=8):
    out = lambda width: pl.BlockSpec((group * L1, width), lambda c: (c, 0))
    return pl.pallas_call(
        functools.partial(transform_kernel, group=group),
        grid=(L2 // group,),
        in_specs=[pl.BlockSpec(memory_space=pltpu.SMEM)]
        + [whole_block(values.shape) for values in (x, short, pair, cosine, sine)]
        + [FAR],
        out_specs=[out(D), out(LANES)],
        out_shape=[
            jax.ShapeDtypeStruct((L, D), F32),
            jax.ShapeDtypeStruct((L, LANES), F32),
        ],
        scratch_shapes=[
            pltpu.VMEM((group * L1, 2 * D), BF16),
            pltpu.VMEM((2 * D, D), BF16),
            pltpu.SemaphoreType.DMA((1,)),
        ]
        + middle_scratch(),
        compiler_params=params(),
        cost_estimate=cost(7 << 30, L, 24 << 20),
        name="transform",
    )(length, x, short, pair, cosine, sine, wide)


def back_kernel(
    length_ref, du_ref, hat_ref, scale_ref, short_ref, pair_ref, cos_ref, sin_ref, vec_ref, wide_ref,
    dx_ref, sums_ref, rh_ref, spec_ref, *middle, group
):
    length = length_ref[0]
    step = pl.program_id(0)
    steps = L2 // group

    @pl.when(step == 0)
    def _():
        sums_ref[...] = jnp.zeros_like(sums_ref)

    @pl.when(step < steps)
    def _():
        du = du_ref[...]
        hat = hat_ref[...]
        rh = norm_back(du, hat, scale_ref[...], vec_ref[0:1, :]).astype(BF16)
        rh_ref[pl.ds(pl.multiple_of(step * group * L1, group * L1), group * L1), :] = rh
        sums_ref[0:8, :] += rows_of_eight(du * hat)
        sums_ref[8:16, :] += rows_of_eight(du)
        real = product(rh, wide_ref[:D, :]).astype(BF16)
        imag = product(rh, wide_ref[D:, :]).astype(BF16)
        for j in range(group):
            spec_ref[j, :L1, :] = real[j * L1 : (j + 1) * L1]
            spec_ref[j, L1:, :] = imag[j * L1 : (j + 1) * L1]
            turned = product(pair_ref[...], spec_ref[j]).astype(BF16).astype(F32)
            for b in range(2):
                for part in range(2):
                    start = (b * 2 + part) * L2
                    spot = part * L1 + b * L2 + step * group + j
                    scatter(middle, spot, turned[start : start + L2])

    @pl.when(step >= steps)
    def _():
        def second(i, carry):
            m = (step - steps) * group + i
            turned = gather(middle, m)
            real, imag = turned[:L1], turned[L1:]
            cosine, sine = lanes(cos_ref[m]), lanes(sin_ref[m])
            back = jnp.concatenate(
                [
                    (real * cosine + imag * sine).astype(BF16),
                    (imag * cosine - real * sine).astype(BF16),
                ],
                axis=0,
            )
            rh = rh_ref[pl.ds(pl.multiple_of(m * L1, L1), L1), :].astype(F32)
            dx = rh + product(short_ref[...], back)
            spots = L2 * lax.broadcasted_iota(jnp.int32, (L1, D), 0) + m
            dx_ref[i] = jnp.where(spots < length, dx, 0.0).astype(BF16)
            return carry

        lax.fori_loop(0, group, second, 0, unroll=4)


def transform_back(length, du, hat, scale, short, pair, cosine, sine, vec, wide, group=8):
    steps = L2 // group
    rows = lambda width: pl.BlockSpec((group * L1, width), lambda c: (jnp.minimum(c, steps - 1), 0))
    return pl.pallas_call(
        functools.partial(back_kernel, group=group),
        grid=(2 * steps,),
        in_specs=[pl.BlockSpec(memory_space=pltpu.SMEM), rows(D), rows(D), rows(LANES)]
        + [whole_block(values.shape) for values in (short, pair, cosine, sine, vec, wide)],
        out_specs=[
            pl.BlockSpec((group, L1, D), lambda c: (jnp.maximum(c - steps, 0), 0, 0)),
            pl.BlockSpec((16, D), lambda c: (0, 0)),
        ],
        out_shape=[
            jax.ShapeDtypeStruct((L2, L1, D), BF16),
            jax.ShapeDtypeStruct((16, D), F32),
        ],
        scratch_shapes=[pltpu.VMEM((L, D), BF16), pltpu.VMEM((group, 2 * L1, D), BF16)]
        + middle_scratch(),
        compiler_params=params(),
        cost_estimate=cost(7 << 30, 0, 20 << 20),
        name="transform_back",
    )(length, du, hat, scale, short, pair, cosine, sine, vec, wide)


def fetch_weights(pieces, plan, holder, sems, chunk):
    step = pl.program_id(0)
    copies = [
        pltpu.make_async_copy(
            pieces[number].at[pl.ds(source, rows), :],
            holder.at[pl.ds(target, rows), :],
            sems.at[i],
        )
        for i, (target, number, source, rows) in enumerate(plan)
    ]

    @pl.when(step == 0)
    def _():
        for copy in copies:
            copy.start()

    for number in range(holder.shape[0] // chunk):
        needed = [copy for copy, run in zip(copies, plan) if run[0] // chunk == number]
        if needed:

            @pl.when(step == number)
            def _():
                for copy in needed:
                    copy.wait()


def runs_of(pieces_codes, codes, share):
    runs = []
    for number, own in enumerate(pieces_codes):
        spots = [codes.index(code) for code in own]
        for source, spot in enumerate(spots):
            if source and spot == spots[source - 1] + 1:
                target, piece, start, rows = runs[-1]
                runs[-1] = (target, piece, start, rows + share)
            else:
                runs.append((spot * share, number, source * share, share))
    return tuple(sorted(runs))


def forward_kernel(*refs, tile, counts, chunk, plans):
    first_hat_ref, b_ref, vec_ref = refs[:3]
    split = 3 + sum(counts)
    firsts, seconds = refs[3 : 3 + counts[0]], refs[3 + counts[0] : split]
    act_ref, slope_ref, out_far, hat_far, scale_far, u_far = refs[split : split + 6]
    y_ref, w1_ref, w2_ref, out_ref, hat_ref, scale_ref, u_ref, sem1, sem2, sem3 = refs[split + 6 :]
    parts = 4
    part = u_ref.shape[0] // parts
    tiles = u_ref.shape[0] // tile
    loads, stores = [], []
    for i in range(parts):
        rows = pl.ds(i * part, part)
        pairs = ((u_ref, u_far), (out_ref, out_far), (hat_ref, hat_far), (scale_ref, scale_far))
        loads.append(
            pltpu.make_async_copy(first_hat_ref.at[rows, :], y_ref.at[rows, :], sem3.at[i, 0])
        )
        stores.append(
            [
                pltpu.make_async_copy(near.at[rows, :], far.at[rows, :], sem3.at[i, 1 + j])
                for j, (near, far) in enumerate(pairs)
            ]
        )

    @pl.when(pl.program_id(0) == 0)
    def _():
        for load in loads:
            load.start()

    fetch_weights(firsts, plans[0], w1_ref, sem1, chunk)
    fetch_weights(seconds, plans[1], w2_ref, sem2, chunk)
    here = pl.ds(pl.multiple_of(pl.program_id(0) * chunk, chunk), chunk)

    @pl.when(pl.program_id(0) == 0)
    def _():
        small = 256

        def begin(i, carry):
            rows = pl.ds(pl.multiple_of(i * small, small), small)
            u = y_ref[rows, :] * vec_ref[2:3, :] + vec_ref[3:4, :]
            u_ref[rows, :] = u.astype(BF16)
            y_ref[rows, :] = u + vec_ref[4:5, :]
            return carry

        for i in range(parts):
            loads[i].wait()
            lax.fori_loop(i * part // small, (i + 1) * part // small, begin, 0)
            stores[i][0].start()


    def step(i, carry):
        rows = pl.ds(pl.multiple_of(i * tile, tile), tile)
        z = product_turned(u_ref[rows, :], w1_ref[here, :]) + b_ref[...]
        square = z * z
        t = jnp.tanh(z * (ROOT_TWO_PI + CUBIC * square))
        half = 0.5 + 0.5 * t
        a = z * half
        low = a.astype(BF16)
        act_ref[rows, :] = low
        slope = half + (a - a * t) * (ROOT_TWO_PI + (3.0 * CUBIC) * square)
        slope_ref[rows, :] = slope.astype(BF16)
        y_ref[rows, :] += product(low, w2_ref[here, :])
        return carry

    lax.fori_loop(0, tiles, step, 0)

    @pl.when(pl.program_id(0) == pl.num_programs(0) - 1)
    def _():
        small = 256

        def finish(i, carry):
            rows = pl.ds(pl.multiple_of(i * small, small), small)
            y = y_ref[rows, :]
            center = y - average(y)
            scale = lax.rsqrt(average(center * center) + EPSILON)
            hat = center * scale
            out_ref[rows, :] = (hat * vec_ref[0:1, :] + vec_ref[1:2, :]).astype(BF16)
            hat_ref[rows, :] = hat.astype(BF16)
            scale_ref[rows, :] = jnp.broadcast_to(scale, (small, LANES))
            return carry

        for i in range(parts):
            lax.fori_loop(i * part // small, (i + 1) * part // small, finish, 0)
            for copy in stores[i][1:]:
                copy.start()
        for store in stores:
            for copy in store:
                copy.wait()


def feed_forward(hat, b, vec, firsts, seconds, plans, chunk=1024, tile=1024):
    tokens, width = hat.shape
    counts = (len(firsts), len(seconds))
    units = b.shape[1]
    acts = lambda: pl.BlockSpec((tokens, chunk), lambda c: (0, c))
    return pl.pallas_call(
        functools.partial(forward_kernel, tile=tile, counts=counts, chunk=chunk, plans=plans),
        grid=(units // chunk,),
        in_specs=[
            FAR,
            pl.BlockSpec((1, chunk), lambda c: (0, c)),
            whole_block(vec.shape),
        ]
        + [FAR] * sum(counts),
        out_specs=[acts(), acts()] + [FAR] * 4,
        out_shape=[
            jax.ShapeDtypeStruct((tokens, units), BF16),
            jax.ShapeDtypeStruct((tokens, units), BF16),
            jax.ShapeDtypeStruct((tokens, width), BF16),
            jax.ShapeDtypeStruct((tokens, width), BF16),
            jax.ShapeDtypeStruct((tokens, LANES), F32),
            jax.ShapeDtypeStruct((tokens, width), BF16),
        ],
        scratch_shapes=[
            pltpu.VMEM((tokens, width), F32),
            pltpu.VMEM((units, width), BF16),
            pltpu.VMEM((units, width), BF16),
            pltpu.VMEM((tokens, width), BF16),
            pltpu.VMEM((tokens, width), BF16),
            pltpu.VMEM((tokens, LANES), F32),
            pltpu.VMEM((tokens, width), BF16),
            pltpu.SemaphoreType.DMA((len(plans[0]),)),
            pltpu.SemaphoreType.DMA((len(plans[1]),)),
            pltpu.SemaphoreType.DMA((4, 5)),
        ],
        compiler_params=params(),
        cost_estimate=cost(4 * tokens * units * width, tokens * units, 50 << 20),
        name="feed_forward",
    )(hat, b, vec, *firsts, *seconds)


def backward_kernel(*refs, tile, counts, chunk, plans):
    g_far, hat_far, scale_far, u_far, vec_ref, act_ref, slope_ref = refs[:7]
    split = 7 + sum(counts)
    firsts, seconds = refs[7 : 7 + counts[0]], refs[7 + counts[0] : split]
    keep1_ref, keep2_ref, send1_ref, send2_ref, db_ref, du_far, sums_ref = refs[split : split + 7]
    e_ref, w1_ref, w2_ref, f_ref, g_ref, hat_ref, scale_ref, u_ref, du_ref = refs[
        split + 7 : split + 16
    ]
    sem1, sem2, sem3, sem4 = refs[split + 16 :]
    parts = 4
    part = u_ref.shape[0] // parts
    loads = []
    for i in range(parts):
        rows = pl.ds(i * part, part)
        loads.append(
            [
                pltpu.make_async_copy(far.at[rows, :], near.at[rows, :], sem3.at[i, j])
                for j, (far, near) in enumerate(
                    ((g_far, g_ref), (hat_far, hat_ref), (scale_far, scale_ref))
                )
            ]
        )
    load_u = pltpu.make_async_copy(u_far, u_ref, sem4.at[0])
    store_du = pltpu.make_async_copy(du_ref, du_far, sem4.at[1])

    @pl.when(pl.program_id(0) == 0)
    def _():
        for load in loads:
            for copy in load:
                copy.start()

    fetch_weights(seconds, plans[1], w2_ref, sem2, chunk)
    fetch_weights(firsts, plans[0], w1_ref, sem1, chunk)
    here = pl.ds(pl.multiple_of(pl.program_id(0) * chunk, chunk), chunk)

    @pl.when(pl.program_id(0) == 0)
    def _():
        small = 256
        sums_ref[...] = jnp.zeros_like(sums_ref)

        def begin(i, carry):
            rows = pl.ds(pl.multiple_of(i * small, small), small)
            g = g_ref[rows, :].astype(F32)
            hat = hat_ref[rows, :].astype(F32)
            dy = norm_back(g, hat, scale_ref[rows, :], vec_ref[0:1, :])
            du_ref[rows, :] = dy
            e_ref[rows, :] = dy.astype(BF16)
            sums_ref[0:8, :] += rows_of_eight(dy)
            sums_ref[8:16, :] += rows_of_eight(g * hat)
            sums_ref[16:24, :] += rows_of_eight(g)
            return carry

        load_u.start()
        for i in range(parts):
            for copy in loads[i]:
                copy.wait()
            lax.fori_loop(i * part // small, (i + 1) * part // small, begin, 0)
        load_u.wait()


    def step(i, db):
        rows = pl.ds(pl.multiple_of(i * tile, tile), tile)
        dz = product_turned(e_ref[rows, :], w2_ref[here, :]) * slope_ref[rows, :].astype(F32)
        low = dz.astype(BF16)
        f_ref[rows, :] = low
        du_ref[rows, :] += product(low, w1_ref[here, :])
        return db + rows_of_eight(dz)

    db = lax.fori_loop(0, u_ref.shape[0] // tile, step, jnp.zeros((8, chunk), F32))
    db_ref[...] = jnp.sum(db, axis=0, keepdims=True)

    @pl.when(pl.program_id(0) == pl.num_programs(0) - 1)
    def _():
        store_du.start()

    dw2 = product_over_rows(act_ref[...], e_ref[...]).astype(BF16)
    dw1 = product_over_rows(f_ref[...], u_ref[...]).astype(BF16)
    half = pl.num_programs(0) // 2

    @pl.when(pl.program_id(0) < half)
    def _():
        keep1_ref[...] = dw1
        keep2_ref[...] = dw2

    @pl.when(pl.program_id(0) >= half)
    def _():
        send1_ref[...] = dw1
        send2_ref[...] = dw2

    @pl.when(pl.program_id(0) == pl.num_programs(0) - 1)
    def _():
        store_du.wait()


def feed_backward(
    g, hat, scale, vec, u, act, slope, firsts, seconds, plans, chunk=512, tile=2048
):
    tokens, width = u.shape
    counts = (len(firsts), len(seconds))
    units = act.shape[1]
    half = units // chunk // 2
    acts = lambda: pl.BlockSpec((tokens, chunk), lambda c: (0, c))
    keep = lambda: pl.BlockSpec((chunk, width), lambda c: (jnp.minimum(c, half - 1), 0))
    send = lambda: pl.BlockSpec((chunk, width), lambda c: (jnp.maximum(c - half, 0), 0))
    grads = jax.ShapeDtypeStruct((units // 2, width), BF16)
    return pl.pallas_call(
        functools.partial(backward_kernel, tile=tile, counts=counts, chunk=chunk, plans=plans),
        grid=(units // chunk,),
        in_specs=[FAR] * 4
        + [whole_block(vec.shape), acts(), acts()]
        + [FAR] * sum(counts),
        out_specs=[
            keep(),
            keep(),
            send(),
            send(),
            pl.BlockSpec((1, chunk), lambda c: (0, c)),
            FAR,
            whole_block((24, width)),
        ],
        out_shape=[grads] * 4
        + [
            jax.ShapeDtypeStruct((1, units), F32),
            jax.ShapeDtypeStruct((tokens, width), F32),
            jax.ShapeDtypeStruct((24, width), F32),
        ],
        scratch_shapes=[
            pltpu.VMEM((tokens, width), BF16),
            pltpu.VMEM((units, width), BF16),
            pltpu.VMEM((units, width), BF16),
            pltpu.VMEM((tokens, chunk), BF16),
            pltpu.VMEM((tokens, width), BF16),
            pltpu.VMEM((tokens, width), BF16),
            pltpu.VMEM((tokens, LANES), F32),
            pltpu.VMEM((tokens, width), BF16),
            pltpu.VMEM((tokens, width), F32),
            pltpu.SemaphoreType.DMA((len(plans[0]),)),
            pltpu.SemaphoreType.DMA((len(plans[1]),)),
            pltpu.SemaphoreType.DMA((4, 3)),
            pltpu.SemaphoreType.DMA((2,)),
        ],
        compiler_params=params(),
        cost_estimate=cost(8 * tokens * units * width, 0, 60 << 20),
        name="feed_backward",
    )(g, hat, scale, u, vec, act, slope, *firsts, *seconds)


def table_pair(points):
    numbers = jnp.arange(points, dtype=jnp.int32)
    coarse = 32 * jnp.arange(points // 32, dtype=jnp.int32)
    fine = jnp.arange(32, dtype=jnp.int32)

    def waves(rows):
        angles = (rows[:, None] * numbers[None, :] % points).astype(F32) * (2.0 * math.pi / points)
        return jnp.cos(angles), jnp.sin(angles)

    factor = 1.0 / math.sqrt(points)
    if points <= 64:
        cosine, sine = waves(numbers)
    else:
        coarse_cos, coarse_sin = waves(coarse)
        fine_cos, fine_sin = waves(fine)
        coarse_cos, coarse_sin, fine_cos, fine_sin = lax.optimization_barrier(
            (coarse_cos, coarse_sin, fine_cos, fine_sin)
        )
        coarse_cos, coarse_sin = coarse_cos[:, None], coarse_sin[:, None]
        fine_cos, fine_sin = fine_cos[None], fine_sin[None]
        cosine = (coarse_cos * fine_cos - coarse_sin * fine_sin).reshape(points, points)
        sine = (coarse_sin * fine_cos + coarse_cos * fine_sin).reshape(points, points)
    return (cosine * factor).astype(BF16), (sine * factor).astype(BF16)


def twiddles():
    row_index = jnp.arange(L1, dtype=jnp.int32)[None, :]
    col_index = jnp.arange(L2, dtype=jnp.int32)[:, None]
    angles = (row_index * col_index % L).astype(F32) * (2.0 * math.pi / L)
    wave = jnp.cos(angles), jnp.sin(angles)
    return [jnp.broadcast_to(values[:, :, None], (L2, L1, LANES)) for values in wave]


def swap(values, step):
    axis, mask = step
    size = lax.axis_size(axis)
    return lax.ppermute(values, axis, [(i, i ^ mask) for i in range(size)])


def bits(size):
    masks = []
    mask = size // 2
    while mask >= 1:
        masks.append(mask)
        mask //= 2
    return masks


def widen(held, step):
    return jnp.concatenate([held, swap(held, step)], axis=0)


def widen_codes(codes, steps, groups):
    for axis, mask in steps:
        code = mask if axis == "seq" else mask * groups
        codes = codes + [held ^ code for held in codes]
    return codes


def spread(pieces, steps):
    for step in steps:
        pieces = pieces + [swap(piece, step) for piece in pieces]
    return pieces


def spread_core(pieces, step_core):
    return pieces + [swap(piece, step_core) for piece in pieces]


def pick(addend, extra):
    values, names, fixed = addend
    chosen = {**fixed, **extra}
    return values[tuple(chosen.get(name, slice(None)) for name in names)]


def total(addends, extra={}):
    parts = [pick(addend, extra) for addend in addends]
    return sum(parts[1:], parts[0].astype(F32))


def settle(addends, send, step):
    values, names, fixed = addends[-1]
    rest = [name for name in names if name not in fixed and name != step]
    kept = [(held, order, {**gone, step: 0}) for held, order, gone in addends]
    return kept + [(swap(send, step), rest, {})]


def fold(addends, step, kind):
    return settle(addends, total(addends, {step: 1}).astype(kind), step)


def after(addends, *others):
    values, names, fixed = addends[-1]
    results = lax.optimization_barrier((values,) + others)
    return (addends[:-1] + [(results[0], names, fixed)],) + tuple(results[1:])


def arrange(rows):
    return with_layout_constraint(rows.transpose(0, 2, 1, 3), Layout(major_to_minor=(0, 1, 2, 3)))


def exchange(rows):
    order = Layout(major_to_minor=(0, 1, 2, 3))
    rows = with_layout_constraint(rows, order)
    rows = lax.all_to_all(rows, "seq", split_axis=0, concat_axis=0, tiled=True)
    return with_layout_constraint(rows, order)


def body(tokens, lengths, labels, picked, cotangent, w_in, b_in, w_out, shifts, norm_gains):
    groups = lax.axis_size("seq")
    me = lax.axis_index("seq")
    here = lax.axis_index("batch") * groups + me
    columns = tokens.shape[2]
    share = w_in.shape[2]
    part = shifts.shape[2]
    blocks = groups * lax.axis_size("batch")

    masks = bits(groups)[:-1]
    steps_plane = [("seq", mask) for mask in masks[:1] + masks[:0:-1]]
    steps_seq = [("seq", mask) for mask in masks[::-1]]
    steps_batch = [("batch", mask) for mask in bits(lax.axis_size("batch"))]
    step_core = ("seq", 1)
    numbers = jnp.arange(blocks, dtype=jnp.int32)

    codes = widen_codes([0], steps_plane + steps_batch + [step_core], groups)
    owner = jnp.array(codes, dtype=jnp.int32) ^ here
    one_hot = (owner[:, None] == numbers[None, :]).astype(F32)

    wide_cos, wide_sin = table_pair(D)
    wide = jnp.concatenate([wide_cos, -wide_sin], axis=0)
    twiddle_cos, twiddle_sin = twiddles()
    short_cos, short_sin = table_pair(L1)
    long_cos, long_sin = table_pair(L2)
    short_table = jnp.concatenate([short_cos, short_sin], axis=0)
    long_table = jnp.stack([jnp.stack([long_cos, -long_sin]), jnp.stack([long_sin, long_cos])])
    both = jnp.eye(2, dtype=BF16)
    pair_table = jnp.einsum("qukm,bc->qkbcum", long_table, both).reshape(4 * L2, 4 * L2)

    length = lax.dynamic_slice_in_dim(lengths, me, 1)
    small = jnp.concatenate([b_in[0], shifts[0].reshape(-1), norm_gains[0].reshape(-1)])
    small = small.astype(F32)[None]
    first_held = w_in[0].T[None]
    second_held = w_out[0][None]
    tokens_late = arrange(tokens)
    steps_second = list(steps_plane)
    if len(steps_plane) == 3 and share % 8 == 0:
        steps_second = [steps_plane[0], steps_plane[2], steps_plane[1]]
    for number, step in enumerate(steps_plane[:-1]):
        first_held = widen(first_held, step)
        second_held = widen(second_held, steps_second[number])
        small = widen(small, step)
        if number == 0:
            tokens_late, small, first_held, second_held = lax.optimization_barrier(
                (tokens_late, small, first_held, second_held)
            )
            x_all = exchange(tokens_late)
    early = (wide, twiddle_cos, twiddle_sin, short_table, pair_table, arrange(cotangent))
    small, first_held, early = lax.optimization_barrier((small, first_held, early))
    wide, twiddle_cos, twiddle_sin, short_table, pair_table, late_cotangent = early
    first_held = widen(first_held, steps_plane[-1])
    seconds, codes_second = [], []
    base = widen_codes([0], steps_second[:-1], groups)
    for piece, turn in zip(spread([second_held], steps_batch), widen_codes([0], steps_batch, groups)):
        seconds += [piece, swap(piece, steps_second[-1])]
        codes_second += [[code ^ turn for code in base]]
        codes_second += [[code ^ turn ^ steps_second[-1][1] for code in base]]
    steps_small = steps_plane[:-1] + steps_batch + [step_core] + steps_plane[-1:]
    small_codes = widen_codes([0], steps_small, groups)
    for step in steps_batch + [step_core]:
        small = widen(small, step)
    small, first_held, second_held = lax.optimization_barrier((small, first_held, second_held))
    small = widen(small, steps_plane[-1])
    places = jnp.array([small_codes.index(code) for code in codes], dtype=jnp.int32)
    place_hot = (places[:, None] == numbers[None, :]).astype(F32)
    small = jnp.sum(place_hot[:, :, None] * small[None], axis=1)
    b_first = small[:, :share].reshape(1, blocks * share)
    rows = jnp.sum(one_hot[:, :, None] * small[:, None, share:], axis=0)
    rows = rows.reshape(blocks, 5, part).transpose(1, 0, 2).reshape(5, D)
    shifts_f = rows[:3]
    gains_f = rows[3:]
    blank = jnp.zeros((3, D), F32)
    vec = jnp.concatenate(
        [gains_f[1:2], shifts_f[2:3], gains_f[0:1], shifts_f[1:2], shifts_f[0:1], blank]
    )
    vec_one = vec[2:]
    vec_one = jnp.concatenate([vec_one, blank[:2]])
    base = widen_codes([0], steps_plane, groups)
    half = len(base) // 2
    turn = steps_batch[0][1] * groups
    firsts = [first_held] + [swap(first_held[k : k + half], steps_batch[0]) for k in (0, half)]
    codes_first = [base] + [[code ^ turn for code in base[k : k + half]] for k in (0, half)]
    x_all, late_cotangent, firsts[0], firsts[1], seconds, vec, vec_one, b_first = (
        lax.optimization_barrier(
            (x_all, late_cotangent, firsts[0], firsts[1], seconds, vec, vec_one, b_first)
        )
    )
    g_all = exchange(late_cotangent)
    for step in steps_batch[1:]:
        firsts = spread(firsts, [step])
        codes_first = codes_first + [
            [code ^ step[1] * groups for code in own] for own in codes_first
        ]
    x_rows = x_all.reshape(L2, L1, D)
    hat_one, scale_one = transform(
        length, x_rows, short_table, pair_table, twiddle_cos, twiddle_sin, wide
    )
    hat_one, firsts, seconds = lax.optimization_barrier((hat_one, firsts, seconds))
    plans = tuple(
        runs_of(own + [[code ^ 1 for code in held] for held in own], codes, share)
        for own in (codes_first, codes_second)
    )
    flat = lambda pieces: [piece.reshape(-1, D) for piece in spread_core(pieces, step_core)]
    firsts, seconds = flat(firsts), flat(seconds)
    act, slope, layer_out, hat_two, scale_two, u = feed_forward(
        hat_one, b_first, vec, firsts, seconds, plans
    )
    out_rows = exchange(layer_out.reshape(groups, columns, L1, D))

    keep_first, keep_second, send_first, send_second, grad_b_first, grad_u, sums_two = feed_backward(
        g_all.reshape(L, D), hat_two, scale_two, vec, u, act, slope, firsts, seconds, plans
    )
    names = steps_batch[::-1] + steps_plane[::-1]
    shape = (2,) * len(names) + (share,)
    came_first = swap(send_first, step_core)
    came_second = swap(send_second, step_core)
    grad_x, sums_one = transform_back(
        length, grad_u, hat_one, scale_one, short_table.T, pair_table.T,
        twiddle_cos, twiddle_sin, vec_one, wide
    )
    grad_x, came_first, came_second, out_rows = lax.optimization_barrier(
        (grad_x, came_first, came_second, out_rows)
    )
    grad_first, grad_second = [
        [(values.reshape(shape + (D,)), names, {}) for values in pair]
        for pair in ((keep_first, came_first), (keep_second, came_second))
    ]
    grad_x = grad_x.reshape(groups, columns, L1, D)
    input_grad = arrange(exchange(grad_x))

    shift_of = jnp.arange(columns, dtype=jnp.int32) + me * columns
    place_of = L2 * jnp.arange(L1, dtype=jnp.int32)[None, :] + shift_of[:, None]
    for step in steps_batch[::-1]:
        grad_first = fold(grad_first, step, BF16)
        grad_second = fold(grad_second, step, BF16)
    grad_first, out_rows, sums_one, sums_two, grad_b_first = after(
        grad_first, out_rows, sums_one, sums_two, grad_b_first
    )
    logits = out_rows.astype(F32)
    highest = jnp.max(logits, axis=-1, keepdims=True)
    powers = jnp.exp(logits - highest)
    denominator = jnp.sum(powers, axis=-1)
    features = jnp.arange(D, dtype=jnp.int32)
    label_rows = labels.transpose(0, 2, 1)
    top = jnp.sum(jnp.where(features == label_rows[..., None], powers, 0.0), axis=-1)
    counted = (picked.transpose(0, 2, 1) > 0) & (place_of[None] < lengths[:, None, None])
    weight = jnp.where(counted, 1.0, 0.0)
    sums = jnp.stack([jnp.sum(weight * (top / denominator)), jnp.sum(weight)])

    sums_two = jnp.sum(sums_two.reshape(3, 8, D), axis=1)
    sums_one = jnp.sum(sums_one.reshape(2, 8, D), axis=1)
    norms = jnp.stack([sums_two[0], sums_one[1], sums_two[2], sums_one[0], sums_two[1]])
    norms = norms.reshape(5, blocks, part).transpose(1, 0, 2).reshape(blocks, 5 * part)
    norms = jnp.sum(one_hot[:, :, None] * norms[None], axis=1)
    sums = jnp.broadcast_to(sums[None], (blocks, 2))
    small_grads = jnp.concatenate([grad_b_first.reshape(blocks, share), norms, sums], axis=1)
    half = blocks // 2
    arrived = swap(small_grads[half:], step_core)
    small = [
        (values.reshape(shape[:-1] + (-1,)), names, {}) for values in (small_grads[:half], arrived)
    ]
    for step in steps_batch[::-1]:
        small = fold(small, step, F32)
    for step in steps_seq:
        grad_first = fold(grad_first, step, BF16)
    current = out_rows
    for number, step in enumerate(steps_seq):
        small, latest, current = after(small, grad_second[-1][0], current)
        grad_second = grad_second[:-1] + [(latest,) + grad_second[-1][1:]]
        if number + 1 == len(steps_seq):
            small, input_grad = after(small, input_grad)
        send = total(grad_second, {step: 1}).astype(BF16)
        if number == 0:
            send, current = lax.optimization_barrier((send, current))
            current = arrange(current)
        grad_second = settle(grad_second, send, step)
        small = fold(small, step, F32)
    small_grads, grad_first, grad_second = total(small), total(grad_first), total(grad_second)
    norms = small_grads[share:-2].reshape(5, part)
    match_rate = D * small_grads[-2] / jnp.maximum(small_grads[-1], 1.0)
    return (
        current,
        input_grad,
        grad_first.T[None],
        small_grads[:share][None],
        grad_second[None],
        norms[:3][None],
        norms[3:][None],
        match_rate,
    )


def solution(mesh):
    in_specs = (
        P("batch", None, "seq", None),
        P("batch"),
        P("batch", None, "seq"),
        P("batch", None, "seq"),
        P("batch", None, "seq", None),
        P(None, None, ("batch", "seq")),
        P(None, ("batch", "seq")),
        P(None, ("batch", "seq"), None),
        P(None, None, ("batch", "seq")),
        P(None, None, ("batch", "seq")),
    )
    out_specs = (
        P("batch", None, "seq", None),
        P("batch", None, "seq", None),
        P(None, None, ("batch", "seq")),
        P(None, ("batch", "seq")),
        P(None, ("batch", "seq"), None),
        P(None, None, ("batch", "seq")),
        P(None, None, ("batch", "seq")),
        P(),
    )
    return jax.shard_map(body, mesh=mesh, in_specs=in_specs, out_specs=out_specs, check_vma=False)
```

```python
import functools
import math

import jax
import jax.numpy as jnp
from jax import lax
from jax.experimental import pallas as pl
from jax.experimental.layout import Layout, with_layout_constraint
from jax.experimental.pallas import tpu as pltpu
from jax.sharding import PartitionSpec as P

D = 768
L1 = 64
L2 = 32
L = 2048
LANES = 128
PAIR = 4 * L2
STRIDE = PAIR + 1

EPSILON = 1e-12
ROOT_TWO_PI = 0.7978845608028654
CUBIC = ROOT_TWO_PI * 0.044715
F32 = jnp.float32
BF16 = jnp.bfloat16
VMEM_BYTES = 60 << 20
FAR = pl.BlockSpec(memory_space=pl.ANY)


def product(left, right):
    return lax.dot_general(left, right, (((1,), (0,)), ((), ())), preferred_element_type=F32)


def product_turned(left, right):
    return lax.dot_general(left, right, (((1,), (1,)), ((), ())), preferred_element_type=F32)


def product_over_rows(left, right):
    return lax.dot_general(left, right, (((0,), (0,)), ((), ())), preferred_element_type=F32)


def lanes(column):
    return jnp.concatenate([column] * (D // LANES), axis=1)


def rows_of_eight(values):
    return jnp.sum(values.reshape(-1, 8, values.shape[-1]), axis=0)


def average(values):
    return jnp.mean(values, axis=1, keepdims=True)


def norm_back(grad, x_hat, scale, gain):
    q = grad * gain
    return lanes(scale) * (q - average(q) - x_hat * average(q * x_hat))


def whole_block(shape):
    return pl.BlockSpec(shape, lambda c: (0,) * len(shape), pipeline_mode=pl.Buffered(1))


def params():
    return pltpu.CompilerParams(vmem_limit_bytes=VMEM_BYTES)


def cost(flops, transcendentals, size):
    return pl.CostEstimate(flops=flops, transcendentals=transcendentals, bytes_accessed=size)


def scatter(refs, start, value):
    for j, ref in enumerate(refs):
        ref[pl.ds(start, L2, stride=STRIDE), :] = value[:, j * LANES : (j + 1) * LANES]


def gather(refs, block):
    return jnp.concatenate([ref[pl.ds(block * STRIDE, PAIR), :] for ref in refs], axis=1)


def middle_scratch():
    return [pltpu.VMEM((L2 * STRIDE, LANES), F32)] * (D // LANES)


def transform_kernel(
    length_ref, x_ref, short_ref, pair_ref, cos_ref, sin_ref, wide_hbm,
    hat_ref, scale_ref, spec_ref, wide_ref, sem, *middle, group
):
    length = length_ref[0]
    step = pl.program_id(0)
    load = pltpu.make_async_copy(wide_hbm, wide_ref, sem.at[0])

    @pl.when(step == 0)
    def _():
        load.start()

        def first(m, carry):
            spots = L2 * lax.broadcasted_iota(jnp.int32, (L1, D), 0) + m
            x = jnp.where(spots < length, x_ref[m].astype(F32), 0.0).astype(BF16)
            y = product(short_ref[...], x)
            real, imag = y[:L1], y[L1:]
            cosine, sine = lanes(cos_ref[m]), lanes(sin_ref[m])
            turned = (real * cosine - imag * sine, real * sine + imag * cosine)
            for b in range(2):
                for part in range(2):
                    scatter(middle, (b * 2 + part) * L2 + m, turned[part][b * L2 : (b + 1) * L2])
            return carry

        lax.fori_loop(0, L2, first, 0, unroll=4)
        load.wait()

    for j in range(group):
        turned = gather(middle, step * group + j).astype(BF16)
        q = product(pair_ref[...], turned).astype(BF16)
        spec_ref[j * L1 : (j + 1) * L1, :D] = q[:L1]
        spec_ref[j * L1 : (j + 1) * L1, D:] = q[L1:]
    mixed = product(spec_ref[...], wide_ref[...])
    number = lax.broadcasted_iota(jnp.int32, (group * L1, D), 0)
    spots = L2 * (number % L1) + step * group + number // L1
    x = x_ref[pl.ds(step * group, group)].reshape(group * L1, D).astype(F32)
    h = jnp.where(spots < length, x, 0.0) + mixed
    center = h - average(h)
    scale = lax.rsqrt(average(center * center) + EPSILON)
    hat_ref[...] = center * scale
    scale_ref[...] = jnp.broadcast_to(scale, scale_ref.shape)


def transform(length, x, short, pair, cosine, sine, wide, group=8):
    out = lambda width: pl.BlockSpec((group * L1, width), lambda c: (c, 0))
    return pl.pallas_call(
        functools.partial(transform_kernel, group=group),
        grid=(L2 // group,),
        in_specs=[pl.BlockSpec(memory_space=pltpu.SMEM)]
        + [whole_block(values.shape) for values in (x, short, pair, cosine, sine)]
        + [FAR],
        out_specs=[out(D), out(LANES)],
        out_shape=[
            jax.ShapeDtypeStruct((L, D), F32),
            jax.ShapeDtypeStruct((L, LANES), F32),
        ],
        scratch_shapes=[
            pltpu.VMEM((group * L1, 2 * D), BF16),
            pltpu.VMEM((2 * D, D), BF16),
            pltpu.SemaphoreType.DMA((1,)),
        ]
        + middle_scratch(),
        compiler_params=params(),
        cost_estimate=cost(7 << 30, L, 24 << 20),
        name="transform",
    )(length, x, short, pair, cosine, sine, wide)


def back_kernel(
    length_ref, du_ref, hat_ref, scale_ref, short_ref, pair_ref, cos_ref, sin_ref, vec_ref, wide_ref,
    dx_ref, sums_ref, rh_ref, spec_ref, *middle, group
):
    length = length_ref[0]
    step = pl.program_id(0)
    steps = L2 // group

    @pl.when(step == 0)
    def _():
        sums_ref[...] = jnp.zeros_like(sums_ref)

    @pl.when(step < steps)
    def _():
        du = du_ref[...]
        hat = hat_ref[...]
        rh = norm_back(du, hat, scale_ref[...], vec_ref[0:1, :]).astype(BF16)
        rh_ref[pl.ds(pl.multiple_of(step * group * L1, group * L1), group * L1), :] = rh
        sums_ref[0:8, :] += rows_of_eight(du * hat)
        sums_ref[8:16, :] += rows_of_eight(du)
        real = product(rh, wide_ref[:D, :]).astype(BF16)
        imag = product(rh, wide_ref[D:, :]).astype(BF16)
        for j in range(group):
            spec_ref[j, :L1, :] = real[j * L1 : (j + 1) * L1]
            spec_ref[j, L1:, :] = imag[j * L1 : (j + 1) * L1]
            turned = product(pair_ref[...], spec_ref[j]).astype(BF16).astype(F32)
            for b in range(2):
                for part in range(2):
                    start = (b * 2 + part) * L2
                    spot = part * L1 + b * L2 + step * group + j
                    scatter(middle, spot, turned[start : start + L2])

    @pl.when(step >= steps)
    def _():
        def second(i, carry):
            m = (step - steps) * group + i
            turned = gather(middle, m)
            real, imag = turned[:L1], turned[L1:]
            cosine, sine = lanes(cos_ref[m]), lanes(sin_ref[m])
            back = jnp.concatenate(
                [
                    (real * cosine + imag * sine).astype(BF16),
                    (imag * cosine - real * sine).astype(BF16),
                ],
                axis=0,
            )
            rh = rh_ref[pl.ds(pl.multiple_of(m * L1, L1), L1), :].astype(F32)
            dx = rh + product(short_ref[...], back)
            spots = L2 * lax.broadcasted_iota(jnp.int32, (L1, D), 0) + m
            dx_ref[i] = jnp.where(spots < length, dx, 0.0).astype(BF16)
            return carry

        lax.fori_loop(0, group, second, 0, unroll=4)


def transform_back(length, du, hat, scale, short, pair, cosine, sine, vec, wide, group=8):
    steps = L2 // group
    rows = lambda width: pl.BlockSpec((group * L1, width), lambda c: (jnp.minimum(c, steps - 1), 0))
    return pl.pallas_call(
        functools.partial(back_kernel, group=group),
        grid=(2 * steps,),
        in_specs=[pl.BlockSpec(memory_space=pltpu.SMEM), rows(D), rows(D), rows(LANES)]
        + [whole_block(values.shape) for values in (short, pair, cosine, sine, vec, wide)],
        out_specs=[
            pl.BlockSpec((group, L1, D), lambda c: (jnp.maximum(c - steps, 0), 0, 0)),
            pl.BlockSpec((16, D), lambda c: (0, 0)),
        ],
        out_shape=[
            jax.ShapeDtypeStruct((L2, L1, D), BF16),
            jax.ShapeDtypeStruct((16, D), F32),
        ],
        scratch_shapes=[pltpu.VMEM((L, D), BF16), pltpu.VMEM((group, 2 * L1, D), BF16)]
        + middle_scratch(),
        compiler_params=params(),
        cost_estimate=cost(7 << 30, 0, 20 << 20),
        name="transform_back",
    )(length, du, hat, scale, short, pair, cosine, sine, vec, wide)


def fetch_weights(pieces, plan, holder, sems, chunk):
    step = pl.program_id(0)
    copies = [
        pltpu.make_async_copy(
            pieces[number].at[pl.ds(source, rows), :],
            holder.at[pl.ds(target, rows), :],
            sems.at[i],
        )
        for i, (target, number, source, rows) in enumerate(plan)
    ]

    @pl.when(step == 0)
    def _():
        for copy in copies:
            copy.start()

    for number in range(holder.shape[0] // chunk):
        needed = [copy for copy, run in zip(copies, plan) if run[0] // chunk == number]
        if needed:

            @pl.when(step == number)
            def _():
                for copy in needed:
                    copy.wait()


def runs_of(pieces_codes, codes, share):
    runs = []
    for number, own in enumerate(pieces_codes):
        spots = [codes.index(code) for code in own]
        for source, spot in enumerate(spots):
            if source and spot == spots[source - 1] + 1:
                target, piece, start, rows = runs[-1]
                runs[-1] = (target, piece, start, rows + share)
            else:
                runs.append((spot * share, number, source * share, share))
    return tuple(sorted(runs))


def forward_kernel(*refs, tile, counts, chunk, plans):
    first_hat_ref, b_ref, vec_ref = refs[:3]
    split = 3 + sum(counts)
    firsts, seconds = refs[3 : 3 + counts[0]], refs[3 + counts[0] : split]
    act_ref, slope_ref, out_far, hat_far, scale_far, u_far = refs[split : split + 6]
    y_ref, w1_ref, w2_ref, out_ref, hat_ref, scale_ref, u_ref, sem1, sem2, sem3 = refs[split + 6 :]
    parts = 4
    part = u_ref.shape[0] // parts
    tiles = u_ref.shape[0] // tile
    loads, stores = [], []
    for i in range(parts):
        rows = pl.ds(i * part, part)
        pairs = ((u_ref, u_far), (out_ref, out_far), (hat_ref, hat_far), (scale_ref, scale_far))
        loads.append(
            pltpu.make_async_copy(first_hat_ref.at[rows, :], y_ref.at[rows, :], sem3.at[i, 0])
        )
        stores.append(
            [
                pltpu.make_async_copy(near.at[rows, :], far.at[rows, :], sem3.at[i, 1 + j])
                for j, (near, far) in enumerate(pairs)
            ]
        )

    @pl.when(pl.program_id(0) == 0)
    def _():
        for load in loads:
            load.start()

    fetch_weights(firsts, plans[0], w1_ref, sem1, chunk)
    fetch_weights(seconds, plans[1], w2_ref, sem2, chunk)
    here = pl.ds(pl.multiple_of(pl.program_id(0) * chunk, chunk), chunk)

    @pl.when(pl.program_id(0) == 0)
    def _():
        small = 256

        def begin(i, carry):
            rows = pl.ds(pl.multiple_of(i * small, small), small)
            u = y_ref[rows, :] * vec_ref[2:3, :] + vec_ref[3:4, :]
            u_ref[rows, :] = u.astype(BF16)
            y_ref[rows, :] = u + vec_ref[4:5, :]
            return carry

        for i in range(parts):
            loads[i].wait()
            lax.fori_loop(i * part // small, (i + 1) * part // small, begin, 0)
            stores[i][0].start()


    def step(i, carry):
        rows = pl.ds(pl.multiple_of(i * tile, tile), tile)
        z = product_turned(u_ref[rows, :], w1_ref[here, :]) + b_ref[...]
        square = z * z
        t = jnp.tanh(z * (ROOT_TWO_PI + CUBIC * square))
        half = 0.5 + 0.5 * t
        a = z * half
        low = a.astype(BF16)
        act_ref[rows, :] = low
        slope = half + (a - a * t) * (ROOT_TWO_PI + (3.0 * CUBIC) * square)
        slope_ref[rows, :] = slope.astype(BF16)
        y_ref[rows, :] += product(low, w2_ref[here, :])
        return carry

    lax.fori_loop(0, tiles, step, 0)

    @pl.when(pl.program_id(0) == pl.num_programs(0) - 1)
    def _():
        small = 256

        def finish(i, carry):
            rows = pl.ds(pl.multiple_of(i * small, small), small)
            y = y_ref[rows, :]
            center = y - average(y)
            scale = lax.rsqrt(average(center * center) + EPSILON)
            hat = center * scale
            out_ref[rows, :] = (hat * vec_ref[0:1, :] + vec_ref[1:2, :]).astype(BF16)
            hat_ref[rows, :] = hat.astype(BF16)
            scale_ref[rows, :] = jnp.broadcast_to(scale, (small, LANES))
            return carry

        for i in range(parts):
            lax.fori_loop(i * part // small, (i + 1) * part // small, finish, 0)
            for copy in stores[i][1:]:
                copy.start()
        for store in stores:
            for copy in store:
                copy.wait()


def feed_forward(hat, b, vec, firsts, seconds, plans, chunk=1024, tile=1024):
    tokens, width = hat.shape
    counts = (len(firsts), len(seconds))
    units = b.shape[1]
    acts = lambda: pl.BlockSpec((tokens, chunk), lambda c: (0, c))
    return pl.pallas_call(
        functools.partial(forward_kernel, tile=tile, counts=counts, chunk=chunk, plans=plans),
        grid=(units // chunk,),
        in_specs=[
            FAR,
            pl.BlockSpec((1, chunk), lambda c: (0, c)),
            whole_block(vec.shape),
        ]
        + [FAR] * sum(counts),
        out_specs=[acts(), acts()] + [FAR] * 4,
        out_shape=[
            jax.ShapeDtypeStruct((tokens, units), BF16),
            jax.ShapeDtypeStruct((tokens, units), BF16),
            jax.ShapeDtypeStruct((tokens, width), BF16),
            jax.ShapeDtypeStruct((tokens, width), BF16),
            jax.ShapeDtypeStruct((tokens, LANES), F32),
            jax.ShapeDtypeStruct((tokens, width), BF16),
        ],
        scratch_shapes=[
            pltpu.VMEM((tokens, width), F32),
            pltpu.VMEM((units, width), BF16),
            pltpu.VMEM((units, width), BF16),
            pltpu.VMEM((tokens, width), BF16),
            pltpu.VMEM((tokens, width), BF16),
            pltpu.VMEM((tokens, LANES), F32),
            pltpu.VMEM((tokens, width), BF16),
            pltpu.SemaphoreType.DMA((len(plans[0]),)),
            pltpu.SemaphoreType.DMA((len(plans[1]),)),
            pltpu.SemaphoreType.DMA((4, 5)),
        ],
        compiler_params=params(),
        cost_estimate=cost(4 * tokens * units * width, tokens * units, 50 << 20),
        name="feed_forward",
    )(hat, b, vec, *firsts, *seconds)


def backward_kernel(*refs, tile, counts, chunk, plans):
    g_far, hat_far, scale_far, u_far, vec_ref, act_ref, slope_ref = refs[:7]
    split = 7 + sum(counts)
    firsts, seconds = refs[7 : 7 + counts[0]], refs[7 + counts[0] : split]
    keep1_ref, keep2_ref, send1_ref, send2_ref, db_ref, du_far, sums_ref = refs[split : split + 7]
    e_ref, w1_ref, w2_ref, f_ref, g_ref, hat_ref, scale_ref, u_ref, du_ref = refs[
        split + 7 : split + 16
    ]
    sem1, sem2, sem3, sem4 = refs[split + 16 :]
    parts = 4
    part = u_ref.shape[0] // parts
    loads = []
    for i in range(parts):
        rows = pl.ds(i * part, part)
        loads.append(
            [
                pltpu.make_async_copy(far.at[rows, :], near.at[rows, :], sem3.at[i, j])
                for j, (far, near) in enumerate(
                    ((g_far, g_ref), (hat_far, hat_ref), (scale_far, scale_ref))
                )
            ]
        )
    load_u = pltpu.make_async_copy(u_far, u_ref, sem4.at[0])
    store_du = pltpu.make_async_copy(du_ref, du_far, sem4.at[1])

    @pl.when(pl.program_id(0) == 0)
    def _():
        for load in loads:
            for copy in load:
                copy.start()

    fetch_weights(seconds, plans[1], w2_ref, sem2, chunk)
    fetch_weights(firsts, plans[0], w1_ref, sem1, chunk)
    here = pl.ds(pl.multiple_of(pl.program_id(0) * chunk, chunk), chunk)

    @pl.when(pl.program_id(0) == 0)
    def _():
        small = 256
        sums_ref[...] = jnp.zeros_like(sums_ref)

        def begin(i, carry):
            rows = pl.ds(pl.multiple_of(i * small, small), small)
            g = g_ref[rows, :].astype(F32)
            hat = hat_ref[rows, :].astype(F32)
            dy = norm_back(g, hat, scale_ref[rows, :], vec_ref[0:1, :])
            du_ref[rows, :] = dy
            e_ref[rows, :] = dy.astype(BF16)
            sums_ref[0:8, :] += rows_of_eight(dy)
            sums_ref[8:16, :] += rows_of_eight(g * hat)
            sums_ref[16:24, :] += rows_of_eight(g)
            return carry

        load_u.start()
        for i in range(parts):
            for copy in loads[i]:
                copy.wait()
            lax.fori_loop(i * part // small, (i + 1) * part // small, begin, 0)
        load_u.wait()


    def step(i, db):
        rows = pl.ds(pl.multiple_of(i * tile, tile), tile)
        dz = product_turned(e_ref[rows, :], w2_ref[here, :]) * slope_ref[rows, :].astype(F32)
        low = dz.astype(BF16)
        f_ref[rows, :] = low
        du_ref[rows, :] += product(low, w1_ref[here, :])
        return db + rows_of_eight(dz)

    db = lax.fori_loop(0, u_ref.shape[0] // tile, step, jnp.zeros((8, chunk), F32))
    db_ref[...] = jnp.sum(db, axis=0, keepdims=True)

    @pl.when(pl.program_id(0) == pl.num_programs(0) - 1)
    def _():
        store_du.start()

    dw2 = product_over_rows(act_ref[...], e_ref[...]).astype(BF16)
    dw1 = product_over_rows(f_ref[...], u_ref[...]).astype(BF16)
    half = pl.num_programs(0) // 2

    @pl.when(pl.program_id(0) < half)
    def _():
        keep1_ref[...] = dw1
        keep2_ref[...] = dw2

    @pl.when(pl.program_id(0) >= half)
    def _():
        send1_ref[...] = dw1
        send2_ref[...] = dw2

    @pl.when(pl.program_id(0) == pl.num_programs(0) - 1)
    def _():
        store_du.wait()


def feed_backward(
    g, hat, scale, vec, u, act, slope, firsts, seconds, plans, chunk=512, tile=2048
):
    tokens, width = u.shape
    counts = (len(firsts), len(seconds))
    units = act.shape[1]
    half = units // chunk // 2
    acts = lambda: pl.BlockSpec((tokens, chunk), lambda c: (0, c))
    keep = lambda: pl.BlockSpec((chunk, width), lambda c: (jnp.minimum(c, half - 1), 0))
    send = lambda: pl.BlockSpec((chunk, width), lambda c: (jnp.maximum(c - half, 0), 0))
    grads = jax.ShapeDtypeStruct((units // 2, width), BF16)
    return pl.pallas_call(
        functools.partial(backward_kernel, tile=tile, counts=counts, chunk=chunk, plans=plans),
        grid=(units // chunk,),
        in_specs=[FAR] * 4
        + [whole_block(vec.shape), acts(), acts()]
        + [FAR] * sum(counts),
        out_specs=[
            keep(),
            keep(),
            send(),
            send(),
            pl.BlockSpec((1, chunk), lambda c: (0, c)),
            FAR,
            whole_block((24, width)),
        ],
        out_shape=[grads] * 4
        + [
            jax.ShapeDtypeStruct((1, units), F32),
            jax.ShapeDtypeStruct((tokens, width), F32),
            jax.ShapeDtypeStruct((24, width), F32),
        ],
        scratch_shapes=[
            pltpu.VMEM((tokens, width), BF16),
            pltpu.VMEM((units, width), BF16),
            pltpu.VMEM((units, width), BF16),
            pltpu.VMEM((tokens, chunk), BF16),
            pltpu.VMEM((tokens, width), BF16),
            pltpu.VMEM((tokens, width), BF16),
            pltpu.VMEM((tokens, LANES), F32),
            pltpu.VMEM((tokens, width), BF16),
            pltpu.VMEM((tokens, width), F32),
            pltpu.SemaphoreType.DMA((len(plans[0]),)),
            pltpu.SemaphoreType.DMA((len(plans[1]),)),
            pltpu.SemaphoreType.DMA((4, 3)),
            pltpu.SemaphoreType.DMA((2,)),
        ],
        compiler_params=params(),
        cost_estimate=cost(8 * tokens * units * width, 0, 60 << 20),
        name="feed_backward",
    )(g, hat, scale, u, vec, act, slope, *firsts, *seconds)


def table_pair(points):
    numbers = jnp.arange(points, dtype=jnp.int32)
    coarse = 32 * jnp.arange(points // 32, dtype=jnp.int32)
    fine = jnp.arange(32, dtype=jnp.int32)

    def waves(rows):
        angles = (rows[:, None] * numbers[None, :] % points).astype(F32) * (2.0 * math.pi / points)
        return jnp.cos(angles), jnp.sin(angles)

    factor = 1.0 / math.sqrt(points)
    if points <= 64:
        cosine, sine = waves(numbers)
    else:
        coarse_cos, coarse_sin = waves(coarse)
        fine_cos, fine_sin = waves(fine)
        coarse_cos, coarse_sin, fine_cos, fine_sin = lax.optimization_barrier(
            (coarse_cos, coarse_sin, fine_cos, fine_sin)
        )
        coarse_cos, coarse_sin = coarse_cos[:, None], coarse_sin[:, None]
        fine_cos, fine_sin = fine_cos[None], fine_sin[None]
        cosine = (coarse_cos * fine_cos - coarse_sin * fine_sin).reshape(points, points)
        sine = (coarse_sin * fine_cos + coarse_cos * fine_sin).reshape(points, points)
    return (cosine * factor).astype(BF16), (sine * factor).astype(BF16)


def twiddles():
    row_index = jnp.arange(L1, dtype=jnp.int32)[None, :]
    col_index = jnp.arange(L2, dtype=jnp.int32)[:, None]
    angles = (row_index * col_index % L).astype(F32) * (2.0 * math.pi / L)
    wave = jnp.cos(angles), jnp.sin(angles)
    return [jnp.broadcast_to(values[:, :, None], (L2, L1, LANES)) for values in wave]


def swap(values, step):
    axis, mask = step
    size = lax.axis_size(axis)
    return lax.ppermute(values, axis, [(i, i ^ mask) for i in range(size)])


def bits(size):
    masks = []
    mask = size // 2
    while mask >= 1:
        masks.append(mask)
        mask //= 2
    return masks


def widen(held, step):
    return jnp.concatenate([held, swap(held, step)], axis=0)


def widen_codes(codes, steps, groups):
    for axis, mask in steps:
        code = mask if axis == "seq" else mask * groups
        codes = codes + [held ^ code for held in codes]
    return codes


def spread(pieces, steps):
    for step in steps:
        pieces = pieces + [swap(piece, step) for piece in pieces]
    return pieces


def spread_core(pieces, step_core):
    return pieces + [swap(piece, step_core) for piece in pieces]


def pick(addend, extra):
    values, names, fixed = addend
    chosen = {**fixed, **extra}
    return values[tuple(chosen.get(name, slice(None)) for name in names)]


def total(addends, extra={}):
    parts = [pick(addend, extra) for addend in addends]
    return sum(parts[1:], parts[0].astype(F32))


def settle(addends, send, step):
    values, names, fixed = addends[-1]
    rest = [name for name in names if name not in fixed and name != step]
    kept = [(held, order, {**gone, step: 0}) for held, order, gone in addends]
    return kept + [(swap(send, step), rest, {})]


def fold(addends, step, kind):
    return settle(addends, total(addends, {step: 1}).astype(kind), step)


def after(addends, *others):
    values, names, fixed = addends[-1]
    results = lax.optimization_barrier((values,) + others)
    return (addends[:-1] + [(results[0], names, fixed)],) + tuple(results[1:])


def arrange(rows):
    return with_layout_constraint(rows.transpose(0, 2, 1, 3), Layout(major_to_minor=(0, 1, 2, 3)))


def exchange(rows):
    order = Layout(major_to_minor=(0, 1, 2, 3))
    rows = with_layout_constraint(rows, order)
    rows = lax.all_to_all(rows, "seq", split_axis=0, concat_axis=0, tiled=True)
    return with_layout_constraint(rows, order)


def body(tokens, lengths, labels, picked, cotangent, w_in, b_in, w_out, shifts, norm_gains):
    groups = lax.axis_size("seq")
    me = lax.axis_index("seq")
    here = lax.axis_index("batch") * groups + me
    columns = tokens.shape[2]
    share = w_in.shape[2]
    part = shifts.shape[2]
    blocks = groups * lax.axis_size("batch")

    masks = bits(groups)[:-1]
    steps_plane = [("seq", mask) for mask in masks[:1] + masks[:0:-1]]
    steps_seq = [("seq", mask) for mask in masks[::-1]]
    steps_batch = [("batch", mask) for mask in bits(lax.axis_size("batch"))]
    step_core = ("seq", 1)
    numbers = jnp.arange(blocks, dtype=jnp.int32)

    codes = widen_codes([0], steps_plane + steps_batch + [step_core], groups)
    owner = jnp.array(codes, dtype=jnp.int32) ^ here
    one_hot = (owner[:, None] == numbers[None, :]).astype(F32)

    wide_cos, wide_sin = table_pair(D)
    wide = jnp.concatenate([wide_cos, -wide_sin], axis=0)
    twiddle_cos, twiddle_sin = twiddles()
    short_cos, short_sin = table_pair(L1)
    long_cos, long_sin = table_pair(L2)
    short_table = jnp.concatenate([short_cos, short_sin], axis=0)
    long_table = jnp.stack([jnp.stack([long_cos, -long_sin]), jnp.stack([long_sin, long_cos])])
    both = jnp.eye(2, dtype=BF16)
    pair_table = jnp.einsum("qukm,bc->qkbcum", long_table, both).reshape(4 * L2, 4 * L2)

    length = lax.dynamic_slice_in_dim(lengths, me, 1)
    small = jnp.concatenate([b_in[0], shifts[0].reshape(-1), norm_gains[0].reshape(-1)])
    small = small.astype(F32)[None]
    first_held = w_in[0].T[None]
    second_held = w_out[0][None]
    tokens_late = arrange(tokens)
    steps_second = list(steps_plane)
    if len(steps_plane) == 3 and share % 8 == 0:
        steps_second = [steps_plane[0], steps_plane[2], steps_plane[1]]
    for number, step in enumerate(steps_plane[:-1]):
        first_held = widen(first_held, step)
        second_held = widen(second_held, steps_second[number])
        small = widen(small, step)
        if number == 0:
            tokens_late, small, first_held, second_held = lax.optimization_barrier(
                (tokens_late, small, first_held, second_held)
            )
            x_all = exchange(tokens_late)
    early = (wide, twiddle_cos, twiddle_sin, short_table, pair_table, arrange(cotangent))
    small, first_held, early = lax.optimization_barrier((small, first_held, early))
    wide, twiddle_cos, twiddle_sin, short_table, pair_table, late_cotangent = early
    first_held = widen(first_held, steps_plane[-1])
    seconds, codes_second = [], []
    base = widen_codes([0], steps_second[:-1], groups)
    for piece, turn in zip(spread([second_held], steps_batch), widen_codes([0], steps_batch, groups)):
        seconds += [piece, swap(piece, steps_second[-1])]
        codes_second += [[code ^ turn for code in base]]
        codes_second += [[code ^ turn ^ steps_second[-1][1] for code in base]]
    steps_small = steps_plane[:-1] + steps_batch + [step_core] + steps_plane[-1:]
    small_codes = widen_codes([0], steps_small, groups)
    for step in steps_batch + [step_core]:
        small = widen(small, step)
    small, first_held, second_held = lax.optimization_barrier((small, first_held, second_held))
    small = widen(small, steps_plane[-1])
    places = jnp.array([small_codes.index(code) for code in codes], dtype=jnp.int32)
    place_hot = (places[:, None] == numbers[None, :]).astype(F32)
    small = jnp.sum(place_hot[:, :, None] * small[None], axis=1)
    b_first = small[:, :share].reshape(1, blocks * share)
    rows = jnp.sum(one_hot[:, :, None] * small[:, None, share:], axis=0)
    rows = rows.reshape(blocks, 5, part).transpose(1, 0, 2).reshape(5, D)
    shifts_f = rows[:3]
    gains_f = rows[3:]
    blank = jnp.zeros((3, D), F32)
    vec = jnp.concatenate(
        [gains_f[1:2], shifts_f[2:3], gains_f[0:1], shifts_f[1:2], shifts_f[0:1], blank]
    )
    vec_one = vec[2:]
    vec_one = jnp.concatenate([vec_one, blank[:2]])
    base = widen_codes([0], steps_plane, groups)
    half = len(base) // 2
    turn = steps_batch[0][1] * groups
    firsts = [first_held] + [swap(first_held[k : k + half], steps_batch[0]) for k in (0, half)]
    codes_first = [base] + [[code ^ turn for code in base[k : k + half]] for k in (0, half)]
    x_all, late_cotangent, firsts[0], firsts[1], seconds, vec, vec_one, b_first = (
        lax.optimization_barrier(
            (x_all, late_cotangent, firsts[0], firsts[1], seconds, vec, vec_one, b_first)
        )
    )
    g_all = exchange(late_cotangent)
    for step in steps_batch[1:]:
        firsts = spread(firsts, [step])
        codes_first = codes_first + [
            [code ^ step[1] * groups for code in own] for own in codes_first
        ]
    x_rows = x_all.reshape(L2, L1, D)
    hat_one, scale_one = transform(
        length, x_rows, short_table, pair_table, twiddle_cos, twiddle_sin, wide
    )
    hat_one, firsts, seconds = lax.optimization_barrier((hat_one, firsts, seconds))
    plans = tuple(
        runs_of(own + [[code ^ 1 for code in held] for held in own], codes, share)
        for own in (codes_first, codes_second)
    )
    flat = lambda pieces: [piece.reshape(-1, D) for piece in spread_core(pieces, step_core)]
    firsts, seconds = flat(firsts), flat(seconds)
    act, slope, layer_out, hat_two, scale_two, u = feed_forward(
        hat_one, b_first, vec, firsts, seconds, plans
    )
    out_rows = exchange(layer_out.reshape(groups, columns, L1, D))

    keep_first, keep_second, send_first, send_second, grad_b_first, grad_u, sums_two = feed_backward(
        g_all.reshape(L, D), hat_two, scale_two, vec, u, act, slope, firsts, seconds, plans
    )
    names = steps_batch[::-1] + steps_plane[::-1]
    shape = (2,) * len(names) + (share,)
    came_first = swap(send_first, step_core)
    grad_x, sums_one = transform_back(
        length, grad_u, hat_one, scale_one, short_table.T, pair_table.T,
        twiddle_cos, twiddle_sin, vec_one, wide
    )
    grad_x, came_first, send_second, out_rows = lax.optimization_barrier(
        (grad_x, came_first, send_second, out_rows)
    )
    came_second = swap(send_second, step_core)
    grad_first, grad_second = [
        [(values.reshape(shape + (D,)), names, {}) for values in pair]
        for pair in ((keep_first, came_first), (keep_second, came_second))
    ]
    grad_x = grad_x.reshape(groups, columns, L1, D)
    input_grad = arrange(exchange(grad_x))

    shift_of = jnp.arange(columns, dtype=jnp.int32) + me * columns
    place_of = L2 * jnp.arange(L1, dtype=jnp.int32)[None, :] + shift_of[:, None]
    for step in steps_batch[::-1]:
        grad_first = fold(grad_first, step, BF16)
        send = total(grad_second, {step: 1}).astype(BF16)
        send, out_rows = lax.optimization_barrier((send, out_rows))
        grad_second = settle(grad_second, send, step)
    grad_first, out_rows, sums_one, sums_two, grad_b_first = after(
        grad_first, out_rows, sums_one, sums_two, grad_b_first
    )
    logits = out_rows.astype(F32)
    highest = jnp.max(logits, axis=-1, keepdims=True)
    powers = jnp.exp(logits - highest)
    denominator = jnp.sum(powers, axis=-1)
    features = jnp.arange(D, dtype=jnp.int32)
    label_rows = labels.transpose(0, 2, 1)
    top = jnp.sum(jnp.where(features == label_rows[..., None], powers, 0.0), axis=-1)
    counted = (picked.transpose(0, 2, 1) > 0) & (place_of[None] < lengths[:, None, None])
    weight = jnp.where(counted, 1.0, 0.0)
    sums = jnp.stack([jnp.sum(weight * (top / denominator)), jnp.sum(weight)])

    sums_two = jnp.sum(sums_two.reshape(3, 8, D), axis=1)
    sums_one = jnp.sum(sums_one.reshape(2, 8, D), axis=1)
    norms = jnp.stack([sums_two[0], sums_one[1], sums_two[2], sums_one[0], sums_two[1]])
    norms = norms.reshape(5, blocks, part).transpose(1, 0, 2).reshape(blocks, 5 * part)
    norms = jnp.sum(one_hot[:, :, None] * norms[None], axis=1)
    sums = jnp.broadcast_to(sums[None], (blocks, 2))
    small_grads = jnp.concatenate([grad_b_first.reshape(blocks, share), norms, sums], axis=1)
    half = blocks // 2
    arrived = swap(small_grads[half:], step_core)
    small = [
        (values.reshape(shape[:-1] + (-1,)), names, {}) for values in (small_grads[:half], arrived)
    ]
    for step in steps_batch[::-1]:
        small = fold(small, step, F32)
    for step in steps_seq:
        grad_first = fold(grad_first, step, BF16)
    current = out_rows
    for number, step in enumerate(steps_seq):
        small, latest, current = after(small, grad_second[-1][0], current)
        grad_second = grad_second[:-1] + [(latest,) + grad_second[-1][1:]]
        if number + 1 == len(steps_seq):
            small, input_grad = after(small, input_grad)
        send = total(grad_second, {step: 1}).astype(BF16)
        if number == 0:
            send, current = lax.optimization_barrier((send, current))
            current = arrange(current)
        grad_second = settle(grad_second, send, step)
        small = fold(small, step, F32)
    small_grads, grad_first, grad_second = total(small), total(grad_first), total(grad_second)
    norms = small_grads[share:-2].reshape(5, part)
    match_rate = D * small_grads[-2] / jnp.maximum(small_grads[-1], 1.0)
    return (
        current,
        input_grad,
        grad_first.T[None],
        small_grads[:share][None],
        grad_second[None],
        norms[:3][None],
        norms[3:][None],
        match_rate,
    )


def solution(mesh):
    in_specs = (
        P("batch", None, "seq", None),
        P("batch"),
        P("batch", None, "seq"),
        P("batch", None, "seq"),
        P("batch", None, "seq", None),
        P(None, None, ("batch", "seq")),
        P(None, ("batch", "seq")),
        P(None, ("batch", "seq"), None),
        P(None, None, ("batch", "seq")),
        P(None, None, ("batch", "seq")),
    )
    out_specs = (
        P("batch", None, "seq", None),
        P("batch", None, "seq", None),
        P(None, None, ("batch", "seq")),
        P(None, ("batch", "seq")),
        P(None, ("batch", "seq"), None),
        P(None, None, ("batch", "seq")),
        P(None, None, ("batch", "seq")),
        P(),
    )
    return jax.shard_map(body, mesh=mesh, in_specs=in_specs, out_specs=out_specs, check_vma=False)
```
